32 devices in a mesh: dp: 8 (over z, y), seq: 4 (over x, core).
Axes of the slice: x: 2, y: 2, z: 4, core: 2. Of those that a mesh axis runs over, the one named last changes fastest.
Arguments:
- tokens: bfloat16 [24, 1024, 768], P('dp', 'seq'), may hold values from -6 to 6
- prefix_len: int32 [24], P('dp'), may hold values from 0 to 1023
- timestep: int32 [24], P('dp'), may hold values from 1 to 1023
- norm_gain: bfloat16 [768], P('dp'), may hold values from 0.25 to 1.75
- norm_bias: bfloat16 [768], P('dp'), may hold values from -4 to 4
- proj_in: bfloat16 [768, 2304], P('dp'), may hold values from -0.21875 to 0.21875
- proj_in_bias: bfloat16 [2304], P('dp'), may hold values from -4 to 4
- proj_out: bfloat16 [768, 768], P('dp'), may hold values from -0.875 to 0.875
- proj_out_bias: bfloat16 [768], P('dp'), may hold values from -4 to 4
- time_table: bfloat16 [1024, 768], P('dp'), may hold values from -6 to 6
- ada_weight: bfloat16 [768, 2304], P('dp'), may hold values from -0.21875 to 0.21875
- ada_bias: bfloat16 [2304], P('dp'), may hold values from -6 to 6
- mlp_up: bfloat16 [768, 3072], P('dp'), may hold values from -0.21875 to 0.21875
- mlp_up_bias: bfloat16 [3072], P('dp'), may hold values from -4 to 4
- mlp_down: bfloat16 [3072, 768], P('dp'), may hold values from -0.109375 to 0.109375
- mlp_down_bias: bfloat16 [768], P('dp'), may hold values from -4 to 4
- out_grad: bfloat16 [24, 1024, 768], P('dp', 'seq'), may hold values from -6 to 6
Outputs:
- block_out: bfloat16 [24, 1024, 768], P('dp', 'seq')
- tokens_grad: float32 [24, 1024, 768], P('dp', 'seq')
- norm_gain_grad: float32 [768], P('dp')
- norm_bias_grad: float32 [768], P('dp')
- proj_in_grad: float32 [768, 2304], P('dp')
- proj_in_bias_grad: float32 [2304], P('dp')
- proj_out_grad: float32 [768, 768], P('dp')
- proj_out_bias_grad: float32 [768], P('dp')
- time_table_grad: float32 [1024, 768], P('dp')
- ada_weight_grad: float32 [768, 2304], P('dp')
- ada_bias_grad: float32 [2304], P('dp')
- mlp_up_grad: float32 [768, 3072], P('dp')
- mlp_up_bias_grad: float32 [3072], P('dp')
- mlp_down_grad: float32 [3072, 768], P('dp')
- mlp_down_bias_grad: float32 [768], P('dp')
The draws below stay inside these ranges and needn't reach their ends.
All inputs are finite; a program needn't handle non-finite values.
Results may differ from the reference program's by a relative error of at most 0.012.
Values may be sent and summed in bfloat16 or wider, within the bound.
No kernel may reach another device: no remote copies, remote signals or barrier semaphores. Data moves between devices by JAX's collectives and lax.ppermute only.
A program may use at most 192 MiB of HBM per device.

```python
import math
import jax
import jax.numpy as jnp
from jax import lax

D = 768
H = 12
HD = 64
FF = 3072
TC = 768
NT = 1024
LENGTH = 1024
SEQS = 24


def touch_ends(entries, stream_key, smallest, high):
    place = [jax.random.randint(jax.random.fold_in(stream_key, axis), (), 0, length) for axis, length in enumerate(entries.shape)]
    main_axis = entries.shape.index(max(entries.shape))
    neighbour = place[:main_axis] + [(place[main_axis] + 1) % entries.shape[main_axis]] + place[main_axis + 1:]
    return entries.at[tuple(place)].set(smallest).at[tuple(neighbour)].set(high)


def levels(key, shape, shards, smallest, top_value):
    factor_of, own = 1.0, jax.random.fold_in(key, 6)
    for position, shards_of in shards:
        draws = jnp.exp(jax.random.uniform(jax.random.fold_in(own, position), (shards_of,), jnp.float32, smallest / len(shards), top_value / len(shards)))
        factor_of = factor_of * jnp.repeat(draws, shape[position] // shards_of).reshape([-1 if axis == position else 1 for axis in range(len(shape))])
    return factor_of


def gaussian(key, extent, deviation, reach, cuts=(), kind=jnp.bfloat16):
    entries = deviation * jax.random.normal(key, extent, jnp.float32)
    if cuts:
        entries = entries * levels(key, extent, cuts, -0.22, 0.18)
    return jnp.clip(entries, -reach, reach).astype(kind)


def setup_inputs(seed: int = 0) -> dict:
    keys = jax.random.split(jax.random.key(seed), 18)
    tokens = gaussian(keys[0], (SEQS, LENGTH, D), 1.0, 6.0, ((0, 8), (1, 4)))
    prefix_len = touch_ends(jax.random.randint(keys[1], (SEQS,), 0, LENGTH), jax.random.fold_in(keys[1], 1), 0, LENGTH - 1).astype(jnp.int32)
    timestep = touch_ends(jax.random.randint(keys[2], (SEQS,), 1, NT), jax.random.fold_in(keys[2], 1), 1, NT - 1).astype(jnp.int32)
    norm_gain = jnp.clip(1.0 + 0.15 * jax.random.normal(keys[3], (D,), jnp.float32), 0.25, 1.75).astype(jnp.bfloat16)
    norm_bias = gaussian(keys[4], (D,), 0.3, 4.0, ((0, 8),))
    proj_in = gaussian(keys[5], (D, 3 * D), D ** -0.5, 0.21875, ((0, 8),))
    proj_in_bias = gaussian(keys[6], (3 * D,), 0.3, 4.0, ((0, 8),))
    proj_out = gaussian(keys[7], (D, D), (D // 16) ** -0.5, 0.875, ((0, 8),))
    proj_out_bias = gaussian(keys[8], (D,), 0.3, 4.0, ((0, 8),))
    time_table = gaussian(keys[9], (NT, TC), 1.0, 6.0, ((0, 8),))
    ada_weight = gaussian(keys[10], (TC, 3 * D), TC ** -0.5, 0.21875, ((0, 8),))
    ada_bias = gaussian(keys[11], (3 * D,), 0.5, 6.0, ((0, 8),))
    mlp_up = gaussian(keys[12], (D, FF), D ** -0.5, 0.21875, ((0, 8),))
    mlp_up_bias = gaussian(keys[13], (FF,), 0.3, 4.0, ((0, 8),))
    mlp_down = gaussian(keys[14], (FF, D), FF ** -0.5, 0.109375, ((0, 8),))
    mlp_down_bias = gaussian(keys[15], (D,), 0.3, 4.0, ((0, 8),))
    out_grad = gaussian(keys[16], (SEQS, LENGTH, D), 1.0, 6.0, ((0, 8), (1, 4)))
    return {"tokens": tokens, "prefix_len": prefix_len, "timestep": timestep, "norm_gain": norm_gain, "norm_bias": norm_bias, "proj_in": proj_in, "proj_in_bias": proj_in_bias, "proj_out": proj_out, "proj_out_bias": proj_out_bias, "time_table": time_table, "ada_weight": ada_weight, "ada_bias": ada_bias, "mlp_up": mlp_up, "mlp_up_bias": mlp_up_bias, "mlp_down": mlp_down, "mlp_down_bias": mlp_down_bias, "out_grad": out_grad}


@jax.custom_vjp
def low(v):
    return lax.optimization_barrier(v.astype(jnp.bfloat16)).astype(jnp.float32)

@jax.custom_vjp
def low_back(v):
    return v

def low_keep(v):
    return (low(v), None)

def low_pass(kept, grad):
    return (grad,)

def back_keep(v):
    return (v, None)

def back_low(kept, grad):
    return (low(grad),)
low.defvjp(low_keep, low_pass)
low_back.defvjp(back_keep, back_low)
eps = 1e-05
neg_fill = -1e+30
highest = lax.Precision.HIGHEST

def standardize(values):
    centred = values - lax.optimization_barrier(jnp.mean(values, axis=-1, keepdims=True))
    inverse = lax.rsqrt(lax.optimization_barrier(jnp.mean(centred * centred, axis=-1, keepdims=True)) + eps)
    return centred * inverse

def rotary_tables(positions, half_width):
    frequency = jnp.exp(jnp.arange(half_width, dtype=jnp.float32) * (-math.log(10000.0) / half_width))
    angles = positions.astype(jnp.float32)[:, None] * frequency[None, :]
    return (jnp.cos(angles), jnp.sin(angles))

def rotate(values, cosine, sine_table):
    half_width = cosine.shape[-1]
    front_half = values[..., :half_width]
    back_half = values[..., half_width:]
    cos_wide = cosine[:, None, :]
    sin_wide = sine_table[:, None, :]
    return jnp.concatenate([front_half * cos_wide - back_half * sin_wide, back_half * cos_wide + front_half * sin_wide], axis=-1)

def matmul(left, right):
    return jnp.dot(left, right, precision=highest, preferred_element_type=jnp.float32)

def group_forward(packed, params):
    tokens_g, prefix_g, step_g = packed
    norm_gain, norm_bias, proj_in, proj_in_bias, proj_out, proj_out_bias, time_table, ada_weight, ada_bias, mlp_up, mlp_up_bias, mlp_down, mlp_down_bias = params
    count = tokens_g.shape[0]
    length = tokens_g.shape[1]
    rows = tokens_g.reshape(-1, D)
    attn_input = low(standardize(rows) * norm_gain + norm_bias)
    projected = low_back(matmul(attn_input, proj_in) + proj_in_bias)
    projected = projected.reshape(count, length, 3, H, HD)
    positions = jnp.arange(length, dtype=jnp.int32)
    cosine, sine_table = rotary_tables(positions, HD // 2)
    queries = low(low_back(rotate(projected[:, :, 0], cosine, sine_table)))
    key_rows = low(low_back(rotate(projected[:, :, 1], cosine, sine_table)))
    values = low(low_back(projected[:, :, 2]))
    scores = low_back(jnp.einsum('gqhd,gkhd->ghqk', queries, key_rows, precision=highest) * HD ** (-0.5))
    clean = positions[None, :] < prefix_g[:, None]
    visible = jnp.logical_or(jnp.logical_not(clean)[:, :, None], clean[:, None, :])
    scores = jnp.where(visible[:, None], scores, neg_fill)
    row_max = lax.optimization_barrier(jnp.max(scores, axis=-1, keepdims=True))
    exponent = jnp.exp(scores - row_max)
    probs = low(exponent / lax.optimization_barrier(jnp.sum(exponent, axis=-1, keepdims=True)))
    mixed_out = jnp.einsum('ghqk,gkhd->gqhd', probs, values, precision=highest)
    mixed_out = low(low_back(mixed_out)).reshape(-1, D)
    attn_out = low_back(matmul(mixed_out, proj_out) + proj_out_bias)
    residual_one = rows + attn_out
    steps_tok = jnp.where(clean, 0, step_g[:, None]).reshape(-1).astype(jnp.int32)
    embedded = jnp.take(time_table, steps_tok, axis=0)
    activated = low(jax.nn.silu(embedded))
    modulation = low_back(matmul(activated, ada_weight) + ada_bias)
    shift_mod = modulation[:, :D]
    scale_mod = modulation[:, D:2 * D]
    gate_mod = modulation[:, 2 * D:]
    mlp_input = low(standardize(residual_one) * (1.0 + scale_mod) + shift_mod)
    pre_act = low_back(matmul(mlp_input, mlp_up) + mlp_up_bias)
    hidden = low(jax.nn.gelu(pre_act, approximate=False))
    branch = low_back(matmul(hidden, mlp_down) + mlp_down_bias)
    return (residual_one + gate_mod * branch).reshape(count, length, D)

def forward_all(tokens_in, params, prefix_len, timestep):
    group_size = math.gcd(SEQS, 2)
    blocks = SEQS // group_size
    packed = (tokens_in.reshape(blocks, group_size, LENGTH, D), prefix_len.reshape(blocks, group_size), timestep.reshape(blocks, group_size))
    checked = jax.checkpoint(group_forward)

    def map_step(element):
        return checked(element, params)
    stacked = lax.map(map_step, packed)
    return stacked.reshape(SEQS, LENGTH, D)

def reference(tokens, prefix_len, timestep, norm_gain, norm_bias, proj_in, proj_in_bias, proj_out, proj_out_bias, time_table, ada_weight, ada_bias, mlp_up, mlp_up_bias, mlp_down, mlp_down_bias, out_grad):
    params = tuple((weight.astype(jnp.float32) for weight in (norm_gain, norm_bias, proj_in, proj_in_bias, proj_out, proj_out_bias, time_table, ada_weight, ada_bias, mlp_up, mlp_up_bias, mlp_down, mlp_down_bias)))

    def wrapped(tokens_in, weights):
        return forward_all(tokens_in, weights, prefix_len, timestep)
    result, pullback = jax.vjp(wrapped, tokens.astype(jnp.float32), params)
    tokens_grad, weight_grads = pullback(out_grad.astype(jnp.float32))
    return (result.astype(jnp.bfloat16), tokens_grad, weight_grads[0], weight_grads[1], weight_grads[2], weight_grads[3], weight_grads[4], weight_grads[5], weight_grads[6], weight_grads[7], weight_grads[8], weight_grads[9], weight_grads[10], weight_grads[11], weight_grads[12])
```

```python
import math

import jax
import jax.numpy as jnp
from jax import lax
from jax.sharding import PartitionSpec as P

H = 12
HD = 64
EPS = 1e-05
NEG = -1e30
F32 = jnp.float32
BF16 = jnp.bfloat16
HIGHEST = lax.Precision.HIGHEST


def standardize(values):
    centred = values - jnp.mean(values, axis=-1, keepdims=True)
    inverse = lax.rsqrt(jnp.mean(centred * centred, axis=-1, keepdims=True) + EPS)
    return centred * inverse, inverse


def norm_back(gradient, normed, inverse):
    return inverse * (
        gradient
        - jnp.mean(gradient, axis=-1, keepdims=True)
        - normed * jnp.mean(gradient * normed, axis=-1, keepdims=True)
    )


def dot(left, right):
    return jnp.dot(left, right, preferred_element_type=F32)


def dot_bt(left, right):
    return lax.dot_general(left, right, (((1,), (1,)), ((), ())), preferred_element_type=F32)


def dot_at(left, right):
    return lax.dot_general(left, right, (((0,), (0,)), ((), ())), preferred_element_type=F32)


def gelu_exact(values):
    return jax.nn.gelu(values, approximate=False)


def seq_swap(value, mask):
    return lax.ppermute(value, "seq", [(s, s ^ mask) for s in range(lax.axis_size("seq"))])


def dp_swap(value):
    return lax.ppermute(value, "dp", [(d, d ^ 1) for d in range(lax.axis_size("dp"))])


def dp_shift(value, step):
    count = lax.axis_size("dp")
    outer = count // 2
    return lax.ppermute(
        value,
        "dp",
        [(((o + step) % outer) * 2 + i, o * 2 + i) for o in range(outer) for i in range(2)],
    )


def dp_gather(block):
    outer = lax.axis_size("dp") // 2
    me = lax.axis_index("dp")
    mine = [block] + [dp_shift(block, k) for k in range(1, outer)]
    theirs = [dp_swap(piece) for piece in mine]
    mine, theirs = jnp.stack(mine), jnp.stack(theirs)
    even = me % 2 == 0
    pairs = jnp.where(even, jnp.stack([mine, theirs], 1), jnp.stack([theirs, mine], 1))
    whole = lax.dynamic_slice_in_dim(
        jnp.concatenate([pairs, pairs], 0), outer - me // 2, outer, 0
    )
    return whole.reshape((-1,) + block.shape[1:])


def dp_reduce(blocks):
    outer = lax.axis_size("dp") // 2
    me = lax.axis_index("dp")
    o, i = me // 2, me % 2
    pairs = blocks.reshape((outer, 2) + blocks.shape[1:])
    away = lax.dynamic_index_in_dim(pairs, 1 - i, 1, keepdims=False).astype(BF16)
    here = lax.dynamic_index_in_dim(pairs, i, 1, keepdims=False).astype(F32)
    half = (here + dp_swap(away).astype(F32)).astype(BF16)
    total = lax.dynamic_index_in_dim(half, o, 0, keepdims=False).astype(F32)
    for k in range(1, outer):
        piece = lax.dynamic_index_in_dim(half, (o - k) % outer, 0, keepdims=False)
        total = total + dp_shift(piece, k).astype(F32)
    return total


def dp_all(value):
    count = lax.axis_size("dp")
    return lax.all_to_all(
        jnp.broadcast_to(value[None], (count,) + value.shape),
        "dp",
        split_axis=0,
        concat_axis=0,
        tiled=True,
    )


def dp_turn(value):
    return lax.all_to_all(value, "dp", split_axis=0, concat_axis=0, tiled=True)


def rotary_tables(positions):
    half_width = HD // 2
    frequency = jnp.exp(jnp.arange(half_width, dtype=F32) * (-math.log(10000.0) / half_width))
    angles = positions.astype(F32)[:, None] * frequency[None, :]
    return jnp.cos(angles), jnp.sin(angles)


def rotate(values, cosine, sine_table):
    half_width = cosine.shape[-1]
    front = values[..., :half_width]
    back = values[..., half_width:]
    cos_wide = cosine[:, None, :]
    sin_wide = sine_table[:, None, :]
    return jnp.concatenate(
        [front * cos_wide - back * sin_wide, back * cos_wide + front * sin_wide], axis=-1
    )


def masked_scores(queries, key_rows, clean):
    scores = jnp.einsum("qhd,khd->hqk", queries, key_rows, preferred_element_type=F32)
    scores = scores * HD ** (-0.5)
    visible = jnp.logical_or(jnp.logical_not(clean)[:, None], clean[None, :])
    return jnp.where(visible[None], scores, NEG)


def attend_forward(packed):
    queries, key_rows, values, clean = packed
    scores = masked_scores(queries, key_rows, clean)
    row_max = jnp.max(scores, axis=-1, keepdims=True)
    exponent = jnp.exp(scores - row_max)
    row_total = jnp.sum(exponent, axis=-1, keepdims=True)
    weights = (exponent / row_total).astype(BF16)
    mixed = jnp.einsum("hqk,khd->qhd", weights, values, preferred_element_type=F32)
    return mixed.astype(BF16), (row_max + jnp.log(row_total))[..., 0]


def attend_backward(packed):
    queries, key_rows, values, clean, log_total, mixed_grad = packed
    scores = masked_scores(queries, key_rows, clean)
    weights = jnp.exp(scores - log_total[..., None])
    weight_grad = jnp.einsum("qhd,khd->hqk", mixed_grad, values, preferred_element_type=F32)
    centre = jnp.sum(weights * weight_grad, axis=-1, keepdims=True)
    score_grad = (weights * (weight_grad - centre)).astype(BF16)
    scale = HD ** (-0.5)
    query_grad = jnp.einsum("hqk,khd->qhd", score_grad, key_rows, preferred_element_type=F32)
    key_grad = jnp.einsum("hqk,qhd->khd", score_grad, queries, preferred_element_type=F32)
    value_grad = jnp.einsum(
        "hqk,qhd->khd", weights.astype(BF16), mixed_grad, preferred_element_type=F32
    )
    return (
        (query_grad * scale).astype(BF16),
        (key_grad * scale).astype(BF16),
        value_grad.astype(BF16),
    )


def shards(
    tokens,
    prefix_len,
    timestep,
    norm_gain,
    norm_bias,
    proj_in,
    proj_in_bias,
    proj_out,
    proj_out_bias,
    time_table,
    ada_weight,
    ada_bias,
    mlp_up,
    mlp_up_bias,
    mlp_down,
    mlp_down_bias,
    out_grad,
):
    count, local_len, width = tokens.shape
    members = lax.axis_size("seq")
    ranks = lax.axis_size("dp")
    s = lax.axis_index("seq")
    d = lax.axis_index("dp")
    c = s % 2
    local_heads = H // members
    head_width = local_heads * HD
    local_rows = count * local_len
    order = [s ^ j for j in range(members)]

    vectors = [
        norm_gain,
        norm_bias,
        proj_in_bias,
        proj_out_bias,
        ada_bias,
        mlp_up_bias,
        mlp_down_bias,
        timestep,
    ]
    packed = dp_all(jnp.concatenate([v.astype(F32) for v in vectors]))
    unpacked, start = [], 0
    for v in vectors:
        unpacked.append(packed[:, start : start + v.shape[0]].reshape(-1))
        start += v.shape[0]
    gain, bias, in_bias, out_bias, ada_bias_full, up_bias, down_bias, steps = unpacked
    steps = steps.astype(jnp.int32).reshape(ranks, count)

    tok_x = seq_swap(tokens, 2)
    tok_c = seq_swap(tokens, 1)
    tok_d = seq_swap(tok_x, 1)
    og_c = seq_swap(out_grad, 1)

    in_local = lax.dynamic_slice_in_dim(
        proj_in.reshape(-1, 3, width), s * head_width, head_width, 2
    ).reshape(-1, 3 * head_width)
    in_w = dp_gather(in_local)
    in_b = lax.dynamic_slice_in_dim(
        in_bias.reshape(3, width), s * head_width, head_width, 1
    ).reshape(-1)
    half_out = width // 2
    out_half = dp_gather(lax.dynamic_slice_in_dim(proj_out, c * half_out, half_out, 1))
    out_other = seq_swap(out_half, 1)
    out_w = jnp.where(
        c == 0,
        jnp.concatenate([out_half, out_other], 1),
        jnp.concatenate([out_other, out_half], 1),
    )
    out_blocks = out_w.reshape(members, head_width, width)
    out_rel = jnp.concatenate([lax.dynamic_index_in_dim(out_blocks, p, 0, False) for p in order], 0)
    own_ff = mlp_down.shape[0]
    half_ff = own_ff // 2
    up_w = dp_gather(
        lax.dynamic_index_in_dim(mlp_up.reshape(-1, ranks, 2, half_ff), c, 2, False).reshape(
            -1, ranks * half_ff
        )
    )
    down_w = dp_gather(lax.dynamic_slice_in_dim(mlp_down, c * half_ff, half_ff, 0))
    up_b = lax.dynamic_index_in_dim(up_bias.reshape(ranks, 2, half_ff), c, 1, False).reshape(-1)

    group = jnp.stack([tokens, tok_c, tok_x, tok_d], axis=1)
    group_rows = group.astype(F32).reshape(-1, width)
    normed_group, _ = standardize(group_rows)
    attn_input = (normed_group * gain + bias).astype(BF16)
    projected = (dot(attn_input, in_w) + in_b).reshape(count, -1, 3, local_heads, HD)
    offsets = jnp.arange(local_len, dtype=jnp.int32)
    positions = jnp.concatenate([p * local_len + offsets for p in order])
    cosine, sine_table = rotary_tables(positions)
    queries = rotate(projected[:, :, 0], cosine, sine_table).astype(BF16)
    key_rows = rotate(projected[:, :, 1], cosine, sine_table).astype(BF16)
    values = projected[:, :, 2].astype(BF16)
    clean_group = positions[None, :] < prefix_len[:, None]
    mixed_heads, log_total = lax.map(
        attend_forward, (queries, key_rows, values, clean_group)
    )
    mixed_heads = mixed_heads.reshape(count, members, local_len, head_width)
    mixed_parts = [mixed_heads[:, 0]] + [
        seq_swap(mixed_heads[:, j], j) for j in range(1, members)
    ]
    mixed = jnp.concatenate(mixed_parts, axis=-1).reshape(local_rows, width)

    table_rows = time_table.shape[0]
    wanted = jnp.concatenate([steps, jnp.zeros((ranks, 1), jnp.int32)], axis=1).reshape(-1)
    kinds = count + 1
    selector = (
        wanted[:, None] == d * table_rows + jnp.arange(table_rows, dtype=jnp.int32)[None, :]
    )
    chosen = dot(selector.astype(BF16), time_table).astype(BF16)
    own_cols = width // ranks
    chosen = dp_turn(
        chosen.reshape(ranks * kinds, ranks, own_cols).transpose(1, 0, 2)
    )
    embedded = jnp.sum(chosen.astype(F32), axis=0)
    activated = jax.nn.silu(embedded).astype(BF16)
    mod_parts = dp_turn(dot(activated, ada_weight).reshape(ranks, kinds, 3 * width))
    modulation = jnp.sum(mod_parts, axis=0) + ada_bias_full

    def token_mod(place, part):
        rows = modulation[:, part * width : (part + 1) * width]
        clean = (place * local_len + offsets)[None, :] < prefix_len[:, None]
        return jnp.where(clean[:, :, None], rows[count][None, None], rows[:count, None]).reshape(
            -1, width
        )

    inputs = tokens.astype(F32).reshape(-1, width)
    residual_one = inputs + (dot(mixed, out_rel) + out_bias)
    shift_mod, scale_mod, gate_mod = (token_mod(s, part) for part in range(3))
    gate_other = token_mod(s ^ 1, 2)
    normed_two, inverse_two = standardize(residual_one)
    mlp_own = (normed_two * (1.0 + scale_mod) + shift_mod).astype(BF16)
    mlp_other = seq_swap(mlp_own, 1)
    mlp_input = jnp.concatenate([mlp_own, mlp_other], 0)
    incoming = out_grad.astype(F32).reshape(-1, width)
    branch_grad_own = (incoming * gate_mod).astype(BF16)
    branch_grad = jnp.concatenate(
        [branch_grad_own, (og_c.astype(F32).reshape(-1, width) * gate_other).astype(BF16)], 0
    )
    pre_act = dot(mlp_input, up_w) + up_b
    hidden = gelu_exact(pre_act).astype(BF16)
    branch_part = dot(hidden, down_w)
    act_grad = dot_bt(branch_grad, down_w)
    pre_grad = jax.vjp(gelu_exact, pre_act)[1](act_grad)[0].astype(BF16)
    input_part = dot_bt(pre_grad, up_w)
    down_grad = dot_at(hidden, branch_grad)
    up_grad = dot_at(mlp_input, pre_grad)
    branch = (
        branch_part[:local_rows]
        + seq_swap(branch_part[local_rows:].astype(BF16), 1).astype(F32)
        + down_bias
    )
    input_two = input_part[:local_rows] + seq_swap(
        input_part[local_rows:].astype(BF16), 1
    ).astype(F32)
    block_out = (residual_one + gate_mod * branch).astype(BF16).reshape(tokens.shape)

    resid_grad = incoming + norm_back(input_two * (1.0 + scale_mod), normed_two, inverse_two)
    attn_grad = resid_grad.astype(BF16)
    mixed_grad = dot_bt(attn_grad, out_rel).astype(BF16).reshape(count, local_len, members, -1)
    grad_parts = [mixed_grad[:, :, 0]] + [
        seq_swap(mixed_grad[:, :, j], j) for j in range(1, members)
    ]
    head_grad = jnp.stack(grad_parts, axis=1).reshape(count, -1, local_heads, HD)
    out_rel_grad = dot_at(mixed, attn_grad).reshape(members, head_width, width)

    mod_grad = (
        jnp.concatenate([input_two, input_two * normed_two, incoming * branch], axis=-1)
        .astype(BF16)
        .reshape(count, local_len, 3 * width)
    )
    clean_own = (s * local_len + offsets)[None, :] < prefix_len[:, None]
    noisy_rows = jnp.einsum(
        "sl,slj->sj",
        jnp.logical_not(clean_own).astype(BF16),
        mod_grad,
        preferred_element_type=F32,
    )
    clean_row = jnp.einsum(
        "sl,slj->j", clean_own.astype(BF16), mod_grad, preferred_element_type=F32
    )
    row_grad = jnp.concatenate([noisy_rows, clean_row[None]], axis=0)
    row_grad = row_grad + seq_swap(row_grad, 1)
    row_grad = row_grad + seq_swap(row_grad, 2)
    all_rows = dp_all(row_grad).reshape(ranks * kinds, 3 * width)
    ada_bias_grad = lax.dynamic_slice_in_dim(
        jnp.sum(all_rows, axis=0), d * ada_bias.shape[0], ada_bias.shape[0], 0
    )
    ada_grad = lax.dot_general(
        activated.astype(F32),
        all_rows,
        (((0,), (0,)), ((), ())),
        precision=HIGHEST,
        preferred_element_type=F32,
    )
    act_rows_grad = lax.dot_general(
        all_rows,
        ada_weight.astype(F32),
        (((1,), (1,)), ((), ())),
        precision=HIGHEST,
        preferred_element_type=F32,
    )
    embed_grad = jax.vjp(jax.nn.silu, embedded)[1](act_rows_grad)[0]
    embed_all = dp_all(embed_grad).transpose(1, 0, 2).reshape(ranks * kinds, width)
    table_grad = lax.dot_general(
        selector.astype(F32),
        embed_all,
        (((0,), (0,)), ((), ())),
        precision=HIGHEST,
        preferred_element_type=F32,
    )

    query_grad, key_grad, value_grad = lax.map(
        attend_backward, (queries, key_rows, values, clean_group, log_total, head_grad)
    )
    proj_grad = (
        jnp.stack(
            [
                rotate(query_grad.astype(F32), cosine, -sine_table),
                rotate(key_grad.astype(F32), cosine, -sine_table),
                value_grad.astype(F32),
            ],
            axis=2,
        )
        .astype(BF16)
        .reshape(-1, 3 * head_width)
    )
    in_grad = dot_at(attn_input, proj_grad)
    normed_part = dot_bt(proj_grad, in_w)
    gain_grad = jnp.sum(normed_part * normed_group, axis=0)
    bias_grad = jnp.sum(normed_part, axis=0)
    parts = normed_part.reshape(count, members, local_len, width)
    got = seq_swap(jnp.stack([parts[:, 1], parts[:, 3]]).astype(BF16), 1).astype(F32)
    mine = parts[:, 0] + got[0]
    across = (parts[:, 2] + got[1]).astype(BF16)
    normed_grad = (mine + seq_swap(across, 2).astype(F32)).reshape(-1, width)
    normed_own, inverse_own = standardize(inputs)
    tokens_grad = (resid_grad + norm_back(normed_grad * gain, normed_own, inverse_own)).reshape(
        tokens.shape
    )

    down_red = dp_reduce(down_grad.reshape(ranks, half_ff, width)).astype(BF16)
    up_red = dp_reduce(up_grad.reshape(ranks, -1, ranks * half_ff)).astype(BF16)
    out_grad_w = jnp.concatenate(
        [lax.dynamic_index_in_dim(out_rel_grad, p, 0, False) for p in order], 0
    )
    out_away = lax.dynamic_slice_in_dim(out_grad_w, (1 - c) * half_out, half_out, 1).astype(BF16)
    out_here = lax.dynamic_slice_in_dim(out_grad_w, c * half_out, half_out, 1)
    out_sum = out_here + seq_swap(out_away, 1).astype(F32)
    out_red = dp_reduce(out_sum.reshape(ranks, -1, half_out)).astype(BF16)
    in_red = dp_reduce(in_grad.reshape(ranks, -1, 3 * head_width)).astype(BF16)

    def both(value, axis):
        total = value.astype(F32) + seq_swap(value, 2).astype(F32)
        other = seq_swap(total, 1)
        return jnp.where(
            c == 0, jnp.stack([total, other], axis), jnp.stack([other, total], axis)
        )

    down_final = both(down_red, 0).reshape(mlp_down.shape)
    up_final = both(up_red.reshape(-1, ranks, half_ff), 2).reshape(mlp_up.shape)
    out_final = both(out_red, 1).reshape(proj_out.shape)
    in_x = seq_swap(in_red, 2)
    in_pair = jnp.stack([in_red, in_x])
    in_pair_c = seq_swap(in_pair, 1)
    in_rel = jnp.stack([in_red, in_pair_c[0], in_x, in_pair_c[1]])
    in_final = (
        jnp.stack([lax.dynamic_index_in_dim(in_rel, p, 0, False) for p in order])
        .reshape(members, -1, 3, head_width)
        .transpose(1, 2, 0, 3)
        .reshape(proj_in.shape)
        .astype(F32)
    )

    in_bias_grad = lax.dynamic_update_slice_in_dim(
        jnp.zeros((3, width), F32),
        jnp.sum(proj_grad, axis=0, dtype=F32).reshape(3, head_width),
        s * head_width,
        1,
    ).reshape(-1)
    up_bias_grad = lax.dynamic_update_slice_in_dim(
        jnp.zeros((ranks, 2, half_ff), F32),
        jnp.sum(pre_grad, axis=0, dtype=F32).reshape(ranks, 1, half_ff),
        c,
        1,
    ).reshape(-1)
    down_bias_grad = jnp.sum(branch_grad_own, axis=0, dtype=F32)
    out_bias_grad = jnp.sum(attn_grad, axis=0, dtype=F32)
    vector_grads = [gain_grad, bias_grad, in_bias_grad, out_bias_grad, up_bias_grad, down_bias_grad]
    vec = jnp.concatenate([g.reshape(ranks, -1) for g in vector_grads], axis=1)
    vec = jnp.sum(dp_turn(vec), axis=0)
    vec = vec + seq_swap(vec, 1)
    vec = vec + seq_swap(vec, 2)
    finals, start = [], 0
    for g in vector_grads:
        size = g.shape[0] // ranks
        finals.append(vec[start : start + size])
        start += size
    gain_f, bias_f, in_bias_f, out_bias_f, up_bias_f, down_bias_f = finals
    return (
        block_out,
        tokens_grad,
        gain_f,
        bias_f,
        in_final,
        in_bias_f,
        out_final,
        out_bias_f,
        table_grad,
        ada_grad,
        ada_bias_grad,
        up_final,
        up_bias_f,
        down_final,
        down_bias_f,
    )


def solution(mesh):
    rows = P("dp", None)
    vector = P("dp")
    stream = P("dp", "seq", None)
    in_specs = (
        stream,
        vector,
        vector,
        vector,
        vector,
        rows,
        vector,
        rows,
        vector,
        rows,
        rows,
        vector,
        rows,
        vector,
        rows,
        vector,
        stream,
    )
    out_specs = (
        stream,
        stream,
        vector,
        vector,
        rows,
        vector,
        rows,
        vector,
        rows,
        rows,
        vector,
        rows,
        vector,
        rows,
        vector,
    )
    return jax.shard_map(shards, mesh=mesh, in_specs=in_specs, out_specs=out_specs, check_vma=False)
```

```python
import functools
import math

import jax
import jax.numpy as jnp
from jax import lax
from jax.experimental import pallas as pl
from jax.experimental.pallas import tpu as pltpu
from jax.sharding import PartitionSpec as P

H = 12
HD = 64
EPS = 1e-05
NEG = -1e30
COST = 1.0
F32 = jnp.float32
BF16 = jnp.bfloat16
HIGHEST = lax.Precision.HIGHEST
VMEM_LIMIT = 62 * 1024 * 1024
EXTRA = 16


def standardize(values):
    centred = values - jnp.mean(values, axis=-1, keepdims=True)
    inverse = lax.rsqrt(jnp.mean(centred * centred, axis=-1, keepdims=True) + EPS)
    return centred * inverse, inverse


def norm_back(gradient, normed, inverse):
    return inverse * (
        gradient
        - jnp.mean(gradient, axis=-1, keepdims=True)
        - normed * jnp.mean(gradient * normed, axis=-1, keepdims=True)
    )


def dot(left, right):
    return jnp.dot(left, right, preferred_element_type=F32)


def dot_bt(left, right):
    return lax.dot_general(left, right, (((1,), (1,)), ((), ())), preferred_element_type=F32)


def dot_at(left, right):
    return lax.dot_general(left, right, (((0,), (0,)), ((), ())), preferred_element_type=F32)


TAIL_P = 0.55
TAIL = (
    0.001045374169866761,
    0.2933056852691112,
    0.41788788917041303,
    -0.08811700935317877,
    0.8046529189842585,
    -0.5409110079247637,
    0.11213617568673577,
)


def gelu_both(values):
    bell = jnp.exp(values * values * -0.5)
    inner = 1.0 / (1.0 + (TAIL_P / math.sqrt(2.0)) * jnp.abs(values))
    tail = TAIL[6]
    for coefficient in TAIL[5::-1]:
        tail = tail * inner + coefficient
    tail = tail * bell * 0.5
    cumulative = jnp.where(values >= 0.0, 1.0 - tail, tail)
    return values * cumulative, cumulative + values * bell * (1.0 / math.sqrt(2.0 * math.pi))


def after(value, *others):
    return lax.optimization_barrier((value, others))[0]


def seq_swap(value, mask):
    return lax.ppermute(value, "seq", [(s, s ^ mask) for s in range(lax.axis_size("seq"))])


def dp_swap(value, mask):
    return lax.ppermute(value, "dp", [(d, d ^ mask) for d in range(lax.axis_size("dp"))])


def dp_collect(value):
    mine = [value] + [dp_swap(value, m) for m in range(2, lax.axis_size("dp"), 2)]
    return mine, dp_swap(jnp.stack(mine), 1)


def quad(value):
    across = seq_swap(value, 2)
    return value, across, seq_swap(jnp.stack([value, across]), 1)


def dp_turn(value, outer_only=False):
    groups = None
    if outer_only:
        outer = lax.axis_size("dp") // 2
        groups = [[o * 2 + i for o in range(outer)] for i in range(2)]
    return lax.all_to_all(
        value, "dp", split_axis=0, concat_axis=0, tiled=True, axis_index_groups=groups
    )


def dp_all(value):
    return dp_turn(jnp.broadcast_to(value[None], (lax.axis_size("dp"),) + value.shape))


def run(body, grid, meta, ins, outs, scratch=(), cost=(0, 0, 0), name=None, held=()):
    specs = [pl.BlockSpec(block, index) for _, block, index in ins]
    specs += [pl.BlockSpec(memory_space=pl.ANY) for _ in held]
    first = 1 + len(ins)
    kernel = body
    if held:

        def kernel(meta, *refs):
            return body(meta, *refs[: len(ins)], *refs[len(ins) + len(held) :])

    return pl.pallas_call(
        kernel,
        grid_spec=pltpu.PrefetchScalarGridSpec(
            num_scalar_prefetch=1,
            grid=grid,
            in_specs=specs,
            out_specs=[pl.BlockSpec(block, index) for _, _, block, index in outs],
            scratch_shapes=list(scratch),
        ),
        out_shape=[jax.ShapeDtypeStruct(shape, dtype) for shape, dtype, _, _ in outs],
        input_output_aliases={first + n: k for n, (_, k) in enumerate(held)},
        compiler_params=pltpu.CompilerParams(
            dimension_semantics=("arbitrary",) * len(grid), vmem_limit_bytes=VMEM_LIMIT
        ),
        cost_estimate=pl.CostEstimate(
            flops=int(cost[0] * COST), bytes_accessed=int(cost[1] * COST), transcendentals=0
        ),
        name=name,
    )(meta, *[array for array, _, _ in ins], *[array for array, _ in held])


def whole(array):
    zeros = (0,) * array.ndim
    return (array, array.shape, lambda *_: zeros)


def out_whole(shape, dtype):
    zeros = (0,) * len(shape)
    return (shape, dtype, shape, lambda *_: zeros)


def partner_lanes(tile):
    lane = lax.broadcasted_iota(jnp.int32, tile.shape, 1)
    ahead = pltpu.roll(tile, 96, 1)
    behind = pltpu.roll(tile, 32, 1)
    return jnp.where((lane & (HD // 2)) == 0, ahead, behind)


def qkv_kernel(meta, x0, x1, gain, bias, w, b, cosine, sine, out):
    half = w.shape[1] // 3
    tokens = jnp.where(pl.program_id(0) == 0, x0[0], x1[0]).astype(F32)
    normed, _ = standardize(tokens)
    attn_input = (normed * gain[...] + bias[...]).astype(BF16)
    projected = dot(attn_input, w[...]) + b[...]
    cos, sin = cosine[...], sine[...]
    scale = HD**-0.5
    lane = lax.broadcasted_iota(jnp.int32, cos.shape, 1)
    for t in range(2 * half // 128):
        tile = projected[:, t * 128 : (t + 1) * 128]
        turned = tile * cos + partner_lanes(tile) * sin
        if (t + 1) * 128 <= half:
            turned = turned * scale
        elif t * 128 < half:
            turned = turned * jnp.where(lane < half - t * 128, scale, 1.0)
        out[0, :, t * 128 : (t + 1) * 128] = turned.astype(BF16)
    out[0, :, 2 * half :] = projected[:, 2 * half :].astype(BF16)


def qkv_call(meta, base, x0, x1, gain, bias, w, b, cosine, sine):
    count, rows, width = x0.shape
    last = count - 1
    return run(
        qkv_kernel,
        (2, count),
        meta,
        [
            (x0, (1, rows, width), lambda p, q, m: (jnp.where(p == 0, q, last), 0, 0)),
            (x1, (1, rows, width), lambda p, q, m: (jnp.where(p == 0, 0, q), 0, 0)),
            whole(gain),
            whole(bias),
            whole(w),
            whole(b),
            (cosine, (rows, 128), lambda p, q, m: (base + p, 0)),
            (sine, (rows, 128), lambda p, q, m: (base + p, 0)),
        ],
        [
            (
                (count, 2 * rows, w.shape[1]),
                BF16,
                (1, rows, w.shape[1]),
                lambda p, q, m: (q, p, 0),
            )
        ],
        cost=(4 * count * rows * width * w.shape[1], 10 * count * rows * width, 0),
        name="qkv",
    )[0]


def fold(rows):
    half = rows.shape[0] // 2
    return jnp.concatenate([rows[:half], rows[half:]], axis=1)


def unfold(pair):
    width = pair.shape[1] // 2
    return jnp.concatenate([pair[:, :width], pair[:, width:]], axis=0)


def attend_kernel(base, meta, qa, qb, o0, o1, weights, recips):
    b, k = pl.program_id(0), pl.program_id(1)
    j = base + k
    s, prefix = meta[0], meta[4 + b]
    rows = o0.shape[1] * 2
    hw = o0.shape[2] // 2
    heads = hw // HD
    half = qa.shape[1]
    source = qb if base else qa
    mine = source[0, pl.ds(pl.multiple_of(k * rows, rows), rows), :hw]
    at = (s ^ j) * rows + lax.broadcasted_iota(jnp.int32, (rows, 1), 0)
    hidden_from = jnp.where(at < prefix, 1.0, 0.0)
    lane = lax.broadcasted_iota(jnp.int32, (1, rows), 1)
    fills = []
    for side in range(2):
        places = [(s ^ (2 * side + piece)) * rows + lane for piece in range(half // rows)]
        where = jnp.concatenate(places, axis=1)
        fills.append(jnp.where(where < prefix, 0.0, NEG))
    lane128 = lax.broadcasted_iota(jnp.int32, (rows, 128), 1)
    kept = jnp.zeros((rows, 128), F32)
    outs = []
    for h in range(heads):
        q = mine[:, h * HD : (h + 1) * HD]
        scores = []
        for side, ref in enumerate((qa, qb)):
            keys = ref[0, :, hw + h * HD : hw + (h + 1) * HD]
            scores.append(dot_bt(q, keys) + hidden_from * fills[side])
        top = jnp.maximum(
            jnp.max(scores[0], axis=1, keepdims=True), jnp.max(scores[1], axis=1, keepdims=True)
        )
        sums = jnp.zeros((rows, 1), F32)
        mixed = jnp.zeros((rows, HD), F32)
        for side, ref in enumerate((qa, qb)):
            v = ref[0, :, 2 * hw + h * HD : 2 * hw + (h + 1) * HD]
            e = jnp.exp(scores[side] - top)
            sums = sums + jnp.sum(e, axis=1, keepdims=True)
            e = e.astype(BF16)
            weights[0, h, :, side * half : (side + 1) * half] = e
            mixed = mixed + dot(e, v)
        recip = 1.0 / sums
        kept = jnp.where(lane128 == h, recip, kept)
        outs.append((mixed * recip).astype(BF16))
    recips[0] = kept
    folded = fold(jnp.concatenate(outs, axis=1))
    for n, ref in enumerate((o0, o1)):

        @pl.when(k == n)
        def _(ref=ref):
            ref[0] = folded


def attend_call(meta, base, qa, qb, rows, held=()):
    count, half, cols = qa.shape
    hw = cols // 3
    heads = hw // HD
    keys = 2 * half
    block = (1, rows // 2, 2 * hw)
    return run(
        functools.partial(attend_kernel, base),
        (count, half // rows),
        meta,
        [
            (qa, (1, half, cols), lambda b, k, m: (b, 0, 0)),
            (qb, (1, half, cols), lambda b, k, m: (b, 0, 0)),
        ],
        [((count,) + block[1:], BF16, block, lambda b, k, m: (b, 0, 0)) for _ in range(2)]
        + [
            (
                (count, heads, keys, keys),
                BF16,
                (1, heads, rows, keys),
                lambda b, k, m: (b, 0, base + k, 0),
            ),
            ((count, keys, 128), F32, (1, rows, 128), lambda b, k, m: (b, base + k, 0)),
        ],
        cost=(
            2 * count * heads * keys * keys * HD * 4,
            count * heads * keys * keys,
            count * heads * keys * keys // 2,
        ),
        name="attend",
        held=[(x, 2 + n) for n, x in enumerate(held)],
    )


def back_kernel(meta, qa, qb, weights, recips, o0, o1, o2, o3, g0, g1, g2, g3, out, dk, dv, og, go):
    j = pl.program_id(0)
    rows = o0.shape[1] * 2
    hw = o0.shape[2] // 2
    heads = hw // HD
    half = qa.shape[1]
    place = lax.rem(j, 2) * rows
    scale = HD**-0.5
    for k, (o, g) in enumerate(((o0, g0), (o1, g1), (o2, g2), (o3, g3))):

        @pl.when(j == k)
        def _(o=o, g=g):
            grad = g[0].astype(F32)
            go[...] = unfold(grad)
            og[...] = unfold(grad * o[0].astype(F32))

    @pl.when(j == 0)
    def _():
        dk[...] = jnp.zeros_like(dk)
        dv[...] = jnp.zeros_like(dv)

    mine = jnp.where(j < 2, qa[0, pl.ds(place, rows), :hw], qb[0, pl.ds(place, rows), :hw])
    query_grads = []
    for h in range(heads):
        cols = slice(h * HD, (h + 1) * HD)
        recip = recips[0, :, h : h + 1]
        grad = (go[:, cols] * recip).astype(BF16)
        centre = jnp.sum(og[:, cols], axis=1, keepdims=True) * recip
        q = mine[:, cols]
        dq = jnp.zeros((rows, HD), F32)
        for side, ref in enumerate((qa, qb)):
            k = ref[0, :, hw + h * HD : hw + (h + 1) * HD]
            v = ref[0, :, 2 * hw + h * HD : 2 * hw + (h + 1) * HD]
            e = weights[0, h, :, side * half : (side + 1) * half]
            ds = (e.astype(F32) * (dot_bt(grad, v) - centre)).astype(BF16)
            dq = dq + dot(ds, k)
            span = pl.ds(side * half, half)
            dk[h, span] += dot_at(ds, q)
            dv[h, span] += dot_at(e, grad)
        query_grads.append((dq * scale).astype(BF16))
    out[0, pl.ds(pl.multiple_of(j * rows, rows), rows), :hw] = jnp.concatenate(query_grads, axis=1)

    @pl.when(j == pl.num_programs(0) - 1)
    def _():
        out[0, :, hw : 2 * hw] = jnp.concatenate(
            [dk[h].astype(BF16) for h in range(heads)], axis=1
        )
        out[0, :, 2 * hw :] = jnp.concatenate([dv[h].astype(BF16) for h in range(heads)], axis=1)


def back_call(meta, b, qa, qb, weights, recips, olds, grads):
    _, half, cols = qa.shape
    hw = cols // 3
    heads = hw // HD
    keys = 2 * half
    rows = olds[0].shape[1] * 2
    block = (1,) + olds[0].shape[1:]
    piece = lambda j, m: (b, 0, 0)
    return run(
        back_kernel,
        (keys // rows,),
        meta,
        [
            (qa, (1, half, cols), piece),
            (qb, (1, half, cols), piece),
            (weights, (1, heads, rows, keys), lambda j, m: (b, 0, j, 0)),
            (recips, (1, rows, 128), lambda j, m: (b, j, 0)),
        ]
        + [(x, block, piece) for x in (*olds, *grads)],
        [((1, keys, cols), BF16, (1, keys, cols), lambda j, m: (0, 0, 0))],
        scratch=[
            pltpu.VMEM((heads, keys, HD), F32),
            pltpu.VMEM((heads, keys, HD), F32),
            pltpu.VMEM((rows, hw), F32),
            pltpu.VMEM((rows, hw), F32),
        ],
        cost=(8 * heads * keys * keys * HD * 4, 2 * heads * keys * keys, 0),
        name="attend_back",
    )[0]


def mix_kernel(meta, m0, m1, m2, m3, tokens, w_own, w_other, out_bias, mods, residual, mlp_in, w):
    b = pl.program_id(0)
    s, c, prefix = meta[0], meta[1], meta[4 + b]
    rows, width = tokens.shape[1:]
    hw = m0.shape[2] // 2

    @pl.when(b == 0)
    def _():
        for j in range(4):
            there = pl.ds(pl.multiple_of((s ^ j) * hw, hw), hw)
            own, other = w_own[there], w_other[there]
            even = c == 0
            w[j * hw : (j + 1) * hw, : width // 2] = jnp.where(even, own, other)
            w[j * hw : (j + 1) * hw, width // 2 :] = jnp.where(even, other, own)

    total = tokens[0].astype(F32) + out_bias[...]
    for j, ref in enumerate((m0, m1, m2, m3)):
        total = total + dot(unfold(ref[0]), w[j * hw : (j + 1) * hw])
    residual[0] = total
    normed, _ = standardize(total)
    at = s * rows + lax.broadcasted_iota(jnp.int32, (rows, 1), 0)
    clean = at < prefix
    count = pl.num_programs(0)
    noisy_row, clean_row = mods[pl.ds(b, 1)], mods[pl.ds(count, 1)]
    shift, scale = (
        jnp.where(
            clean,
            clean_row[:, part * width : (part + 1) * width],
            noisy_row[:, part * width : (part + 1) * width],
        )
        for part in range(2)
    )
    mlp_in[0] = (normed * (1.0 + scale) + shift).astype(BF16)


def mix_call(meta, parts, tokens, w_own, w_other, out_bias, mods):
    count, rows, width = tokens.shape
    seq = lambda b, m: (b, 0, 0)
    block = (1, rows, width)
    return run(
        mix_kernel,
        (count,),
        meta,
        [(p, (1,) + p.shape[1:], seq) for p in parts]
        + [(tokens, block, seq), whole(w_own), whole(w_other), whole(out_bias), whole(mods)],
        [
            (tokens.shape, F32, block, seq),
            (tokens.shape, BF16, block, seq),
            out_whole((width, width), BF16),
        ],
        cost=(2 * count * rows * width * width, 12 * count * rows * width, 0),
        name="mix",
    )


def mlp_kernel(
    meta,
    x0,
    x1,
    og0,
    og1,
    up,
    up_bias,
    down,
    mods,
    own_branch,
    own_input,
    other,
    up_here,
    up_away,
    down_here,
    down_away,
    up_bias_grad,
    up_acc,
    down_acc,
):
    p, b = pl.program_id(0), pl.program_id(1)
    count = pl.num_programs(1)
    s, i, prefix = meta[0], meta[3], meta[4 + b]
    rows, width = x0.shape[1:]
    first = p == 0
    x = jnp.where(first, x0[0], x1[0])
    incoming = jnp.where(first, og0[0], og1[0]).astype(F32)
    at = (s ^ p) * rows + lax.broadcasted_iota(jnp.int32, (rows, 1), 0)
    gate = jnp.where(
        at < prefix, mods[pl.ds(count, 1), 2 * width :], mods[pl.ds(b, 1), 2 * width :]
    )
    grad = (incoming * gate).astype(BF16)
    hidden, slope = gelu_both(dot(x, up[...]) + up_bias[...])
    hidden = hidden.astype(BF16)
    branch = dot(hidden, down[...])
    pre = (dot_bt(grad, down[...]) * slope)
    pre_low = pre.astype(BF16)
    back = dot_bt(pre_low, up[...])
    sums = jnp.sum(pre_low.astype(F32), axis=0, keepdims=True)

    @pl.when(first)
    def _():
        own_branch[0] = branch
        own_input[0] = back

    @pl.when(p == 1)
    def _():
        other[0, 0] = branch.astype(BF16)
        other[1, 0] = back.astype(BF16)

    start = jnp.logical_and(first, b == 0)

    @pl.when(start)
    def _():
        up_acc[...] = dot_at(x, pre_low)
        down_acc[...] = dot_at(hidden, grad)
        up_bias_grad[...] = sums

    @pl.when(jnp.logical_not(start))
    def _():
        up_acc[...] += dot_at(x, pre_low)
        down_acc[...] += dot_at(hidden, grad)
        up_bias_grad[...] += sums

    @pl.when(jnp.logical_and(p == 1, b == count - 1))
    def _():
        outer, deep = up_here.shape[0], up_here.shape[1]
        for d in range(2 * outer):
            upper = up_acc[d * deep : (d + 1) * deep].astype(BF16)
            base = d * 2 * deep
            lower = jnp.concatenate(
                [down_acc[base : base + deep], down_acc[base + deep : base + 2 * deep]], axis=1
            ).astype(BF16)

            @pl.when(i == d % 2)
            def _(d=d, upper=upper, lower=lower):
                up_here[d // 2] = upper
                down_here[d // 2] = lower

            @pl.when(i != d % 2)
            def _(d=d, upper=upper, lower=lower):
                up_away[d // 2] = upper
                down_away[d // 2] = lower


def mlp_call(meta, x0, x1, og0, og1, up, up_bias, down, mods, ranks):
    count, rows, width = x0.shape
    hidden = up.shape[1]
    last = count - 1
    block = (1, rows, width)
    first = lambda p, b, m: (jnp.where(p == 0, b, last), 0, 0)
    second = lambda p, b, m: (jnp.where(p == 0, 0, b), 0, 0)
    shared = (ranks // 2, width // ranks, hidden)
    return run(
        mlp_kernel,
        (2, count),
        meta,
        [
            (x0, block, first),
            (x1, block, second),
            (og0, block, first),
            (og1, block, second),
            whole(up),
            whole(up_bias),
            whole(down),
            whole(mods),
        ],
        [
            (x0.shape, F32, block, first),
            (x0.shape, F32, block, first),
            (
                (2,) + x0.shape,
                BF16,
                (2,) + block,
                lambda p, b, m: (0, jnp.where(p == 0, 0, b), 0, 0),
            ),
            out_whole(shared, BF16),
            out_whole(shared, BF16),
            out_whole(shared, BF16),
            out_whole(shared, BF16),
            out_whole((1, hidden), F32),
        ],
        scratch=[pltpu.VMEM((width, hidden), F32), pltpu.VMEM((hidden, width), F32)],
        cost=(24 * count * rows * width * hidden, 20 * count * rows * width, 0),
        name="mlp",
    )


def turn_kernel(
    meta,
    residual,
    out_grad,
    own_branch,
    own_input,
    got,
    down_bias,
    mods,
    m0,
    m1,
    m2,
    m3,
    w,
    block_out,
    resid_grad,
    g0,
    g1,
    g2,
    g3,
    sums,
    biases,
    out_here,
    out_away,
    acc,
):
    b = pl.program_id(0)
    count = pl.num_programs(0)
    s, c, prefix = meta[0], meta[1], meta[4 + b]
    rows, width = residual.shape[1:]
    hw = m0.shape[2] // 2
    resid = residual[0]
    incoming = out_grad[0].astype(F32)
    at = s * rows + lax.broadcasted_iota(jnp.int32, (rows, 1), 0)
    clean = at < prefix
    noisy_row, clean_row = mods[pl.ds(b, 1)], mods[pl.ds(count, 1)]
    scale, gate = (
        jnp.where(
            clean,
            clean_row[:, part * width : (part + 1) * width],
            noisy_row[:, part * width : (part + 1) * width],
        )
        for part in (1, 2)
    )
    branch = own_branch[0] + got[0, 0].astype(F32) + down_bias[...]
    input_two = own_input[0] + got[1, 0].astype(F32)
    block_out[0] = (resid + gate * branch).astype(BF16)
    normed, inverse = standardize(resid)
    grads = incoming + norm_back(input_two * (1.0 + scale), normed, inverse)
    resid_grad[0] = grads
    low = grads.astype(BF16)
    keep = jnp.where(clean, 1.0, 0.0)
    for part, value in enumerate((input_two, input_two * normed, incoming * branch)):
        value = value.astype(BF16).astype(F32)
        cols = slice(part * width, (part + 1) * width)
        everything = jnp.sum(value, axis=0, keepdims=True)
        old = jnp.sum(value * keep, axis=0, keepdims=True)
        sums[0, 0:1, cols] = everything - old
        sums[0, 1:2, cols] = old
    branch_low = (incoming * gate).astype(BF16).astype(F32)
    down_sum = jnp.sum(branch_low, axis=0, keepdims=True)
    out_sum = jnp.sum(low.astype(F32), axis=0, keepdims=True)

    @pl.when(b == 0)
    def _():
        acc[...] = jnp.zeros_like(acc)
        biases[...] = jnp.zeros_like(biases)

    biases[0:1] += down_sum
    biases[1:2] += out_sum
    for j, (m, g) in enumerate(((m0, g0), (m1, g1), (m2, g2), (m3, g3))):
        g[0] = fold(dot_bt(low, w[j * hw : (j + 1) * hw])).astype(BF16)
        acc[j * hw : (j + 1) * hw] += dot_at(unfold(m[0]), low)

    @pl.when(b == count - 1)
    def _():
        for j in range(4):
            here = pl.ds(pl.multiple_of((s ^ j) * hw, hw), hw)
            block = acc[j * hw : (j + 1) * hw].astype(BF16)
            left, right = block[:, : width // 2], block[:, width // 2 :]
            even = c == 0
            out_here[here] = jnp.where(even, left, right)
            out_away[here] = jnp.where(even, right, left)


def turn_call(meta, residual, out_grad, own_branch, own_input, got, down_bias, mods, parts, w):
    count, rows, width = residual.shape
    seq = lambda b, m: (b, 0, 0)
    block = (1, rows, width)
    return run(
        turn_kernel,
        (count,),
        meta,
        [
            (residual, block, seq),
            (out_grad, block, seq),
            (own_branch, block, seq),
            (own_input, block, seq),
            (got, (2,) + block, lambda b, m: (0, b, 0, 0)),
            whole(down_bias),
            whole(mods),
        ]
        + [(p, (1,) + p.shape[1:], seq) for p in parts]
        + [whole(w)],
        [
            (residual.shape, BF16, block, seq),
            (residual.shape, F32, block, seq),
        ]
        + [(p.shape, BF16, (1,) + p.shape[1:], seq) for p in parts]
        + [
            ((count, 2, 3 * width), F32, (1, 2, 3 * width), seq),
            out_whole((8, width), F32),
            out_whole((width, width // 2), BF16),
            out_whole((width, width // 2), BF16),
        ],
        scratch=[pltpu.VMEM((width, width), F32)],
        cost=(4 * count * rows * width * width, 24 * count * rows * width, 0),
        name="turn",
    )


def proj_back_kernel(pieces, do_in, parts, has_carry, has_got, ranks, meta, *refs):
    refs = list(refs)
    xs = [refs.pop(0) for _ in pieces]
    raws = [refs.pop(0) for _ in pieces]
    tables = [(refs.pop(0), refs.pop(0)) for _ in pieces]
    gain, bias, w = refs.pop(0), refs.pop(0), refs.pop(0)
    do_norm = parts > 0
    kept = 2 * do_in + do_norm
    carry = [refs.pop(0) for _ in range(kept)] if has_carry else None
    got = refs.pop(0) if has_got else None
    extra = [refs.pop(0) for _ in range(2)] if ranks else None
    parts = [refs.pop(0) for _ in range(parts)]
    out = refs.pop(0) if ranks else None
    totals = refs
    acc, in_bias = totals[:2] if do_in else (None, None)
    vec = totals[-1] if do_norm else None
    hw = w.shape[1] // 3
    if has_carry:
        for ref, old in zip(totals, carry):
            ref[...] = old[...]
    else:
        for ref in totals:
            ref[...] = jnp.zeros_like(ref)

    for k, (x, raw, (cosine, sine)) in enumerate(zip(xs, raws, tables)):
        normed, _ = standardize(x[0].astype(F32))
        cos, sin = cosine[...], sine[...]
        tiles = []
        for t in range(2 * hw // 128):
            tile = raw[0, :, t * 128 : (t + 1) * 128].astype(F32)
            tiles.append((tile * cos - partner_lanes(tile) * sin).astype(BF16))
        tiles.append(raw[0, :, 2 * hw :])
        grads = jnp.concatenate(tiles, axis=1)
        if do_in:
            attn_input = (normed * gain[...] + bias[...]).astype(BF16)
            acc[...] += dot_at(attn_input, grads)
            in_bias[...] += jnp.sum(grads.astype(F32), axis=0, keepdims=True)
        if do_norm:
            back = dot_bt(grads, w[...])
            vec[0:1] += jnp.sum(back * normed, axis=0, keepdims=True)
            vec[1:2] += jnp.sum(back, axis=0, keepdims=True)
            if has_got and k == 0:
                back = back + got[1, 0].astype(F32)
            if len(parts) == 1:
                parts[0][k, 0] = back.astype(parts[0].dtype)
            else:
                parts[k][0] = back.astype(parts[k].dtype)

    if ranks:
        deep, cols = acc.shape[0] // ranks, acc.shape[1]
        up_bias, biases = extra
        flat = jnp.concatenate(
            [in_bias[...], up_bias[...], vec[0:1], vec[1:2], biases[1:2], biases[0:1]], axis=1
        )
        count = flat.shape[1] // cols
        extra = jnp.concatenate(
            [flat[:, r * cols : (r + 1) * cols] for r in range(count)]
            + [jnp.zeros((EXTRA - count, cols), F32)],
            axis=0,
        ).astype(BF16)
        for k in range(ranks):
            out[k, :deep] = acc[k * deep : (k + 1) * deep].astype(BF16)
            out[k, deep:] = extra


def proj_back_call(
    meta,
    b,
    pieces,
    xs,
    raw,
    gain,
    bias,
    w,
    cosine,
    sine,
    dtypes,
    carry=(),
    got=None,
    do_in=True,
    ranks=0,
    extra=(),
):
    _, rows, width = xs[0].shape
    cols = w.shape[1]
    do_norm = bool(dtypes)
    ins = [(x, (1, rows, width), lambda i, m: (b, 0, 0)) for x in xs]
    ins += [(raw, (1, rows, cols), lambda i, m, j=j: (0, j, 0)) for j in pieces]
    for j in pieces:
        ins += [(t, (rows, 128), lambda i, m, j=j: (j, 0)) for t in (cosine, sine)]
    ins += [whole(gain), whole(bias), whole(w)]
    ins += [whole(v) for v in carry]
    if got is not None:
        ins.append(whole(got))
    ins += [whole(x) for x in extra]
    n = len(pieces)
    lead = (n,) if len(dtypes) == 1 else ()
    outs = [out_whole(lead + (1, rows, width), dtype) for dtype in dtypes]
    totals = [((width, cols), F32), ((1, cols), F32)] * do_in + [((8, width), F32)] * do_norm
    scratch = []
    if ranks:
        scratch = [pltpu.VMEM(shape, dtype) for shape, dtype in totals]
        outs.append(out_whole((ranks, width // ranks + EXTRA, cols), BF16))
    else:
        outs += [out_whole(*entry) for entry in totals]
    return run(
        functools.partial(
            proj_back_kernel,
            tuple(pieces),
            do_in,
            len(dtypes),
            bool(carry),
            got is not None,
            ranks,
        ),
        (1,),
        meta,
        ins,
        outs,
        scratch=scratch,
        cost=(2 * (do_in + do_norm) * n * rows * width * cols, 6 * n * rows * width, 0),
        name="proj_back",
    )


def last_kernel(meta, tokens, resid_grad, mine, got, across, gain, out):
    normed, inverse = standardize(tokens[0].astype(F32))
    grad = mine[0] + got[0, 0].astype(F32) + across[0].astype(F32)
    out[0] = resid_grad[0] + norm_back(grad * gain[...], normed, inverse)


def last_call(meta, b, tokens, resid_grad, mine, got, across, gain, held):
    _, rows, width = tokens.shape
    seq = lambda i, m: (b, 0, 0)
    one = lambda i, m: (0, 0, 0)
    block = (1, rows, width)
    return run(
        last_kernel,
        (1,),
        meta,
        [
            (tokens, block, seq),
            (resid_grad, block, seq),
            (mine, block, one),
            (got, (1,) + block, lambda i, m: (0, 0, 0, 0)),
            (across, block, one),
            whole(gain),
        ],
        [(tokens.shape, F32, block, seq)],
        cost=(0, 20 * rows * width, 0),
        name="last",
        held=[(x, 0) for x in held],
    )[0]


def pack_in_kernel(meta, proj_in, vec, out):
    s = meta[0]
    deep, width = proj_in.shape[0], proj_in.shape[1] // 3
    cols = out.shape[1]
    hw = cols // 3
    for k in range(width // hw):

        @pl.when(s == k)
        def _(k=k):
            for t in range(3):
                start = t * width + k * hw
                out[:deep, t * hw : (t + 1) * hw] = proj_in[:, start : start + hw]

    out[deep:] = jnp.zeros((out.shape[0] - deep, cols), BF16)
    size = vec.shape[1]
    for r in range(pl.cdiv(size, cols)):
        width_r = min(cols, size - r * cols)
        out[deep + r : deep + r + 1, :width_r] = vec[:, r * cols : r * cols + width_r]


def place_in_kernel(sizes, meta, *refs):
    outer = len(refs) - 13
    pieces, odd, rows, refs = refs[:outer], refs[outer], refs[outer + 1], refs[outer + 2 :]
    w, gain, bias, in_b, out_bias, ada_bias, up_b, down_bias, chosen, wanted, table = refs
    ranks = 2 * outer
    s, c, d = meta[0], meta[1], meta[2]
    deep, cols = w.shape[0] // ranks, w.shape[1]
    hw = cols // 3
    for m in range(ranks):
        piece = odd.at[m // 2] if m % 2 else pieces[m // 2]
        owner = d ^ m
        w[pl.ds(pl.multiple_of(owner * deep, deep), deep)] = piece[:deep]
        table[pl.ds(owner, 1)] = piece[deep:].astype(F32)[None]
    used = -(-sum(sizes) // cols)
    flat = [
        jnp.concatenate([table[k, r : r + 1] for r in range(used)], axis=1) for k in range(ranks)
    ]
    full, start = [], 0
    for size in sizes:
        full.append([f[:, start : start + size] for f in flat])
        start += size
    steps = [high * 32.0 + low for high, low in zip(full[7], full[8])]
    full = [jnp.concatenate(x, axis=1) for x in full]
    gain[...], bias[...], out_bias[...], ada_bias[...], down_bias[...] = (
        full[0],
        full[1],
        full[3],
        full[4],
        full[6],
    )
    width = w.shape[0]
    half = sizes[5] // 2
    for k in range(width // hw):

        @pl.when(s == k)
        def _(k=k):
            in_b[...] = jnp.concatenate(
                [full[2][:, t * width + k * hw : t * width + (k + 1) * hw] for t in range(3)], axis=1
            )

    for k in range(2):

        @pl.when(c == k)
        def _(k=k):
            up_b[...] = jnp.concatenate(
                [full[5][:, (2 * n + k) * half : (2 * n + k + 1) * half] for n in range(ranks)],
                axis=1,
            )

    want = jnp.concatenate([x for step in steps for x in (step, jnp.zeros((1, 1), F32))], axis=1)
    wanted[...] = want
    at = d * rows.shape[0] + lax.broadcasted_iota(jnp.int32, (rows.shape[0], 1), 0)
    picked = dot_at((at.astype(F32) == want).astype(BF16), rows[...]).astype(BF16)
    part = rows.shape[1] // ranks
    for k in range(ranks):
        chosen[k] = picked[:, k * part : (k + 1) * part]


def pack_rest_kernel(meta, up, down, proj_out, out):
    c = meta[1]
    deep = up.shape[0]
    width = down.shape[1]
    half = down.shape[0] // 2
    ff = up.shape[1] // 2
    for k in range(2):

        @pl.when(c == k)
        def _(k=k):
            for d in range(ff // half):
                out[:, d * half : (d + 1) * half] = up[:, (2 * d + k) * half : (2 * d + k + 1) * half]
            out[:, ff : ff + width] = down[k * half : k * half + deep]
            out[:, ff + width : ff + 2 * width] = down[k * half + deep : (k + 1) * half]
            out[:, ff + 2 * width :] = proj_out[:, k * width // 2 : (k + 1) * width // 2]


def place_rest_kernel(meta, *refs):
    *pieces, up, down, out = refs
    d = meta[2]
    deep = up.shape[0] // len(pieces)
    ff, width = up.shape[1], down.shape[1]
    for m, piece in enumerate(pieces):
        owner = d ^ m
        base = pl.multiple_of(owner * deep, deep)
        up[pl.ds(base, deep)] = piece[:, :ff]
        out[pl.ds(base, deep)] = piece[:, ff + 2 * width :]
        base = pl.multiple_of(owner * (2 * deep), deep)
        down[pl.ds(base, deep)] = piece[:, ff : ff + width]
        base = pl.multiple_of(owner * (2 * deep) + deep, deep)
        down[pl.ds(base, deep)] = piece[:, ff + width : ff + 2 * width]


def half_kernel(meta, here, came, *outs):
    o = meta[2] // 2
    for m, out in enumerate(outs):
        at = pl.ds(o ^ m, 1)
        out[...] = (here[at].astype(F32) + came[at].astype(F32))[0].astype(BF16)


def split_kernel(meta, here, came, out):
    out[...] = (here[...].astype(F32) + came[...].astype(F32)).astype(BF16)


def total(refs):
    result = 0.0
    for ref in refs:
        for k in range(ref.shape[0] if len(ref.shape) == 3 else 1):
            result = result + (ref[k] if len(ref.shape) == 3 else ref[...]).astype(F32)
    return result


def gather_kernel(counts, meta, *refs):
    *refs, out = refs
    start, place = 0, 0
    for n in counts:
        value = total(refs[start : start + n])
        out[:, place : place + value.shape[1]] = value.astype(BF16)
        start, place = start + n, place + value.shape[1]


def gather_call(meta, groups):
    refs = [x for g in groups for x in g]
    shape = (groups[0][0].shape[-2], sum(g[0].shape[-1] for g in groups))
    return run(
        functools.partial(gather_kernel, tuple(len(g) for g in groups)),
        (1,),
        meta,
        [whole(x) for x in refs],
        [out_whole(shape, BF16)],
        cost=(0, 2 * sum(x.size for x in refs), 0),
        name="gather",
    )[0]


def close_rest_kernel(meta, own, across, pair, up, down, out):
    c = meta[1]
    deep = own.shape[0]
    width = out.shape[1]
    half = down.shape[0] // 2
    ff = up.shape[1] // 2
    mine = own[...].astype(F32) + across[...].astype(F32)
    other = pair[0].astype(F32) + pair[1].astype(F32)
    for k in range(2):
        value = jnp.where(c == k, mine, other)
        for d in range(ff // half):
            up[:, (2 * d + k) * half : (2 * d + k + 1) * half] = value[:, d * half : (d + 1) * half]
        down[k * half : k * half + deep] = value[:, ff : ff + width]
        down[k * half + deep : (k + 1) * half] = value[:, ff + width : ff + 2 * width]
        out[:, k * width // 2 : (k + 1) * width // 2] = value[:, ff + 2 * width :]


def close_in_kernel(ranks, meta, own, across, pair, w, gain, bias, in_bias, out_bias, up_bias, down_bias, held):
    s, d = meta[0], meta[2]
    deep, width = w.shape[0], w.shape[1] // 3
    cols = own.shape[1]
    hw = cols // 3
    held[pl.ds(s, 1)] = own[...].astype(F32)[None]
    held[pl.ds(s ^ 2, 1)] = across[...].astype(F32)[None]
    held[pl.ds(s ^ 1, 1)] = pair[0].astype(F32)[None]
    held[pl.ds(s ^ 3, 1)] = pair[1].astype(F32)[None]
    for k in range(4):
        for t in range(3):
            w[:, t * width + k * hw : t * width + (k + 1) * hw] = held[k, :deep, t * hw : (t + 1) * hw]
    rows = [
        jnp.concatenate([held[k, deep + r : deep + r + 1] for r in range(EXTRA)], axis=1)
        for k in range(4)
    ]
    biases = jnp.concatenate(
        [rows[k][:, t * hw : (t + 1) * hw] for t in range(3) for k in range(4)], axis=1
    )
    ff = 2 * width
    ups = [rows[0][:, cols : cols + ff] + rows[2][:, cols : cols + ff]]
    ups.append(rows[1][:, cols : cols + ff] + rows[3][:, cols : cols + ff])
    rest = rows[0] + rows[1] + rows[2] + rows[3]
    rest = rest[:, cols + ff :]
    part, third, half = width // ranks, 3 * width // ranks, ff // ranks
    for k in range(ranks):

        @pl.when(d == k)
        def _(k=k):
            for n, out in enumerate((gain, bias, out_bias, down_bias)):
                out[...] = rest[:, n * width + k * part : n * width + (k + 1) * part]
            in_bias[...] = biases[:, k * third : (k + 1) * third]
            up_bias[...] = jnp.concatenate([u[:, k * half : (k + 1) * half] for u in ups], axis=1)


def shards(
    tokens,
    prefix_len,
    timestep,
    norm_gain,
    norm_bias,
    proj_in,
    proj_in_bias,
    proj_out,
    proj_out_bias,
    time_table,
    ada_weight,
    ada_bias,
    mlp_up,
    mlp_up_bias,
    mlp_down,
    mlp_down_bias,
    out_grad,
):
    count, local_len, width = tokens.shape
    members = lax.axis_size("seq")
    ranks = lax.axis_size("dp")
    s = lax.axis_index("seq")
    d = lax.axis_index("dp")
    hw = H // members * HD
    deep = proj_in.shape[0]
    half_ff = mlp_down.shape[0] // 2
    ff = ranks * half_ff
    half_out = width // 2
    meta = jnp.concatenate([jnp.stack([s, s % 2, d, d % 2]).astype(jnp.int32), prefix_len])

    tok_x = seq_swap(tokens, 2)

    vectors = [
        norm_gain,
        norm_bias,
        proj_in_bias,
        proj_out_bias,
        ada_bias,
        mlp_up_bias,
        mlp_down_bias,
        (timestep // 32).astype(BF16),
        (timestep % 32).astype(BF16),
    ]
    sizes = tuple(v.shape[0] for v in vectors)
    pack_in = run(
        pack_in_kernel,
        (1,),
        meta,
        [whole(proj_in), whole(jnp.concatenate(vectors)[None])],
        [out_whole((deep + EXTRA, 3 * hw), BF16)],
        name="pack_in",
    )[0]
    in_even, in_odd = dp_collect(pack_in)
    tok_c = seq_swap(after(tokens, pack_in), 1)
    pack_rest = run(
        pack_rest_kernel,
        (1,),
        meta,
        [whole(after(mlp_up, pack_in)), whole(mlp_down), whole(proj_out)],
        [out_whole((deep, ff + 2 * width + half_out), BF16)],
        name="pack_rest",
    )[0]
    in_odd = after(in_odd, pack_rest)
    kinds = count + 1
    in_w, gain, bias, in_b, out_bias, ada_bias_full, up_b, down_bias, chosen, wanted = run(
        functools.partial(place_in_kernel, sizes),
        (1,),
        meta,
        [whole(x) for x in (*in_even, in_odd, time_table)],
        [
            out_whole((width, 3 * hw), BF16),
            out_whole((1, width), F32),
            out_whole((1, width), F32),
            out_whole((1, 3 * hw), F32),
            out_whole((1, width), F32),
            out_whole((1, 3 * width), F32),
            out_whole((1, ff), F32),
            out_whole((1, width), F32),
            out_whole((ranks, ranks * kinds, width // ranks), BF16),
            out_whole((1, ranks * kinds), F32),
        ],
        scratch=[pltpu.VMEM((ranks, EXTRA, 3 * hw), F32)],
        name="place_in",
    )
    chosen_got = dp_turn(chosen)

    outer = ranks // 2
    early = max(1, outer // 4)
    soon = after(pack_rest, in_even)
    later = after(pack_rest, in_odd)
    rest_even = [pack_rest]
    rest_even += [dp_swap(soon if m <= early else later, 2 * m) for m in range(1, outer)]
    rest_odd = [dp_swap(soon, 1)]

    offsets = jnp.arange(local_len, dtype=jnp.int32)
    positions = jnp.concatenate([(s ^ j) * local_len + offsets for j in range(members)]).astype(F32)
    half_width = HD // 2
    frequency = jnp.exp(jnp.arange(half_width, dtype=F32) * (-math.log(10000.0) / half_width))
    angles = positions[:, None] * frequency[None, :]
    cosine, sine = jnp.cos(angles), jnp.sin(angles)
    cosine = jnp.concatenate([cosine] * 4, axis=1)
    sine = jnp.concatenate([-sine, sine] * 2, axis=1)

    one, two = slice(1, 1 + early), slice(1 + early, 1 + 2 * early)
    three = slice(1 + 2 * early, outer)
    qkv_near = qkv_call(meta, 0, tokens, tok_c, gain, bias, in_w, in_b, cosine, sine)
    rest_odd += [dp_swap(piece, 1) for piece in rest_even[one]]
    tok_x = after(tok_x, qkv_near)
    tok_d = seq_swap(tok_x, 1)
    embedded = jnp.sum(after(chosen_got, qkv_near).astype(F32), axis=0)
    activated = jax.nn.silu(embedded).astype(BF16)
    mod_parts = dot(activated, ada_weight).reshape(ranks, kinds, 3 * width)
    mod_got = dp_turn(mod_parts)
    og_other = seq_swap(after(out_grad, qkv_near), 1)
    qkv_far = qkv_call(
        meta,
        2,
        tok_x,
        tok_d,
        gain,
        bias,
        in_w,
        in_b,
        after(cosine, mod_parts, rest_even[one], rest_odd[0]),
        sine,
    )
    near_again, rest_even[two] = after((qkv_near, rest_even[two]), qkv_far, og_other)
    rest_odd += [dp_swap(piece, 1) for piece in rest_even[two]]
    mixed_2, mixed_3, weights, recips = attend_call(meta, 2, near_again, qkv_far, local_len)
    across_2, across_3 = seq_swap(mixed_2, 2), seq_swap(mixed_3, 3)
    near_again = after(qkv_near, mixed_2, rest_odd[one])
    mixed_0, mixed_1, weights, recips = attend_call(
        meta, 0, near_again, qkv_far, local_len, (weights, recips)
    )
    mixed = [mixed_0, mixed_1, mixed_2, mixed_3]
    mixed_own = [mixed_0, seq_swap(mixed_1, 1), across_2, across_3]
    rest_even[three] = after(rest_even[three], mixed_0)
    rest_odd += [dp_swap(piece, 1) for piece in rest_even[three]]
    mods = jnp.sum(after(mod_got, mixed_0), axis=0) + ada_bias_full
    up_w, down_w, out_own = run(
        place_rest_kernel,
        (1,),
        meta,
        [whole(x) for pair in zip(rest_even, rest_odd) for x in pair],
        [
            out_whole((width, ff), BF16),
            out_whole((ff, width), BF16),
            out_whole((width, half_out), BF16),
        ],
        name="place_rest",
    )
    out_other = seq_swap(out_own, 1)

    residual, mlp_own, out_rel = mix_call(
        meta, mixed_own, tokens, out_own, out_other, out_bias, mods
    )
    mlp_other = seq_swap(mlp_own, 1)
    own_branch, own_input, other, up_here, up_away, down_here, down_away, up_bias_part = mlp_call(
        meta, mlp_own, mlp_other, out_grad, og_other, up_w, up_b, down_w, mods, ranks
    )
    got = seq_swap(other, 1)
    up_came = dp_swap(up_away, 1)
    down_came = dp_swap(down_away, 1)
    block_out, resid_grad, *others = turn_call(
        meta, residual, out_grad, own_branch, own_input, got, down_bias, mods, mixed_own, out_rel
    )
    mixed_grads, (row_sums, biases, out_here, out_away) = others[:4], others[4:]
    head_grads = [mixed_grads[0]] + [seq_swap(mixed_grads[j], j) for j in range(1, members)]

    def halves(here, came):
        pieces = run(
            half_kernel,
            (1,),
            meta,
            [whole(here), whole(came)],
            [out_whole(here.shape[1:], BF16) for _ in range(ranks // 2)],
            name="half",
        )
        return pieces[0], [pieces[0]] + [dp_swap(p, 2 * m) for m, p in enumerate(pieces) if m]

    out_came = seq_swap(out_away, 1)
    row_grad = jnp.concatenate([row_sums[:, 0], jnp.sum(row_sums[:, 1], axis=0)[None]], axis=0)
    row_grad = row_grad + seq_swap(row_grad, 1)
    out_sum = run(
        split_kernel,
        (1,),
        meta,
        [whole(out_here), whole(after(out_came, row_grad))],
        [out_whole(out_here.shape, BF16)],
        name="split",
    )[0]
    out_got = dp_turn(out_sum.reshape(ranks, deep, half_out))
    up_half, up_got = halves(after(up_here, out_sum), up_came)

    shared = (gain, bias, in_w, cosine, sine)
    near, far = (tok_c, tok_d), (tok_x, tokens)

    def attend_back(b, *others):
        return back_call(
            meta, b, after(qkv_near, *others), qkv_far, weights, recips, mixed, head_grads
        )

    row_away = seq_swap(row_grad, 2)
    raw_0 = attend_back(0, up_half, row_grad)
    row_grad = row_grad + after(row_away, raw_0)
    rows_got = dp_all(row_grad)
    sent, *carry = proj_back_call(meta, 0, (1, 3), near, after(raw_0, row_grad), *shared, (BF16,))
    came_0 = seq_swap(sent, 1)
    up_sum = gather_call(meta, [after(up_got, sent)])
    down_half, down_got = halves(after(down_here, up_sum), down_came)
    out_got = after(out_got, down_half)

    raw_1 = attend_back(1, sent, down_half, out_got)
    across, mine_0, *carry = proj_back_call(
        meta, 0, (2, 0), far, after(raw_0, raw_1), *shared, (BF16, F32), carry, came_0
    )
    across_0 = seq_swap(across, 2)
    sent, *carry = proj_back_call(
        meta, 1, (1, 3), near, after(raw_1, across), *shared, (BF16,), carry
    )
    came_1 = seq_swap(sent, 1)

    all_rows = after(rows_got, sent).reshape(ranks * kinds, 3 * width)
    exact = functools.partial(lax.dot_general, precision=HIGHEST, preferred_element_type=F32)
    act_rows_grad = exact(all_rows, ada_weight.astype(F32), (((1,), (1,)), ((), ())))
    embed_grad = jax.vjp(jax.nn.silu, embedded)[1](act_rows_grad)[0]
    embed_got = dp_all(embed_grad)
    rest_sum = gather_call(meta, [(up_sum,), after(down_got, sent), (out_got,)])
    across, mine_1, *carry = proj_back_call(
        meta, 1, (2, 0), far, after(raw_1, rest_sum, embed_grad), *shared, (BF16, F32), carry, came_1
    )
    across_1 = seq_swap(across, 2)
    rest_x = seq_swap(after(rest_sum, across), 2)
    tokens_grad = last_call(
        meta, 0, tokens, after(resid_grad, across), mine_0, came_0, across_0, gain, ()
    )
    raw_2 = attend_back(2, tokens_grad)
    sent, *carry = proj_back_call(meta, 2, (1, 3), near, raw_2, *shared, (BF16,), carry)
    came_2 = seq_swap(sent, 1)
    tokens_grad = last_call(
        meta, 1, tokens, after(resid_grad, sent), mine_1, came_1, across_1, gain, (tokens_grad,)
    )
    across, mine_2, in_sent = proj_back_call(
        meta,
        2,
        (2, 0),
        far,
        after(raw_2, tokens_grad),
        *shared,
        (BF16, F32),
        carry,
        came_2,
        True,
        ranks,
        (up_bias_part, biases),
    )
    across_2 = seq_swap(across, 2)
    in_got = dp_turn(in_sent)
    rest_x = after(rest_x, in_sent)
    rest_pair = seq_swap(jnp.stack([rest_sum, rest_x]), 1)
    all_rows = after(all_rows, in_sent)
    ada_bias_grad = lax.dynamic_slice_in_dim(
        jnp.sum(all_rows, axis=0), d * ada_bias.shape[0], ada_bias.shape[0], 0
    )
    ada_grad = exact(activated.astype(F32), all_rows, (((0,), (0,)), ((), ())))
    table_at = d * time_table.shape[0] + jnp.arange(time_table.shape[0], dtype=jnp.int32)
    selector = (table_at.astype(F32)[:, None] == wanted).astype(F32)
    embed_all = after(embed_got, in_sent).transpose(1, 0, 2).reshape(ranks * kinds, width)
    table_grad = exact(selector, embed_all, (((1,), (0,)), ((), ())))
    up_final, down_final, out_final = run(
        close_rest_kernel,
        (1,),
        meta,
        [whole(x) for x in (rest_sum, rest_x, rest_pair)],
        [
            out_whole(mlp_up.shape, F32),
            out_whole(mlp_down.shape, F32),
            out_whole(proj_out.shape, F32),
        ],
        name="close_rest",
    )

    in_sum = gather_call(meta, [(after(in_got, up_final, table_grad, ada_grad),)])
    in_x = seq_swap(in_sum, 2)
    tokens_grad = last_call(
        meta, 2, tokens, after(resid_grad, in_sum), mine_2, came_2, across_2, gain, (tokens_grad,)
    )
    in_pair = seq_swap(jnp.stack([in_sum, after(in_x, tokens_grad)]), 1)
    part, third, ff_part = width // ranks, 3 * width // ranks, 4 * width // ranks
    in_final, gain_f, bias_f, in_bias_f, out_bias_f, up_bias_f, down_bias_f = run(
        functools.partial(close_in_kernel, ranks),
        (1,),
        meta,
        [whole(x) for x in (in_sum, in_x, in_pair)],
        [
            out_whole(proj_in.shape, F32),
            out_whole((1, part), F32),
            out_whole((1, part), F32),
            out_whole((1, third), F32),
            out_whole((1, part), F32),
            out_whole((1, ff_part), F32),
            out_whole((1, part), F32),
        ],
        scratch=[pltpu.VMEM((members, deep + EXTRA, 3 * hw), F32)],
        name="close_in",
    )
    return (
        block_out,
        tokens_grad,
        gain_f[0],
        bias_f[0],
        in_final,
        in_bias_f[0],
        out_final,
        out_bias_f[0],
        table_grad,
        ada_grad,
        ada_bias_grad,
        up_final,
        up_bias_f[0],
        down_final,
        down_bias_f[0],
    )


def solution(mesh):
    rows = P("dp", None)
    vector = P("dp")
    stream = P("dp", "seq", None)
    in_specs = (
        stream,
        vector,
        vector,
        vector,
        vector,
        rows,
        vector,
        rows,
        vector,
        rows,
        rows,
        vector,
        rows,
        vector,
        rows,
        vector,
        stream,
    )
    out_specs = (
        stream,
        stream,
        vector,
        vector,
        rows,
        vector,
        rows,
        vector,
        rows,
        rows,
        vector,
        rows,
        vector,
        rows,
        vector,
    )
    return jax.shard_map(shards, mesh=mesh, in_specs=in_specs, out_specs=out_specs, check_vma=False)
```

```python
import functools
import math

import jax
import jax.numpy as jnp
from jax import lax
from jax.experimental import pallas as pl
from jax.experimental.pallas import tpu as pltpu
from jax.sharding import PartitionSpec as P

H = 12
HD = 64
EPS = 1e-05
NEG = -1e30
COST = 30
F32 = jnp.float32
BF16 = jnp.bfloat16
HIGHEST = lax.Precision.HIGHEST
VMEM_LIMIT = 62 * 1024 * 1024
ROWS = 48
EXTRA = 16


def standardize(values):
    centred = values - jnp.mean(values, axis=-1, keepdims=True)
    inverse = lax.rsqrt(jnp.mean(centred * centred, axis=-1, keepdims=True) + EPS)
    return centred * inverse, inverse


def norm_back(gradient, normed, inverse):
    return inverse * (
        gradient
        - jnp.mean(gradient, axis=-1, keepdims=True)
        - normed * jnp.mean(gradient * normed, axis=-1, keepdims=True)
    )


def dot(left, right):
    return jnp.dot(left, right, preferred_element_type=F32)


def dot_bt(left, right):
    return lax.dot_general(left, right, (((1,), (1,)), ((), ())), preferred_element_type=F32)


def dot_at(left, right):
    return lax.dot_general(left, right, (((0,), (0,)), ((), ())), preferred_element_type=F32)


TAIL_P = 0.55
TAIL = (
    0.001045374169866761,
    0.2933056852691112,
    0.41788788917041303,
    -0.08811700935317877,
    0.8046529189842585,
    -0.5409110079247637,
    0.11213617568673577,
)


def gelu_both(values):
    bell = jnp.exp(values * values * -0.5)
    inner = 1.0 / (1.0 + (TAIL_P / math.sqrt(2.0)) * jnp.abs(values))
    tail = TAIL[6]
    for coefficient in TAIL[5::-1]:
        tail = tail * inner + coefficient
    tail = tail * bell * 0.5
    cumulative = jnp.where(values >= 0.0, 1.0 - tail, tail)
    return values * cumulative, cumulative + values * bell * (1.0 / math.sqrt(2.0 * math.pi))


def after(value, *others):
    return lax.optimization_barrier((value, others))[0]


def seq_swap(value, mask):
    return lax.ppermute(value, "seq", [(s, s ^ mask) for s in range(lax.axis_size("seq"))])


def dp_swap(value, mask):
    return lax.ppermute(value, "dp", [(d, d ^ mask) for d in range(lax.axis_size("dp"))])


def dp_collect(value):
    mine = [value] + [dp_swap(value, m) for m in range(2, lax.axis_size("dp"), 2)]
    return mine, dp_swap(jnp.stack(mine), 1)


def quad(value):
    across = seq_swap(value, 2)
    return value, across, seq_swap(jnp.stack([value, across]), 1)


def dp_turn(value, outer_only=False):
    groups = None
    if outer_only:
        outer = lax.axis_size("dp") // 2
        groups = [[o * 2 + i for o in range(outer)] for i in range(2)]
    return lax.all_to_all(
        value, "dp", split_axis=0, concat_axis=0, tiled=True, axis_index_groups=groups
    )


def dp_all(value):
    return dp_turn(jnp.broadcast_to(value[None], (lax.axis_size("dp"),) + value.shape))


def run(body, grid, meta, ins, outs, scratch=(), cost=(0, 0, 0), name=None, held=()):
    specs = [pl.BlockSpec(block, index) for _, block, index in ins]
    specs += [pl.BlockSpec(memory_space=pl.ANY) for _ in held]
    first = 1 + len(ins)
    kernel = body
    if held:

        def kernel(meta, *refs):
            return body(meta, *refs[: len(ins)], *refs[len(ins) + len(held) :])

    return pl.pallas_call(
        kernel,
        grid_spec=pltpu.PrefetchScalarGridSpec(
            num_scalar_prefetch=1,
            grid=grid,
            in_specs=specs,
            out_specs=[pl.BlockSpec(block, index) for _, _, block, index in outs],
            scratch_shapes=list(scratch),
        ),
        out_shape=[jax.ShapeDtypeStruct(shape, dtype) for shape, dtype, _, _ in outs],
        input_output_aliases={first + n: k for n, (_, k) in enumerate(held)},
        compiler_params=pltpu.CompilerParams(
            dimension_semantics=("arbitrary",) * len(grid), vmem_limit_bytes=VMEM_LIMIT
        ),
        cost_estimate=pl.CostEstimate(
            flops=int(cost[0] * COST), bytes_accessed=int(cost[1] * COST), transcendentals=0
        ),
        name=name,
    )(meta, *[array for array, _, _ in ins], *[array for array, _ in held])


def whole(array):
    zeros = (0,) * array.ndim
    return (array, array.shape, lambda *_: zeros)


def out_whole(shape, dtype):
    zeros = (0,) * len(shape)
    return (shape, dtype, shape, lambda *_: zeros)


def partner_lanes(tile):
    lane = lax.broadcasted_iota(jnp.int32, tile.shape, 1)
    ahead = pltpu.roll(tile, 96, 1)
    behind = pltpu.roll(tile, 32, 1)
    return jnp.where((lane & (HD // 2)) == 0, ahead, behind)


def qkv_kernel(meta, x0, x1, gain, bias, w, b, cosine, sine, out):
    half = w.shape[1] // 3
    tokens = jnp.where(pl.program_id(0) == 0, x0[0], x1[0]).astype(F32)
    normed, _ = standardize(tokens)
    attn_input = (normed * gain[...] + bias[...]).astype(BF16)
    projected = dot(attn_input, w[...]) + b[...]
    cos, sin = cosine[...], sine[...]
    scale = HD**-0.5
    lane = lax.broadcasted_iota(jnp.int32, cos.shape, 1)
    for t in range(2 * half // 128):
        tile = projected[:, t * 128 : (t + 1) * 128]
        turned = tile * cos + partner_lanes(tile) * sin
        if (t + 1) * 128 <= half:
            turned = turned * scale
        elif t * 128 < half:
            turned = turned * jnp.where(lane < half - t * 128, scale, 1.0)
        out[0, :, t * 128 : (t + 1) * 128] = turned.astype(BF16)
    out[0, :, 2 * half :] = projected[:, 2 * half :].astype(BF16)


def qkv_call(meta, base, x0, x1, gain, bias, w, b, cosine, sine):
    count, rows, width = x0.shape
    last = count - 1
    return run(
        qkv_kernel,
        (2, count),
        meta,
        [
            (x0, (1, rows, width), lambda p, q, m: (jnp.where(p == 0, q, last), 0, 0)),
            (x1, (1, rows, width), lambda p, q, m: (jnp.where(p == 0, 0, q), 0, 0)),
            whole(gain),
            whole(bias),
            whole(w),
            whole(b),
            (cosine, (rows, 128), lambda p, q, m: (base + p, 0)),
            (sine, (rows, 128), lambda p, q, m: (base + p, 0)),
        ],
        [
            (
                (count, 2 * rows, w.shape[1]),
                BF16,
                (1, rows, w.shape[1]),
                lambda p, q, m: (q, p, 0),
            )
        ],
        cost=(4 * count * rows * width * w.shape[1], 10 * count * rows * width, 0),
        name="qkv",
    )[0]


def fold(rows):
    half = rows.shape[0] // 2
    return jnp.concatenate([rows[:half], rows[half:]], axis=1)


def unfold(pair):
    width = pair.shape[1] // 2
    return jnp.concatenate([pair[:, :width], pair[:, width:]], axis=0)


def attend_kernel(base, meta, qa, qb, o0, o1, weights, recips):
    b, k = pl.program_id(0), pl.program_id(1)
    j = base + k
    s, prefix = meta[0], meta[4 + b]
    rows = o0.shape[1] * 2
    hw = o0.shape[2] // 2
    heads = hw // HD
    half = qa.shape[1]
    source = qb if base else qa
    mine = source[0, pl.ds(pl.multiple_of(k * rows, rows), rows), :hw]
    at = (s ^ j) * rows + lax.broadcasted_iota(jnp.int32, (rows, 1), 0)
    hidden_from = jnp.where(at < prefix, 1.0, 0.0)
    lane = lax.broadcasted_iota(jnp.int32, (1, rows), 1)
    fills = []
    for side in range(2):
        places = [(s ^ (2 * side + piece)) * rows + lane for piece in range(half // rows)]
        where = jnp.concatenate(places, axis=1)
        fills.append(jnp.where(where < prefix, 0.0, NEG))
    lane128 = lax.broadcasted_iota(jnp.int32, (rows, 128), 1)
    kept = jnp.zeros((rows, 128), F32)
    outs = []
    for h in range(heads):
        q = mine[:, h * HD : (h + 1) * HD]
        scores = []
        for side, ref in enumerate((qa, qb)):
            keys = ref[0, :, hw + h * HD : hw + (h + 1) * HD]
            scores.append(dot_bt(q, keys) + hidden_from * fills[side])
        top = jnp.maximum(
            jnp.max(scores[0], axis=1, keepdims=True), jnp.max(scores[1], axis=1, keepdims=True)
        )
        sums = jnp.zeros((rows, 1), F32)
        mixed = jnp.zeros((rows, HD), F32)
        for side, ref in enumerate((qa, qb)):
            v = ref[0, :, 2 * hw + h * HD : 2 * hw + (h + 1) * HD]
            e = jnp.exp(scores[side] - top)
            sums = sums + jnp.sum(e, axis=1, keepdims=True)
            e = e.astype(BF16)
            weights[0, h, :, side * half : (side + 1) * half] = e
            mixed = mixed + dot(e, v)
        recip = 1.0 / sums
        kept = jnp.where(lane128 == h, recip, kept)
        outs.append((mixed * recip).astype(BF16))
    recips[0] = kept
    folded = fold(jnp.concatenate(outs, axis=1))
    for n, ref in enumerate((o0, o1)):

        @pl.when(k == n)
        def _(ref=ref):
            ref[0] = folded


def attend_call(meta, base, qa, qb, rows, held=()):
    count, half, cols = qa.shape
    hw = cols // 3
    heads = hw // HD
    keys = 2 * half
    block = (1, rows // 2, 2 * hw)
    return run(
        functools.partial(attend_kernel, base),
        (count, half // rows),
        meta,
        [
            (qa, (1, half, cols), lambda b, k, m: (b, 0, 0)),
            (qb, (1, half, cols), lambda b, k, m: (b, 0, 0)),
        ],
        [((count,) + block[1:], BF16, block, lambda b, k, m: (b, 0, 0)) for _ in range(2)]
        + [
            (
                (count, heads, keys, keys),
                BF16,
                (1, heads, rows, keys),
                lambda b, k, m: (b, 0, base + k, 0),
            ),
            ((count, keys, 128), F32, (1, rows, 128), lambda b, k, m: (b, base + k, 0)),
        ],
        cost=(
            2 * count * heads * keys * keys * HD * 4,
            count * heads * keys * keys,
            count * heads * keys * keys // 2,
        ),
        name="attend",
        held=[(x, 2 + n) for n, x in enumerate(held)],
    )


def back_kernel(meta, qa, qb, weights, recips, o0, o1, o2, o3, g0, g1, g2, g3, out, dk, dv, og, go):
    j = pl.program_id(1)
    rows = o0.shape[1] * 2
    hw = o0.shape[2] // 2
    heads = hw // HD
    half = qa.shape[1]
    place = lax.rem(j, 2) * rows
    scale = HD**-0.5
    for k, (o, g) in enumerate(((o0, g0), (o1, g1), (o2, g2), (o3, g3))):

        @pl.when(j == k)
        def _(o=o, g=g):
            grad = g[...].astype(F32)
            go[...] = unfold(grad)
            og[...] = unfold(grad * o[0].astype(F32))

    @pl.when(j == 0)
    def _():
        dk[...] = jnp.zeros_like(dk)
        dv[...] = jnp.zeros_like(dv)

    mine = jnp.where(j < 2, qa[0, pl.ds(place, rows), :hw], qb[0, pl.ds(place, rows), :hw])
    query_grads = []
    for h in range(heads):
        cols = slice(h * HD, (h + 1) * HD)
        recip = recips[0, :, h : h + 1]
        grad = (go[:, cols] * recip).astype(BF16)
        centre = jnp.sum(og[:, cols], axis=1, keepdims=True) * recip
        q = mine[:, cols]
        dq = jnp.zeros((rows, HD), F32)
        for side, ref in enumerate((qa, qb)):
            k = ref[0, :, hw + h * HD : hw + (h + 1) * HD]
            v = ref[0, :, 2 * hw + h * HD : 2 * hw + (h + 1) * HD]
            e = weights[0, h, :, side * half : (side + 1) * half]
            ds = (e.astype(F32) * (dot_bt(grad, v) - centre)).astype(BF16)
            dq = dq + dot(ds, k)
            span = pl.ds(side * half, half)
            dk[h, span] += dot_at(ds, q)
            dv[h, span] += dot_at(e, grad)
        query_grads.append((dq * scale).astype(BF16))
    out[0, pl.ds(pl.multiple_of(j * rows, rows), rows), :hw] = jnp.concatenate(query_grads, axis=1)

    @pl.when(j == pl.num_programs(1) - 1)
    def _():
        out[0, :, hw : 2 * hw] = jnp.concatenate(
            [dk[h].astype(BF16) for h in range(heads)], axis=1
        )
        out[0, :, 2 * hw :] = jnp.concatenate([dv[h].astype(BF16) for h in range(heads)], axis=1)


def back_call(meta, base, some, qa, qb, weights, recips, olds, grads, held=()):
    count, half, cols = qa.shape
    hw = cols // 3
    heads = hw // HD
    keys = 2 * half
    rows = olds[0].shape[1] * 2
    block = (1,) + olds[0].shape[1:]
    piece = lambda b, j, m: (base + b, 0, 0)
    ins = [
        (qa, (1, half, cols), piece),
        (qb, (1, half, cols), piece),
        (weights, (1, heads, rows, keys), lambda b, j, m: (base + b, 0, j, 0)),
        (recips, (1, rows, 128), lambda b, j, m: (base + b, j, 0)),
    ]
    ins += [(x, block, piece) for x in olds]
    for k, x in enumerate(grads):
        first = base + (x.shape[0] - ROWS - count * block[1]) // block[1]
        ins.append((x, block[1:], lambda b, j, m, first=first: (first + b, 0)))
    return run(
        back_kernel,
        (some, keys // rows),
        meta,
        ins,
        [((count, keys, cols), BF16, (1, keys, cols), piece)],
        scratch=[
            pltpu.VMEM((heads, keys, HD), F32),
            pltpu.VMEM((heads, keys, HD), F32),
            pltpu.VMEM((rows, hw), F32),
            pltpu.VMEM((rows, hw), F32),
        ],
        cost=(8 * some * heads * keys * keys * HD * 4, 2 * some * heads * keys * keys, 0),
        name="attend_back",
        held=[(x, 0) for x in held],
    )[0]


def mix_kernel(meta, m0, m1, m2, m3, tokens, w_own, w_other, out_bias, mods, residual, mlp_in, w):
    b = pl.program_id(0)
    s, c, prefix = meta[0], meta[1], meta[4 + b]
    rows, width = tokens.shape[1:]
    hw = m0.shape[2] // 2

    @pl.when(b == 0)
    def _():
        for j in range(4):
            there = pl.ds(pl.multiple_of((s ^ j) * hw, hw), hw)
            own, other = w_own[there], w_other[there]
            even = c == 0
            w[j * hw : (j + 1) * hw, : width // 2] = jnp.where(even, own, other)
            w[j * hw : (j + 1) * hw, width // 2 :] = jnp.where(even, other, own)

    total = tokens[0].astype(F32) + out_bias[...]
    for j, ref in enumerate((m0, m1, m2, m3)):
        total = total + dot(unfold(ref[0]), w[j * hw : (j + 1) * hw])
    residual[0] = total
    normed, _ = standardize(total)
    at = s * rows + lax.broadcasted_iota(jnp.int32, (rows, 1), 0)
    clean = at < prefix
    count = pl.num_programs(0)
    noisy_row, clean_row = mods[pl.ds(b, 1)], mods[pl.ds(count, 1)]
    shift, scale = (
        jnp.where(
            clean,
            clean_row[:, part * width : (part + 1) * width],
            noisy_row[:, part * width : (part + 1) * width],
        )
        for part in range(2)
    )
    mlp_in[0] = (normed * (1.0 + scale) + shift).astype(BF16)


def mix_call(meta, parts, tokens, w_own, w_other, out_bias, mods):
    count, rows, width = tokens.shape
    seq = lambda b, m: (b, 0, 0)
    block = (1, rows, width)
    return run(
        mix_kernel,
        (count,),
        meta,
        [(p, (1,) + p.shape[1:], seq) for p in parts]
        + [(tokens, block, seq), whole(w_own), whole(w_other), whole(out_bias), whole(mods)],
        [
            (tokens.shape, F32, block, seq),
            (tokens.shape, BF16, block, seq),
            out_whole((width, width), BF16),
        ],
        cost=(2 * count * rows * width * width, 12 * count * rows * width, 0),
        name="mix",
    )


def mlp_kernel(
    meta,
    x0,
    x1,
    og0,
    og1,
    up,
    up_bias,
    down,
    mods,
    own_branch,
    own_input,
    other,
    up_here,
    up_away,
    down_here,
    down_away,
    up_bias_grad,
    up_acc,
    down_acc,
):
    p, b = pl.program_id(0), pl.program_id(1)
    count = pl.num_programs(1)
    s, i, prefix = meta[0], meta[3], meta[4 + b]
    rows, width = x0.shape[1:]
    first = p == 0
    x = jnp.where(first, x0[0], x1[0])
    incoming = jnp.where(first, og0[0], og1[0]).astype(F32)
    at = (s ^ p) * rows + lax.broadcasted_iota(jnp.int32, (rows, 1), 0)
    gate = jnp.where(
        at < prefix, mods[pl.ds(count, 1), 2 * width :], mods[pl.ds(b, 1), 2 * width :]
    )
    grad = (incoming * gate).astype(BF16)
    hidden, slope = gelu_both(dot(x, up[...]) + up_bias[...])
    hidden = hidden.astype(BF16)
    branch = dot(hidden, down[...])
    pre = (dot_bt(grad, down[...]) * slope)
    pre_low = pre.astype(BF16)
    back = dot_bt(pre_low, up[...])
    sums = jnp.sum(pre_low.astype(F32), axis=0, keepdims=True)

    @pl.when(first)
    def _():
        own_branch[0] = branch
        own_input[0] = back

    @pl.when(p == 1)
    def _():
        other[0, 0] = branch.astype(BF16)
        other[1, 0] = back.astype(BF16)

    start = jnp.logical_and(first, b == 0)

    @pl.when(start)
    def _():
        up_acc[...] = dot_at(x, pre_low)
        down_acc[...] = dot_at(hidden, grad)
        up_bias_grad[...] = sums

    @pl.when(jnp.logical_not(start))
    def _():
        up_acc[...] += dot_at(x, pre_low)
        down_acc[...] += dot_at(hidden, grad)
        up_bias_grad[...] += sums

    @pl.when(jnp.logical_and(p == 1, b == count - 1))
    def _():
        outer, deep = up_here.shape[0], up_here.shape[1]
        for d in range(2 * outer):
            upper = up_acc[d * deep : (d + 1) * deep].astype(BF16)
            base = d * 2 * deep
            lower = jnp.concatenate(
                [down_acc[base : base + deep], down_acc[base + deep : base + 2 * deep]], axis=1
            ).astype(BF16)

            @pl.when(i == d % 2)
            def _(d=d, upper=upper, lower=lower):
                up_here[d // 2] = upper
                down_here[d // 2] = lower

            @pl.when(i != d % 2)
            def _(d=d, upper=upper, lower=lower):
                up_away[d // 2] = upper
                down_away[d // 2] = lower


def mlp_call(meta, x0, x1, og0, og1, up, up_bias, down, mods, ranks):
    count, rows, width = x0.shape
    hidden = up.shape[1]
    last = count - 1
    block = (1, rows, width)
    first = lambda p, b, m: (jnp.where(p == 0, b, last), 0, 0)
    second = lambda p, b, m: (jnp.where(p == 0, 0, b), 0, 0)
    shared = (ranks // 2, width // ranks, hidden)
    return run(
        mlp_kernel,
        (2, count),
        meta,
        [
            (x0, block, first),
            (x1, block, second),
            (og0, block, first),
            (og1, block, second),
            whole(up),
            whole(up_bias),
            whole(down),
            whole(mods),
        ],
        [
            (x0.shape, F32, block, first),
            (x0.shape, F32, block, first),
            (
                (2,) + x0.shape,
                BF16,
                (2,) + block,
                lambda p, b, m: (0, jnp.where(p == 0, 0, b), 0, 0),
            ),
            out_whole(shared, BF16),
            out_whole(shared, BF16),
            out_whole(shared, BF16),
            out_whole(shared, BF16),
            out_whole((1, hidden), F32),
        ],
        scratch=[pltpu.VMEM((width, hidden), F32), pltpu.VMEM((hidden, width), F32)],
        cost=(24 * count * rows * width * hidden, 20 * count * rows * width, 0),
        name="mlp",
    )


def turn_kernel(
    meta,
    residual,
    out_grad,
    own_branch,
    own_input,
    got,
    down_bias,
    mods,
    m0,
    m1,
    m2,
    m3,
    w,
    block_out,
    resid_grad,
    g0,
    g1,
    g2,
    g3,
    biases,
    out_here,
    sums,
    acc,
):
    b = pl.program_id(0)
    count = pl.num_programs(0)
    s, c, prefix = meta[0], meta[1], meta[4 + b]
    rows, width = residual.shape[1:]
    hw = m0.shape[2] // 2
    resid = residual[0]
    incoming = out_grad[0].astype(F32)
    at = s * rows + lax.broadcasted_iota(jnp.int32, (rows, 1), 0)
    clean = at < prefix
    noisy_row, clean_row = mods[pl.ds(b, 1)], mods[pl.ds(count, 1)]
    scale, gate = (
        jnp.where(
            clean,
            clean_row[:, part * width : (part + 1) * width],
            noisy_row[:, part * width : (part + 1) * width],
        )
        for part in (1, 2)
    )
    branch = own_branch[0] + got[0, 0].astype(F32) + down_bias[...]
    input_two = own_input[0] + got[1, 0].astype(F32)
    block_out[0] = (resid + gate * branch).astype(BF16)
    normed, inverse = standardize(resid)
    grads = incoming + norm_back(input_two * (1.0 + scale), normed, inverse)
    resid_grad[0] = grads
    low = grads.astype(BF16)
    keep = jnp.where(clean, 1.0, 0.0)
    kept = []
    for part, value in enumerate((input_two, input_two * normed, incoming * branch)):
        value = value.astype(BF16).astype(F32)
        cols = slice(part * width, (part + 1) * width)
        everything = jnp.sum(value, axis=0, keepdims=True)
        old = jnp.sum(value * keep, axis=0, keepdims=True)
        kept.append((everything - old, old))
    branch_low = (incoming * gate).astype(BF16).astype(F32)
    down_sum = jnp.sum(branch_low, axis=0, keepdims=True)
    out_sum = jnp.sum(low.astype(F32), axis=0, keepdims=True)

    @pl.when(b == 0)
    def _():
        acc[...] = jnp.zeros_like(acc)
        biases[...] = jnp.zeros_like(biases)
        sums[...] = jnp.zeros_like(sums)

    for part, (noisy, old) in enumerate(kept):
        cols = slice(part * width, (part + 1) * width)
        sums[pl.ds(b, 1), cols] = noisy
        sums[pl.ds(count, 1), cols] += old
    biases[0:1] += down_sum
    biases[1:2] += out_sum
    for j, (m, g) in enumerate(((m0, g0), (m1, g1), (m2, g2), (m3, g3))):
        at = (width if j == 1 else 0) + b * (rows // 2)
        at = pl.ds(pl.multiple_of(at, rows // 2), rows // 2)
        g[at] = fold(dot_bt(low, w[j * hw : (j + 1) * hw])).astype(BF16)
        acc[j * hw : (j + 1) * hw] += dot_at(unfold(m[0]), low)

    @pl.when(b == count - 1)
    def _():
        for j in range(4):
            here = pl.ds(pl.multiple_of((s ^ j) * hw, hw), hw)
            block = acc[j * hw : (j + 1) * hw].astype(BF16)
            left, right = block[:, : width // 2], block[:, width // 2 :]
            even = c == 0
            out_here[here] = jnp.where(even, left, right)
            g1[here] = jnp.where(even, right, left)
        cols = g0.shape[1]
        kinds = ROWS * cols // (2 * 3 * width)
        value = sums[:kinds]
        high = value.astype(BF16)
        low_part = (value - high.astype(F32)).astype(BF16)
        lines = [
            x[k : k + 1, n * cols : (n + 1) * cols]
            for x in (high, low_part)
            for k in range(kinds)
            for n in range(3 * width // cols)
        ]
        lines = jnp.concatenate(lines, axis=0)
        for g in (g0, g1, g2, g3):
            g[g.shape[0] - ROWS :] = lines


def turn_call(meta, residual, out_grad, own_branch, own_input, got, down_bias, mods, parts, w):
    count, rows, width = residual.shape
    seq = lambda b, m: (b, 0, 0)
    block = (1, rows, width)
    return run(
        turn_kernel,
        (count,),
        meta,
        [
            (residual, block, seq),
            (out_grad, block, seq),
            (own_branch, block, seq),
            (own_input, block, seq),
            (got, (2,) + block, lambda b, m: (0, b, 0, 0)),
            whole(down_bias),
            whole(mods),
        ]
        + [(p, (1,) + p.shape[1:], seq) for p in parts]
        + [whole(w)],
        [
            (residual.shape, BF16, block, seq),
            (residual.shape, F32, block, seq),
        ]
        + [
            out_whole((extra + p.shape[0] * p.shape[1] + ROWS, p.shape[2]), BF16)
            for p, extra in zip(parts, (0, width, 0, 0))
        ]
        + [out_whole((8, width), F32), out_whole((width, width // 2), BF16)],
        scratch=[pltpu.VMEM((8, 3 * width), F32), pltpu.VMEM((width, width), F32)],
        cost=(4 * count * rows * width * width, 24 * count * rows * width, 0),
        name="turn",
    )


def rows_kernel(meta, g0, g1, g2, g3, out):
    def value(g):
        high = g[: g.shape[0] // 2].astype(F32)
        return high + g[g.shape[0] // 2 :].astype(F32)

    both = (value(g0) + value(g1)) + (value(g2) + value(g3))
    each = out.shape[1] // g0.shape[1]
    for k in range(out.shape[0]):
        out[k : k + 1] = jnp.concatenate(
            [both[k * each + n : k * each + n + 1] for n in range(each)], axis=1
        )


def proj_grad_kernel(meta, x0, x1, x2, x3, raw, w, gain, bias, up_bias, biases, cosine, sine, out, even, odd, acc, in_bias):
    b = pl.program_id(0)
    rows = x0.shape[1]
    hw = w.shape[1] // 3

    @pl.when(b == 0)
    def _():
        acc[...] = jnp.zeros_like(acc)
        in_bias[...] = jnp.zeros_like(in_bias)

    for k, x in enumerate((x0, x1, x2, x3)):
        at = slice(k * rows, (k + 1) * rows)
        normed, _ = standardize(x[0].astype(F32))
        cos, sin = cosine[at], sine[at]
        tiles = []
        for t in range(2 * hw // 128):
            tile = raw[0, at, t * 128 : (t + 1) * 128].astype(F32)
            tiles.append((tile * cos - partner_lanes(tile) * sin).astype(BF16))
        tiles.append(raw[0, at, 2 * hw :])
        grads = jnp.concatenate(tiles, axis=1)
        out[0, at] = grads
        acc[...] += dot_at(normed.astype(BF16), grads)
        in_bias[...] += jnp.sum(grads.astype(F32), axis=0, keepdims=True)

    @pl.when(b == pl.num_programs(0) - 1)
    def _():
        ranks = 2 * even.shape[0]
        deep, cols = acc.shape[0] // ranks, acc.shape[1]
        exact = functools.partial(
            lax.dot_general, precision=HIGHEST, preferred_element_type=F32
        )
        wide = w[...].astype(F32)
        ones = jnp.ones((8, cols), F32)
        last = (((1,), (1,)), ((), ()))
        gain_grad = exact(ones, acc[...] * wide, last)[0:1]
        bias_grad = exact(jnp.broadcast_to(in_bias[...], (8, cols)), wide, last)[0:1]
        flat = jnp.concatenate(
            [in_bias[...], up_bias[...], gain_grad, bias_grad, biases[1:2], biases[0:1]], axis=1
        )
        count = flat.shape[1] // cols
        extra = jnp.concatenate(
            [flat[:, r * cols : (r + 1) * cols] for r in range(count)]
            + [jnp.zeros((EXTRA - count, cols), F32)],
            axis=0,
        ).astype(BF16)
        gains, biases_in = (
            jnp.transpose(jnp.broadcast_to(x[...], (128, x.shape[1])))[:, :1] for x in (gain, bias)
        )
        acc[...] = acc[...] * gains + biases_in * in_bias[...]
        d = meta[2]
        for m in range(ranks):
            at = pl.ds(pl.multiple_of((d ^ m) * deep, deep), deep)
            value = acc[at]
            ref = odd if m % 2 else even
            ref[m // 2, :deep] = value.astype(BF16)
            ref[m // 2, deep:] = extra


def proj_grad_call(meta, xs, raw, w, gain, bias, up_bias, biases, cosine, sine, ranks):
    count, rows, width = xs[0].shape
    cols = w.shape[1]
    seq = lambda b, m: (b, 0, 0)
    keys = raw.shape[1]
    shared = (ranks // 2, width // ranks + EXTRA, cols)
    return run(
        proj_grad_kernel,
        (count,),
        meta,
        [(x, (1, rows, width), seq) for x in xs]
        + [(raw, (1, keys, cols), seq)]
        + [whole(x) for x in (w, gain, bias, up_bias, biases, cosine, sine)],
        [
            (raw.shape, BF16, (1, keys, cols), seq),
            out_whole(shared, BF16),
            out_whole(shared, BF16),
        ],
        scratch=[pltpu.VMEM((width, cols), F32), pltpu.VMEM((1, cols), F32)],
        cost=(2 * count * keys * width * cols, 6 * count * keys * width, 0),
        name="proj_grad",
    )


def token_grad_kernel(meta, g1, g3, w, sent):
    sent[0, 0] = dot_bt(g1[0], w[...]).astype(BF16)
    sent[1, 0] = dot_bt(g3[0], w[...]).astype(BF16)


def token_grad_call(meta, grads, w, shape):
    count, rows, width = shape
    cols = w.shape[1]
    return run(
        token_grad_kernel,
        (count,),
        meta,
        [
            (grads, (1, rows, cols), lambda b, m: (b, 1, 0)),
            (grads, (1, rows, cols), lambda b, m: (b, 3, 0)),
            whole(w),
        ],
        [((2,) + shape, BF16, (2, 1, rows, width), lambda b, m: (0, b, 0, 0))],
        cost=(4 * count * rows * width * cols, 8 * count * rows * width, 0),
        name="token_grad",
    )[0]


def across_kernel(meta, g2, w, got, across):
    across[0] = (dot_bt(g2[0], w[...]) + got[0, 0].astype(F32)).astype(BF16)


def across_call(meta, grads, w, got):
    _, count, rows, width = got.shape
    cols = w.shape[1]
    return run(
        across_kernel,
        (count,),
        meta,
        [
            (grads, (1, rows, cols), lambda b, m: (b, 2, 0)),
            whole(w),
            (got, (1, 1, rows, width), lambda b, m: (1, b, 0, 0)),
        ],
        [((count, rows, width), BF16, (1, rows, width), lambda b, m: (b, 0, 0))],
        cost=(2 * count * rows * width * cols, 8 * count * rows * width, 0),
        name="across",
    )[0]


def last_kernel(meta, tokens, resid_grad, g0, w, got, across, gain, out):
    normed, inverse = standardize(tokens[0].astype(F32))
    grad = dot_bt(g0[0], w[...]) + got[0, 0].astype(F32) + across[0].astype(F32)
    out[0] = resid_grad[0] + norm_back(grad * gain[...], normed, inverse)


def last_call(meta, tokens, resid_grad, grads, w, got, across, gain):
    count, rows, width = tokens.shape
    cols = w.shape[1]
    seq = lambda b, m: (b, 0, 0)
    block = (1, rows, width)
    return run(
        last_kernel,
        (count,),
        meta,
        [
            (tokens, block, seq),
            (resid_grad, block, seq),
            (grads, (1, rows, cols), seq),
            whole(w),
            (got, (1,) + block, lambda b, m: (0, b, 0, 0)),
            (across, block, seq),
            whole(gain),
        ],
        [(tokens.shape, F32, block, seq)],
        cost=(2 * count * rows * width * cols, 20 * count * rows * width, 0),
        name="last",
    )[0]


def pack_in_kernel(meta, proj_in, *refs):
    *vectors, out = refs
    s = meta[0]
    deep, width = proj_in.shape[0], proj_in.shape[1] // 3
    cols = out.shape[1]
    hw = cols // 3
    for k in range(width // hw):

        @pl.when(s == k)
        def _(k=k):
            for t in range(3):
                start = t * width + k * hw
                out[:deep, t * hw : (t + 1) * hw] = proj_in[:, start : start + hw]

    out[deep:] = jnp.zeros((out.shape[0] - deep, cols), BF16)
    vec = jnp.concatenate([v[...].astype(F32) for v in vectors], axis=1)
    size = vec.shape[1]
    for r in range(pl.cdiv(size, cols)):
        width_r = min(cols, size - r * cols)
        out[deep + r : deep + r + 1, :width_r] = vec[:, r * cols : r * cols + width_r].astype(BF16)


def place_in_kernel(sizes, meta, *refs):
    outer = len(refs) - 13
    pieces, odd, rows, refs = refs[:outer], refs[outer], refs[outer + 1], refs[outer + 2 :]
    w, gain, bias, in_b, out_bias, ada_bias, up_b, down_bias, chosen, wanted, table = refs
    ranks = 2 * outer
    s, c, d = meta[0], meta[1], meta[2]
    deep, cols = w.shape[0] // ranks, w.shape[1]
    hw = cols // 3
    for m in range(ranks):
        piece = odd.at[m // 2] if m % 2 else pieces[m // 2]
        owner = d ^ m
        w[pl.ds(pl.multiple_of(owner * deep, deep), deep)] = piece[:deep]
        table[pl.ds(owner, 1)] = piece[deep:].astype(F32)[None]
    used = -(-sum(sizes) // cols)
    flat = [
        jnp.concatenate([table[k, r : r + 1] for r in range(used)], axis=1) for k in range(ranks)
    ]
    full, start = [], 0
    for size in sizes:
        full.append([f[:, start : start + size] for f in flat])
        start += size
    steps = [high * 32.0 + low for high, low in zip(full[7], full[8])]
    full = [jnp.concatenate(x, axis=1) for x in full]
    gain[...], bias[...], out_bias[...], ada_bias[...], down_bias[...] = (
        full[0],
        full[1],
        full[3],
        full[4],
        full[6],
    )
    width = w.shape[0]
    half = sizes[5] // 2
    for k in range(width // hw):

        @pl.when(s == k)
        def _(k=k):
            in_b[...] = jnp.concatenate(
                [full[2][:, t * width + k * hw : t * width + (k + 1) * hw] for t in range(3)], axis=1
            )

    for k in range(2):

        @pl.when(c == k)
        def _(k=k):
            up_b[...] = jnp.concatenate(
                [full[5][:, (2 * n + k) * half : (2 * n + k + 1) * half] for n in range(ranks)],
                axis=1,
            )

    want = jnp.concatenate([x for step in steps for x in (step, jnp.zeros((1, 1), F32))], axis=1)
    wanted[...] = want
    at = d * rows.shape[0] + lax.broadcasted_iota(jnp.int32, (rows.shape[0], 1), 0)
    picked = dot_at((at.astype(F32) == want).astype(BF16), rows[...]).astype(BF16)
    part = rows.shape[1] // ranks
    for k in range(ranks):
        chosen[k] = picked[:, k * part : (k + 1) * part]


def pack_rest_kernel(meta, up, down, proj_out, out):
    c = meta[1]
    deep = up.shape[0]
    width = down.shape[1]
    half = down.shape[0] // 2
    ff = up.shape[1] // 2
    for k in range(2):

        @pl.when(c == k)
        def _(k=k):
            for d in range(ff // half):
                out[:, d * half : (d + 1) * half] = up[:, (2 * d + k) * half : (2 * d + k + 1) * half]
            out[:, ff : ff + width] = down[k * half : k * half + deep]
            out[:, ff + width : ff + 2 * width] = down[k * half + deep : (k + 1) * half]
            out[:, ff + 2 * width :] = proj_out[:, k * width // 2 : (k + 1) * width // 2]


def place_rest_kernel(meta, *refs):
    *pieces, up, down, out = refs
    d = meta[2]
    deep = up.shape[0] // len(pieces)
    ff, width = up.shape[1], down.shape[1]
    for m, piece in enumerate(pieces):
        owner = d ^ m
        base = pl.multiple_of(owner * deep, deep)
        up[pl.ds(base, deep)] = piece[:, :ff]
        out[pl.ds(base, deep)] = piece[:, ff + 2 * width :]
        base = pl.multiple_of(owner * (2 * deep), deep)
        down[pl.ds(base, deep)] = piece[:, ff : ff + width]
        base = pl.multiple_of(owner * (2 * deep) + deep, deep)
        down[pl.ds(base, deep)] = piece[:, ff + width : ff + 2 * width]


def half_kernel(meta, here, came, *outs):
    o = meta[2] // 2
    for m, out in enumerate(outs):
        at = pl.ds(o ^ m, 1)
        out[...] = (here[at].astype(F32) + came[at].astype(F32))[0].astype(BF16)


def join_kernel(meta, down_here, down_away, out_here, out_came, here, away):
    i = meta[3]
    outer, deep, wide = down_here.shape
    here[:, :, :wide] = down_here[...]
    away[:, :, :wide] = down_away[...]
    for k in range(2 * outer):
        rows = slice(k * deep, (k + 1) * deep)
        value = (out_here[rows].astype(F32) + out_came[rows].astype(F32)).astype(BF16)

        @pl.when(i == k % 2)
        def _(k=k, value=value):
            here[k // 2, :, wide:] = value

        @pl.when(i != k % 2)
        def _(k=k, value=value):
            away[k // 2, :, wide:] = value


def pair_kernel(meta, even, came, *outs):
    for m, out in enumerate(outs):
        out[...] = (even[m].astype(F32) + came[m].astype(F32)).astype(out.dtype)


def pair_call(meta, even, odd):
    outer = even.shape[0]
    pieces = run(
        pair_kernel,
        (1,),
        meta,
        [whole(even), whole(dp_swap(odd, 1))],
        [out_whole(even.shape[1:], even.dtype) for _ in range(outer)],
        name="pair",
    )
    return pieces[0], [pieces[0]] + [dp_swap(p, 2 * m) for m, p in enumerate(pieces) if m]


def total(refs):
    result = 0.0
    for ref in refs:
        for k in range(ref.shape[0] if len(ref.shape) == 3 else 1):
            result = result + (ref[k] if len(ref.shape) == 3 else ref[...]).astype(F32)
    return result


def gather_kernel(counts, meta, *refs):
    *refs, out = refs
    start, place = 0, 0
    for n in counts:
        value = total(refs[start : start + n])
        out[:, place : place + value.shape[1]] = value.astype(BF16)
        start, place = start + n, place + value.shape[1]


def gather_call(meta, groups):
    refs = [x for g in groups for x in g]
    shape = (groups[0][0].shape[-2], sum(g[0].shape[-1] for g in groups))
    return run(
        functools.partial(gather_kernel, tuple(len(g) for g in groups)),
        (1,),
        meta,
        [whole(x) for x in refs],
        [out_whole(shape, BF16)],
        cost=(0, 2 * sum(x.size for x in refs), 0),
        name="gather",
    )[0]


def close_rest_kernel(meta, own, across, pair, up, down, out):
    c = meta[1]
    deep = own.shape[0]
    width = out.shape[1]
    half = down.shape[0] // 2
    ff = up.shape[1] // 2
    mine = own[...].astype(F32) + across[...].astype(F32)
    other = pair[0].astype(F32) + pair[1].astype(F32)
    for k in range(2):
        value = jnp.where(c == k, mine, other)
        for d in range(ff // half):
            up[:, (2 * d + k) * half : (2 * d + k + 1) * half] = value[:, d * half : (d + 1) * half]
        down[k * half : k * half + deep] = value[:, ff : ff + width]
        down[k * half + deep : (k + 1) * half] = value[:, ff + width : ff + 2 * width]
        out[:, k * width // 2 : (k + 1) * width // 2] = value[:, ff + 2 * width :]


def close_in_kernel(ranks, meta, own, across, pair, w, gain, bias, in_bias, out_bias, up_bias, down_bias, held):
    s, d = meta[0], meta[2]
    deep, width = w.shape[0], w.shape[1] // 3
    cols = own.shape[1]
    hw = cols // 3
    held[pl.ds(s, 1)] = own[...].astype(F32)[None]
    held[pl.ds(s ^ 2, 1)] = across[...].astype(F32)[None]
    held[pl.ds(s ^ 1, 1)] = pair[0].astype(F32)[None]
    held[pl.ds(s ^ 3, 1)] = pair[1].astype(F32)[None]
    for k in range(4):
        for t in range(3):
            w[:, t * width + k * hw : t * width + (k + 1) * hw] = held[k, :deep, t * hw : (t + 1) * hw]
    rows = [
        jnp.concatenate([held[k, deep + r : deep + r + 1] for r in range(EXTRA)], axis=1)
        for k in range(4)
    ]
    biases = jnp.concatenate(
        [rows[k][:, t * hw : (t + 1) * hw] for t in range(3) for k in range(4)], axis=1
    )
    ff = 2 * width
    ups = [rows[0][:, cols : cols + ff] + rows[2][:, cols : cols + ff]]
    ups.append(rows[1][:, cols : cols + ff] + rows[3][:, cols : cols + ff])
    rest = rows[0] + rows[1] + rows[2] + rows[3]
    rest = rest[:, cols + ff :]
    part, third, half = width // ranks, 3 * width // ranks, ff // ranks
    for k in range(ranks):

        @pl.when(d == k)
        def _(k=k):
            for n, out in enumerate((gain, bias, out_bias, down_bias)):
                out[...] = rest[:, n * width + k * part : n * width + (k + 1) * part]
            in_bias[...] = biases[:, k * third : (k + 1) * third]
            up_bias[...] = jnp.concatenate([u[:, k * half : (k + 1) * half] for u in ups], axis=1)


def shards(
    tokens,
    prefix_len,
    timestep,
    norm_gain,
    norm_bias,
    proj_in,
    proj_in_bias,
    proj_out,
    proj_out_bias,
    time_table,
    ada_weight,
    ada_bias,
    mlp_up,
    mlp_up_bias,
    mlp_down,
    mlp_down_bias,
    out_grad,
):
    count, local_len, width = tokens.shape
    members = lax.axis_size("seq")
    ranks = lax.axis_size("dp")
    s = lax.axis_index("seq")
    d = lax.axis_index("dp")
    hw = H // members * HD
    deep = proj_in.shape[0]
    half_ff = mlp_down.shape[0] // 2
    ff = ranks * half_ff
    half_out = width // 2
    meta = jnp.concatenate([jnp.stack([s, s % 2, d, d % 2]).astype(jnp.int32), prefix_len])

    tok_x = seq_swap(tokens, 2)

    offsets = jnp.arange(local_len, dtype=jnp.int32)
    positions = jnp.concatenate([(s ^ j) * local_len + offsets for j in range(members)]).astype(F32)
    half_width = HD // 2
    frequency = jnp.exp(jnp.arange(half_width, dtype=F32) * (-math.log(10000.0) / half_width))
    angles = positions[:, None] * frequency[None, :]
    cosine, sine = jnp.cos(angles), jnp.sin(angles)
    cosine = jnp.concatenate([cosine] * 4, axis=1)
    sine = jnp.concatenate([-sine, sine] * 2, axis=1)

    vectors = [
        norm_gain,
        norm_bias,
        proj_in_bias,
        proj_out_bias,
        ada_bias,
        mlp_up_bias,
        mlp_down_bias,
        timestep // 32,
        timestep % 32,
    ]
    sizes = tuple(v.shape[0] for v in vectors)
    pack_in = run(
        pack_in_kernel,
        (1,),
        meta,
        [whole(proj_in), *(whole(v[None]) for v in vectors)],
        [out_whole((deep + EXTRA, 3 * hw), BF16)],
        name="pack_in",
    )[0]
    in_even = [pack_in] + [dp_swap(pack_in, m) for m in range(2, ranks, 2)]
    pack_rest = run(
        pack_rest_kernel,
        (1,),
        meta,
        [whole(after(mlp_up, pack_in)), whole(mlp_down), whole(proj_out)],
        [out_whole((deep, ff + 2 * width + half_out), BF16)],
        name="pack_rest",
    )[0]
    in_even = after(in_even, pack_rest, cosine, sine)
    in_stack = jnp.stack(in_even)
    in_odd = dp_swap(in_stack, 1)
    tok_c = seq_swap(after(tokens, in_stack), 1)
    kinds = count + 1
    in_w, gain, bias, in_b, out_bias, ada_bias_full, up_b, down_bias, chosen, wanted = run(
        functools.partial(place_in_kernel, sizes),
        (1,),
        meta,
        [whole(x) for x in (*in_even, in_odd, time_table)],
        [
            out_whole((width, 3 * hw), BF16),
            out_whole((1, width), F32),
            out_whole((1, width), F32),
            out_whole((1, 3 * hw), F32),
            out_whole((1, width), F32),
            out_whole((1, 3 * width), F32),
            out_whole((1, ff), F32),
            out_whole((1, width), F32),
            out_whole((ranks, ranks * kinds, width // ranks), BF16),
            out_whole((1, ranks * kinds), F32),
        ],
        scratch=[pltpu.VMEM((ranks, EXTRA, 3 * hw), F32)],
        name="place_in",
    )
    chosen_got = dp_turn(chosen)

    outer = ranks // 2
    early = max(1, outer // 4)
    one, two = slice(1, 1 + early), slice(1 + early, 1 + 2 * early)
    three = slice(1 + 2 * early, outer)
    rest_even = [pack_rest] + [
        dp_swap(after(pack_rest, in_even) if m > early else pack_rest, 2 * m)
        for m in range(1, 1 + 2 * early)
    ]
    rest_odd = [dp_swap(after(pack_rest, in_w), 1)]

    cosine_near = cosine
    qkv_near = qkv_call(meta, 0, tokens, tok_c, gain, bias, in_w, in_b, cosine_near, sine)
    rest_even += [
        dp_swap(after(pack_rest, qkv_near), 2 * m) for m in range(1 + 2 * early, outer)
    ]
    rest_even[one] = after(rest_even[one], qkv_near)
    rest_odd += [dp_swap(piece, 1) for piece in rest_even[one]]
    tok_x = after(tok_x, in_stack)
    tok_d = seq_swap(tok_x, 1)
    qkv_far = qkv_call(meta, 2, tok_x, tok_d, gain, bias, in_w, in_b, after(cosine, qkv_near, rest_odd[0]), sine)
    near_again = after(qkv_near, rest_even[two])
    rest_even[two] = after(rest_even[two], qkv_far)
    rest_odd += [dp_swap(piece, 1) for piece in rest_even[two]]
    mixed_2, mixed_3, weights, recips = attend_call(meta, 2, near_again, qkv_far, local_len)
    across_2, across_3 = seq_swap(mixed_2, 2), seq_swap(mixed_3, 3)
    embedded = jnp.sum(after(chosen_got, mixed_2).astype(F32), axis=0)
    activated = jax.nn.silu(embedded).astype(BF16)
    mod_parts = dot(activated, ada_weight).reshape(ranks, kinds, 3 * width)
    mod_got = dp_turn(mod_parts)
    near_again = after(
        qkv_near, mixed_2, mod_parts, rest_odd[one], rest_odd[two], rest_even[three]
    )
    rest_even[three] = after(rest_even[three], mixed_2)
    rest_odd += [dp_swap(piece, 1) for piece in rest_even[three]]
    mixed_0, mixed_1, weights, recips = attend_call(
        meta, 0, near_again, qkv_far, local_len, (weights, recips)
    )
    mixed = [mixed_0, mixed_1, mixed_2, mixed_3]
    mixed_own = [mixed_0, seq_swap(mixed_1, 1), across_2, across_3]
    mods = jnp.sum(after(mod_got, mixed_0), axis=0) + ada_bias_full
    up_w, down_w, out_own = run(
        place_rest_kernel,
        (1,),
        meta,
        [whole(x) for pair in zip([after(pack_rest, mixed_0), *rest_even[1:]], rest_odd) for x in pair],
        [
            out_whole((width, ff), BF16),
            out_whole((ff, width), BF16),
            out_whole((width, half_out), BF16),
        ],
        name="place_rest",
    )
    out_other = seq_swap(out_own, 1)
    og_other = seq_swap(after(out_grad, up_w), 1)

    residual, mlp_own, out_rel = mix_call(
        meta, mixed_own, tokens, out_own, out_other, out_bias, mods
    )
    mlp_other = seq_swap(mlp_own, 1)
    own_branch, own_input, other, up_here, up_away, down_here, down_away, up_bias_part = mlp_call(
        meta, mlp_own, mlp_other, out_grad, og_other, up_w, up_b, down_w, mods, ranks
    )
    got = seq_swap(other, 1)
    up_came = dp_swap(up_away, 1)
    block_out, resid_grad, *others = turn_call(
        meta, residual, out_grad, own_branch, own_input, got, down_bias, mods, mixed_own, out_rel
    )
    grads_sent, (biases, out_here) = others[:4], others[4:]
    head_grads = [grads_sent[0]] + [seq_swap(grads_sent[j], j) for j in (1, 2, 3)]

    def halves(here, came):
        return run(
            half_kernel,
            (1,),
            meta,
            [whole(here), whole(came)],
            [out_whole(here.shape[1:], BF16) for _ in range(outer)],
            name="half",
        )

    def spread(pieces):
        return [pieces[0]] + [dp_swap(p, 2 * m) for m, p in enumerate(pieces) if m]

    joined = (outer, deep, ff + half_out)
    down_here, down_away = run(
        join_kernel,
        (1,),
        meta,
        [
            whole(down_here),
            whole(down_away),
            whole(out_here),
            (head_grads[1], (width, half_out), lambda i, m: (0, 0)),
        ],
        [out_whole(joined, BF16), out_whole(joined, BF16)],
        name="join",
    )
    down_came = dp_swap(down_away, 1)
    up_half = halves(after(up_here, down_away), up_came)
    row_grad = run(
        rows_kernel,
        (1,),
        meta,
        [
            (g, (ROWS, g.shape[1]), lambda i, m, n=g.shape[0] // ROWS - 1: (n, 0))
            for g in after(head_grads, up_half)
        ],
        [out_whole((kinds, 3 * width), F32)],
        name="rows",
    )[0]
    rows_got = dp_all(row_grad)
    up_got = spread(after(up_half, head_grads))

    raw = back_call(
        meta, 0, count - 1, after(qkv_near, row_grad), qkv_far, weights, recips, mixed, head_grads
    )
    down_half = halves(after(down_here, raw), down_came)
    down_got = spread(down_half)
    up_sum = gather_call(meta, [after(up_got, raw)])
    all_rows = after(rows_got, raw).reshape(ranks * kinds, 3 * width)
    exact = functools.partial(lax.dot_general, precision=HIGHEST, preferred_element_type=F32)
    act_rows_grad = exact(all_rows, ada_weight.astype(F32), (((1,), (1,)), ((), ())))
    embed_grad = jax.vjp(jax.nn.silu, embedded)[1](act_rows_grad)[0]
    embed_got = dp_all(embed_grad)
    raw = back_call(
        meta,
        count - 1,
        1,
        after(qkv_near, down_half, up_sum, embed_grad),
        qkv_far,
        weights,
        recips,
        mixed,
        head_grads,
        (raw,),
    )
    grads, in_even, in_odd = proj_grad_call(
        meta,
        (tokens, tok_c, tok_x, tok_d),
        after(raw, embed_got),
        in_w,
        gain,
        bias,
        up_bias_part,
        biases,
        cosine,
        sine,
        ranks,
    )
    in_came = dp_swap(in_odd, 1)
    sent = token_grad_call(meta, grads, in_w, tokens.shape)
    rest_sum = gather_call(meta, [(up_sum,), after(down_got, sent)])
    came = seq_swap(after(sent, rest_sum), 1)
    rest_x = seq_swap(rest_sum, 2)
    across = across_call(meta, after(grads, rest_sum), in_w, came)
    across_got = seq_swap(across, 2)
    in_pieces = run(
        pair_kernel,
        (1,),
        meta,
        [whole(after(in_even, across)), whole(in_came)],
        [out_whole(in_even.shape[1:], BF16) for _ in range(outer)],
        name="pair",
    )
    in_got = spread(in_pieces)
    all_rows = after(all_rows, in_pieces[0])
    ada_bias_grad = lax.dynamic_slice_in_dim(
        jnp.sum(all_rows, axis=0), d * ada_bias.shape[0], ada_bias.shape[0], 0
    )
    ada_grad = exact(activated.astype(F32), all_rows, (((0,), (0,)), ((), ())))
    embed_all = after(embed_got, in_pieces[0]).transpose(1, 0, 2).reshape(ranks * kinds, width)
    table_at = d * time_table.shape[0] + jnp.arange(time_table.shape[0], dtype=jnp.int32)
    selector = (table_at.astype(F32)[:, None] == wanted).astype(F32)
    table_grad = exact(selector, embed_all, (((1,), (0,)), ((), ())))
    rest_x = after(rest_x, in_pieces[0])
    rest_pair = seq_swap(jnp.stack([rest_sum, rest_x]), 1)

    in_sum = gather_call(meta, [after(in_got, table_grad, ada_grad)])
    in_x = seq_swap(in_sum, 2)
    up_final, down_final, out_final = run(
        close_rest_kernel,
        (1,),
        meta,
        [whole(x) for x in (after(rest_sum, in_sum), rest_x, rest_pair)],
        [
            out_whole(mlp_up.shape, F32),
            out_whole(mlp_down.shape, F32),
            out_whole(proj_out.shape, F32),
        ],
        name="close_rest",
    )
    tokens_grad = last_call(
        meta, tokens, after(resid_grad, up_final), grads, in_w, came, across_got, gain
    )
    in_pair = seq_swap(jnp.stack([in_sum, after(in_x, up_final)]), 1)
    part, third, ff_part = width // ranks, 3 * width // ranks, 4 * width // ranks
    in_final, gain_f, bias_f, in_bias_f, out_bias_f, up_bias_f, down_bias_f = run(
        functools.partial(close_in_kernel, ranks),
        (1,),
        meta,
        [whole(x) for x in (in_sum, in_x, in_pair)],
        [
            out_whole(proj_in.shape, F32),
            out_whole((1, part), F32),
            out_whole((1, part), F32),
            out_whole((1, third), F32),
            out_whole((1, part), F32),
            out_whole((1, ff_part), F32),
            out_whole((1, part), F32),
        ],
        scratch=[pltpu.VMEM((members, deep + EXTRA, 3 * hw), F32)],
        name="close_in",
    )
    return (
        block_out,
        tokens_grad,
        gain_f[0],
        bias_f[0],
        in_final,
        in_bias_f[0],
        out_final,
        out_bias_f[0],
        table_grad,
        ada_grad,
        ada_bias_grad,
        up_final,
        up_bias_f[0],
        down_final,
        down_bias_f[0],
    )


def solution(mesh):
    rows = P("dp", None)
    vector = P("dp")
    stream = P("dp", "seq", None)
    in_specs = (
        stream,
        vector,
        vector,
        vector,
        vector,
        rows,
        vector,
        rows,
        vector,
        rows,
        rows,
        vector,
        rows,
        vector,
        rows,
        vector,
        stream,
    )
    out_specs = (
        stream,
        stream,
        vector,
        vector,
        rows,
        vector,
        rows,
        vector,
        rows,
        rows,
        vector,
        rows,
        vector,
        rows,
        vector,
    )
    return jax.shard_map(shards, mesh=mesh, in_specs=in_specs, out_specs=out_specs, check_vma=False)
```

```python
import functools
import math

import jax
import jax.numpy as jnp
import numpy as np
from jax import lax
from jax.experimental import pallas as pl
from jax.experimental.pallas import tpu as pltpu
from jax.sharding import PartitionSpec as P

H = 12
HD = 64
EPS = 1e-05
NEG = -1e30
COST = 30
F32 = jnp.float32
BF16 = jnp.bfloat16
HIGHEST = lax.Precision.HIGHEST
VMEM_LIMIT = 62 * 1024 * 1024
ROWS = 48
EXTRA = 16


def standardize(values):
    centred = values - jnp.mean(values, axis=-1, keepdims=True)
    inverse = lax.rsqrt(jnp.mean(centred * centred, axis=-1, keepdims=True) + EPS)
    return centred * inverse, inverse


def norm_back(gradient, normed, inverse):
    return inverse * (
        gradient
        - jnp.mean(gradient, axis=-1, keepdims=True)
        - normed * jnp.mean(gradient * normed, axis=-1, keepdims=True)
    )


def dot(left, right):
    return jnp.dot(left, right, preferred_element_type=F32)


def dot_bt(left, right):
    return lax.dot_general(left, right, (((1,), (1,)), ((), ())), preferred_element_type=F32)


def dot_at(left, right):
    return lax.dot_general(left, right, (((0,), (0,)), ((), ())), preferred_element_type=F32)


TAIL_P = 0.55
TAIL = (
    0.001045374169866761,
    0.2933056852691112,
    0.41788788917041303,
    -0.08811700935317877,
    0.8046529189842585,
    -0.5409110079247637,
    0.11213617568673577,
)


def gelu_both(values):
    bell = jnp.exp(values * values * -0.5)
    inner = 1.0 / (1.0 + (TAIL_P / math.sqrt(2.0)) * jnp.abs(values))
    tail = TAIL[6]
    for coefficient in TAIL[5::-1]:
        tail = tail * inner + coefficient
    tail = tail * bell * 0.5
    cumulative = jnp.where(values >= 0.0, 1.0 - tail, tail)
    return values * cumulative, cumulative + values * bell * (1.0 / math.sqrt(2.0 * math.pi))


def after(value, *others):
    return lax.optimization_barrier((value, others))[0]


def seq_swap(value, mask):
    return lax.ppermute(value, "seq", [(s, s ^ mask) for s in range(lax.axis_size("seq"))])


def dp_swap(value, mask):
    return lax.ppermute(value, "dp", [(d, d ^ mask) for d in range(lax.axis_size("dp"))])


def dp_collect(value):
    mine = [value] + [dp_swap(value, m) for m in range(2, lax.axis_size("dp"), 2)]
    return mine, dp_swap(jnp.stack(mine), 1)


def quad(value):
    across = seq_swap(value, 2)
    return value, across, seq_swap(jnp.stack([value, across]), 1)


def dp_turn(value, outer_only=False):
    groups = None
    if outer_only:
        outer = lax.axis_size("dp") // 2
        groups = [[o * 2 + i for o in range(outer)] for i in range(2)]
    return lax.all_to_all(
        value, "dp", split_axis=0, concat_axis=0, tiled=True, axis_index_groups=groups
    )


def dp_all(value):
    return dp_turn(jnp.broadcast_to(value[None], (lax.axis_size("dp"),) + value.shape))


def run(body, grid, meta, ins, outs, scratch=(), cost=(0, 0, 0), name=None, held=()):
    specs = [pl.BlockSpec(block, index) for _, block, index in ins]
    specs += [pl.BlockSpec(memory_space=pl.ANY) for _ in held]
    first = 1 + len(ins)
    kernel = body
    if held:

        def kernel(meta, *refs):
            return body(meta, *refs[: len(ins)], *refs[len(ins) + len(held) :])

    return pl.pallas_call(
        kernel,
        grid_spec=pltpu.PrefetchScalarGridSpec(
            num_scalar_prefetch=1,
            grid=grid,
            in_specs=specs,
            out_specs=[pl.BlockSpec(block, index) for _, _, block, index in outs],
            scratch_shapes=list(scratch),
        ),
        out_shape=[jax.ShapeDtypeStruct(shape, dtype) for shape, dtype, _, _ in outs],
        input_output_aliases={first + n: k for n, (_, k) in enumerate(held)},
        compiler_params=pltpu.CompilerParams(
            dimension_semantics=("arbitrary",) * len(grid), vmem_limit_bytes=VMEM_LIMIT
        ),
        cost_estimate=pl.CostEstimate(
            flops=int(cost[0] * COST), bytes_accessed=int(cost[1] * COST), transcendentals=0
        ),
        name=name,
    )(meta, *[array for array, _, _ in ins], *[array for array, _ in held])


def whole(array):
    zeros = (0,) * array.ndim
    return (array, array.shape, lambda *_: zeros)


def out_whole(shape, dtype):
    zeros = (0,) * len(shape)
    return (shape, dtype, shape, lambda *_: zeros)


def partner_lanes(tile):
    lane = lax.broadcasted_iota(jnp.int32, tile.shape, 1)
    ahead = pltpu.roll(tile, 96, 1)
    behind = pltpu.roll(tile, 32, 1)
    return jnp.where((lane & (HD // 2)) == 0, ahead, behind)


def qkv_kernel(meta, x0, x1, gain, bias, w, b, cosine, sine, out):
    half = w.shape[1] // 3
    tokens = jnp.where(pl.program_id(0) == 0, x0[0], x1[0]).astype(F32)
    normed, _ = standardize(tokens)
    attn_input = (normed * gain[...] + bias[...]).astype(BF16)
    projected = dot(attn_input, w[...]) + b[...]
    cos, sin = cosine[...], sine[...]
    scale = HD**-0.5
    lane = lax.broadcasted_iota(jnp.int32, cos.shape, 1)
    for t in range(2 * half // 128):
        tile = projected[:, t * 128 : (t + 1) * 128]
        turned = tile * cos + partner_lanes(tile) * sin
        if (t + 1) * 128 <= half:
            turned = turned * scale
        elif t * 128 < half:
            turned = turned * jnp.where(lane < half - t * 128, scale, 1.0)
        out[0, :, t * 128 : (t + 1) * 128] = turned.astype(BF16)
    out[0, :, 2 * half :] = projected[:, 2 * half :].astype(BF16)


def qkv_call(meta, base, x0, x1, gain, bias, w, b, cosine, sine):
    count, rows, width = x0.shape
    last = count - 1
    return run(
        qkv_kernel,
        (2, count),
        meta,
        [
            (x0, (1, rows, width), lambda p, q, m: (jnp.where(p == 0, q, last), 0, 0)),
            (x1, (1, rows, width), lambda p, q, m: (jnp.where(p == 0, 0, q), 0, 0)),
            whole(gain),
            whole(bias),
            whole(w),
            whole(b),
            (cosine, (rows, 128), lambda p, q, m: (base + p, 0)),
            (sine, (rows, 128), lambda p, q, m: (base + p, 0)),
        ],
        [
            (
                (count, 2 * rows, w.shape[1]),
                BF16,
                (1, rows, w.shape[1]),
                lambda p, q, m: (q, p, 0),
            )
        ],
        cost=(4 * count * rows * width * w.shape[1], 10 * count * rows * width, 0),
        name="qkv",
    )[0]


def fold(rows):
    half = rows.shape[0] // 2
    return jnp.concatenate([rows[:half], rows[half:]], axis=1)


def unfold(pair):
    width = pair.shape[1] // 2
    return jnp.concatenate([pair[:, :width], pair[:, width:]], axis=0)


def attend_kernel(base, meta, qa, qb, o0, o1, weights, recips):
    b, k = pl.program_id(0), pl.program_id(1)
    j = base + k
    s, prefix = meta[0], meta[4 + b]
    rows = o0.shape[1] * 2
    hw = o0.shape[2] // 2
    heads = hw // HD
    half = qa.shape[1]
    source = qb if base else qa
    mine = source[0, pl.ds(pl.multiple_of(k * rows, rows), rows), :hw]
    at = (s ^ j) * rows + lax.broadcasted_iota(jnp.int32, (rows, 1), 0)
    hidden_from = jnp.where(at < prefix, 1.0, 0.0)
    lane = lax.broadcasted_iota(jnp.int32, (1, rows), 1)
    fills = []
    for side in range(2):
        places = [(s ^ (2 * side + piece)) * rows + lane for piece in range(half // rows)]
        where = jnp.concatenate(places, axis=1)
        fills.append(jnp.where(where < prefix, 0.0, NEG))
    lane128 = lax.broadcasted_iota(jnp.int32, (rows, 128), 1)
    kept = jnp.zeros((rows, 128), F32)
    outs = []
    for h in range(heads):
        q = mine[:, h * HD : (h + 1) * HD]
        scores = []
        for side, ref in enumerate((qa, qb)):
            keys = ref[0, :, hw + h * HD : hw + (h + 1) * HD]
            scores.append(dot_bt(q, keys) + hidden_from * fills[side])
        top = jnp.maximum(
            jnp.max(scores[0], axis=1, keepdims=True), jnp.max(scores[1], axis=1, keepdims=True)
        )
        sums = jnp.zeros((rows, 1), F32)
        mixed = jnp.zeros((rows, HD), F32)
        for side, ref in enumerate((qa, qb)):
            v = ref[0, :, 2 * hw + h * HD : 2 * hw + (h + 1) * HD]
            e = jnp.exp(scores[side] - top)
            sums = sums + jnp.sum(e, axis=1, keepdims=True)
            e = e.astype(BF16)
            weights[0, h, :, side * half : (side + 1) * half] = e
            mixed = mixed + dot(e, v)
        recip = 1.0 / sums
        kept = jnp.where(lane128 == h, recip, kept)
        outs.append((mixed * recip).astype(BF16))
    recips[0] = kept
    folded = fold(jnp.concatenate(outs, axis=1))
    for n, ref in enumerate((o0, o1)):

        @pl.when(k == n)
        def _(ref=ref):
            ref[0] = folded


def attend_call(meta, base, qa, qb, rows, held=()):
    count, half, cols = qa.shape
    hw = cols // 3
    heads = hw // HD
    keys = 2 * half
    block = (1, rows // 2, 2 * hw)
    return run(
        functools.partial(attend_kernel, base),
        (count, half // rows),
        meta,
        [
            (qa, (1, half, cols), lambda b, k, m: (b, 0, 0)),
            (qb, (1, half, cols), lambda b, k, m: (b, 0, 0)),
        ],
        [((count,) + block[1:], BF16, block, lambda b, k, m: (b, 0, 0)) for _ in range(2)]
        + [
            (
                (count, heads, keys, keys),
                BF16,
                (1, heads, rows, keys),
                lambda b, k, m: (b, 0, base + k, 0),
            ),
            ((count, keys, 128), F32, (1, rows, 128), lambda b, k, m: (b, base + k, 0)),
        ],
        cost=(
            2 * count * heads * keys * keys * HD * 4,
            count * heads * keys * keys,
            count * heads * keys * keys // 2,
        ),
        name="attend",
        held=[(x, 2 + n) for n, x in enumerate(held)],
    )


def back_kernel(meta, qa, qb, weights, recips, o0, o1, o2, o3, g0, g1, g2, g3, out, dk, dv, og, go):
    j = pl.program_id(1)
    rows = o0.shape[1] * 2
    hw = o0.shape[2] // 2
    heads = hw // HD
    half = qa.shape[1]
    place = lax.rem(j, 2) * rows
    scale = HD**-0.5
    for k, (o, g) in enumerate(((o0, g0), (o1, g1), (o2, g2), (o3, g3))):

        @pl.when(j == k)
        def _(o=o, g=g):
            grad = g[...].astype(F32)
            go[...] = unfold(grad)
            og[...] = unfold(grad * o[0].astype(F32))

    @pl.when(j == 0)
    def _():
        dk[...] = jnp.zeros_like(dk)
        dv[...] = jnp.zeros_like(dv)

    mine = jnp.where(j < 2, qa[0, pl.ds(place, rows), :hw], qb[0, pl.ds(place, rows), :hw])
    query_grads = []
    for h in range(heads):
        cols = slice(h * HD, (h + 1) * HD)
        recip = recips[0, :, h : h + 1]
        grad = (go[:, cols] * recip).astype(BF16)
        centre = jnp.sum(og[:, cols], axis=1, keepdims=True) * recip
        q = mine[:, cols]
        dq = jnp.zeros((rows, HD), F32)
        for side, ref in enumerate((qa, qb)):
            k = ref[0, :, hw + h * HD : hw + (h + 1) * HD]
            v = ref[0, :, 2 * hw + h * HD : 2 * hw + (h + 1) * HD]
            e = weights[0, h, :, side * half : (side + 1) * half]
            ds = (e.astype(F32) * (dot_bt(grad, v) - centre)).astype(BF16)
            dq = dq + dot(ds, k)
            span = pl.ds(side * half, half)
            dk[h, span] += dot_at(ds, q)
            dv[h, span] += dot_at(e, grad)
        query_grads.append((dq * scale).astype(BF16))
    out[0, pl.ds(pl.multiple_of(j * rows, rows), rows), :hw] = jnp.concatenate(query_grads, axis=1)

    @pl.when(j == pl.num_programs(1) - 1)
    def _():
        out[0, :, hw : 2 * hw] = jnp.concatenate(
            [dk[h].astype(BF16) for h in range(heads)], axis=1
        )
        out[0, :, 2 * hw :] = jnp.concatenate([dv[h].astype(BF16) for h in range(heads)], axis=1)


def back_call(meta, base, some, qa, qb, weights, recips, olds, grads, held=()):
    count, half, cols = qa.shape
    hw = cols // 3
    heads = hw // HD
    keys = 2 * half
    rows = olds[0].shape[1] * 2
    block = (1,) + olds[0].shape[1:]
    piece = lambda b, j, m: (base + b, 0, 0)
    ins = [
        (qa, (1, half, cols), piece),
        (qb, (1, half, cols), piece),
        (weights, (1, heads, rows, keys), lambda b, j, m: (base + b, 0, j, 0)),
        (recips, (1, rows, 128), lambda b, j, m: (base + b, j, 0)),
    ]
    ins += [(x, block, piece) for x in olds]
    for k, x in enumerate(grads):
        first = base + (x.shape[0] - ROWS - count * block[1]) // block[1]
        ins.append((x, block[1:], lambda b, j, m, first=first: (first + b, 0)))
    return run(
        back_kernel,
        (some, keys // rows),
        meta,
        ins,
        [((count, keys, cols), BF16, (1, keys, cols), piece)],
        scratch=[
            pltpu.VMEM((heads, keys, HD), F32),
            pltpu.VMEM((heads, keys, HD), F32),
            pltpu.VMEM((rows, hw), F32),
            pltpu.VMEM((rows, hw), F32),
        ],
        cost=(8 * some * heads * keys * keys * HD * 4, 2 * some * heads * keys * keys, 0),
        name="attend_back",
        held=[(x, 0) for x in held],
    )[0]


def mix_kernel(meta, m0, m1, m2, m3, tokens, w_own, w_other, out_bias, mods, residual, mlp_in, w):
    b = pl.program_id(0)
    s, c, prefix = meta[0], meta[1], meta[4 + b]
    rows, width = tokens.shape[1:]
    hw = m0.shape[2] // 2

    @pl.when(b == 0)
    def _():
        for j in range(4):
            there = pl.ds(pl.multiple_of((s ^ j) * hw, hw), hw)
            own, other = w_own[there], w_other[there]
            even = c == 0
            w[j * hw : (j + 1) * hw, : width // 2] = jnp.where(even, own, other)
            w[j * hw : (j + 1) * hw, width // 2 :] = jnp.where(even, other, own)

    total = tokens[0].astype(F32) + out_bias[...]
    for j, ref in enumerate((m0, m1, m2, m3)):
        total = total + dot(unfold(ref[0]), w[j * hw : (j + 1) * hw])
    residual[0] = total
    normed, _ = standardize(total)
    at = s * rows + lax.broadcasted_iota(jnp.int32, (rows, 1), 0)
    clean = at < prefix
    count = pl.num_programs(0)
    noisy_row, clean_row = mods[pl.ds(b, 1)], mods[pl.ds(count, 1)]
    shift, scale = (
        jnp.where(
            clean,
            clean_row[:, part * width : (part + 1) * width],
            noisy_row[:, part * width : (part + 1) * width],
        )
        for part in range(2)
    )
    mlp_in[0] = (normed * (1.0 + scale) + shift).astype(BF16)


def mix_call(meta, parts, tokens, w_own, w_other, out_bias, mods):
    count, rows, width = tokens.shape
    seq = lambda b, m: (b, 0, 0)
    block = (1, rows, width)
    return run(
        mix_kernel,
        (count,),
        meta,
        [(p, (1,) + p.shape[1:], seq) for p in parts]
        + [(tokens, block, seq), whole(w_own), whole(w_other), whole(out_bias), whole(mods)],
        [
            (tokens.shape, F32, block, seq),
            (tokens.shape, BF16, block, seq),
            out_whole((width, width), BF16),
        ],
        cost=(2 * count * rows * width * width, 12 * count * rows * width, 0),
        name="mix",
    )


def mlp_kernel(
    meta,
    x0,
    x1,
    og0,
    og1,
    up,
    up_bias,
    down,
    mods,
    own_branch,
    own_input,
    other,
    up_here,
    up_away,
    down_here,
    down_away,
    up_bias_grad,
    up_acc,
    down_acc,
):
    p, b = pl.program_id(0), pl.program_id(1)
    count = pl.num_programs(1)
    s, i, prefix = meta[0], meta[3], meta[4 + b]
    rows, width = x0.shape[1:]
    first = p == 0
    x = jnp.where(first, x0[0], x1[0])
    incoming = jnp.where(first, og0[0], og1[0]).astype(F32)
    at = (s ^ p) * rows + lax.broadcasted_iota(jnp.int32, (rows, 1), 0)
    gate = jnp.where(
        at < prefix, mods[pl.ds(count, 1), 2 * width :], mods[pl.ds(b, 1), 2 * width :]
    )
    grad = (incoming * gate).astype(BF16)
    hidden, slope = gelu_both(dot(x, up[...]) + up_bias[...])
    hidden = hidden.astype(BF16)
    branch = dot(hidden, down[...])
    pre = (dot_bt(grad, down[...]) * slope)
    pre_low = pre.astype(BF16)
    back = dot_bt(pre_low, up[...])
    sums = jnp.sum(pre_low.astype(F32), axis=0, keepdims=True)

    @pl.when(first)
    def _():
        own_branch[0] = branch
        own_input[0] = back

    @pl.when(p == 1)
    def _():
        other[0, 0] = branch.astype(BF16)
        other[1, 0] = back.astype(BF16)

    start = jnp.logical_and(first, b == 0)

    @pl.when(start)
    def _():
        up_acc[...] = dot_at(x, pre_low)
        down_acc[...] = dot_at(hidden, grad)
        up_bias_grad[...] = sums

    @pl.when(jnp.logical_not(start))
    def _():
        up_acc[...] += dot_at(x, pre_low)
        down_acc[...] += dot_at(hidden, grad)
        up_bias_grad[...] += sums

    @pl.when(jnp.logical_and(p == 1, b == count - 1))
    def _():
        outer, deep = up_here.shape[0], up_here.shape[1]

        def blocks(o, _):
            for parity in range(2):
                d = 2 * o + parity
                upper = up_acc[pl.ds(pl.multiple_of(d * deep, deep), deep)].astype(BF16)
                base = d * (2 * deep)
                lower = jnp.concatenate(
                    [
                        down_acc[pl.ds(pl.multiple_of(base + n * deep, deep), deep)]
                        for n in range(2)
                    ],
                    axis=1,
                ).astype(BF16)

                @pl.when(i == parity)
                def _(upper=upper, lower=lower):
                    up_here[pl.ds(o, 1)] = upper[None]
                    down_here[pl.ds(o, 1)] = lower[None]

                @pl.when(i != parity)
                def _(upper=upper, lower=lower):
                    up_away[pl.ds(o, 1)] = upper[None]
                    down_away[pl.ds(o, 1)] = lower[None]

            return 0

        lax.fori_loop(0, outer, blocks, 0)


def mlp_call(meta, x0, x1, og0, og1, up, up_bias, down, mods, ranks):
    count, rows, width = x0.shape
    hidden = up.shape[1]
    last = count - 1
    block = (1, rows, width)
    first = lambda p, b, m: (jnp.where(p == 0, b, last), 0, 0)
    second = lambda p, b, m: (jnp.where(p == 0, 0, b), 0, 0)
    shared = (ranks // 2, width // ranks, hidden)
    return run(
        mlp_kernel,
        (2, count),
        meta,
        [
            (x0, block, first),
            (x1, block, second),
            (og0, block, first),
            (og1, block, second),
            whole(up),
            whole(up_bias),
            whole(down),
            whole(mods),
        ],
        [
            (x0.shape, F32, block, first),
            (x0.shape, F32, block, first),
            (
                (2,) + x0.shape,
                BF16,
                (2,) + block,
                lambda p, b, m: (0, jnp.where(p == 0, 0, b), 0, 0),
            ),
            out_whole(shared, BF16),
            out_whole(shared, BF16),
            out_whole(shared, BF16),
            out_whole(shared, BF16),
            out_whole((1, hidden), F32),
        ],
        scratch=[pltpu.VMEM((width, hidden), F32), pltpu.VMEM((hidden, width), F32)],
        cost=(24 * count * rows * width * hidden, 20 * count * rows * width, 0),
        name="mlp",
    )


def turn_kernel(
    meta,
    residual,
    out_grad,
    own_branch,
    own_input,
    got,
    down_bias,
    mods,
    m0,
    m1,
    m2,
    m3,
    w,
    block_out,
    resid_grad,
    g0,
    g1,
    g2,
    g3,
    biases,
    out_here,
    sums,
    acc,
):
    b = pl.program_id(0)
    count = pl.num_programs(0)
    s, c, prefix = meta[0], meta[1], meta[4 + b]
    rows, width = residual.shape[1:]
    hw = m0.shape[2] // 2
    resid = residual[0]
    incoming = out_grad[0].astype(F32)
    at = s * rows + lax.broadcasted_iota(jnp.int32, (rows, 1), 0)
    clean = at < prefix
    noisy_row, clean_row = mods[pl.ds(b, 1)], mods[pl.ds(count, 1)]
    scale, gate = (
        jnp.where(
            clean,
            clean_row[:, part * width : (part + 1) * width],
            noisy_row[:, part * width : (part + 1) * width],
        )
        for part in (1, 2)
    )
    branch = own_branch[0] + got[0, 0].astype(F32) + down_bias[...]
    input_two = own_input[0] + got[1, 0].astype(F32)
    block_out[0] = (resid + gate * branch).astype(BF16)
    normed, inverse = standardize(resid)
    grads = incoming + norm_back(input_two * (1.0 + scale), normed, inverse)
    resid_grad[0] = grads
    low = grads.astype(BF16)
    keep = jnp.where(clean, 1.0, 0.0)
    kept = []
    for part, value in enumerate((input_two, input_two * normed, incoming * branch)):
        value = value.astype(BF16).astype(F32)
        cols = slice(part * width, (part + 1) * width)
        everything = jnp.sum(value, axis=0, keepdims=True)
        old = jnp.sum(value * keep, axis=0, keepdims=True)
        kept.append((everything - old, old))
    branch_low = (incoming * gate).astype(BF16).astype(F32)
    down_sum = jnp.sum(branch_low, axis=0, keepdims=True)
    out_sum = jnp.sum(low.astype(F32), axis=0, keepdims=True)

    @pl.when(b == 0)
    def _():
        acc[...] = jnp.zeros_like(acc)
        biases[...] = jnp.zeros_like(biases)
        sums[...] = jnp.zeros_like(sums)

    for part, (noisy, old) in enumerate(kept):
        cols = slice(part * width, (part + 1) * width)
        sums[pl.ds(b, 1), cols] = noisy
        sums[pl.ds(count, 1), cols] += old
    biases[0:1] += down_sum
    biases[1:2] += out_sum
    for j, (m, g) in enumerate(((m0, g0), (m1, g1), (m2, g2), (m3, g3))):
        at = (width if j == 1 else 0) + b * (rows // 2)
        at = pl.ds(pl.multiple_of(at, rows // 2), rows // 2)
        g[at] = fold(dot_bt(low, w[j * hw : (j + 1) * hw])).astype(BF16)
        acc[j * hw : (j + 1) * hw] += dot_at(unfold(m[0]), low)

    @pl.when(b == count - 1)
    def _():
        for j in range(4):
            here = pl.ds(pl.multiple_of((s ^ j) * hw, hw), hw)
            block = acc[j * hw : (j + 1) * hw].astype(BF16)
            left, right = block[:, : width // 2], block[:, width // 2 :]
            even = c == 0
            out_here[here] = jnp.where(even, left, right)
            g1[here] = jnp.where(even, right, left)
        cols = g0.shape[1]
        kinds = ROWS * cols // (2 * 3 * width)
        value = sums[:kinds]
        high = value.astype(BF16)
        low_part = (value - high.astype(F32)).astype(BF16)
        lines = [
            x[k : k + 1, n * cols : (n + 1) * cols]
            for x in (high, low_part)
            for k in range(kinds)
            for n in range(3 * width // cols)
        ]
        lines = jnp.concatenate(lines, axis=0)
        for g in (g0, g1, g2, g3):
            g[g.shape[0] - ROWS :] = lines


def turn_call(meta, residual, out_grad, own_branch, own_input, got, down_bias, mods, parts, w):
    count, rows, width = residual.shape
    seq = lambda b, m: (b, 0, 0)
    block = (1, rows, width)
    return run(
        turn_kernel,
        (count,),
        meta,
        [
            (residual, block, seq),
            (out_grad, block, seq),
            (own_branch, block, seq),
            (own_input, block, seq),
            (got, (2,) + block, lambda b, m: (0, b, 0, 0)),
            whole(down_bias),
            whole(mods),
        ]
        + [(p, (1,) + p.shape[1:], seq) for p in parts]
        + [whole(w)],
        [
            (residual.shape, BF16, block, seq),
            (residual.shape, F32, block, seq),
        ]
        + [
            out_whole((extra + p.shape[0] * p.shape[1] + ROWS, p.shape[2]), BF16)
            for p, extra in zip(parts, (0, width, 0, 0))
        ]
        + [out_whole((8, width), F32), out_whole((width, width // 2), BF16)],
        scratch=[pltpu.VMEM((8, 3 * width), F32), pltpu.VMEM((width, width), F32)],
        cost=(4 * count * rows * width * width, 24 * count * rows * width, 0),
        name="turn",
    )


def rows_kernel(meta, g0, g1, g2, g3, out):
    def value(g):
        high = g[: g.shape[0] // 2].astype(F32)
        return high + g[g.shape[0] // 2 :].astype(F32)

    both = (value(g0) + value(g1)) + (value(g2) + value(g3))
    each = out.shape[1] // g0.shape[1]
    for k in range(out.shape[0]):
        out[k : k + 1] = jnp.concatenate(
            [both[k * each + n : k * each + n + 1] for n in range(each)], axis=1
        )


def proj_grad_kernel(meta, x0, x1, x2, x3, raw, w, gain, bias, up_bias, biases, cosine, sine, out, even, odd, acc, in_bias):
    b, k = pl.program_id(0), pl.program_id(1)
    hw = w.shape[1] // 3

    @pl.when(jnp.logical_and(b == 0, k == 0))
    def _():
        acc[...] = jnp.zeros_like(acc)
        in_bias[...] = jnp.zeros_like(in_bias)

    x = jnp.where(k < 2, jnp.where(k == 0, x0[0], x1[0]), jnp.where(k == 2, x2[0], x3[0]))
    normed, _ = standardize(x.astype(F32))
    cos, sin = cosine[...], sine[...]
    tiles = []
    for t in range(2 * hw // 128):
        tile = raw[0, :, t * 128 : (t + 1) * 128].astype(F32)
        tiles.append((tile * cos - partner_lanes(tile) * sin).astype(BF16))
    tiles.append(raw[0, :, 2 * hw :])
    grads = jnp.concatenate(tiles, axis=1)
    out[0] = grads
    acc[...] += dot_at(normed.astype(BF16), grads)
    in_bias[...] += jnp.sum(grads.astype(F32), axis=0, keepdims=True)

    @pl.when(jnp.logical_and(b == pl.num_programs(0) - 1, k == 3))
    def _():
        ranks = 2 * even.shape[0]
        deep, cols = acc.shape[0] // ranks, acc.shape[1]
        wide = w[...].astype(F32)
        lane = lax.broadcasted_iota(jnp.int32, (acc.shape[0], 128), 1)
        sums = jnp.where(
            lane == 0,
            jnp.sum(acc[...] * wide, axis=1, keepdims=True),
            jnp.sum(wide * in_bias[...], axis=1, keepdims=True),
        )
        sums = jnp.transpose(sums)
        flat = jnp.concatenate(
            [in_bias[...], up_bias[...], sums[0:1], sums[1:2], biases[1:2], biases[0:1]], axis=1
        )
        count = flat.shape[1] // cols
        extra = jnp.concatenate(
            [flat[:, r * cols : (r + 1) * cols] for r in range(count)]
            + [jnp.zeros((EXTRA - count, cols), F32)],
            axis=0,
        ).astype(BF16)
        gains, biases_in = (
            jnp.transpose(jnp.broadcast_to(x[...], (128, x.shape[1])))[:, :1] for x in (gain, bias)
        )
        acc[...] = acc[...] * gains + biases_in * in_bias[...]
        d = meta[2]
        for m in range(ranks):
            at = pl.ds(pl.multiple_of((d ^ m) * deep, deep), deep)
            ref = odd if m % 2 else even
            ref[m // 2, :deep] = acc[at].astype(BF16)
            ref[m // 2, deep:] = extra


def proj_grad_call(meta, xs, raw, w, gain, bias, up_bias, biases, cosine, sine, ranks):
    count, rows, width = xs[0].shape
    cols = w.shape[1]
    seq = lambda b, k, m: (b, 0, 0)
    part = lambda b, k, m: (b, k, 0)
    keys = raw.shape[1]
    shared = (ranks // 2, width // ranks + EXTRA, cols)
    return run(
        proj_grad_kernel,
        (count, keys // rows),
        meta,
        [(x, (1, rows, width), seq) for x in xs]
        + [(raw, (1, rows, cols), part)]
        + [whole(x) for x in (w, gain, bias, up_bias, biases)]
        + [(t, (rows, 128), lambda b, k, m: (k, 0)) for t in (cosine, sine)],
        [
            (raw.shape, BF16, (1, rows, cols), part),
            out_whole(shared, BF16),
            out_whole(shared, BF16),
        ],
        scratch=[pltpu.VMEM((width, cols), F32), pltpu.VMEM((1, cols), F32)],
        cost=(2 * count * keys * width * cols, 6 * count * keys * width, 0),
        name="proj_grad",
    )


def token_grad_kernel(meta, g1, g3, w, sent):
    sent[0, 0] = dot_bt(g1[0], w[...]).astype(BF16)
    sent[1, 0] = dot_bt(g3[0], w[...]).astype(BF16)


def token_grad_call(meta, grads, w, shape):
    count, rows, width = shape
    cols = w.shape[1]
    return run(
        token_grad_kernel,
        (count,),
        meta,
        [
            (grads, (1, rows, cols), lambda b, m: (b, 1, 0)),
            (grads, (1, rows, cols), lambda b, m: (b, 3, 0)),
            whole(w),
        ],
        [((2,) + shape, BF16, (2, 1, rows, width), lambda b, m: (0, b, 0, 0))],
        name="token_grad",
    )[0]


def across_kernel(meta, g2, w, got, across):
    across[0] = (dot_bt(g2[0], w[...]) + got[0, 0].astype(F32)).astype(BF16)


def across_call(meta, grads, w, got):
    _, count, rows, width = got.shape
    cols = w.shape[1]
    return run(
        across_kernel,
        (count,),
        meta,
        [
            (grads, (1, rows, cols), lambda b, m: (b, 2, 0)),
            whole(w),
            (got, (1, 1, rows, width), lambda b, m: (1, b, 0, 0)),
        ],
        [((count, rows, width), BF16, (1, rows, width), lambda b, m: (b, 0, 0))],
        name="across",
    )[0]


def last_kernel(meta, tokens, resid_grad, g0, w, got, across, gain, out):
    normed, inverse = standardize(tokens[0].astype(F32))
    grad = dot_bt(g0[0], w[...]) + got[0, 0].astype(F32) + across[0].astype(F32)
    out[0] = resid_grad[0] + norm_back(grad * gain[...], normed, inverse)


def last_call(meta, tokens, resid_grad, grads, w, got, across, gain):
    count, rows, width = tokens.shape
    cols = w.shape[1]
    seq = lambda b, m: (b, 0, 0)
    block = (1, rows, width)
    return run(
        last_kernel,
        (count,),
        meta,
        [
            (tokens, block, seq),
            (resid_grad, block, seq),
            (grads, (1, rows, cols), seq),
            whole(w),
            (got, (1,) + block, lambda b, m: (0, b, 0, 0)),
            (across, block, seq),
            whole(gain),
        ],
        [(tokens.shape, F32, block, seq)],
        cost=(2 * count * rows * width * cols, 20 * count * rows * width, 0),
        name="last",
    )[0]


def pack_in_kernel(meta, proj_in, *refs):
    *vectors, out = refs
    s = meta[0]
    deep, width = proj_in.shape[0], proj_in.shape[1] // 3
    cols = out.shape[1]
    hw = cols // 3
    for k in range(width // hw):

        @pl.when(s == k)
        def _(k=k):
            for t in range(3):
                start = t * width + k * hw
                out[:deep, t * hw : (t + 1) * hw] = proj_in[:, start : start + hw]

    out[deep:] = jnp.zeros((out.shape[0] - deep, cols), BF16)
    steps = vectors.pop()[...]
    vectors = [v[...].astype(F32) for v in vectors]
    vectors += [(steps >> 5).astype(F32), (steps & 31).astype(F32)]
    vec = jnp.concatenate(vectors, axis=1)
    size = vec.shape[1]
    for r in range(pl.cdiv(size, cols)):
        width_r = min(cols, size - r * cols)
        out[deep + r : deep + r + 1, :width_r] = vec[:, r * cols : r * cols + width_r].astype(BF16)


def place_in_kernel(sizes, meta, *refs):
    outer = len(refs) - 13
    pieces, odd, rows, refs = refs[:outer], refs[outer], refs[outer + 1], refs[outer + 2 :]
    w, gain, bias, in_b, out_bias, ada_bias, up_b, down_bias, chosen, wanted, table = refs
    ranks = 2 * outer
    s, c, d = meta[0], meta[1], meta[2]
    deep, cols = w.shape[0] // ranks, w.shape[1]
    hw = cols // 3
    for m in range(ranks):
        piece = odd.at[m // 2] if m % 2 else pieces[m // 2]
        owner = d ^ m
        w[pl.ds(pl.multiple_of(owner * deep, deep), deep)] = piece[:deep]
        table[pl.ds(owner, 1)] = piece[deep:].astype(F32)[None]
    used = -(-sum(sizes) // cols)
    flat = [
        jnp.concatenate([table[k, r : r + 1] for r in range(used)], axis=1) for k in range(ranks)
    ]
    full, start = [], 0
    for size in sizes:
        full.append([f[:, start : start + size] for f in flat])
        start += size
    steps = [high * 32.0 + low for high, low in zip(full[7], full[8])]
    full = [jnp.concatenate(x, axis=1) for x in full]
    gain[...], bias[...], out_bias[...], ada_bias[...], down_bias[...] = (
        full[0],
        full[1],
        full[3],
        full[4],
        full[6],
    )
    width = w.shape[0]
    half = sizes[5] // 2
    for k in range(width // hw):

        @pl.when(s == k)
        def _(k=k):
            in_b[...] = jnp.concatenate(
                [full[2][:, t * width + k * hw : t * width + (k + 1) * hw] for t in range(3)], axis=1
            )

    for k in range(2):

        @pl.when(c == k)
        def _(k=k):
            up_b[...] = jnp.concatenate(
                [full[5][:, (2 * n + k) * half : (2 * n + k + 1) * half] for n in range(ranks)],
                axis=1,
            )

    want = jnp.concatenate([x for step in steps for x in (step, jnp.zeros((1, 1), F32))], axis=1)
    wanted[...] = want
    at = d * rows.shape[0] + lax.broadcasted_iota(jnp.int32, (rows.shape[0], 1), 0)
    picked = dot_at((at.astype(F32) == want).astype(BF16), rows[...]).astype(BF16)
    part = rows.shape[1] // ranks
    for k in range(ranks):
        chosen[k] = picked[:, k * part : (k + 1) * part]


def pack_rest_kernel(meta, up, down, proj_out, out):
    c = meta[1]
    deep = up.shape[0]
    width = down.shape[1]
    half = down.shape[0] // 2
    ff = up.shape[1] // 2
    for k in range(2):

        @pl.when(c == k)
        def _(k=k):
            for d in range(ff // half):
                out[:, d * half : (d + 1) * half] = up[:, (2 * d + k) * half : (2 * d + k + 1) * half]
            out[:, ff : ff + width] = down[k * half : k * half + deep]
            out[:, ff + width : ff + 2 * width] = down[k * half + deep : (k + 1) * half]
            out[:, ff + 2 * width :] = proj_out[:, k * width // 2 : (k + 1) * width // 2]


def place_rest_kernel(meta, *refs):
    *pieces, up, down, out = refs
    d = meta[2]
    deep = up.shape[0] // len(pieces)
    ff, width = up.shape[1], down.shape[1]
    for m, piece in enumerate(pieces):
        owner = d ^ m
        base = pl.multiple_of(owner * deep, deep)
        up[pl.ds(base, deep)] = piece[:, :ff]
        out[pl.ds(base, deep)] = piece[:, ff + 2 * width :]
        base = pl.multiple_of(owner * (2 * deep), deep)
        down[pl.ds(base, deep)] = piece[:, ff : ff + width]
        base = pl.multiple_of(owner * (2 * deep) + deep, deep)
        down[pl.ds(base, deep)] = piece[:, ff + width : ff + 2 * width]


def half_kernel(meta, here, came, *outs):
    o = meta[2] // 2
    for m, out in enumerate(outs):
        at = pl.ds(o ^ m, 1)
        out[...] = (here[at].astype(F32) + came[at].astype(F32))[0].astype(BF16)


def join_kernel(meta, down_here, down_away, out_here, out_came, here, away):
    i = meta[3]
    outer, deep, wide = down_here.shape
    here[:, :, :wide] = down_here[...]
    away[:, :, :wide] = down_away[...]
    for k in range(2 * outer):
        rows = slice(k * deep, (k + 1) * deep)
        value = (out_here[rows].astype(F32) + out_came[rows].astype(F32)).astype(BF16)

        @pl.when(i == k % 2)
        def _(k=k, value=value):
            here[k // 2, :, wide:] = value

        @pl.when(i != k % 2)
        def _(k=k, value=value):
            away[k // 2, :, wide:] = value


def pair_kernel(meta, even, came, *outs):
    for m, out in enumerate(outs):
        out[...] = (even[m].astype(F32) + came[m].astype(F32)).astype(out.dtype)


def pair_call(meta, even, odd):
    outer = even.shape[0]
    pieces = run(
        pair_kernel,
        (1,),
        meta,
        [whole(even), whole(dp_swap(odd, 1))],
        [out_whole(even.shape[1:], even.dtype) for _ in range(outer)],
        name="pair",
    )
    return pieces[0], [pieces[0]] + [dp_swap(p, 2 * m) for m, p in enumerate(pieces) if m]


def total(refs):
    result = 0.0
    for ref in refs:
        for k in range(ref.shape[0] if len(ref.shape) == 3 else 1):
            result = result + (ref[k] if len(ref.shape) == 3 else ref[...]).astype(F32)
    return result


def gather_kernel(counts, meta, *refs):
    *refs, out = refs
    start, place = 0, 0
    for n in counts:
        value = total(refs[start : start + n])
        out[:, place : place + value.shape[1]] = value.astype(BF16)
        start, place = start + n, place + value.shape[1]


def gather_call(meta, groups):
    refs = [x for g in groups for x in g]
    shape = (groups[0][0].shape[-2], sum(g[0].shape[-1] for g in groups))
    return run(
        functools.partial(gather_kernel, tuple(len(g) for g in groups)),
        (1,),
        meta,
        [whole(x) for x in refs],
        [out_whole(shape, BF16)],
        name="gather",
    )[0]


def close_rest_kernel(meta, own, across, pair, up, down, out):
    c = meta[1]
    deep = own.shape[0]
    width = out.shape[1]
    half = down.shape[0] // 2
    ff = up.shape[1] // 2
    mine = own[...].astype(F32) + across[...].astype(F32)
    other = pair[0].astype(F32) + pair[1].astype(F32)
    for k in range(2):
        value = jnp.where(c == k, mine, other)
        for d in range(ff // half):
            up[:, (2 * d + k) * half : (2 * d + k + 1) * half] = value[:, d * half : (d + 1) * half]
        down[k * half : k * half + deep] = value[:, ff : ff + width]
        down[k * half + deep : (k + 1) * half] = value[:, ff + width : ff + 2 * width]
        out[:, k * width // 2 : (k + 1) * width // 2] = value[:, ff + 2 * width :]


def close_in_kernel(ranks, meta, own, across, beside, beyond, w, gain, bias, in_bias, out_bias, up_bias, down_bias, held):
    s, d = meta[0], meta[2]
    deep, width = w.shape[0], w.shape[1] // 3
    cols = own.shape[1]
    hw = cols // 3
    held[pl.ds(s, 1)] = own[...].astype(F32)[None]
    held[pl.ds(s ^ 2, 1)] = across[...].astype(F32)[None]
    held[pl.ds(s ^ 1, 1)] = beside[...].astype(F32)[None]
    held[pl.ds(s ^ 3, 1)] = beyond[...].astype(F32)[None]
    for k in range(4):
        for t in range(3):
            w[:, t * width + k * hw : t * width + (k + 1) * hw] = held[k, :deep, t * hw : (t + 1) * hw]
    rows = [
        jnp.concatenate([held[k, deep + r : deep + r + 1] for r in range(EXTRA)], axis=1)
        for k in range(4)
    ]
    biases = jnp.concatenate(
        [rows[k][:, t * hw : (t + 1) * hw] for t in range(3) for k in range(4)], axis=1
    )
    ff = 2 * width
    ups = [rows[0][:, cols : cols + ff] + rows[2][:, cols : cols + ff]]
    ups.append(rows[1][:, cols : cols + ff] + rows[3][:, cols : cols + ff])
    rest = rows[0] + rows[1] + rows[2] + rows[3]
    rest = rest[:, cols + ff :]
    part, third, half = width // ranks, 3 * width // ranks, ff // ranks
    for k in range(ranks):

        @pl.when(d == k)
        def _(k=k):
            for n, out in enumerate((gain, bias, out_bias, down_bias)):
                out[...] = rest[0, n * width + k * part : n * width + (k + 1) * part]
            in_bias[...] = biases[0, k * third : (k + 1) * third]
            up_bias[...] = jnp.concatenate([u[:, k * half : (k + 1) * half] for u in ups], axis=1)[0]


def shards(
    tokens,
    prefix_len,
    timestep,
    norm_gain,
    norm_bias,
    proj_in,
    proj_in_bias,
    proj_out,
    proj_out_bias,
    time_table,
    ada_weight,
    ada_bias,
    mlp_up,
    mlp_up_bias,
    mlp_down,
    mlp_down_bias,
    out_grad,
):
    count, local_len, width = tokens.shape
    members = lax.axis_size("seq")
    ranks = lax.axis_size("dp")
    s = lax.axis_index("seq")
    d = lax.axis_index("dp")
    hw = H // members * HD
    deep = proj_in.shape[0]
    half_ff = mlp_down.shape[0] // 2
    ff = ranks * half_ff
    half_out = width // 2
    meta = jnp.concatenate([jnp.stack([s, s % 2, d, d % 2]).astype(jnp.int32), prefix_len])

    tok_x = seq_swap(tokens, 2)

    half_width = HD // 2
    frequency = np.exp(np.arange(half_width) * (-math.log(10000.0) / half_width))
    angles = np.arange(local_len)[:, None] * frequency[None, :]
    cos_in, sin_in = (jnp.asarray(f(angles), F32)[None] for f in (np.cos, np.sin))
    starts = (jnp.stack([s ^ j for j in range(members)]) * local_len).astype(F32)
    starts = starts[:, None] * jnp.asarray(frequency, F32)[None, :]
    cos_at, sin_at = jnp.cos(starts)[:, None], jnp.sin(starts)[:, None]
    cosine = (cos_at * cos_in - sin_at * sin_in).reshape(-1, half_width)
    sine = (sin_at * cos_in + cos_at * sin_in).reshape(-1, half_width)
    cosine = jnp.concatenate([cosine] * 4, axis=1)
    sine = jnp.concatenate([-sine, sine] * 2, axis=1)

    vectors = [
        norm_gain,
        norm_bias,
        proj_in_bias,
        proj_out_bias,
        ada_bias,
        mlp_up_bias,
        mlp_down_bias,
        timestep,
    ]
    sizes = tuple(v.shape[0] for v in (*vectors, timestep))
    pack_in = run(
        pack_in_kernel,
        (1,),
        meta,
        [whole(proj_in), *(whole(v[None]) for v in vectors)],
        [out_whole((deep + EXTRA, 3 * hw), BF16)],
        name="pack_in",
    )[0]
    in_even = [pack_in] + [dp_swap(pack_in, m) for m in range(2, ranks, 2)]
    pack_rest = run(
        pack_rest_kernel,
        (1,),
        meta,
        [whole(after(mlp_up, pack_in)), whole(mlp_down), whole(proj_out)],
        [out_whole((deep, ff + 2 * width + half_out), BF16)],
        name="pack_rest",
    )[0]
    in_even = after(in_even, pack_rest, cosine, sine)
    in_stack = jnp.stack(in_even)
    in_odd = dp_swap(in_stack, 1)
    tok_c = seq_swap(after(tokens, in_stack), 1)
    kinds = count + 1
    in_w, gain, bias, in_b, out_bias, ada_bias_full, up_b, down_bias, chosen, wanted = run(
        functools.partial(place_in_kernel, sizes),
        (1,),
        meta,
        [whole(x) for x in (*in_even, in_odd, time_table)],
        [
            out_whole((width, 3 * hw), BF16),
            out_whole((1, width), F32),
            out_whole((1, width), F32),
            out_whole((1, 3 * hw), F32),
            out_whole((1, width), F32),
            out_whole((1, 3 * width), F32),
            out_whole((1, ff), F32),
            out_whole((1, width), F32),
            out_whole((ranks, ranks * kinds, width // ranks), BF16),
            out_whole((1, ranks * kinds), F32),
        ],
        scratch=[pltpu.VMEM((ranks, EXTRA, 3 * hw), F32)],
        name="place_in",
    )
    chosen_got = dp_turn(chosen)

    outer = ranks // 2
    early = max(1, outer // 4)
    one, two = slice(1, 1 + early), slice(1 + early, 1 + 2 * early)
    three = slice(1 + 2 * early, outer)
    rest_even = [pack_rest] + [
        dp_swap(after(pack_rest, in_even) if m > early else pack_rest, 2 * m)
        for m in range(1, 1 + 2 * early)
    ]
    rest_odd = [dp_swap(after(pack_rest, in_w), 1)]

    cosine_near = cosine
    qkv_near = qkv_call(meta, 0, tokens, tok_c, gain, bias, in_w, in_b, cosine_near, sine)
    rest_even += [
        dp_swap(after(pack_rest, qkv_near), 2 * m) for m in range(1 + 2 * early, outer)
    ]
    rest_even[one] = after(rest_even[one], qkv_near)
    rest_odd += [dp_swap(piece, 1) for piece in rest_even[one]]
    tok_x = after(tok_x, in_stack)
    tok_d = seq_swap(tok_x, 1)
    qkv_far = qkv_call(meta, 2, tok_x, tok_d, gain, bias, in_w, in_b, after(cosine, qkv_near, rest_odd[0]), sine)
    near_again = after(qkv_near, rest_even[two])
    rest_even[two] = after(rest_even[two], qkv_far)
    rest_odd += [dp_swap(piece, 1) for piece in rest_even[two]]
    mixed_2, mixed_3, weights, recips = attend_call(meta, 2, near_again, qkv_far, local_len)
    across_2, across_3 = seq_swap(mixed_2, 2), seq_swap(mixed_3, 3)
    embedded = jnp.sum(after(chosen_got, mixed_2).astype(F32), axis=0)
    activated = jax.nn.silu(embedded).astype(BF16)
    mod_parts = dot(activated, ada_weight).reshape(ranks, kinds, 3 * width)
    mod_got = dp_turn(mod_parts)
    near_again = after(
        qkv_near, mixed_2, mod_parts, rest_odd[one], rest_odd[two], rest_even[three]
    )
    rest_even[three] = after(rest_even[three], mixed_2)
    rest_odd += [dp_swap(piece, 1) for piece in rest_even[three]]
    mixed_0, mixed_1, weights, recips = attend_call(
        meta, 0, near_again, qkv_far, local_len, (weights, recips)
    )
    mixed = [mixed_0, mixed_1, mixed_2, mixed_3]
    mixed_own = [mixed_0, seq_swap(mixed_1, 1), across_2, across_3]
    mods = jnp.sum(after(mod_got, mixed_0), axis=0) + ada_bias_full
    up_w, down_w, out_own = run(
        place_rest_kernel,
        (1,),
        meta,
        [whole(x) for pair in zip([after(pack_rest, mixed_0), *rest_even[1:]], rest_odd) for x in pair],
        [
            out_whole((width, ff), BF16),
            out_whole((ff, width), BF16),
            out_whole((width, half_out), BF16),
        ],
        name="place_rest",
    )
    out_other = seq_swap(out_own, 1)
    og_other = seq_swap(after(out_grad, up_w), 1)

    residual, mlp_own, out_rel = mix_call(
        meta, mixed_own, tokens, out_own, out_other, out_bias, mods
    )
    mlp_other = seq_swap(mlp_own, 1)
    own_branch, own_input, other, up_here, up_away, down_here, down_away, up_bias_part = mlp_call(
        meta, mlp_own, mlp_other, out_grad, og_other, up_w, up_b, down_w, mods, ranks
    )
    got = seq_swap(other, 1)
    up_came = dp_swap(up_away, 1)
    block_out, resid_grad, *others = turn_call(
        meta, residual, out_grad, own_branch, own_input, got, down_bias, mods, mixed_own, out_rel
    )
    grads_sent, (biases, out_here) = others[:4], others[4:]
    head_grads = [grads_sent[0]] + [seq_swap(grads_sent[j], j) for j in (1, 2, 3)]

    def halves(here, came):
        return run(
            half_kernel,
            (1,),
            meta,
            [whole(here), whole(came)],
            [out_whole(here.shape[1:], BF16) for _ in range(outer)],
            name="half",
        )

    def spread(pieces):
        return [pieces[0]] + [dp_swap(p, 2 * m) for m, p in enumerate(pieces) if m]

    joined = (outer, deep, ff + half_out)
    down_here, down_away = run(
        join_kernel,
        (1,),
        meta,
        [
            whole(down_here),
            whole(down_away),
            whole(out_here),
            (head_grads[1], (width, half_out), lambda i, m: (0, 0)),
        ],
        [out_whole(joined, BF16), out_whole(joined, BF16)],
        name="join",
    )
    down_came = dp_swap(down_away, 1)
    up_half = halves(after(up_here, down_away), up_came)
    up_got = spread(after(up_half, head_grads))

    raw = back_call(
        meta, 0, count, after(qkv_near, up_half), qkv_far, weights, recips, mixed, head_grads
    )
    down_half = halves(after(down_here, raw), down_came)
    down_got = spread(down_half)
    up_sum = gather_call(meta, [after(up_got, raw)])
    row_grad = run(
        rows_kernel,
        (1,),
        meta,
        [
            (g, (ROWS, g.shape[1]), lambda i, m, n=g.shape[0] // ROWS - 1: (n, 0))
            for g in after(head_grads, down_half)
        ],
        [out_whole((kinds, 3 * width), F32)],
        name="rows",
    )[0]
    rows_got = dp_all(row_grad)
    grads, in_even, in_odd = proj_grad_call(
        meta,
        (tokens, tok_c, tok_x, tok_d),
        after(raw, down_half, up_sum, row_grad),
        in_w,
        gain,
        bias,
        up_bias_part,
        biases,
        cosine,
        sine,
        ranks,
    )
    in_came = dp_swap(in_odd, 1)
    sent = token_grad_call(meta, grads, in_w, tokens.shape)
    rest_sum = gather_call(meta, [(up_sum,), after(down_got, sent, rows_got)])
    came = seq_swap(after(sent, rest_sum), 1)
    rest_x = seq_swap(rest_sum, 2)
    across = across_call(meta, after(grads, rest_sum), in_w, came)
    across_got = seq_swap(across, 2)

    in_pieces = run(
        pair_kernel,
        (1,),
        meta,
        [whole(after(in_even, across)), whole(in_came)],
        [out_whole(in_even.shape[1:], BF16) for _ in range(outer)],
        name="pair",
    )
    in_got = spread(in_pieces)
    exact = functools.partial(lax.dot_general, precision=HIGHEST, preferred_element_type=F32)
    all_rows = after(rows_got, in_pieces[0]).reshape(ranks * kinds, 3 * width)
    act_rows_grad = exact(all_rows, ada_weight.astype(F32), (((1,), (1,)), ((), ())))
    embed_grad = jax.vjp(jax.nn.silu, embedded)[1](act_rows_grad)[0]
    ada_bias_grad = lax.dynamic_slice_in_dim(
        jnp.sum(after(all_rows, in_pieces[0]), axis=0), d * ada_bias.shape[0], ada_bias.shape[0], 0
    )
    ada_grad = exact(activated.astype(F32), after(all_rows, in_pieces[0]), (((0,), (0,)), ((), ())))
    rest_x = after(rest_x, in_pieces[0])
    rest_pair = seq_swap(jnp.stack([rest_sum, rest_x]), 1)
    up_final, down_final, out_final = run(
        close_rest_kernel,
        (1,),
        meta,
        [whole(x) for x in (after(rest_sum, in_pieces[0]), rest_x, rest_pair)],
        [
            out_whole(mlp_up.shape, F32),
            out_whole(mlp_down.shape, F32),
            out_whole(proj_out.shape, F32),
        ],
        name="close_rest",
    )

    in_sum = gather_call(meta, [after(in_got, ada_bias_grad, ada_grad, up_final)])
    in_parts = [in_sum] + [seq_swap(in_sum, j) for j in (2, 1, 3)]
    embed_got = dp_all(after(embed_grad, in_sum))
    tokens_grad = last_call(
        meta, tokens, after(resid_grad, in_sum), grads, in_w, came, across_got, gain
    )
    embed_all = after(embed_got, tokens_grad).transpose(1, 0, 2).reshape(ranks * kinds, width)
    table_at = d * time_table.shape[0] + jnp.arange(time_table.shape[0], dtype=jnp.int32)
    selector = (table_at.astype(F32)[:, None] == wanted).astype(F32)
    table_grad = exact(selector, embed_all, (((1,), (0,)), ((), ())))
    part, third, ff_part = width // ranks, 3 * width // ranks, 4 * width // ranks
    in_final, gain_f, bias_f, in_bias_f, out_bias_f, up_bias_f, down_bias_f = run(
        functools.partial(close_in_kernel, ranks),
        (1,),
        meta,
        [whole(x) for x in in_parts],
        [
            out_whole(proj_in.shape, F32),
            out_whole((part,), F32),
            out_whole((part,), F32),
            out_whole((third,), F32),
            out_whole((part,), F32),
            out_whole((ff_part,), F32),
            out_whole((part,), F32),
        ],
        scratch=[pltpu.VMEM((members, deep + EXTRA, 3 * hw), F32)],
        name="close_in",
    )
    return (
        block_out,
        tokens_grad,
        gain_f.reshape(-1),
        bias_f.reshape(-1),
        in_final,
        in_bias_f.reshape(-1),
        out_final,
        out_bias_f.reshape(-1),
        table_grad,
        ada_grad,
        ada_bias_grad,
        up_final,
        up_bias_f.reshape(-1),
        down_final,
        down_bias_f.reshape(-1),
    )


def solution(mesh):
    rows = P("dp", None)
    vector = P("dp")
    stream = P("dp", "seq", None)
    in_specs = (
        stream,
        vector,
        vector,
        vector,
        vector,
        rows,
        vector,
        rows,
        vector,
        rows,
        rows,
        vector,
        rows,
        vector,
        rows,
        vector,
        stream,
    )
    out_specs = (
        stream,
        stream,
        vector,
        vector,
        rows,
        vector,
        rows,
        vector,
        rows,
        rows,
        vector,
        rows,
        vector,
        rows,
        vector,
    )
    return jax.shard_map(shards, mesh=mesh, in_specs=in_specs, out_specs=out_specs, check_vma=False)
```

```python
import functools
import math

import jax
import jax.numpy as jnp
import numpy as np
from jax import lax
from jax.experimental import pallas as pl
from jax.experimental.pallas import tpu as pltpu
from jax.sharding import PartitionSpec as P

H = 12
HD = 64
EPS = 1e-05
NEG = -1e30
COST = 30
F32 = jnp.float32
BF16 = jnp.bfloat16
HIGHEST = lax.Precision.HIGHEST
VMEM_LIMIT = 62 * 1024 * 1024
ROWS = 48
EXTRA = 16


def standardize(values):
    centred = values - jnp.mean(values, axis=-1, keepdims=True)
    inverse = lax.rsqrt(jnp.mean(centred * centred, axis=-1, keepdims=True) + EPS)
    return centred * inverse, inverse


def norm_back(gradient, normed, inverse):
    return inverse * (
        gradient
        - jnp.mean(gradient, axis=-1, keepdims=True)
        - normed * jnp.mean(gradient * normed, axis=-1, keepdims=True)
    )


def dot(left, right):
    return jnp.dot(left, right, preferred_element_type=F32)


def dot_bt(left, right):
    return lax.dot_general(left, right, (((1,), (1,)), ((), ())), preferred_element_type=F32)


def dot_at(left, right):
    return lax.dot_general(left, right, (((0,), (0,)), ((), ())), preferred_element_type=F32)


TAIL_P = 0.55
TAIL = (
    0.001045374169866761,
    0.2933056852691112,
    0.41788788917041303,
    -0.08811700935317877,
    0.8046529189842585,
    -0.5409110079247637,
    0.11213617568673577,
)


def gelu_both(values):
    bell = jnp.exp(values * values * -0.5)
    inner = 1.0 / (1.0 + (TAIL_P / math.sqrt(2.0)) * jnp.abs(values))
    tail = TAIL[6]
    for coefficient in TAIL[5::-1]:
        tail = tail * inner + coefficient
    tail = tail * bell * 0.5
    cumulative = jnp.where(values >= 0.0, 1.0 - tail, tail)
    return values * cumulative, cumulative + values * bell * (1.0 / math.sqrt(2.0 * math.pi))


def after(value, *others):
    return lax.optimization_barrier((value, others))[0]


def seq_swap(value, mask):
    return lax.ppermute(value, "seq", [(s, s ^ mask) for s in range(lax.axis_size("seq"))])


def dp_swap(value, mask):
    return lax.ppermute(value, "dp", [(d, d ^ mask) for d in range(lax.axis_size("dp"))])


def dp_collect(value):
    mine = [value] + [dp_swap(value, m) for m in range(2, lax.axis_size("dp"), 2)]
    return mine, dp_swap(jnp.stack(mine), 1)


def quad(value):
    across = seq_swap(value, 2)
    return value, across, seq_swap(jnp.stack([value, across]), 1)


def dp_turn(value, outer_only=False):
    groups = None
    if outer_only:
        outer = lax.axis_size("dp") // 2
        groups = [[o * 2 + i for o in range(outer)] for i in range(2)]
    return lax.all_to_all(
        value, "dp", split_axis=0, concat_axis=0, tiled=True, axis_index_groups=groups
    )


def dp_all(value):
    return dp_turn(jnp.broadcast_to(value[None], (lax.axis_size("dp"),) + value.shape))


def run(body, grid, meta, ins, outs, scratch=(), cost=(0, 0, 0), name=None, held=()):
    specs = [pl.BlockSpec(block, index) for _, block, index in ins]
    specs += [pl.BlockSpec(memory_space=pl.ANY) for _ in held]
    first = 1 + len(ins)
    kernel = body
    if held:

        def kernel(meta, *refs):
            return body(meta, *refs[: len(ins)], *refs[len(ins) + len(held) :])

    return pl.pallas_call(
        kernel,
        grid_spec=pltpu.PrefetchScalarGridSpec(
            num_scalar_prefetch=1,
            grid=grid,
            in_specs=specs,
            out_specs=[pl.BlockSpec(block, index) for _, _, block, index in outs],
            scratch_shapes=list(scratch),
        ),
        out_shape=[jax.ShapeDtypeStruct(shape, dtype) for shape, dtype, _, _ in outs],
        input_output_aliases={first + n: k for n, (_, k) in enumerate(held)},
        compiler_params=pltpu.CompilerParams(
            dimension_semantics=("arbitrary",) * len(grid), vmem_limit_bytes=VMEM_LIMIT
        ),
        cost_estimate=pl.CostEstimate(
            flops=int(cost[0] * COST), bytes_accessed=int(cost[1] * COST), transcendentals=0
        ),
        name=name,
    )(meta, *[array for array, _, _ in ins], *[array for array, _ in held])


def whole(array):
    zeros = (0,) * array.ndim
    return (array, array.shape, lambda *_: zeros)


def out_whole(shape, dtype):
    zeros = (0,) * len(shape)
    return (shape, dtype, shape, lambda *_: zeros)


def partner_lanes(tile):
    lane = lax.broadcasted_iota(jnp.int32, tile.shape, 1)
    ahead = pltpu.roll(tile, 96, 1)
    behind = pltpu.roll(tile, 32, 1)
    return jnp.where((lane & (HD // 2)) == 0, ahead, behind)


def qkv_kernel(meta, x0, x1, gain, bias, w, b, cosine, sine, out):
    half = w.shape[1] // 3
    tokens = jnp.where(pl.program_id(0) == 0, x0[0], x1[0]).astype(F32)
    normed, _ = standardize(tokens)
    attn_input = (normed * gain[...] + bias[...]).astype(BF16)
    projected = dot(attn_input, w[...]) + b[...]
    cos, sin = cosine[...], sine[...]
    scale = HD**-0.5
    lane = lax.broadcasted_iota(jnp.int32, cos.shape, 1)
    for t in range(2 * half // 128):
        tile = projected[:, t * 128 : (t + 1) * 128]
        turned = tile * cos + partner_lanes(tile) * sin
        if (t + 1) * 128 <= half:
            turned = turned * scale
        elif t * 128 < half:
            turned = turned * jnp.where(lane < half - t * 128, scale, 1.0)
        out[0, :, t * 128 : (t + 1) * 128] = turned.astype(BF16)
    out[0, :, 2 * half :] = projected[:, 2 * half :].astype(BF16)


def qkv_call(meta, base, x0, x1, gain, bias, w, b, cosine, sine):
    count, rows, width = x0.shape
    last = count - 1
    return run(
        qkv_kernel,
        (2, count),
        meta,
        [
            (x0, (1, rows, width), lambda p, q, m: (jnp.where(p == 0, q, last), 0, 0)),
            (x1, (1, rows, width), lambda p, q, m: (jnp.where(p == 0, 0, q), 0, 0)),
            whole(gain),
            whole(bias),
            whole(w),
            whole(b),
            (cosine, (rows, 128), lambda p, q, m: (base + p, 0)),
            (sine, (rows, 128), lambda p, q, m: (base + p, 0)),
        ],
        [
            (
                (count, 2 * rows, w.shape[1]),
                BF16,
                (1, rows, w.shape[1]),
                lambda p, q, m: (q, p, 0),
            )
        ],
        cost=(4 * count * rows * width * w.shape[1], 10 * count * rows * width, 0),
        name="qkv",
    )[0]


def fold(rows):
    half = rows.shape[0] // 2
    return jnp.concatenate([rows[:half], rows[half:]], axis=1)


def unfold(pair):
    width = pair.shape[1] // 2
    return jnp.concatenate([pair[:, :width], pair[:, width:]], axis=0)


def flip(value):
    rows, width = value.shape
    spare = -width % 128
    if spare:
        value = jnp.concatenate([value, jnp.zeros((rows, spare), value.dtype)], axis=1)
    return jnp.transpose(value)[:width]


def unflip(parts):
    width = sum(p.shape[0] for p in parts)
    spare = -width % 128
    if spare:
        parts = [*parts, jnp.zeros((spare, parts[0].shape[1]), parts[0].dtype)]
    return jnp.transpose(jnp.concatenate(parts, axis=0))[:, :width]


def attend_kernel(base, meta, qa, qb, o0, o1, weights, recips):
    b, k = pl.program_id(0), pl.program_id(1)
    j = base + k
    s, prefix = meta[0], meta[4 + b]
    rows = o0.shape[1] * 2
    hw = o0.shape[2] // 2
    heads = hw // HD
    half = qa.shape[1]
    source = qb if base else qa
    mine = source[0, pl.ds(pl.multiple_of(k * rows, rows), rows), :hw]
    at = (s ^ j) * rows + lax.broadcasted_iota(jnp.int32, (rows, 1), 0)
    hidden_from = jnp.where(at < prefix, 1.0, 0.0)
    lane = lax.broadcasted_iota(jnp.int32, (1, rows), 1)
    fills = []
    for side in range(2):
        places = [(s ^ (2 * side + piece)) * rows + lane for piece in range(half // rows)]
        where = jnp.concatenate(places, axis=1)
        fills.append(jnp.where(where < prefix, 0.0, NEG))
    lane128 = lax.broadcasted_iota(jnp.int32, (rows, 128), 1)
    kept = jnp.zeros((rows, 128), F32)
    outs = []
    for h in range(heads):
        q = mine[:, h * HD : (h + 1) * HD]
        scores = []
        for side, ref in enumerate((qa, qb)):
            keys = ref[0, :, hw + h * HD : hw + (h + 1) * HD]
            scores.append(dot_bt(q, keys) + hidden_from * fills[side])
        top = jnp.maximum(
            jnp.max(scores[0], axis=1, keepdims=True), jnp.max(scores[1], axis=1, keepdims=True)
        )
        sums = jnp.zeros((rows, 1), F32)
        mixed = jnp.zeros((rows, HD), F32)
        for side, ref in enumerate((qa, qb)):
            v = ref[0, :, 2 * hw + h * HD : 2 * hw + (h + 1) * HD]
            e = jnp.exp(scores[side] - top)
            sums = sums + jnp.sum(e, axis=1, keepdims=True)
            e = e.astype(BF16)
            weights[0, h, :, side * half : (side + 1) * half] = e
            mixed = mixed + dot(e, v)
        recip = 1.0 / sums
        kept = jnp.where(lane128 == h, recip, kept)
        outs.append((mixed * recip).astype(BF16))
    recips[0] = kept
    folded = fold(jnp.concatenate(outs, axis=1))
    for n, ref in enumerate((o0, o1)):

        @pl.when(k == n)
        def _(ref=ref):
            ref[0] = folded


def attend_call(meta, base, qa, qb, rows, held=()):
    count, half, cols = qa.shape
    hw = cols // 3
    heads = hw // HD
    keys = 2 * half
    block = (1, rows // 2, 2 * hw)
    return run(
        functools.partial(attend_kernel, base),
        (count, half // rows),
        meta,
        [
            (qa, (1, half, cols), lambda b, k, m: (b, 0, 0)),
            (qb, (1, half, cols), lambda b, k, m: (b, 0, 0)),
        ],
        [((count,) + block[1:], BF16, block, lambda b, k, m: (b, 0, 0)) for _ in range(2)]
        + [
            (
                (count, heads, keys, keys),
                BF16,
                (1, heads, rows, keys),
                lambda b, k, m: (b, 0, base + k, 0),
            ),
            ((count, keys, 128), F32, (1, rows, 128), lambda b, k, m: (b, base + k, 0)),
        ],
        cost=(
            2 * count * heads * keys * keys * HD * 4,
            count * heads * keys * keys,
            count * heads * keys * keys // 2,
        ),
        name="attend",
        held=[(x, 2 + n) for n, x in enumerate(held)],
    )


def back_kernel(meta, qa, qb, weights, recips, o0, o1, o2, o3, g0, g1, g2, g3, out, dk, dv, og, go):
    j = pl.program_id(1)
    rows = o0.shape[1] * 2
    hw = o0.shape[2] // 2
    heads = hw // HD
    half = qa.shape[1]
    place = lax.rem(j, 2) * rows
    scale = HD**-0.5
    for k, (o, g) in enumerate(((o0, g0), (o1, g1), (o2, g2), (o3, g3))):

        @pl.when(j == k)
        def _(o=o, g=g):
            grad = g[...].astype(F32)
            go[...] = unfold(grad)
            og[...] = unfold(grad * o[0].astype(F32))

    @pl.when(j == 0)
    def _():
        dk[...] = jnp.zeros_like(dk)
        dv[...] = jnp.zeros_like(dv)

    mine = jnp.where(j < 2, qa[0, pl.ds(place, rows), :hw], qb[0, pl.ds(place, rows), :hw])
    grads = []
    for h in range(heads):
        cols = slice(h * HD, (h + 1) * HD)
        grads.append((go[:, cols] * recips[0, :, h : h + 1]).astype(BF16))
    turned, turned_q = flip(jnp.concatenate(grads, axis=1)), flip(mine)
    query_grads = []
    for h in range(heads):
        cols = slice(h * HD, (h + 1) * HD)
        centre = jnp.sum(og[:, cols], axis=1, keepdims=True) * recips[0, :, h : h + 1]
        dq = jnp.zeros((rows, HD), F32)
        for side, ref in enumerate((qa, qb)):
            k = ref[0, :, hw + h * HD : hw + (h + 1) * HD]
            v = ref[0, :, 2 * hw + h * HD : 2 * hw + (h + 1) * HD]
            span = slice(side * half, (side + 1) * half)
            e = weights[0, h, :, span]
            ds = (e.astype(F32) * (dot_bt(grads[h], v) - centre)).astype(BF16)
            dq = dq + dot(ds, k)
            dk[h, :, span] += dot(turned_q[cols], ds)
            dv[h, :, span] += dot(turned[cols], e)
        query_grads.append((dq * scale).astype(BF16))
    out[0, pl.ds(pl.multiple_of(j * rows, rows), rows), :hw] = jnp.concatenate(query_grads, axis=1)

    @pl.when(j == pl.num_programs(1) - 1)
    def _():
        out[0, :, hw : 2 * hw] = unflip([dk[h] for h in range(heads)]).astype(BF16)
        out[0, :, 2 * hw :] = unflip([dv[h] for h in range(heads)]).astype(BF16)


def back_call(meta, base, some, qa, qb, weights, recips, olds, grads, held=()):
    count, half, cols = qa.shape
    hw = cols // 3
    heads = hw // HD
    keys = 2 * half
    rows = olds[0].shape[1] * 2
    block = (1,) + olds[0].shape[1:]
    piece = lambda b, j, m: (base + b, 0, 0)
    ins = [
        (qa, (1, half, cols), piece),
        (qb, (1, half, cols), piece),
        (weights, (1, heads, rows, keys), lambda b, j, m: (base + b, 0, j, 0)),
        (recips, (1, rows, 128), lambda b, j, m: (base + b, j, 0)),
    ]
    ins += [(x, block, piece) for x in olds]
    for k, x in enumerate(grads):
        first = base + (x.shape[0] - ROWS - count * block[1]) // block[1]
        ins.append((x, block[1:], lambda b, j, m, first=first: (first + b, 0)))
    return run(
        back_kernel,
        (some, keys // rows),
        meta,
        ins,
        [((count, keys, cols), BF16, (1, keys, cols), piece)],
        scratch=[
            pltpu.VMEM((heads, HD, keys), F32),
            pltpu.VMEM((heads, HD, keys), F32),
            pltpu.VMEM((rows, hw), F32),
            pltpu.VMEM((rows, hw), F32),
        ],
        cost=(8 * some * heads * keys * keys * HD * 4, 2 * some * heads * keys * keys, 0),
        name="attend_back",
        held=[(x, 0) for x in held],
    )[0]


def mix_kernel(meta, m0, m1, m2, m3, tokens, w_own, w_other, out_bias, mods, residual, mlp_in, w):
    b = pl.program_id(0)
    s, c, prefix = meta[0], meta[1], meta[4 + b]
    rows, width = tokens.shape[1:]
    hw = m0.shape[2] // 2

    @pl.when(b == 0)
    def _():
        for j in range(4):
            there = pl.ds(pl.multiple_of((s ^ j) * hw, hw), hw)
            own, other = w_own[there], w_other[there]
            even = c == 0
            w[j * hw : (j + 1) * hw, : width // 2] = jnp.where(even, own, other)
            w[j * hw : (j + 1) * hw, width // 2 :] = jnp.where(even, other, own)

    total = tokens[0].astype(F32) + out_bias[...]
    for j, ref in enumerate((m0, m1, m2, m3)):
        total = total + dot(unfold(ref[0]), w[j * hw : (j + 1) * hw])
    residual[0] = total
    normed, _ = standardize(total)
    at = s * rows + lax.broadcasted_iota(jnp.int32, (rows, 1), 0)
    clean = at < prefix
    count = pl.num_programs(0)
    noisy_row, clean_row = mods[pl.ds(b, 1)], mods[pl.ds(count, 1)]
    shift, scale = (
        jnp.where(
            clean,
            clean_row[:, part * width : (part + 1) * width],
            noisy_row[:, part * width : (part + 1) * width],
        )
        for part in range(2)
    )
    mlp_in[0] = (normed * (1.0 + scale) + shift).astype(BF16)


def mix_call(meta, parts, tokens, w_own, w_other, out_bias, mods):
    count, rows, width = tokens.shape
    seq = lambda b, m: (b, 0, 0)
    block = (1, rows, width)
    return run(
        mix_kernel,
        (count,),
        meta,
        [(p, (1,) + p.shape[1:], seq) for p in parts]
        + [(tokens, block, seq), whole(w_own), whole(w_other), whole(out_bias), whole(mods)],
        [
            (tokens.shape, F32, block, seq),
            (tokens.shape, BF16, block, seq),
            out_whole((width, width), BF16),
        ],
        cost=(2 * count * rows * width * width, 12 * count * rows * width, 0),
        name="mix",
    )


def mlp_kernel(
    meta,
    x0,
    x1,
    og0,
    og1,
    up,
    up_bias,
    down,
    mods,
    own_branch,
    own_input,
    other,
    up_here,
    up_away,
    down_here,
    down_away,
    up_bias_grad,
    up_acc,
    down_acc,
):
    p, b = pl.program_id(0), pl.program_id(1)
    count = pl.num_programs(1)
    s, i, prefix = meta[0], meta[3], meta[4 + b]
    rows, width = x0.shape[1:]
    first = p == 0
    x = jnp.where(first, x0[0], x1[0])
    incoming = jnp.where(first, og0[0], og1[0]).astype(F32)
    at = (s ^ p) * rows + lax.broadcasted_iota(jnp.int32, (rows, 1), 0)
    gate = jnp.where(
        at < prefix, mods[pl.ds(count, 1), 2 * width :], mods[pl.ds(b, 1), 2 * width :]
    )
    grad = (incoming * gate).astype(BF16)
    hidden, slope = gelu_both(dot(x, up[...]) + up_bias[...])
    hidden = hidden.astype(BF16)
    branch = dot(hidden, down[...])
    pre = (dot_bt(grad, down[...]) * slope)
    pre_low = pre.astype(BF16)
    back = dot_bt(pre_low, up[...])
    sums = jnp.sum(pre_low.astype(F32), axis=0, keepdims=True)

    @pl.when(first)
    def _():
        own_branch[0] = branch
        own_input[0] = back

    @pl.when(p == 1)
    def _():
        other[0, 0] = branch.astype(BF16)
        other[1, 0] = back.astype(BF16)

    start = jnp.logical_and(first, b == 0)

    @pl.when(start)
    def _():
        up_acc[...] = dot_at(x, pre_low)
        down_acc[...] = dot_at(hidden, grad)
        up_bias_grad[...] = sums

    @pl.when(jnp.logical_not(start))
    def _():
        up_acc[...] += dot_at(x, pre_low)
        down_acc[...] += dot_at(hidden, grad)
        up_bias_grad[...] += sums

    @pl.when(jnp.logical_and(p == 1, b == count - 1))
    def _():
        outer, deep = up_here.shape[0], up_here.shape[1]

        def blocks(o, _):
            for parity in range(2):
                d = 2 * o + parity
                upper = up_acc[pl.ds(pl.multiple_of(d * deep, deep), deep)].astype(BF16)
                base = d * (2 * deep)
                lower = jnp.concatenate(
                    [
                        down_acc[pl.ds(pl.multiple_of(base + n * deep, deep), deep)]
                        for n in range(2)
                    ],
                    axis=1,
                ).astype(BF16)

                @pl.when(i == parity)
                def _(upper=upper, lower=lower):
                    up_here[pl.ds(o, 1)] = upper[None]
                    down_here[pl.ds(o, 1)] = lower[None]

                @pl.when(i != parity)
                def _(upper=upper, lower=lower):
                    up_away[pl.ds(o, 1)] = upper[None]
                    down_away[pl.ds(o, 1)] = lower[None]

            return 0

        lax.fori_loop(0, outer, blocks, 0)


def mlp_call(meta, x0, x1, og0, og1, up, up_bias, down, mods, ranks):
    count, rows, width = x0.shape
    hidden = up.shape[1]
    last = count - 1
    block = (1, rows, width)
    first = lambda p, b, m: (jnp.where(p == 0, b, last), 0, 0)
    second = lambda p, b, m: (jnp.where(p == 0, 0, b), 0, 0)
    shared = (ranks // 2, width // ranks, hidden)
    return run(
        mlp_kernel,
        (2, count),
        meta,
        [
            (x0, block, first),
            (x1, block, second),
            (og0, block, first),
            (og1, block, second),
            whole(up),
            whole(up_bias),
            whole(down),
            whole(mods),
        ],
        [
            (x0.shape, F32, block, first),
            (x0.shape, F32, block, first),
            (
                (2,) + x0.shape,
                BF16,
                (2,) + block,
                lambda p, b, m: (0, jnp.where(p == 0, 0, b), 0, 0),
            ),
            out_whole(shared, BF16),
            out_whole(shared, BF16),
            out_whole(shared, BF16),
            out_whole(shared, BF16),
            out_whole((1, hidden), F32),
        ],
        scratch=[pltpu.VMEM((width, hidden), F32), pltpu.VMEM((hidden, width), F32)],
        cost=(24 * count * rows * width * hidden, 20 * count * rows * width, 0),
        name="mlp",
    )


def turn_kernel(
    meta,
    residual,
    out_grad,
    own_branch,
    own_input,
    got,
    down_bias,
    mods,
    m0,
    m1,
    m2,
    m3,
    w,
    block_out,
    resid_grad,
    g0,
    g1,
    g2,
    g3,
    biases,
    out_here,
    sums,
    acc,
):
    b = pl.program_id(0)
    count = pl.num_programs(0)
    s, c, prefix = meta[0], meta[1], meta[4 + b]
    rows, width = residual.shape[1:]
    hw = m0.shape[2] // 2
    resid = residual[0]
    incoming = out_grad[0].astype(F32)
    at = s * rows + lax.broadcasted_iota(jnp.int32, (rows, 1), 0)
    clean = at < prefix
    noisy_row, clean_row = mods[pl.ds(b, 1)], mods[pl.ds(count, 1)]
    scale, gate = (
        jnp.where(
            clean,
            clean_row[:, part * width : (part + 1) * width],
            noisy_row[:, part * width : (part + 1) * width],
        )
        for part in (1, 2)
    )
    branch = own_branch[0] + got[0, 0].astype(F32) + down_bias[...]
    input_two = own_input[0] + got[1, 0].astype(F32)
    block_out[0] = (resid + gate * branch).astype(BF16)
    normed, inverse = standardize(resid)
    grads = incoming + norm_back(input_two * (1.0 + scale), normed, inverse)
    resid_grad[0] = grads
    low = grads.astype(BF16)
    keep = jnp.where(clean, 1.0, 0.0)
    kept = []
    for part, value in enumerate((input_two, input_two * normed, incoming * branch)):
        value = value.astype(BF16).astype(F32)
        cols = slice(part * width, (part + 1) * width)
        everything = jnp.sum(value, axis=0, keepdims=True)
        old = jnp.sum(value * keep, axis=0, keepdims=True)
        kept.append((everything - old, old))
    branch_low = (incoming * gate).astype(BF16).astype(F32)
    down_sum = jnp.sum(branch_low, axis=0, keepdims=True)
    out_sum = jnp.sum(low.astype(F32), axis=0, keepdims=True)

    @pl.when(b == 0)
    def _():
        acc[...] = jnp.zeros_like(acc)
        biases[...] = jnp.zeros_like(biases)
        sums[...] = jnp.zeros_like(sums)

    for part, (noisy, old) in enumerate(kept):
        cols = slice(part * width, (part + 1) * width)
        sums[pl.ds(b, 1), cols] = noisy
        sums[pl.ds(count, 1), cols] += old
    biases[0:1] += down_sum
    biases[1:2] += out_sum
    for j, (m, g) in enumerate(((m0, g0), (m1, g1), (m2, g2), (m3, g3))):
        at = (width if j == 1 else 0) + b * (rows // 2)
        at = pl.ds(pl.multiple_of(at, rows // 2), rows // 2)
        g[at] = fold(dot_bt(low, w[j * hw : (j + 1) * hw])).astype(BF16)
        acc[j * hw : (j + 1) * hw] += dot_at(unfold(m[0]), low)

    @pl.when(b == count - 1)
    def _():
        for j in range(4):
            here = pl.ds(pl.multiple_of((s ^ j) * hw, hw), hw)
            block = acc[j * hw : (j + 1) * hw].astype(BF16)
            left, right = block[:, : width // 2], block[:, width // 2 :]
            even = c == 0
            out_here[here] = jnp.where(even, left, right)
            g1[here] = jnp.where(even, right, left)
        cols = g0.shape[1]
        kinds = ROWS * cols // (2 * 3 * width)
        value = sums[:kinds]
        high = value.astype(BF16)
        low_part = (value - high.astype(F32)).astype(BF16)
        lines = [
            x[k : k + 1, n * cols : (n + 1) * cols]
            for x in (high, low_part)
            for k in range(kinds)
            for n in range(3 * width // cols)
        ]
        lines = jnp.concatenate(lines, axis=0)
        for g in (g0, g1, g2, g3):
            g[g.shape[0] - ROWS :] = lines


def turn_call(meta, residual, out_grad, own_branch, own_input, got, down_bias, mods, parts, w):
    count, rows, width = residual.shape
    seq = lambda b, m: (b, 0, 0)
    block = (1, rows, width)
    return run(
        turn_kernel,
        (count,),
        meta,
        [
            (residual, block, seq),
            (out_grad, block, seq),
            (own_branch, block, seq),
            (own_input, block, seq),
            (got, (2,) + block, lambda b, m: (0, b, 0, 0)),
            whole(down_bias),
            whole(mods),
        ]
        + [(p, (1,) + p.shape[1:], seq) for p in parts]
        + [whole(w)],
        [
            (residual.shape, BF16, block, seq),
            (residual.shape, F32, block, seq),
        ]
        + [
            out_whole((extra + p.shape[0] * p.shape[1] + ROWS, p.shape[2]), BF16)
            for p, extra in zip(parts, (0, width, 0, 0))
        ]
        + [out_whole((8, width), F32), out_whole((width, width // 2), BF16)],
        scratch=[pltpu.VMEM((8, 3 * width), F32), pltpu.VMEM((width, width), F32)],
        cost=(4 * count * rows * width * width, 24 * count * rows * width, 0),
        name="turn",
    )


def rows_kernel(meta, g0, g1, g2, g3, out):
    def value(g):
        high = g[: g.shape[0] // 2].astype(F32)
        return high + g[g.shape[0] // 2 :].astype(F32)

    both = (value(g0) + value(g1)) + (value(g2) + value(g3))
    each = out.shape[1] // g0.shape[1]
    for k in range(out.shape[0]):
        out[k : k + 1] = jnp.concatenate(
            [both[k * each + n : k * each + n + 1] for n in range(each)], axis=1
        )


def proj_grad_kernel(meta, x0, x1, x2, x3, raw, w, gain, bias, up_bias, biases, cosine, sine, out, even, odd, acc, in_bias):
    b, k = pl.program_id(0), pl.program_id(1)
    hw = w.shape[1] // 3

    @pl.when(jnp.logical_and(b == 0, k == 0))
    def _():
        acc[...] = jnp.zeros_like(acc)
        in_bias[...] = jnp.zeros_like(in_bias)

    x = jnp.where(k < 2, jnp.where(k == 0, x0[0], x1[0]), jnp.where(k == 2, x2[0], x3[0]))
    normed, _ = standardize(x.astype(F32))
    cos, sin = cosine[...], sine[...]
    tiles = []
    for t in range(2 * hw // 128):
        tile = raw[0, :, t * 128 : (t + 1) * 128].astype(F32)
        tiles.append((tile * cos - partner_lanes(tile) * sin).astype(BF16))
    tiles.append(raw[0, :, 2 * hw :])
    grads = jnp.concatenate(tiles, axis=1)
    out[0] = grads
    acc[...] += dot_at(normed.astype(BF16), grads)
    in_bias[...] += jnp.sum(grads.astype(F32), axis=0, keepdims=True)

    @pl.when(jnp.logical_and(b == pl.num_programs(0) - 1, k == 3))
    def _():
        ranks = 2 * even.shape[0]
        deep, cols = acc.shape[0] // ranks, acc.shape[1]
        wide = w[...].astype(F32)
        lane = lax.broadcasted_iota(jnp.int32, (acc.shape[0], 128), 1)
        sums = jnp.where(
            lane == 0,
            jnp.sum(acc[...] * wide, axis=1, keepdims=True),
            jnp.sum(wide * in_bias[...], axis=1, keepdims=True),
        )
        sums = jnp.transpose(sums)
        flat = jnp.concatenate(
            [in_bias[...], up_bias[...], sums[0:1], sums[1:2], biases[1:2], biases[0:1]], axis=1
        )
        count = flat.shape[1] // cols
        extra = jnp.concatenate(
            [flat[:, r * cols : (r + 1) * cols] for r in range(count)]
            + [jnp.zeros((EXTRA - count, cols), F32)],
            axis=0,
        ).astype(BF16)
        gains, biases_in = (
            jnp.transpose(jnp.broadcast_to(x[...], (128, x.shape[1])))[:, :1] for x in (gain, bias)
        )
        acc[...] = acc[...] * gains + biases_in * in_bias[...]
        d = meta[2]
        for m in range(ranks):
            at = pl.ds(pl.multiple_of((d ^ m) * deep, deep), deep)
            ref = odd if m % 2 else even
            ref[m // 2, :deep] = acc[at].astype(BF16)
            ref[m // 2, deep:] = extra


def proj_grad_call(meta, xs, raw, w, gain, bias, up_bias, biases, cosine, sine, ranks):
    count, rows, width = xs[0].shape
    cols = w.shape[1]
    seq = lambda b, k, m: (b, 0, 0)
    part = lambda b, k, m: (b, k, 0)
    keys = raw.shape[1]
    shared = (ranks // 2, width // ranks + EXTRA, cols)
    return run(
        proj_grad_kernel,
        (count, keys // rows),
        meta,
        [(x, (1, rows, width), seq) for x in xs]
        + [(raw, (1, rows, cols), part)]
        + [whole(x) for x in (w, gain, bias, up_bias, biases)]
        + [(t, (rows, 128), lambda b, k, m: (k, 0)) for t in (cosine, sine)],
        [
            (raw.shape, BF16, (1, rows, cols), part),
            out_whole(shared, BF16),
            out_whole(shared, BF16),
        ],
        scratch=[pltpu.VMEM((width, cols), F32), pltpu.VMEM((1, cols), F32)],
        cost=(2 * count * keys * width * cols, 6 * count * keys * width, 0),
        name="proj_grad",
    )


def token_grad_kernel(meta, g1, g3, w, sent):
    sent[0, 0] = dot_bt(g1[0], w[...]).astype(BF16)
    sent[1, 0] = dot_bt(g3[0], w[...]).astype(BF16)


def token_grad_call(meta, grads, w, shape):
    count, rows, width = shape
    cols = w.shape[1]
    return run(
        token_grad_kernel,
        (count,),
        meta,
        [
            (grads, (1, rows, cols), lambda b, m: (b, 1, 0)),
            (grads, (1, rows, cols), lambda b, m: (b, 3, 0)),
            whole(w),
        ],
        [((2,) + shape, BF16, (2, 1, rows, width), lambda b, m: (0, b, 0, 0))],
        name="token_grad",
    )[0]


def across_kernel(meta, g2, w, got, across):
    across[0] = (dot_bt(g2[0], w[...]) + got[0, 0].astype(F32)).astype(BF16)


def across_call(meta, grads, w, got):
    _, count, rows, width = got.shape
    cols = w.shape[1]
    return run(
        across_kernel,
        (count,),
        meta,
        [
            (grads, (1, rows, cols), lambda b, m: (b, 2, 0)),
            whole(w),
            (got, (1, 1, rows, width), lambda b, m: (1, b, 0, 0)),
        ],
        [((count, rows, width), BF16, (1, rows, width), lambda b, m: (b, 0, 0))],
        name="across",
    )[0]


def last_kernel(meta, tokens, resid_grad, g0, w, got, across, gain, out):
    normed, inverse = standardize(tokens[0].astype(F32))
    grad = dot_bt(g0[0], w[...]) + got[0, 0].astype(F32) + across[0].astype(F32)
    out[0] = resid_grad[0] + norm_back(grad * gain[...], normed, inverse)


def last_call(meta, tokens, resid_grad, grads, w, got, across, gain):
    count, rows, width = tokens.shape
    cols = w.shape[1]
    seq = lambda b, m: (b, 0, 0)
    block = (1, rows, width)
    return run(
        last_kernel,
        (count,),
        meta,
        [
            (tokens, block, seq),
            (resid_grad, block, seq),
            (grads, (1, rows, cols), seq),
            whole(w),
            (got, (1,) + block, lambda b, m: (0, b, 0, 0)),
            (across, block, seq),
            whole(gain),
        ],
        [(tokens.shape, F32, block, seq)],
        cost=(2 * count * rows * width * cols, 20 * count * rows * width, 0),
        name="last",
    )[0]


def pack_in_kernel(meta, proj_in, *refs):
    *vectors, out = refs
    s = meta[0]
    deep, width = proj_in.shape[0], proj_in.shape[1] // 3
    cols = out.shape[1]
    hw = cols // 3
    for k in range(width // hw):

        @pl.when(s == k)
        def _(k=k):
            for t in range(3):
                start = t * width + k * hw
                out[:deep, t * hw : (t + 1) * hw] = proj_in[:, start : start + hw]

    out[deep:] = jnp.zeros((out.shape[0] - deep, cols), BF16)
    steps = vectors.pop()[...]
    vectors = [v[...].astype(F32) for v in vectors]
    vectors += [(steps >> 5).astype(F32), (steps & 31).astype(F32)]
    vec = jnp.concatenate(vectors, axis=1)
    size = vec.shape[1]
    for r in range(pl.cdiv(size, cols)):
        width_r = min(cols, size - r * cols)
        out[deep + r : deep + r + 1, :width_r] = vec[:, r * cols : r * cols + width_r].astype(BF16)


def place_in_kernel(sizes, meta, *refs):
    outer = len(refs) - 13
    pieces, odd, rows, refs = refs[:outer], refs[outer], refs[outer + 1], refs[outer + 2 :]
    w, gain, bias, in_b, out_bias, ada_bias, up_b, down_bias, chosen, wanted, table = refs
    ranks = 2 * outer
    s, c, d = meta[0], meta[1], meta[2]
    deep, cols = w.shape[0] // ranks, w.shape[1]
    hw = cols // 3
    for m in range(ranks):
        piece = odd.at[m // 2] if m % 2 else pieces[m // 2]
        owner = d ^ m
        w[pl.ds(pl.multiple_of(owner * deep, deep), deep)] = piece[:deep]
        table[pl.ds(owner, 1)] = piece[deep:].astype(F32)[None]
    used = -(-sum(sizes) // cols)
    flat = [
        jnp.concatenate([table[k, r : r + 1] for r in range(used)], axis=1) for k in range(ranks)
    ]
    full, start = [], 0
    for size in sizes:
        full.append([f[:, start : start + size] for f in flat])
        start += size
    steps = [high * 32.0 + low for high, low in zip(full[7], full[8])]
    full = [jnp.concatenate(x, axis=1) for x in full]
    gain[...], bias[...], out_bias[...], ada_bias[...], down_bias[...] = (
        full[0],
        full[1],
        full[3],
        full[4],
        full[6],
    )
    width = w.shape[0]
    half = sizes[5] // 2
    for k in range(width // hw):

        @pl.when(s == k)
        def _(k=k):
            in_b[...] = jnp.concatenate(
                [full[2][:, t * width + k * hw : t * width + (k + 1) * hw] for t in range(3)], axis=1
            )

    for k in range(2):

        @pl.when(c == k)
        def _(k=k):
            up_b[...] = jnp.concatenate(
                [full[5][:, (2 * n + k) * half : (2 * n + k + 1) * half] for n in range(ranks)],
                axis=1,
            )

    want = jnp.concatenate([x for step in steps for x in (step, jnp.zeros((1, 1), F32))], axis=1)
    wanted[...] = want
    at = d * rows.shape[0] + lax.broadcasted_iota(jnp.int32, (rows.shape[0], 1), 0)
    picked = dot_at((at.astype(F32) == want).astype(BF16), rows[...]).astype(BF16)
    part = rows.shape[1] // ranks
    for k in range(ranks):
        chosen[k] = picked[:, k * part : (k + 1) * part]


def pack_rest_kernel(meta, up, down, proj_out, out):
    c = meta[1]
    deep = up.shape[0]
    width = down.shape[1]
    half = down.shape[0] // 2
    ff = up.shape[1] // 2
    for k in range(2):

        @pl.when(c == k)
        def _(k=k):
            for d in range(ff // half):
                out[:, d * half : (d + 1) * half] = up[:, (2 * d + k) * half : (2 * d + k + 1) * half]
            out[:, ff : ff + width] = down[k * half : k * half + deep]
            out[:, ff + width : ff + 2 * width] = down[k * half + deep : (k + 1) * half]
            out[:, ff + 2 * width :] = proj_out[:, k * width // 2 : (k + 1) * width // 2]


def place_rest_kernel(meta, *refs):
    *pieces, up, down, out = refs
    d = meta[2]
    deep = up.shape[0] // len(pieces)
    ff, width = up.shape[1], down.shape[1]
    for m, piece in enumerate(pieces):
        owner = d ^ m
        base = pl.multiple_of(owner * deep, deep)
        up[pl.ds(base, deep)] = piece[:, :ff]
        out[pl.ds(base, deep)] = piece[:, ff + 2 * width :]
        base = pl.multiple_of(owner * (2 * deep), deep)
        down[pl.ds(base, deep)] = piece[:, ff : ff + width]
        base = pl.multiple_of(owner * (2 * deep) + deep, deep)
        down[pl.ds(base, deep)] = piece[:, ff + width : ff + 2 * width]


def half_kernel(meta, here, came, *outs):
    o = meta[2] // 2
    for m, out in enumerate(outs):
        at = pl.ds(o ^ m, 1)
        out[...] = (here[at].astype(F32) + came[at].astype(F32))[0].astype(BF16)


def join_kernel(meta, down_here, down_away, out_here, out_came, here, away):
    i = meta[3]
    outer, deep, wide = down_here.shape
    here[:, :, :wide] = down_here[...]
    away[:, :, :wide] = down_away[...]
    for k in range(2 * outer):
        rows = slice(k * deep, (k + 1) * deep)
        value = (out_here[rows].astype(F32) + out_came[rows].astype(F32)).astype(BF16)

        @pl.when(i == k % 2)
        def _(k=k, value=value):
            here[k // 2, :, wide:] = value

        @pl.when(i != k % 2)
        def _(k=k, value=value):
            away[k // 2, :, wide:] = value


def pair_kernel(meta, even, came, *outs):
    for m, out in enumerate(outs):
        out[...] = (even[m].astype(F32) + came[m].astype(F32)).astype(out.dtype)


def pair_call(meta, even, odd):
    outer = even.shape[0]
    pieces = run(
        pair_kernel,
        (1,),
        meta,
        [whole(even), whole(dp_swap(odd, 1))],
        [out_whole(even.shape[1:], even.dtype) for _ in range(outer)],
        name="pair",
    )
    return pieces[0], [pieces[0]] + [dp_swap(p, 2 * m) for m, p in enumerate(pieces) if m]


def total(refs):
    result = 0.0
    for ref in refs:
        for k in range(ref.shape[0] if len(ref.shape) == 3 else 1):
            result = result + (ref[k] if len(ref.shape) == 3 else ref[...]).astype(F32)
    return result


def gather_kernel(counts, meta, *refs):
    *refs, out = refs
    start, place = 0, 0
    for n in counts:
        value = total(refs[start : start + n])
        out[:, place : place + value.shape[1]] = value.astype(BF16)
        start, place = start + n, place + value.shape[1]


def gather_call(meta, groups):
    refs = [x for g in groups for x in g]
    shape = (groups[0][0].shape[-2], sum(g[0].shape[-1] for g in groups))
    return run(
        functools.partial(gather_kernel, tuple(len(g) for g in groups)),
        (1,),
        meta,
        [whole(x) for x in refs],
        [out_whole(shape, BF16)],
        name="gather",
    )[0]


def close_rest_kernel(meta, own, across, pair, up, down, out):
    c = meta[1]
    deep = own.shape[0]
    width = out.shape[1]
    half = down.shape[0] // 2
    ff = up.shape[1] // 2
    mine = own[...].astype(F32) + across[...].astype(F32)
    other = pair[0].astype(F32) + pair[1].astype(F32)
    for k in range(2):
        value = jnp.where(c == k, mine, other)
        for d in range(ff // half):
            up[:, (2 * d + k) * half : (2 * d + k + 1) * half] = value[:, d * half : (d + 1) * half]
        down[k * half : k * half + deep] = value[:, ff : ff + width]
        down[k * half + deep : (k + 1) * half] = value[:, ff + width : ff + 2 * width]
        out[:, k * width // 2 : (k + 1) * width // 2] = value[:, ff + 2 * width :]


def close_in_kernel(ranks, meta, own, across, beside, beyond, w, gain, bias, in_bias, out_bias, up_bias, down_bias, held):
    s, d = meta[0], meta[2]
    deep, width = w.shape[0], w.shape[1] // 3
    cols = own.shape[1]
    hw = cols // 3
    held[pl.ds(s, 1)] = own[...].astype(F32)[None]
    held[pl.ds(s ^ 2, 1)] = across[...].astype(F32)[None]
    held[pl.ds(s ^ 1, 1)] = beside[...].astype(F32)[None]
    held[pl.ds(s ^ 3, 1)] = beyond[...].astype(F32)[None]
    for k in range(4):
        for t in range(3):
            w[:, t * width + k * hw : t * width + (k + 1) * hw] = held[k, :deep, t * hw : (t + 1) * hw]
    rows = [
        jnp.concatenate([held[k, deep + r : deep + r + 1] for r in range(EXTRA)], axis=1)
        for k in range(4)
    ]
    biases = jnp.concatenate(
        [rows[k][:, t * hw : (t + 1) * hw] for t in range(3) for k in range(4)], axis=1
    )
    ff = 2 * width
    ups = [rows[0][:, cols : cols + ff] + rows[2][:, cols : cols + ff]]
    ups.append(rows[1][:, cols : cols + ff] + rows[3][:, cols : cols + ff])
    rest = rows[0] + rows[1] + rows[2] + rows[3]
    rest = rest[:, cols + ff :]
    part, third, half = width // ranks, 3 * width // ranks, ff // ranks
    for k in range(ranks):

        @pl.when(d == k)
        def _(k=k):
            for n, out in enumerate((gain, bias, out_bias, down_bias)):
                out[...] = rest[0, n * width + k * part : n * width + (k + 1) * part]
            in_bias[...] = biases[0, k * third : (k + 1) * third]
            up_bias[...] = jnp.concatenate([u[:, k * half : (k + 1) * half] for u in ups], axis=1)[0]


def shards(
    tokens,
    prefix_len,
    timestep,
    norm_gain,
    norm_bias,
    proj_in,
    proj_in_bias,
    proj_out,
    proj_out_bias,
    time_table,
    ada_weight,
    ada_bias,
    mlp_up,
    mlp_up_bias,
    mlp_down,
    mlp_down_bias,
    out_grad,
):
    count, local_len, width = tokens.shape
    members = lax.axis_size("seq")
    ranks = lax.axis_size("dp")
    s = lax.axis_index("seq")
    d = lax.axis_index("dp")
    hw = H // members * HD
    deep = proj_in.shape[0]
    half_ff = mlp_down.shape[0] // 2
    ff = ranks * half_ff
    half_out = width // 2
    meta = jnp.concatenate([jnp.stack([s, s % 2, d, d % 2]).astype(jnp.int32), prefix_len])

    tok_x = seq_swap(tokens, 2)

    half_width = HD // 2
    frequency = np.exp(np.arange(half_width) * (-math.log(10000.0) / half_width))
    angles = np.arange(local_len)[:, None] * frequency[None, :]
    cos_in, sin_in = (jnp.asarray(f(angles), F32)[None] for f in (np.cos, np.sin))
    starts = (jnp.stack([s ^ j for j in range(members)]) * local_len).astype(F32)
    starts = starts[:, None] * jnp.asarray(frequency, F32)[None, :]
    cos_at, sin_at = jnp.cos(starts)[:, None], jnp.sin(starts)[:, None]
    cosine = (cos_at * cos_in - sin_at * sin_in).reshape(-1, half_width)
    sine = (sin_at * cos_in + cos_at * sin_in).reshape(-1, half_width)
    cosine = jnp.concatenate([cosine] * 4, axis=1)
    sine = jnp.concatenate([-sine, sine] * 2, axis=1)

    vectors = [
        norm_gain,
        norm_bias,
        proj_in_bias,
        proj_out_bias,
        ada_bias,
        mlp_up_bias,
        mlp_down_bias,
        timestep,
    ]
    sizes = tuple(v.shape[0] for v in (*vectors, timestep))
    pack_in = run(
        pack_in_kernel,
        (1,),
        meta,
        [whole(proj_in), *(whole(v[None]) for v in vectors)],
        [out_whole((deep + EXTRA, 3 * hw), BF16)],
        name="pack_in",
    )[0]
    in_even = [pack_in] + [dp_swap(pack_in, m) for m in range(2, ranks, 2)]
    pack_rest = run(
        pack_rest_kernel,
        (1,),
        meta,
        [whole(after(mlp_up, pack_in)), whole(mlp_down), whole(proj_out)],
        [out_whole((deep, ff + 2 * width + half_out), BF16)],
        name="pack_rest",
    )[0]
    in_even = after(in_even, pack_rest, cosine, sine)
    in_stack = jnp.stack(in_even)
    in_odd = dp_swap(in_stack, 1)
    tok_c = seq_swap(after(tokens, in_stack), 1)
    kinds = count + 1
    in_w, gain, bias, in_b, out_bias, ada_bias_full, up_b, down_bias, chosen, wanted = run(
        functools.partial(place_in_kernel, sizes),
        (1,),
        meta,
        [whole(x) for x in (*in_even, in_odd, time_table)],
        [
            out_whole((width, 3 * hw), BF16),
            out_whole((1, width), F32),
            out_whole((1, width), F32),
            out_whole((1, 3 * hw), F32),
            out_whole((1, width), F32),
            out_whole((1, 3 * width), F32),
            out_whole((1, ff), F32),
            out_whole((1, width), F32),
            out_whole((ranks, ranks * kinds, width // ranks), BF16),
            out_whole((1, ranks * kinds), F32),
        ],
        scratch=[pltpu.VMEM((ranks, EXTRA, 3 * hw), F32)],
        name="place_in",
    )
    chosen_got = dp_turn(chosen)

    outer = ranks // 2
    early = max(1, outer // 4)
    one, two = slice(1, 1 + early), slice(1 + early, 1 + 2 * early)
    three = slice(1 + 2 * early, outer)
    rest_even = [pack_rest] + [
        dp_swap(after(pack_rest, in_even) if m > early else pack_rest, 2 * m)
        for m in range(1, 1 + 2 * early)
    ]
    rest_odd = [dp_swap(after(pack_rest, in_w), 1)]

    cosine_near = cosine
    qkv_near = qkv_call(meta, 0, tokens, tok_c, gain, bias, in_w, in_b, cosine_near, sine)
    rest_even += [
        dp_swap(after(pack_rest, qkv_near), 2 * m) for m in range(1 + 2 * early, outer)
    ]
    rest_even[one] = after(rest_even[one], qkv_near)
    rest_odd += [dp_swap(piece, 1) for piece in rest_even[one]]
    tok_x = after(tok_x, in_stack)
    tok_d = seq_swap(tok_x, 1)
    qkv_far = qkv_call(meta, 2, tok_x, tok_d, gain, bias, in_w, in_b, after(cosine, qkv_near, rest_odd[0]), sine)
    near_again = after(qkv_near, rest_even[two])
    rest_even[two] = after(rest_even[two], qkv_far)
    rest_odd += [dp_swap(piece, 1) for piece in rest_even[two]]
    mixed_2, mixed_3, weights, recips = attend_call(meta, 2, near_again, qkv_far, local_len)
    across_2, across_3 = seq_swap(mixed_2, 2), seq_swap(mixed_3, 3)
    embedded = jnp.sum(after(chosen_got, mixed_2).astype(F32), axis=0)
    activated = jax.nn.silu(embedded).astype(BF16)
    mod_parts = dot(activated, ada_weight).reshape(ranks, kinds, 3 * width)
    mod_got = dp_turn(mod_parts)
    near_again = after(
        qkv_near, mixed_2, mod_parts, rest_odd[one], rest_odd[two], rest_even[three]
    )
    rest_even[three] = after(rest_even[three], mixed_2)
    rest_odd += [dp_swap(piece, 1) for piece in rest_even[three]]
    mixed_0, mixed_1, weights, recips = attend_call(
        meta, 0, near_again, qkv_far, local_len, (weights, recips)
    )
    mixed = [mixed_0, mixed_1, mixed_2, mixed_3]
    mixed_own = [mixed_0, seq_swap(mixed_1, 1), across_2, across_3]
    mods = jnp.sum(after(mod_got, mixed_0), axis=0) + ada_bias_full
    up_w, down_w, out_own = run(
        place_rest_kernel,
        (1,),
        meta,
        [whole(x) for pair in zip([after(pack_rest, mixed_0), *rest_even[1:]], rest_odd) for x in pair],
        [
            out_whole((width, ff), BF16),
            out_whole((ff, width), BF16),
            out_whole((width, half_out), BF16),
        ],
        name="place_rest",
    )
    out_other = seq_swap(out_own, 1)
    og_other = seq_swap(after(out_grad, up_w), 1)

    residual, mlp_own, out_rel = mix_call(
        meta, mixed_own, tokens, out_own, out_other, out_bias, mods
    )
    mlp_other = seq_swap(mlp_own, 1)
    own_branch, own_input, other, up_here, up_away, down_here, down_away, up_bias_part = mlp_call(
        meta, mlp_own, mlp_other, out_grad, og_other, up_w, up_b, down_w, mods, ranks
    )
    got = seq_swap(other, 1)
    up_came = dp_swap(up_away, 1)
    block_out, resid_grad, *others = turn_call(
        meta, residual, out_grad, own_branch, own_input, got, down_bias, mods, mixed_own, out_rel
    )
    grads_sent, (biases, out_here) = others[:4], others[4:]
    head_grads = [grads_sent[0]] + [seq_swap(grads_sent[j], j) for j in (1, 2, 3)]

    def halves(here, came):
        return run(
            half_kernel,
            (1,),
            meta,
            [whole(here), whole(came)],
            [out_whole(here.shape[1:], BF16) for _ in range(outer)],
            name="half",
        )

    def spread(pieces):
        return [pieces[0]] + [dp_swap(p, 2 * m) for m, p in enumerate(pieces) if m]

    joined = (outer, deep, ff + half_out)
    down_here, down_away = run(
        join_kernel,
        (1,),
        meta,
        [
            whole(down_here),
            whole(down_away),
            whole(out_here),
            (head_grads[1], (width, half_out), lambda i, m: (0, 0)),
        ],
        [out_whole(joined, BF16), out_whole(joined, BF16)],
        name="join",
    )
    down_came = dp_swap(down_away, 1)
    up_half = halves(after(up_here, down_away), up_came)
    up_got = spread(after(up_half, head_grads))

    raw = back_call(
        meta, 0, count, after(qkv_near, up_half), qkv_far, weights, recips, mixed, head_grads
    )
    down_half = halves(after(down_here, raw), down_came)
    down_got = spread(down_half)
    up_sum = gather_call(meta, [after(up_got, raw)])
    row_grad = run(
        rows_kernel,
        (1,),
        meta,
        [
            (g, (ROWS, g.shape[1]), lambda i, m, n=g.shape[0] // ROWS - 1: (n, 0))
            for g in after(head_grads, down_half)
        ],
        [out_whole((kinds, 3 * width), F32)],
        name="rows",
    )[0]
    rows_got = dp_all(row_grad)
    grads, in_even, in_odd = proj_grad_call(
        meta,
        (tokens, tok_c, tok_x, tok_d),
        after(raw, down_half, up_sum, row_grad),
        in_w,
        gain,
        bias,
        up_bias_part,
        biases,
        cosine,
        sine,
        ranks,
    )
    in_came = dp_swap(in_odd, 1)
    sent = token_grad_call(meta, grads, in_w, tokens.shape)
    rest_sum = gather_call(meta, [(up_sum,), after(down_got, sent, rows_got)])
    came = seq_swap(after(sent, rest_sum), 1)
    rest_x = seq_swap(rest_sum, 2)
    across = across_call(meta, after(grads, rest_sum), in_w, came)
    across_got = seq_swap(across, 2)

    in_pieces = run(
        pair_kernel,
        (1,),
        meta,
        [whole(after(in_even, across)), whole(in_came)],
        [out_whole(in_even.shape[1:], BF16) for _ in range(outer)],
        name="pair",
    )
    in_got = spread(in_pieces)
    exact = functools.partial(lax.dot_general, precision=HIGHEST, preferred_element_type=F32)
    all_rows = after(rows_got, in_pieces[0]).reshape(ranks * kinds, 3 * width)
    act_rows_grad = exact(all_rows, ada_weight.astype(F32), (((1,), (1,)), ((), ())))
    embed_grad = jax.vjp(jax.nn.silu, embedded)[1](act_rows_grad)[0]
    ada_bias_grad = lax.dynamic_slice_in_dim(
        jnp.sum(after(all_rows, in_pieces[0]), axis=0), d * ada_bias.shape[0], ada_bias.shape[0], 0
    )
    ada_grad = exact(activated.astype(F32), after(all_rows, in_pieces[0]), (((0,), (0,)), ((), ())))
    rest_x = after(rest_x, in_pieces[0])
    rest_pair = seq_swap(jnp.stack([rest_sum, rest_x]), 1)
    up_final, down_final, out_final = run(
        close_rest_kernel,
        (1,),
        meta,
        [whole(x) for x in (after(rest_sum, in_pieces[0]), rest_x, rest_pair)],
        [
            out_whole(mlp_up.shape, F32),
            out_whole(mlp_down.shape, F32),
            out_whole(proj_out.shape, F32),
        ],
        name="close_rest",
    )

    in_sum = gather_call(meta, [after(in_got, ada_bias_grad, ada_grad, up_final)])
    in_parts = [in_sum] + [seq_swap(in_sum, j) for j in (2, 1, 3)]
    embed_got = dp_all(after(embed_grad, in_sum))
    tokens_grad = last_call(
        meta, tokens, after(resid_grad, in_sum), grads, in_w, came, across_got, gain
    )
    embed_all = after(embed_got, tokens_grad).transpose(1, 0, 2).reshape(ranks * kinds, width)
    table_at = d * time_table.shape[0] + jnp.arange(time_table.shape[0], dtype=jnp.int32)
    selector = (table_at.astype(F32)[:, None] == wanted).astype(F32)
    table_grad = exact(selector, embed_all, (((1,), (0,)), ((), ())))
    part, third, ff_part = width // ranks, 3 * width // ranks, 4 * width // ranks
    in_final, gain_f, bias_f, in_bias_f, out_bias_f, up_bias_f, down_bias_f = run(
        functools.partial(close_in_kernel, ranks),
        (1,),
        meta,
        [whole(x) for x in in_parts],
        [
            out_whole(proj_in.shape, F32),
            out_whole((part,), F32),
            out_whole((part,), F32),
            out_whole((third,), F32),
            out_whole((part,), F32),
            out_whole((ff_part,), F32),
            out_whole((part,), F32),
        ],
        scratch=[pltpu.VMEM((members, deep + EXTRA, 3 * hw), F32)],
        name="close_in",
    )
    return (
        block_out,
        tokens_grad,
        gain_f.reshape(-1),
        bias_f.reshape(-1),
        in_final,
        in_bias_f.reshape(-1),
        out_final,
        out_bias_f.reshape(-1),
        table_grad,
        ada_grad,
        ada_bias_grad,
        up_final,
        up_bias_f.reshape(-1),
        down_final,
        down_bias_f.reshape(-1),
    )


def solution(mesh):
    rows = P("dp", None)
    vector = P("dp")
    stream = P("dp", "seq", None)
    in_specs = (
        stream,
        vector,
        vector,
        vector,
        vector,
        rows,
        vector,
        rows,
        vector,
        rows,
        rows,
        vector,
        rows,
        vector,
        rows,
        vector,
        stream,
    )
    out_specs = (
        stream,
        stream,
        vector,
        vector,
        rows,
        vector,
        rows,
        vector,
        rows,
        rows,
        vector,
        rows,
        vector,
        rows,
        vector,
    )
    return jax.shard_map(shards, mesh=mesh, in_specs=in_specs, out_specs=out_specs, check_vma=False)
```

```python
import functools
import math

import jax
import jax.numpy as jnp
import numpy as np
from jax import lax
from jax.experimental import pallas as pl
from jax.experimental.pallas import tpu as pltpu
from jax.sharding import PartitionSpec as P

H = 12
HD = 64
EPS = 1e-05
NEG = -1e30
COST = 30
F32 = jnp.float32
BF16 = jnp.bfloat16
HIGHEST = lax.Precision.HIGHEST
VMEM_LIMIT = 62 * 1024 * 1024
ROWS = 48
EXTRA = 16


def standardize(values):
    centred = values - jnp.mean(values, axis=-1, keepdims=True)
    inverse = lax.rsqrt(jnp.mean(centred * centred, axis=-1, keepdims=True) + EPS)
    return centred * inverse, inverse


def norm_back(gradient, normed, inverse):
    return inverse * (
        gradient
        - jnp.mean(gradient, axis=-1, keepdims=True)
        - normed * jnp.mean(gradient * normed, axis=-1, keepdims=True)
    )


def dot(left, right):
    return jnp.dot(left, right, preferred_element_type=F32)


def dot_bt(left, right):
    return lax.dot_general(left, right, (((1,), (1,)), ((), ())), preferred_element_type=F32)


def dot_at(left, right):
    return lax.dot_general(left, right, (((0,), (0,)), ((), ())), preferred_element_type=F32)


TAIL_P = 0.55
TAIL = (
    0.001045374169866761,
    0.2933056852691112,
    0.41788788917041303,
    -0.08811700935317877,
    0.8046529189842585,
    -0.5409110079247637,
    0.11213617568673577,
)


def gelu_both(values):
    bell = jnp.exp(values * values * -0.5)
    inner = 1.0 / (1.0 + (TAIL_P / math.sqrt(2.0)) * jnp.abs(values))
    tail = TAIL[6]
    for coefficient in TAIL[5::-1]:
        tail = tail * inner + coefficient
    tail = tail * bell * 0.5
    cumulative = jnp.where(values >= 0.0, 1.0 - tail, tail)
    return values * cumulative, cumulative + values * bell * (1.0 / math.sqrt(2.0 * math.pi))


def after(value, *others):
    return lax.optimization_barrier((value, others))[0]


def seq_swap(value, mask):
    return lax.ppermute(value, "seq", [(s, s ^ mask) for s in range(lax.axis_size("seq"))])


def dp_swap(value, mask):
    return lax.ppermute(value, "dp", [(d, d ^ mask) for d in range(lax.axis_size("dp"))])


def dp_collect(value):
    mine = [value] + [dp_swap(value, m) for m in range(2, lax.axis_size("dp"), 2)]
    return mine, dp_swap(jnp.stack(mine), 1)


def quad(value):
    across = seq_swap(value, 2)
    return value, across, seq_swap(jnp.stack([value, across]), 1)


def dp_turn(value, outer_only=False):
    groups = None
    if outer_only:
        outer = lax.axis_size("dp") // 2
        groups = [[o * 2 + i for o in range(outer)] for i in range(2)]
    return lax.all_to_all(
        value, "dp", split_axis=0, concat_axis=0, tiled=True, axis_index_groups=groups
    )


def dp_all(value):
    return dp_turn(jnp.broadcast_to(value[None], (lax.axis_size("dp"),) + value.shape))


def run(body, grid, meta, ins, outs, scratch=(), cost=(0, 0, 0), name=None, held=()):
    specs = [pl.BlockSpec(block, index) for _, block, index in ins]
    specs += [pl.BlockSpec(memory_space=pl.ANY) for _ in held]
    first = 1 + len(ins)
    kernel = body
    if held:

        def kernel(meta, *refs):
            return body(meta, *refs[: len(ins)], *refs[len(ins) + len(held) :])

    return pl.pallas_call(
        kernel,
        grid_spec=pltpu.PrefetchScalarGridSpec(
            num_scalar_prefetch=1,
            grid=grid,
            in_specs=specs,
            out_specs=[pl.BlockSpec(block, index) for _, _, block, index in outs],
            scratch_shapes=list(scratch),
        ),
        out_shape=[jax.ShapeDtypeStruct(shape, dtype) for shape, dtype, _, _ in outs],
        input_output_aliases={first + n: k for n, (_, k) in enumerate(held)},
        compiler_params=pltpu.CompilerParams(
            dimension_semantics=("arbitrary",) * len(grid), vmem_limit_bytes=VMEM_LIMIT
        ),
        cost_estimate=pl.CostEstimate(
            flops=int(cost[0] * COST), bytes_accessed=int(cost[1] * COST), transcendentals=0
        ),
        name=name,
    )(meta, *[array for array, _, _ in ins], *[array for array, _ in held])


def whole(array):
    zeros = (0,) * array.ndim
    return (array, array.shape, lambda *_: zeros)


def out_whole(shape, dtype):
    zeros = (0,) * len(shape)
    return (shape, dtype, shape, lambda *_: zeros)


def partner_lanes(tile):
    lane = lax.broadcasted_iota(jnp.int32, tile.shape, 1)
    ahead = pltpu.roll(tile, 96, 1)
    behind = pltpu.roll(tile, 32, 1)
    return jnp.where((lane & (HD // 2)) == 0, ahead, behind)


def qkv_kernel(meta, x0, x1, gain, bias, w, b, cosine, sine, out):
    half = w.shape[1] // 3
    tokens = jnp.where(pl.program_id(0) == 0, x0[0], x1[0]).astype(F32)
    normed, _ = standardize(tokens)
    attn_input = (normed * gain[...] + bias[...]).astype(BF16)
    projected = dot(attn_input, w[...]) + b[...]
    cos, sin = cosine[...], sine[...]
    scale = HD**-0.5
    lane = lax.broadcasted_iota(jnp.int32, cos.shape, 1)
    for t in range(2 * half // 128):
        tile = projected[:, t * 128 : (t + 1) * 128]
        turned = tile * cos + partner_lanes(tile) * sin
        if (t + 1) * 128 <= half:
            turned = turned * scale
        elif t * 128 < half:
            turned = turned * jnp.where(lane < half - t * 128, scale, 1.0)
        out[0, :, t * 128 : (t + 1) * 128] = turned.astype(BF16)
    out[0, :, 2 * half :] = projected[:, 2 * half :].astype(BF16)


def qkv_call(meta, base, x0, x1, gain, bias, w, b, cosine, sine):
    count, rows, width = x0.shape
    last = count - 1
    return run(
        qkv_kernel,
        (2, count),
        meta,
        [
            (x0, (1, rows, width), lambda p, q, m: (jnp.where(p == 0, q, last), 0, 0)),
            (x1, (1, rows, width), lambda p, q, m: (jnp.where(p == 0, 0, q), 0, 0)),
            whole(gain),
            whole(bias),
            whole(w),
            whole(b),
            (cosine, (rows, 128), lambda p, q, m: (base + p, 0)),
            (sine, (rows, 128), lambda p, q, m: (base + p, 0)),
        ],
        [
            (
                (count, 2 * rows, w.shape[1]),
                BF16,
                (1, rows, w.shape[1]),
                lambda p, q, m: (q, p, 0),
            )
        ],
        cost=(4 * count * rows * width * w.shape[1], 10 * count * rows * width, 0),
        name="qkv",
    )[0]


def fold(rows):
    half = rows.shape[0] // 2
    return jnp.concatenate([rows[:half], rows[half:]], axis=1)


def unfold(pair):
    width = pair.shape[1] // 2
    return jnp.concatenate([pair[:, :width], pair[:, width:]], axis=0)


def flip(value):
    rows, width = value.shape
    spare = -width % 128
    if spare:
        value = jnp.concatenate([value, jnp.zeros((rows, spare), value.dtype)], axis=1)
    return jnp.transpose(value)[:width]


def unflip(parts):
    width = sum(p.shape[0] for p in parts)
    spare = -width % 128
    if spare:
        parts = [*parts, jnp.zeros((spare, parts[0].shape[1]), parts[0].dtype)]
    return jnp.transpose(jnp.concatenate(parts, axis=0))[:, :width]


def attend_kernel(base, meta, qa, qb, o0, o1, weights, recips):
    b, k = pl.program_id(0), pl.program_id(1)
    j = base + k
    s, prefix = meta[0], meta[4 + b]
    rows = o0.shape[1] * 2
    hw = o0.shape[2] // 2
    heads = hw // HD
    half = qa.shape[1]
    source = qb if base else qa
    mine = source[0, pl.ds(pl.multiple_of(k * rows, rows), rows), :hw]
    at = (s ^ j) * rows + lax.broadcasted_iota(jnp.int32, (rows, 1), 0)
    hidden_from = jnp.where(at < prefix, 1.0, 0.0)
    lane = lax.broadcasted_iota(jnp.int32, (1, rows), 1)
    fills = []
    for side in range(2):
        places = [(s ^ (2 * side + piece)) * rows + lane for piece in range(half // rows)]
        where = jnp.concatenate(places, axis=1)
        fills.append(jnp.where(where < prefix, 0.0, NEG))
    lane128 = lax.broadcasted_iota(jnp.int32, (rows, 128), 1)
    kept = jnp.zeros((rows, 128), F32)
    outs = []
    for h in range(heads):
        q = mine[:, h * HD : (h + 1) * HD]
        scores = []
        for side, ref in enumerate((qa, qb)):
            keys = ref[0, :, hw + h * HD : hw + (h + 1) * HD]
            scores.append(dot_bt(q, keys) + hidden_from * fills[side])
        top = jnp.maximum(
            jnp.max(scores[0], axis=1, keepdims=True), jnp.max(scores[1], axis=1, keepdims=True)
        )
        sums = jnp.zeros((rows, 1), F32)
        mixed = jnp.zeros((rows, HD), F32)
        for side, ref in enumerate((qa, qb)):
            v = ref[0, :, 2 * hw + h * HD : 2 * hw + (h + 1) * HD]
            e = jnp.exp(scores[side] - top)
            sums = sums + jnp.sum(e, axis=1, keepdims=True)
            e = e.astype(BF16)
            weights[0, h, :, side * half : (side + 1) * half] = e
            mixed = mixed + dot(e, v)
        recip = 1.0 / sums
        kept = jnp.where(lane128 == h, recip, kept)
        outs.append((mixed * recip).astype(BF16))
    recips[0] = kept
    folded = fold(jnp.concatenate(outs, axis=1))
    for n, ref in enumerate((o0, o1)):

        @pl.when(k == n)
        def _(ref=ref):
            ref[0] = folded


def attend_call(meta, base, qa, qb, rows, held=()):
    count, half, cols = qa.shape
    hw = cols // 3
    heads = hw // HD
    keys = 2 * half
    block = (1, rows // 2, 2 * hw)
    return run(
        functools.partial(attend_kernel, base),
        (count, half // rows),
        meta,
        [
            (qa, (1, half, cols), lambda b, k, m: (b, 0, 0)),
            (qb, (1, half, cols), lambda b, k, m: (b, 0, 0)),
        ],
        [((count,) + block[1:], BF16, block, lambda b, k, m: (b, 0, 0)) for _ in range(2)]
        + [
            (
                (count, heads, keys, keys),
                BF16,
                (1, heads, rows, keys),
                lambda b, k, m: (b, 0, base + k, 0),
            ),
            ((count, keys, 128), F32, (1, rows, 128), lambda b, k, m: (b, base + k, 0)),
        ],
        cost=(
            2 * count * heads * keys * keys * HD * 4,
            count * heads * keys * keys,
            count * heads * keys * keys // 2,
        ),
        name="attend",
        held=[(x, 2 + n) for n, x in enumerate(held)],
    )


def back_kernel(meta, qa, qb, weights, recips, o0, o1, o2, o3, g0, g1, g2, g3, out, dk, dv, og, go):
    j = pl.program_id(1)
    rows = o0.shape[1] * 2
    hw = o0.shape[2] // 2
    heads = hw // HD
    half = qa.shape[1]
    place = lax.rem(j, 2) * rows
    scale = HD**-0.5
    for k, (o, g) in enumerate(((o0, g0), (o1, g1), (o2, g2), (o3, g3))):

        @pl.when(j == k)
        def _(o=o, g=g):
            grad = g[...].astype(F32)
            go[...] = unfold(grad)
            og[...] = unfold(grad * o[0].astype(F32))

    @pl.when(j == 0)
    def _():
        dk[...] = jnp.zeros_like(dk)
        dv[...] = jnp.zeros_like(dv)

    mine = jnp.where(j < 2, qa[0, pl.ds(place, rows), :hw], qb[0, pl.ds(place, rows), :hw])
    grads = []
    for h in range(heads):
        cols = slice(h * HD, (h + 1) * HD)
        grads.append((go[:, cols] * recips[0, :, h : h + 1]).astype(BF16))
    turned, turned_q = flip(jnp.concatenate(grads, axis=1)), flip(mine)
    query_grads = []
    for h in range(heads):
        cols = slice(h * HD, (h + 1) * HD)
        centre = jnp.sum(og[:, cols], axis=1, keepdims=True) * recips[0, :, h : h + 1]
        dq = jnp.zeros((rows, HD), F32)
        for side, ref in enumerate((qa, qb)):
            k = ref[0, :, hw + h * HD : hw + (h + 1) * HD]
            v = ref[0, :, 2 * hw + h * HD : 2 * hw + (h + 1) * HD]
            span = slice(side * half, (side + 1) * half)
            e = weights[0, h, :, span]
            ds = (e.astype(F32) * (dot_bt(grads[h], v) - centre)).astype(BF16)
            dq = dq + dot(ds, k)
            dk[h, :, span] += dot(turned_q[cols], ds)
            dv[h, :, span] += dot(turned[cols], e)
        query_grads.append((dq * scale).astype(BF16))
    out[0, pl.ds(pl.multiple_of(j * rows, rows), rows), :hw] = jnp.concatenate(query_grads, axis=1)

    @pl.when(j == pl.num_programs(1) - 1)
    def _():
        out[0, :, hw : 2 * hw] = unflip([dk[h] for h in range(heads)]).astype(BF16)
        out[0, :, 2 * hw :] = unflip([dv[h] for h in range(heads)]).astype(BF16)


def back_call(meta, base, some, qa, qb, weights, recips, olds, grads, held=()):
    count, half, cols = qa.shape
    hw = cols // 3
    heads = hw // HD
    keys = 2 * half
    rows = olds[0].shape[1] * 2
    block = (1,) + olds[0].shape[1:]
    piece = lambda b, j, m: (base + b, 0, 0)
    ins = [
        (qa, (1, half, cols), piece),
        (qb, (1, half, cols), piece),
        (weights, (1, heads, rows, keys), lambda b, j, m: (base + b, 0, j, 0)),
        (recips, (1, rows, 128), lambda b, j, m: (base + b, j, 0)),
    ]
    ins += [(x, block, piece) for x in olds]
    for k, x in enumerate(grads):
        first = base + (x.shape[0] - ROWS - count * block[1]) // block[1]
        ins.append((x, block[1:], lambda b, j, m, first=first: (first + b, 0)))
    return run(
        back_kernel,
        (some, keys // rows),
        meta,
        ins,
        [((count, keys, cols), BF16, (1, keys, cols), piece)],
        scratch=[
            pltpu.VMEM((heads, HD, keys), F32),
            pltpu.VMEM((heads, HD, keys), F32),
            pltpu.VMEM((rows, hw), F32),
            pltpu.VMEM((rows, hw), F32),
        ],
        cost=(8 * some * heads * keys * keys * HD * 4, 2 * some * heads * keys * keys, 0),
        name="attend_back",
        held=[(x, 0) for x in held],
    )[0]


def mix_kernel(meta, m0, m1, m2, m3, tokens, w_own, w_other, out_bias, mods, residual, mlp_in, w):
    b = pl.program_id(0)
    s, c, prefix = meta[0], meta[1], meta[4 + b]
    rows, width = tokens.shape[1:]
    hw = m0.shape[2] // 2

    @pl.when(b == 0)
    def _():
        for j in range(4):
            there = pl.ds(pl.multiple_of((s ^ j) * hw, hw), hw)
            own, other = w_own[there], w_other[there]
            even = c == 0
            w[j * hw : (j + 1) * hw, : width // 2] = jnp.where(even, own, other)
            w[j * hw : (j + 1) * hw, width // 2 :] = jnp.where(even, other, own)

    total = tokens[0].astype(F32) + out_bias[...]
    for j, ref in enumerate((m0, m1, m2, m3)):
        total = total + dot(unfold(ref[0]), w[j * hw : (j + 1) * hw])
    residual[0] = total
    normed, _ = standardize(total)
    at = s * rows + lax.broadcasted_iota(jnp.int32, (rows, 1), 0)
    clean = at < prefix
    count = pl.num_programs(0)
    noisy_row, clean_row = mods[pl.ds(b, 1)], mods[pl.ds(count, 1)]
    shift, scale = (
        jnp.where(
            clean,
            clean_row[:, part * width : (part + 1) * width],
            noisy_row[:, part * width : (part + 1) * width],
        )
        for part in range(2)
    )
    mlp_in[0] = (normed * (1.0 + scale) + shift).astype(BF16)


def mix_call(meta, parts, tokens, w_own, w_other, out_bias, mods):
    count, rows, width = tokens.shape
    seq = lambda b, m: (b, 0, 0)
    block = (1, rows, width)
    return run(
        mix_kernel,
        (count,),
        meta,
        [(p, (1,) + p.shape[1:], seq) for p in parts]
        + [(tokens, block, seq), whole(w_own), whole(w_other), whole(out_bias), whole(mods)],
        [
            (tokens.shape, F32, block, seq),
            (tokens.shape, BF16, block, seq),
            out_whole((width, width), BF16),
        ],
        cost=(2 * count * rows * width * width, 12 * count * rows * width, 0),
        name="mix",
    )


def mlp_kernel(ranks, meta, x0, x1, og0, og1, up_bias, mods, *refs):
    pieces, refs = refs[:ranks], refs[ranks:]
    own_branch, own_input, other, up_here, up_away, down_here, down_away, *refs = refs
    up_bias_grad, up_acc, down_acc, up, down = refs
    p, b = pl.program_id(0), pl.program_id(1)
    count = pl.num_programs(1)
    s, i, prefix = meta[0], meta[3], meta[4 + b]
    @pl.when(jnp.logical_and(p == 0, b == 0))
    def _():
        place_ff(meta, pieces, up, down)

    rows, width = x0.shape[1:]
    first = p == 0
    x = jnp.where(first, x0[0], x1[0])
    incoming = jnp.where(first, og0[0], og1[0]).astype(F32)
    at = (s ^ p) * rows + lax.broadcasted_iota(jnp.int32, (rows, 1), 0)
    gate = jnp.where(
        at < prefix, mods[pl.ds(count, 1), 2 * width :], mods[pl.ds(b, 1), 2 * width :]
    )
    grad = (incoming * gate).astype(BF16)
    hidden, slope = gelu_both(dot(x, up[...]) + up_bias[...])
    hidden = hidden.astype(BF16)
    branch = dot(hidden, down[...])
    pre = (dot_bt(grad, down[...]) * slope)
    pre_low = pre.astype(BF16)
    back = dot_bt(pre_low, up[...])
    sums = jnp.sum(pre_low.astype(F32), axis=0, keepdims=True)

    @pl.when(first)
    def _():
        own_branch[0] = branch
        own_input[0] = back

    @pl.when(p == 1)
    def _():
        other[0, 0] = branch.astype(BF16)
        other[1, 0] = back.astype(BF16)

    start = jnp.logical_and(first, b == 0)

    @pl.when(start)
    def _():
        up_acc[...] = dot_at(x, pre_low)
        down_acc[...] = dot_at(hidden, grad)
        up_bias_grad[...] = sums

    @pl.when(jnp.logical_not(start))
    def _():
        up_acc[...] += dot_at(x, pre_low)
        down_acc[...] += dot_at(hidden, grad)
        up_bias_grad[...] += sums

    @pl.when(jnp.logical_and(p == 1, b == count - 1))
    def _():
        outer, deep = up_here.shape[0], up_here.shape[1]

        def blocks(o, _):
            for parity in range(2):
                d = 2 * o + parity
                upper = up_acc[pl.ds(pl.multiple_of(d * deep, deep), deep)].astype(BF16)
                base = d * (2 * deep)
                lower = jnp.concatenate(
                    [
                        down_acc[pl.ds(pl.multiple_of(base + n * deep, deep), deep)]
                        for n in range(2)
                    ],
                    axis=1,
                ).astype(BF16)

                @pl.when(i == parity)
                def _(upper=upper, lower=lower):
                    up_here[pl.ds(o, 1)] = upper[None]
                    down_here[pl.ds(o, 1)] = lower[None]

                @pl.when(i != parity)
                def _(upper=upper, lower=lower):
                    up_away[pl.ds(o, 1)] = upper[None]
                    down_away[pl.ds(o, 1)] = lower[None]

            return 0

        lax.fori_loop(0, outer, blocks, 0)


def mlp_call(meta, x0, x1, og0, og1, pieces, up_bias, mods):
    count, rows, width = x0.shape
    hidden, ranks = up_bias.shape[1], len(pieces)
    last = count - 1
    block = (1, rows, width)
    first = lambda p, b, m: (jnp.where(p == 0, b, last), 0, 0)
    second = lambda p, b, m: (jnp.where(p == 0, 0, b), 0, 0)
    shared = (ranks // 2, width // ranks, hidden)
    return run(
        functools.partial(mlp_kernel, ranks),
        (2, count),
        meta,
        [
            (x0, block, first),
            (x1, block, second),
            (og0, block, first),
            (og1, block, second),
            whole(up_bias),
            whole(mods),
            *(whole(x) for x in pieces),
        ],
        [
            (x0.shape, F32, block, first),
            (x0.shape, F32, block, first),
            (
                (2,) + x0.shape,
                BF16,
                (2,) + block,
                lambda p, b, m: (0, jnp.where(p == 0, 0, b), 0, 0),
            ),
            out_whole(shared, BF16),
            out_whole(shared, BF16),
            out_whole(shared, BF16),
            out_whole(shared, BF16),
            out_whole((1, hidden), F32),
        ],
        scratch=[
            pltpu.VMEM((width, hidden), F32),
            pltpu.VMEM((hidden, width), F32),
            pltpu.VMEM((width, hidden), BF16),
            pltpu.VMEM((hidden, width), BF16),
        ],
        cost=(24 * count * rows * width * hidden, 20 * count * rows * width, 0),
        name="mlp",
    )


def turn_kernel(
    meta,
    residual,
    out_grad,
    own_branch,
    own_input,
    got,
    down_bias,
    mods,
    m0,
    m1,
    m2,
    m3,
    w,
    block_out,
    resid_grad,
    g0,
    g1,
    g2,
    g3,
    biases,
    out_here,
    sums,
    acc,
):
    b = pl.program_id(0)
    count = pl.num_programs(0)
    s, c, prefix = meta[0], meta[1], meta[4 + b]
    rows, width = residual.shape[1:]
    hw = m0.shape[2] // 2
    resid = residual[0]
    incoming = out_grad[0].astype(F32)
    at = s * rows + lax.broadcasted_iota(jnp.int32, (rows, 1), 0)
    clean = at < prefix
    noisy_row, clean_row = mods[pl.ds(b, 1)], mods[pl.ds(count, 1)]
    scale, gate = (
        jnp.where(
            clean,
            clean_row[:, part * width : (part + 1) * width],
            noisy_row[:, part * width : (part + 1) * width],
        )
        for part in (1, 2)
    )
    branch = own_branch[0] + got[0, 0].astype(F32) + down_bias[...]
    input_two = own_input[0] + got[1, 0].astype(F32)
    block_out[0] = (resid + gate * branch).astype(BF16)
    normed, inverse = standardize(resid)
    grads = incoming + norm_back(input_two * (1.0 + scale), normed, inverse)
    resid_grad[0] = grads
    low = grads.astype(BF16)
    keep = jnp.where(clean, 1.0, 0.0)
    kept = []
    for part, value in enumerate((input_two, input_two * normed, incoming * branch)):
        value = value.astype(BF16).astype(F32)
        cols = slice(part * width, (part + 1) * width)
        everything = jnp.sum(value, axis=0, keepdims=True)
        old = jnp.sum(value * keep, axis=0, keepdims=True)
        kept.append((everything - old, old))
    branch_low = (incoming * gate).astype(BF16).astype(F32)
    down_sum = jnp.sum(branch_low, axis=0, keepdims=True)
    out_sum = jnp.sum(low.astype(F32), axis=0, keepdims=True)

    @pl.when(b == 0)
    def _():
        acc[...] = jnp.zeros_like(acc)
        biases[...] = jnp.zeros_like(biases)
        sums[...] = jnp.zeros_like(sums)

    for part, (noisy, old) in enumerate(kept):
        cols = slice(part * width, (part + 1) * width)
        sums[pl.ds(b, 1), cols] = noisy
        sums[pl.ds(count, 1), cols] += old
    biases[0:1] += down_sum
    biases[1:2] += out_sum
    for j, (m, g) in enumerate(((m0, g0), (m1, g1), (m2, g2), (m3, g3))):
        at = (width if j == 1 else 0) + b * (rows // 2)
        at = pl.ds(pl.multiple_of(at, rows // 2), rows // 2)
        g[at] = fold(dot_bt(low, w[j * hw : (j + 1) * hw])).astype(BF16)
        acc[j * hw : (j + 1) * hw] += dot_at(unfold(m[0]), low)

    @pl.when(b == count - 1)
    def _():
        for j in range(4):
            here = pl.ds(pl.multiple_of((s ^ j) * hw, hw), hw)
            block = acc[j * hw : (j + 1) * hw].astype(BF16)
            left, right = block[:, : width // 2], block[:, width // 2 :]
            even = c == 0
            out_here[here] = jnp.where(even, left, right)
            g1[here] = jnp.where(even, right, left)
        cols = g0.shape[1]
        kinds = ROWS * cols // (2 * 3 * width)
        value = sums[:kinds]
        high = value.astype(BF16)
        low_part = (value - high.astype(F32)).astype(BF16)
        lines = [
            x[k : k + 1, n * cols : (n + 1) * cols]
            for x in (high, low_part)
            for k in range(kinds)
            for n in range(3 * width // cols)
        ]
        lines = jnp.concatenate(lines, axis=0)
        for g in (g0, g1, g2, g3):
            g[g.shape[0] - ROWS :] = lines


def turn_call(meta, residual, out_grad, own_branch, own_input, got, down_bias, mods, parts, w):
    count, rows, width = residual.shape
    seq = lambda b, m: (b, 0, 0)
    block = (1, rows, width)
    return run(
        turn_kernel,
        (count,),
        meta,
        [
            (residual, block, seq),
            (out_grad, block, seq),
            (own_branch, block, seq),
            (own_input, block, seq),
            (got, (2,) + block, lambda b, m: (0, b, 0, 0)),
            whole(down_bias),
            whole(mods),
        ]
        + [(p, (1,) + p.shape[1:], seq) for p in parts]
        + [whole(w)],
        [
            (residual.shape, BF16, block, seq),
            (residual.shape, F32, block, seq),
        ]
        + [
            out_whole((extra + p.shape[0] * p.shape[1] + ROWS, p.shape[2]), BF16)
            for p, extra in zip(parts, (0, width, 0, 0))
        ]
        + [out_whole((8, width), F32), out_whole((width, width // 2), BF16)],
        scratch=[pltpu.VMEM((8, 3 * width), F32), pltpu.VMEM((width, width), F32)],
        cost=(4 * count * rows * width * width, 24 * count * rows * width, 0),
        name="turn",
    )


def rows_kernel(meta, g0, g1, g2, g3, out):
    def value(g):
        high = g[: g.shape[0] // 2].astype(F32)
        return high + g[g.shape[0] // 2 :].astype(F32)

    both = (value(g0) + value(g1)) + (value(g2) + value(g3))
    each = out.shape[1] // g0.shape[1]
    for k in range(out.shape[0]):
        out[k : k + 1] = jnp.concatenate(
            [both[k * each + n : k * each + n + 1] for n in range(each)], axis=1
        )


def proj_grad_kernel(meta, x0, x1, x2, x3, raw, w, gain, bias, up_bias, biases, cosine, sine, out, even, odd, acc, in_bias):
    b, k = pl.program_id(0), pl.program_id(1)
    hw = w.shape[1] // 3

    @pl.when(jnp.logical_and(b == 0, k == 0))
    def _():
        acc[...] = jnp.zeros_like(acc)
        in_bias[...] = jnp.zeros_like(in_bias)

    x = jnp.where(k < 2, jnp.where(k == 0, x0[0], x1[0]), jnp.where(k == 2, x2[0], x3[0]))
    normed, _ = standardize(x.astype(F32))
    cos, sin = cosine[...], sine[...]
    tiles = []
    for t in range(2 * hw // 128):
        tile = raw[0, :, t * 128 : (t + 1) * 128].astype(F32)
        tiles.append((tile * cos - partner_lanes(tile) * sin).astype(BF16))
    tiles.append(raw[0, :, 2 * hw :])
    grads = jnp.concatenate(tiles, axis=1)
    out[0] = grads
    acc[...] += dot_at(normed.astype(BF16), grads)
    in_bias[...] += jnp.sum(grads.astype(F32), axis=0, keepdims=True)

    @pl.when(jnp.logical_and(b == pl.num_programs(0) - 1, k == 3))
    def _():
        ranks = 2 * even.shape[0]
        deep, cols = acc.shape[0] // ranks, acc.shape[1]
        wide = w[...].astype(F32)
        lane = lax.broadcasted_iota(jnp.int32, (acc.shape[0], 128), 1)
        sums = jnp.where(
            lane == 0,
            jnp.sum(acc[...] * wide, axis=1, keepdims=True),
            jnp.sum(wide * in_bias[...], axis=1, keepdims=True),
        )
        sums = jnp.transpose(sums)
        flat = jnp.concatenate(
            [in_bias[...], up_bias[...], sums[0:1], sums[1:2], biases[1:2], biases[0:1]], axis=1
        )
        count = flat.shape[1] // cols
        extra = jnp.concatenate(
            [flat[:, r * cols : (r + 1) * cols] for r in range(count)]
            + [jnp.zeros((EXTRA - count, cols), F32)],
            axis=0,
        ).astype(BF16)
        gains, biases_in = (
            jnp.transpose(jnp.broadcast_to(x[...], (128, x.shape[1])))[:, :1] for x in (gain, bias)
        )
        acc[...] = acc[...] * gains + biases_in * in_bias[...]
        d = meta[2]
        for m in range(ranks):
            at = pl.ds(pl.multiple_of((d ^ m) * deep, deep), deep)
            ref = odd if m % 2 else even
            ref[m // 2, :deep] = acc[at].astype(BF16)
            ref[m // 2, deep:] = extra


def proj_grad_call(meta, xs, raw, w, gain, bias, up_bias, biases, cosine, sine, ranks):
    count, rows, width = xs[0].shape
    cols = w.shape[1]
    seq = lambda b, k, m: (b, 0, 0)
    part = lambda b, k, m: (b, k, 0)
    keys = raw.shape[1]
    shared = (ranks // 2, width // ranks + EXTRA, cols)
    return run(
        proj_grad_kernel,
        (count, keys // rows),
        meta,
        [(x, (1, rows, width), seq) for x in xs]
        + [(raw, (1, rows, cols), part)]
        + [whole(x) for x in (w, gain, bias, up_bias, biases)]
        + [(t, (rows, 128), lambda b, k, m: (k, 0)) for t in (cosine, sine)],
        [
            (raw.shape, BF16, (1, rows, cols), part),
            out_whole(shared, BF16),
            out_whole(shared, BF16),
        ],
        scratch=[pltpu.VMEM((width, cols), F32), pltpu.VMEM((1, cols), F32)],
        cost=(2 * count * keys * width * cols, 6 * count * keys * width, 0),
        name="proj_grad",
    )


def token_grad_kernel(meta, g1, g3, w, sent):
    sent[0, 0] = dot_bt(g1[0], w[...]).astype(BF16)
    sent[1, 0] = dot_bt(g3[0], w[...]).astype(BF16)


def token_grad_call(meta, grads, w, shape):
    count, rows, width = shape
    cols = w.shape[1]
    return run(
        token_grad_kernel,
        (count,),
        meta,
        [
            (grads, (1, rows, cols), lambda b, m: (b, 1, 0)),
            (grads, (1, rows, cols), lambda b, m: (b, 3, 0)),
            whole(w),
        ],
        [((2,) + shape, BF16, (2, 1, rows, width), lambda b, m: (0, b, 0, 0))],
        name="token_grad",
    )[0]


def across_kernel(meta, g2, w, got, across):
    across[0] = (dot_bt(g2[0], w[...]) + got[0, 0].astype(F32)).astype(BF16)


def across_call(meta, grads, w, got):
    _, count, rows, width = got.shape
    cols = w.shape[1]
    return run(
        across_kernel,
        (count,),
        meta,
        [
            (grads, (1, rows, cols), lambda b, m: (b, 2, 0)),
            whole(w),
            (got, (1, 1, rows, width), lambda b, m: (1, b, 0, 0)),
        ],
        [((count, rows, width), BF16, (1, rows, width), lambda b, m: (b, 0, 0))],
        name="across",
    )[0]


def last_kernel(meta, tokens, resid_grad, g0, w, got, across, gain, out):
    normed, inverse = standardize(tokens[0].astype(F32))
    grad = dot_bt(g0[0], w[...]) + got[0, 0].astype(F32) + across[0].astype(F32)
    out[0] = resid_grad[0] + norm_back(grad * gain[...], normed, inverse)


def last_call(meta, tokens, resid_grad, grads, w, got, across, gain):
    count, rows, width = tokens.shape
    cols = w.shape[1]
    seq = lambda b, m: (b, 0, 0)
    block = (1, rows, width)
    return run(
        last_kernel,
        (count,),
        meta,
        [
            (tokens, block, seq),
            (resid_grad, block, seq),
            (grads, (1, rows, cols), seq),
            whole(w),
            (got, (1,) + block, lambda b, m: (0, b, 0, 0)),
            (across, block, seq),
            whole(gain),
        ],
        [(tokens.shape, F32, block, seq)],
        cost=(2 * count * rows * width * cols, 20 * count * rows * width, 0),
        name="last",
    )[0]


def pack_in_kernel(meta, proj_in, *refs):
    *vectors, out = refs
    s = meta[0]
    deep, width = proj_in.shape[0], proj_in.shape[1] // 3
    cols = out.shape[1]
    hw = cols // 3
    for k in range(width // hw):

        @pl.when(s == k)
        def _(k=k):
            for t in range(3):
                start = t * width + k * hw
                out[:deep, t * hw : (t + 1) * hw] = proj_in[:, start : start + hw]

    out[deep:] = jnp.zeros((out.shape[0] - deep, cols), BF16)
    steps = vectors.pop()[...]
    vectors = [v[...].astype(F32) for v in vectors]
    vectors += [(steps >> 5).astype(F32), (steps & 31).astype(F32)]
    vec = jnp.concatenate(vectors, axis=1)
    size = vec.shape[1]
    for r in range(pl.cdiv(size, cols)):
        width_r = min(cols, size - r * cols)
        out[deep + r : deep + r + 1, :width_r] = vec[:, r * cols : r * cols + width_r].astype(BF16)


def place_in_kernel(sizes, meta, *refs):
    outer = len(refs) - 13
    pieces, odd, rows, refs = refs[:outer], refs[outer], refs[outer + 1], refs[outer + 2 :]
    w, gain, bias, in_b, out_bias, ada_bias, up_b, down_bias, chosen, wanted, table = refs
    ranks = 2 * outer
    s, c, d = meta[0], meta[1], meta[2]
    deep, cols = w.shape[0] // ranks, w.shape[1]
    hw = cols // 3
    for m in range(ranks):
        piece = odd.at[m // 2] if m % 2 else pieces[m // 2]
        owner = d ^ m
        w[pl.ds(pl.multiple_of(owner * deep, deep), deep)] = piece[:deep]
        table[pl.ds(owner, 1)] = piece[deep:].astype(F32)[None]
    used = -(-sum(sizes) // cols)
    flat = [
        jnp.concatenate([table[k, r : r + 1] for r in range(used)], axis=1) for k in range(ranks)
    ]
    full, start = [], 0
    for size in sizes:
        full.append([f[:, start : start + size] for f in flat])
        start += size
    steps = [high * 32.0 + low for high, low in zip(full[7], full[8])]
    full = [jnp.concatenate(x, axis=1) for x in full]
    gain[...], bias[...], out_bias[...], ada_bias[...], down_bias[...] = (
        full[0],
        full[1],
        full[3],
        full[4],
        full[6],
    )
    width = w.shape[0]
    half = sizes[5] // 2
    for k in range(width // hw):

        @pl.when(s == k)
        def _(k=k):
            in_b[...] = jnp.concatenate(
                [full[2][:, t * width + k * hw : t * width + (k + 1) * hw] for t in range(3)], axis=1
            )

    for k in range(2):

        @pl.when(c == k)
        def _(k=k):
            up_b[...] = jnp.concatenate(
                [full[5][:, (2 * n + k) * half : (2 * n + k + 1) * half] for n in range(ranks)],
                axis=1,
            )

    want = jnp.concatenate([x for step in steps for x in (step, jnp.zeros((1, 1), F32))], axis=1)
    wanted[...] = want
    at = d * rows.shape[0] + lax.broadcasted_iota(jnp.int32, (rows.shape[0], 1), 0)
    picked = dot_at((at.astype(F32) == want).astype(BF16), rows[...]).astype(BF16)
    part = rows.shape[1] // ranks
    for k in range(ranks):
        chosen[k] = picked[:, k * part : (k + 1) * part]


def pack_rest_kernel(meta, up, down, proj_out, out):
    c = meta[1]
    deep = up.shape[0]
    width = down.shape[1]
    half = down.shape[0] // 2
    ff = up.shape[1] // 2
    for k in range(2):

        @pl.when(c == k)
        def _(k=k):
            for d in range(ff // half):
                out[:, d * half : (d + 1) * half] = up[:, (2 * d + k) * half : (2 * d + k + 1) * half]
            out[:, ff : ff + width] = down[k * half : k * half + deep]
            out[:, ff + width : ff + 2 * width] = down[k * half + deep : (k + 1) * half]
            out[:, ff + 2 * width :] = proj_out[:, k * width // 2 : (k + 1) * width // 2]


def place_out_kernel(meta, *refs):
    *pieces, out = refs
    d = meta[2]
    deep = out.shape[0] // len(pieces)
    for m, piece in enumerate(pieces):
        out[pl.ds(pl.multiple_of((d ^ m) * deep, deep), deep)] = piece[...]


def place_ff(meta, pieces, up, down):
    d = meta[2]
    deep = up.shape[0] // len(pieces)
    ff, width = up.shape[1], down.shape[1]
    for m, piece in enumerate(pieces):
        owner = d ^ m
        up[pl.ds(pl.multiple_of(owner * deep, deep), deep)] = piece[:, :ff]
        for n in range(2):
            base = pl.multiple_of(owner * (2 * deep) + n * deep, deep)
            down[pl.ds(base, deep)] = piece[:, ff + n * width : ff + (n + 1) * width]


def half_kernel(meta, here, came, *outs):
    o = meta[2] // 2
    for m, out in enumerate(outs):
        at = pl.ds(o ^ m, 1)
        out[...] = (here[at].astype(F32) + came[at].astype(F32))[0].astype(BF16)


def join_kernel(meta, down_here, down_away, out_here, out_came, here, away):
    i = meta[3]
    outer, deep, wide = down_here.shape
    here[:, :, :wide] = down_here[...]
    away[:, :, :wide] = down_away[...]
    for k in range(2 * outer):
        rows = slice(k * deep, (k + 1) * deep)
        value = (out_here[rows].astype(F32) + out_came[rows].astype(F32)).astype(BF16)

        @pl.when(i == k % 2)
        def _(k=k, value=value):
            here[k // 2, :, wide:] = value

        @pl.when(i != k % 2)
        def _(k=k, value=value):
            away[k // 2, :, wide:] = value


def pair_kernel(meta, even, came, *outs):
    for m, out in enumerate(outs):
        out[...] = (even[m].astype(F32) + came[m].astype(F32)).astype(out.dtype)


def pair_call(meta, even, odd):
    outer = even.shape[0]
    pieces = run(
        pair_kernel,
        (1,),
        meta,
        [whole(even), whole(dp_swap(odd, 1))],
        [out_whole(even.shape[1:], even.dtype) for _ in range(outer)],
        name="pair",
    )
    return pieces[0], [pieces[0]] + [dp_swap(p, 2 * m) for m, p in enumerate(pieces) if m]


def total(refs):
    result = 0.0
    for ref in refs:
        for k in range(ref.shape[0] if len(ref.shape) == 3 else 1):
            result = result + (ref[k] if len(ref.shape) == 3 else ref[...]).astype(F32)
    return result


def gather_kernel(counts, meta, *refs):
    *refs, out = refs
    start, place = 0, 0
    for n in counts:
        value = total(refs[start : start + n])
        out[:, place : place + value.shape[1]] = value.astype(BF16)
        start, place = start + n, place + value.shape[1]


def gather_call(meta, groups):
    refs = [x for g in groups for x in g]
    shape = (groups[0][0].shape[-2], sum(g[0].shape[-1] for g in groups))
    return run(
        functools.partial(gather_kernel, tuple(len(g) for g in groups)),
        (1,),
        meta,
        [whole(x) for x in refs],
        [out_whole(shape, BF16)],
        name="gather",
    )[0]


def close_rest_kernel(meta, own, across, pair, up, down, out):
    c = meta[1]
    deep = own.shape[0]
    width = out.shape[1]
    half = down.shape[0] // 2
    ff = up.shape[1] // 2
    mine = own[...].astype(F32) + across[...].astype(F32)
    other = pair[0].astype(F32) + pair[1].astype(F32)
    for k in range(2):
        value = jnp.where(c == k, mine, other)
        for d in range(ff // half):
            up[:, (2 * d + k) * half : (2 * d + k + 1) * half] = value[:, d * half : (d + 1) * half]
        down[k * half : k * half + deep] = value[:, ff : ff + width]
        down[k * half + deep : (k + 1) * half] = value[:, ff + width : ff + 2 * width]
        out[:, k * width // 2 : (k + 1) * width // 2] = value[:, ff + 2 * width :]


def close_in_kernel(ranks, meta, own, across, beside, beyond, w, gain, bias, in_bias, out_bias, up_bias, down_bias, held):
    s, d = meta[0], meta[2]
    deep, width = w.shape[0], w.shape[1] // 3
    cols = own.shape[1]
    hw = cols // 3
    held[pl.ds(s, 1)] = own[...].astype(F32)[None]
    held[pl.ds(s ^ 2, 1)] = across[...].astype(F32)[None]
    held[pl.ds(s ^ 1, 1)] = beside[...].astype(F32)[None]
    held[pl.ds(s ^ 3, 1)] = beyond[...].astype(F32)[None]
    for k in range(4):
        for t in range(3):
            w[:, t * width + k * hw : t * width + (k + 1) * hw] = held[k, :deep, t * hw : (t + 1) * hw]
    rows = [
        jnp.concatenate([held[k, deep + r : deep + r + 1] for r in range(EXTRA)], axis=1)
        for k in range(4)
    ]
    biases = jnp.concatenate(
        [rows[k][:, t * hw : (t + 1) * hw] for t in range(3) for k in range(4)], axis=1
    )
    ff = 2 * width
    ups = [rows[0][:, cols : cols + ff] + rows[2][:, cols : cols + ff]]
    ups.append(rows[1][:, cols : cols + ff] + rows[3][:, cols : cols + ff])
    rest = rows[0] + rows[1] + rows[2] + rows[3]
    rest = rest[:, cols + ff :]
    part, third, half = width // ranks, 3 * width // ranks, ff // ranks
    for k in range(ranks):

        @pl.when(d == k)
        def _(k=k):
            for n, out in enumerate((gain, bias, out_bias, down_bias)):
                out[...] = rest[0, n * width + k * part : n * width + (k + 1) * part]
            in_bias[...] = biases[0, k * third : (k + 1) * third]
            up_bias[...] = jnp.concatenate([u[:, k * half : (k + 1) * half] for u in ups], axis=1)[0]


def shards(
    tokens,
    prefix_len,
    timestep,
    norm_gain,
    norm_bias,
    proj_in,
    proj_in_bias,
    proj_out,
    proj_out_bias,
    time_table,
    ada_weight,
    ada_bias,
    mlp_up,
    mlp_up_bias,
    mlp_down,
    mlp_down_bias,
    out_grad,
):
    count, local_len, width = tokens.shape
    members = lax.axis_size("seq")
    ranks = lax.axis_size("dp")
    s = lax.axis_index("seq")
    d = lax.axis_index("dp")
    hw = H // members * HD
    deep = proj_in.shape[0]
    half_ff = mlp_down.shape[0] // 2
    ff = ranks * half_ff
    half_out = width // 2
    meta = jnp.concatenate([jnp.stack([s, s % 2, d, d % 2]).astype(jnp.int32), prefix_len])

    tok_x = seq_swap(tokens, 2)

    half_width = HD // 2
    frequency = np.exp(np.arange(half_width) * (-math.log(10000.0) / half_width))
    angles = np.arange(local_len)[:, None] * frequency[None, :]
    cos_in, sin_in = (jnp.asarray(f(angles), F32)[None] for f in (np.cos, np.sin))
    starts = (jnp.stack([s ^ j for j in range(members)]) * local_len).astype(F32)
    starts = starts[:, None] * jnp.asarray(frequency, F32)[None, :]
    cos_at, sin_at = jnp.cos(starts)[:, None], jnp.sin(starts)[:, None]
    cosine = (cos_at * cos_in - sin_at * sin_in).reshape(-1, half_width)
    sine = (sin_at * cos_in + cos_at * sin_in).reshape(-1, half_width)
    cosine = jnp.concatenate([cosine] * 4, axis=1)
    sine = jnp.concatenate([-sine, sine] * 2, axis=1)

    vectors = [
        norm_gain,
        norm_bias,
        proj_in_bias,
        proj_out_bias,
        ada_bias,
        mlp_up_bias,
        mlp_down_bias,
        timestep,
    ]
    sizes = tuple(v.shape[0] for v in (*vectors, timestep))
    pack_in = run(
        pack_in_kernel,
        (1,),
        meta,
        [whole(proj_in), *(whole(v[None]) for v in vectors)],
        [out_whole((deep + EXTRA, 3 * hw), BF16)],
        name="pack_in",
    )[0]
    in_even = [pack_in] + [dp_swap(pack_in, m) for m in range(2, ranks, 2)]
    pack_rest = run(
        pack_rest_kernel,
        (1,),
        meta,
        [whole(after(mlp_up, pack_in)), whole(mlp_down), whole(proj_out)],
        [out_whole((deep, ff + 2 * width + half_out), BF16)],
        name="pack_rest",
    )[0]
    in_even = after(in_even, pack_rest, cosine, sine)
    in_stack = jnp.stack(in_even)
    in_odd = dp_swap(in_stack, 1)
    tok_c = seq_swap(after(tokens, in_stack), 1)
    kinds = count + 1
    in_w, gain, bias, in_b, out_bias, ada_bias_full, up_b, down_bias, chosen, wanted = run(
        functools.partial(place_in_kernel, sizes),
        (1,),
        meta,
        [whole(x) for x in (*in_even, in_odd, time_table)],
        [
            out_whole((width, 3 * hw), BF16),
            out_whole((1, width), F32),
            out_whole((1, width), F32),
            out_whole((1, 3 * hw), F32),
            out_whole((1, width), F32),
            out_whole((1, 3 * width), F32),
            out_whole((1, ff), F32),
            out_whole((1, width), F32),
            out_whole((ranks, ranks * kinds, width // ranks), BF16),
            out_whole((1, ranks * kinds), F32),
        ],
        scratch=[pltpu.VMEM((ranks, EXTRA, 3 * hw), F32)],
        name="place_in",
    )
    chosen_got = dp_turn(chosen)

    outer = ranks // 2
    early = max(1, outer // 4)
    one, two = slice(1, 1 + early), slice(1 + early, 1 + 2 * early)
    three = slice(1 + 2 * early, outer)
    rest_even = [pack_rest] + [
        dp_swap(after(pack_rest, in_even) if m > early else pack_rest, 2 * m)
        for m in range(1, 1 + 2 * early)
    ]
    rest_odd = [dp_swap(after(pack_rest, in_w), 1)]

    cosine_near = cosine
    qkv_near = qkv_call(meta, 0, tokens, tok_c, gain, bias, in_w, in_b, cosine_near, sine)
    rest_even += [
        dp_swap(after(pack_rest, qkv_near), 2 * m) for m in range(1 + 2 * early, outer)
    ]
    rest_even[one] = after(rest_even[one], qkv_near)
    rest_odd += [dp_swap(piece, 1) for piece in rest_even[one]]
    tok_x = after(tok_x, in_stack)
    tok_d = seq_swap(tok_x, 1)
    qkv_far = qkv_call(meta, 2, tok_x, tok_d, gain, bias, in_w, in_b, after(cosine, qkv_near, rest_odd[0]), sine)
    near_again = after(qkv_near, rest_even[two])
    rest_even[two] = after(rest_even[two], qkv_far)
    rest_odd += [dp_swap(piece, 1) for piece in rest_even[two]]
    mixed_2, mixed_3, weights, recips = attend_call(meta, 2, near_again, qkv_far, local_len)
    across_2, across_3 = seq_swap(mixed_2, 2), seq_swap(mixed_3, 3)
    embedded = jnp.sum(after(chosen_got, mixed_2).astype(F32), axis=0)
    activated = jax.nn.silu(embedded).astype(BF16)
    mod_parts = dot(activated, ada_weight).reshape(ranks, kinds, 3 * width)
    mod_got = dp_turn(mod_parts)
    near_again = after(
        qkv_near, mixed_2, mod_parts, rest_odd[one], rest_odd[two], rest_even[three]
    )
    rest_even[three] = after(rest_even[three], mixed_2)
    rest_odd += [dp_swap(piece, 1) for piece in rest_even[three]]
    mixed_0, mixed_1, weights, recips = attend_call(
        meta, 0, near_again, qkv_far, local_len, (weights, recips)
    )
    mixed = [mixed_0, mixed_1, mixed_2, mixed_3]
    mixed_own = [mixed_0, seq_swap(mixed_1, 1), across_2, across_3]
    mods = jnp.sum(after(mod_got, mixed_0), axis=0) + ada_bias_full
    pieces = [
        x for pair in zip([after(pack_rest, mixed_0), *rest_even[1:]], rest_odd) for x in pair
    ]
    last_cols = (ff + 2 * width) // half_out
    out_own = run(
        place_out_kernel,
        (1,),
        meta,
        [(x, (deep, half_out), lambda i, m: (0, last_cols)) for x in pieces],
        [out_whole((width, half_out), BF16)],
        name="place_out",
    )[0]
    out_other = seq_swap(out_own, 1)
    og_other = seq_swap(after(out_grad, out_own), 1)

    residual, mlp_own, out_rel = mix_call(
        meta, mixed_own, tokens, out_own, out_other, out_bias, mods
    )
    mlp_other = seq_swap(mlp_own, 1)
    own_branch, own_input, other, up_here, up_away, down_here, down_away, up_bias_part = mlp_call(
        meta, mlp_own, mlp_other, out_grad, og_other, pieces, up_b, mods
    )
    got = seq_swap(other, 1)
    up_came = dp_swap(up_away, 1)
    block_out, resid_grad, *others = turn_call(
        meta, residual, out_grad, own_branch, own_input, got, down_bias, mods, mixed_own, out_rel
    )
    grads_sent, (biases, out_here) = others[:4], others[4:]
    head_grads = [grads_sent[0]] + [seq_swap(grads_sent[j], j) for j in (1, 2, 3)]

    def halves(here, came):
        return run(
            half_kernel,
            (1,),
            meta,
            [whole(here), whole(came)],
            [out_whole(here.shape[1:], BF16) for _ in range(outer)],
            name="half",
        )

    def spread(pieces):
        return [pieces[0]] + [dp_swap(p, 2 * m) for m, p in enumerate(pieces) if m]

    joined = (outer, deep, ff + half_out)
    down_here, down_away = run(
        join_kernel,
        (1,),
        meta,
        [
            whole(down_here),
            whole(down_away),
            whole(out_here),
            (head_grads[1], (width, half_out), lambda i, m: (0, 0)),
        ],
        [out_whole(joined, BF16), out_whole(joined, BF16)],
        name="join",
    )
    down_came = dp_swap(down_away, 1)
    up_half = halves(after(up_here, down_away), up_came)
    up_got = spread(after(up_half, head_grads))

    raw = back_call(
        meta, 0, count, after(qkv_near, up_half), qkv_far, weights, recips, mixed, head_grads
    )
    down_half = halves(after(down_here, raw), down_came)
    down_got = spread(down_half)
    row_grad = run(
        rows_kernel,
        (1,),
        meta,
        [
            (g, (ROWS, g.shape[1]), lambda i, m, n=g.shape[0] // ROWS - 1: (n, 0))
            for g in after(head_grads, down_half)
        ],
        [out_whole((kinds, 3 * width), F32)],
        name="rows",
    )[0]
    rows_got = dp_all(row_grad)
    grads, in_even, in_odd = proj_grad_call(
        meta,
        (tokens, tok_c, tok_x, tok_d),
        after(raw, down_half, up_got, row_grad),
        in_w,
        gain,
        bias,
        up_bias_part,
        biases,
        cosine,
        sine,
        ranks,
    )
    in_came = dp_swap(in_odd, 1)
    sent = token_grad_call(meta, grads, in_w, tokens.shape)
    rest_sum = gather_call(meta, [up_got, after(down_got, sent, rows_got)])
    came = seq_swap(after(sent, rest_sum), 1)
    rest_x = seq_swap(rest_sum, 2)
    across = across_call(meta, after(grads, rest_sum), in_w, came)
    across_got = seq_swap(across, 2)

    in_pieces = run(
        pair_kernel,
        (1,),
        meta,
        [whole(after(in_even, across)), whole(in_came)],
        [out_whole(in_even.shape[1:], BF16) for _ in range(outer)],
        name="pair",
    )
    in_got = spread(in_pieces)
    exact = functools.partial(lax.dot_general, precision=HIGHEST, preferred_element_type=F32)
    all_rows = after(rows_got, in_pieces[0]).reshape(ranks * kinds, 3 * width)
    act_rows_grad = exact(all_rows, ada_weight.astype(F32), (((1,), (1,)), ((), ())))
    embed_grad = jax.vjp(jax.nn.silu, embedded)[1](act_rows_grad)[0]
    ada_bias_grad = lax.dynamic_slice_in_dim(
        jnp.sum(after(all_rows, in_pieces[0]), axis=0), d * ada_bias.shape[0], ada_bias.shape[0], 0
    )
    ada_grad = exact(activated.astype(F32), after(all_rows, in_pieces[0]), (((0,), (0,)), ((), ())))
    rest_x = after(rest_x, in_pieces[0])
    rest_pair = seq_swap(jnp.stack([rest_sum, rest_x]), 1)
    up_final, down_final, out_final = run(
        close_rest_kernel,
        (1,),
        meta,
        [whole(x) for x in (after(rest_sum, in_pieces[0]), rest_x, rest_pair)],
        [
            out_whole(mlp_up.shape, F32),
            out_whole(mlp_down.shape, F32),
            out_whole(proj_out.shape, F32),
        ],
        name="close_rest",
    )

    in_sum = gather_call(meta, [after(in_got, ada_bias_grad, ada_grad, up_final)])
    in_parts = [in_sum] + [seq_swap(in_sum, j) for j in (2, 1, 3)]
    embed_got = dp_all(after(embed_grad, in_sum))
    tokens_grad = last_call(
        meta, tokens, after(resid_grad, in_sum), grads, in_w, came, across_got, gain
    )
    embed_all = after(embed_got, tokens_grad).transpose(1, 0, 2).reshape(ranks * kinds, width)
    table_at = d * time_table.shape[0] + jnp.arange(time_table.shape[0], dtype=jnp.int32)
    selector = (table_at.astype(F32)[:, None] == wanted).astype(F32)
    table_grad = exact(selector, embed_all, (((1,), (0,)), ((), ())))
    part, third, ff_part = width // ranks, 3 * width // ranks, 4 * width // ranks
    in_final, gain_f, bias_f, in_bias_f, out_bias_f, up_bias_f, down_bias_f = run(
        functools.partial(close_in_kernel, ranks),
        (1,),
        meta,
        [whole(x) for x in in_parts],
        [
            out_whole(proj_in.shape, F32),
            out_whole((part,), F32),
            out_whole((part,), F32),
            out_whole((third,), F32),
            out_whole((part,), F32),
            out_whole((ff_part,), F32),
            out_whole((part,), F32),
        ],
        scratch=[pltpu.VMEM((members, deep + EXTRA, 3 * hw), F32)],
        name="close_in",
    )
    return (
        block_out,
        tokens_grad,
        gain_f.reshape(-1),
        bias_f.reshape(-1),
        in_final,
        in_bias_f.reshape(-1),
        out_final,
        out_bias_f.reshape(-1),
        table_grad,
        ada_grad,
        ada_bias_grad,
        up_final,
        up_bias_f.reshape(-1),
        down_final,
        down_bias_f.reshape(-1),
    )


def solution(mesh):
    rows = P("dp", None)
    vector = P("dp")
    stream = P("dp", "seq", None)
    in_specs = (
        stream,
        vector,
        vector,
        vector,
        vector,
        rows,
        vector,
        rows,
        vector,
        rows,
        rows,
        vector,
        rows,
        vector,
        rows,
        vector,
        stream,
    )
    out_specs = (
        stream,
        stream,
        vector,
        vector,
        rows,
        vector,
        rows,
        vector,
        rows,
        rows,
        vector,
        rows,
        vector,
        rows,
        vector,
    )
    return jax.shard_map(shards, mesh=mesh, in_specs=in_specs, out_specs=out_specs, check_vma=False)
```

```python
import functools
import math

import jax
import jax.numpy as jnp
import numpy as np
from jax import lax
from jax.experimental import pallas as pl
from jax.experimental.pallas import tpu as pltpu
from jax.sharding import PartitionSpec as P

H = 12
HD = 64
EPS = 1e-05
NEG = -1e30
COST = 30
F32 = jnp.float32
BF16 = jnp.bfloat16
HIGHEST = lax.Precision.HIGHEST
VMEM_LIMIT = 62 * 1024 * 1024
ROWS = 48
EXTRA = 16


def standardize(values):
    centred = values - jnp.mean(values, axis=-1, keepdims=True)
    inverse = lax.rsqrt(jnp.mean(centred * centred, axis=-1, keepdims=True) + EPS)
    return centred * inverse, inverse


def norm_back(gradient, normed, inverse):
    return inverse * (
        gradient
        - jnp.mean(gradient, axis=-1, keepdims=True)
        - normed * jnp.mean(gradient * normed, axis=-1, keepdims=True)
    )


def dot(left, right):
    return jnp.dot(left, right, preferred_element_type=F32)


def dot_bt(left, right):
    return lax.dot_general(left, right, (((1,), (1,)), ((), ())), preferred_element_type=F32)


def dot_at(left, right):
    return lax.dot_general(left, right, (((0,), (0,)), ((), ())), preferred_element_type=F32)


TAIL_P = 0.55
TAIL = (
    0.001045374169866761,
    0.2933056852691112,
    0.41788788917041303,
    -0.08811700935317877,
    0.8046529189842585,
    -0.5409110079247637,
    0.11213617568673577,
)


def gelu_both(values):
    bell = jnp.exp(values * values * -0.5)
    inner = 1.0 / (1.0 + (TAIL_P / math.sqrt(2.0)) * jnp.abs(values))
    tail = TAIL[6]
    for coefficient in TAIL[5::-1]:
        tail = tail * inner + coefficient
    tail = tail * bell * 0.5
    cumulative = jnp.where(values >= 0.0, 1.0 - tail, tail)
    return values * cumulative, cumulative + values * bell * (1.0 / math.sqrt(2.0 * math.pi))


def after(value, *others):
    return lax.optimization_barrier((value, others))[0]


def seq_swap(value, mask):
    return lax.ppermute(value, "seq", [(s, s ^ mask) for s in range(lax.axis_size("seq"))])


def dp_swap(value, mask):
    return lax.ppermute(value, "dp", [(d, d ^ mask) for d in range(lax.axis_size("dp"))])


def dp_collect(value):
    mine = [value] + [dp_swap(value, m) for m in range(2, lax.axis_size("dp"), 2)]
    return mine, dp_swap(jnp.stack(mine), 1)


def quad(value):
    across = seq_swap(value, 2)
    return value, across, seq_swap(jnp.stack([value, across]), 1)


def dp_turn(value, outer_only=False):
    groups = None
    if outer_only:
        outer = lax.axis_size("dp") // 2
        groups = [[o * 2 + i for o in range(outer)] for i in range(2)]
    return lax.all_to_all(
        value, "dp", split_axis=0, concat_axis=0, tiled=True, axis_index_groups=groups
    )


def dp_all(value):
    return dp_turn(jnp.broadcast_to(value[None], (lax.axis_size("dp"),) + value.shape))


def run(body, grid, meta, ins, outs, scratch=(), cost=(0, 0, 0), name=None, held=()):
    specs = [pl.BlockSpec(block, index) for _, block, index in ins]
    specs += [pl.BlockSpec(memory_space=pl.ANY) for _ in held]
    first = 1 + len(ins)
    kernel = body
    if held:

        def kernel(meta, *refs):
            return body(meta, *refs[: len(ins)], *refs[len(ins) + len(held) :])

    return pl.pallas_call(
        kernel,
        grid_spec=pltpu.PrefetchScalarGridSpec(
            num_scalar_prefetch=1,
            grid=grid,
            in_specs=specs,
            out_specs=[pl.BlockSpec(block, index) for _, _, block, index in outs],
            scratch_shapes=list(scratch),
        ),
        out_shape=[jax.ShapeDtypeStruct(shape, dtype) for shape, dtype, _, _ in outs],
        input_output_aliases={first + n: k for n, (_, k) in enumerate(held)},
        compiler_params=pltpu.CompilerParams(
            dimension_semantics=("arbitrary",) * len(grid), vmem_limit_bytes=VMEM_LIMIT
        ),
        cost_estimate=pl.CostEstimate(
            flops=int(cost[0] * COST), bytes_accessed=int(cost[1] * COST), transcendentals=0
        ),
        name=name,
    )(meta, *[array for array, _, _ in ins], *[array for array, _ in held])


def whole(array):
    zeros = (0,) * array.ndim
    return (array, array.shape, lambda *_: zeros)


def out_whole(shape, dtype):
    zeros = (0,) * len(shape)
    return (shape, dtype, shape, lambda *_: zeros)


def partner_lanes(tile):
    lane = lax.broadcasted_iota(jnp.int32, tile.shape, 1)
    ahead = pltpu.roll(tile, 96, 1)
    behind = pltpu.roll(tile, 32, 1)
    return jnp.where((lane & (HD // 2)) == 0, ahead, behind)


def qkv_kernel(meta, x0, x1, gain, bias, w, b, cosine, sine, out):
    half = w.shape[1] // 3
    tokens = jnp.where(pl.program_id(0) == 0, x0[0], x1[0]).astype(F32)
    normed, _ = standardize(tokens)
    attn_input = (normed * gain[...] + bias[...]).astype(BF16)
    projected = dot(attn_input, w[...]) + b[...]
    cos, sin = cosine[...], sine[...]
    scale = HD**-0.5
    lane = lax.broadcasted_iota(jnp.int32, cos.shape, 1)
    for t in range(2 * half // 128):
        tile = projected[:, t * 128 : (t + 1) * 128]
        turned = tile * cos + partner_lanes(tile) * sin
        if (t + 1) * 128 <= half:
            turned = turned * scale
        elif t * 128 < half:
            turned = turned * jnp.where(lane < half - t * 128, scale, 1.0)
        out[0, :, t * 128 : (t + 1) * 128] = turned.astype(BF16)
    out[0, :, 2 * half :] = projected[:, 2 * half :].astype(BF16)


def qkv_call(meta, base, x0, x1, gain, bias, w, b, cosine, sine):
    count, rows, width = x0.shape
    last = count - 1
    return run(
        qkv_kernel,
        (2, count),
        meta,
        [
            (x0, (1, rows, width), lambda p, q, m: (jnp.where(p == 0, q, last), 0, 0)),
            (x1, (1, rows, width), lambda p, q, m: (jnp.where(p == 0, 0, q), 0, 0)),
            whole(gain),
            whole(bias),
            whole(w),
            whole(b),
            (cosine, (rows, 128), lambda p, q, m: (base + p, 0)),
            (sine, (rows, 128), lambda p, q, m: (base + p, 0)),
        ],
        [
            (
                (count, 2 * rows, w.shape[1]),
                BF16,
                (1, rows, w.shape[1]),
                lambda p, q, m: (q, p, 0),
            )
        ],
        cost=(4 * count * rows * width * w.shape[1], 10 * count * rows * width, 0),
        name="qkv",
    )[0]


def fold(rows):
    half = rows.shape[0] // 2
    return jnp.concatenate([rows[:half], rows[half:]], axis=1)


def unfold(pair):
    width = pair.shape[1] // 2
    return jnp.concatenate([pair[:, :width], pair[:, width:]], axis=0)


def flip(value):
    rows, width = value.shape
    spare = -width % 128
    if spare:
        value = jnp.concatenate([value, jnp.zeros((rows, spare), value.dtype)], axis=1)
    return jnp.transpose(value)[:width]


def unflip(parts):
    width = sum(p.shape[0] for p in parts)
    spare = -width % 128
    if spare:
        parts = [*parts, jnp.zeros((spare, parts[0].shape[1]), parts[0].dtype)]
    return jnp.transpose(jnp.concatenate(parts, axis=0))[:, :width]


def attend_kernel(base, meta, qa, qb, o0, o1, weights, recips):
    b, k = pl.program_id(0), pl.program_id(1)
    j = base + k
    s, prefix = meta[0], meta[4 + b]
    rows = o0.shape[1] * 2
    hw = o0.shape[2] // 2
    heads = hw // HD
    half = qa.shape[1]
    source = qb if base else qa
    mine = source[0, pl.ds(pl.multiple_of(k * rows, rows), rows), :hw]
    at = (s ^ j) * rows + lax.broadcasted_iota(jnp.int32, (rows, 1), 0)
    hidden_from = jnp.where(at < prefix, 1.0, 0.0)
    lane = lax.broadcasted_iota(jnp.int32, (1, rows), 1)
    fills = []
    for side in range(2):
        places = [(s ^ (2 * side + piece)) * rows + lane for piece in range(half // rows)]
        where = jnp.concatenate(places, axis=1)
        fills.append(jnp.where(where < prefix, 0.0, NEG))
    lane128 = lax.broadcasted_iota(jnp.int32, (rows, 128), 1)
    kept = jnp.zeros((rows, 128), F32)
    outs = []
    for h in range(heads):
        q = mine[:, h * HD : (h + 1) * HD]
        scores = []
        for side, ref in enumerate((qa, qb)):
            keys = ref[0, :, hw + h * HD : hw + (h + 1) * HD]
            scores.append(dot_bt(q, keys) + hidden_from * fills[side])
        top = jnp.maximum(
            jnp.max(scores[0], axis=1, keepdims=True), jnp.max(scores[1], axis=1, keepdims=True)
        )
        sums = jnp.zeros((rows, 1), F32)
        mixed = jnp.zeros((rows, HD), F32)
        for side, ref in enumerate((qa, qb)):
            v = ref[0, :, 2 * hw + h * HD : 2 * hw + (h + 1) * HD]
            e = jnp.exp(scores[side] - top)
            sums = sums + jnp.sum(e, axis=1, keepdims=True)
            e = e.astype(BF16)
            weights[0, h, :, side * half : (side + 1) * half] = e
            mixed = mixed + dot(e, v)
        recip = 1.0 / sums
        kept = jnp.where(lane128 == h, recip, kept)
        outs.append((mixed * recip).astype(BF16))
    recips[0] = kept
    folded = fold(jnp.concatenate(outs, axis=1))
    for n, ref in enumerate((o0, o1)):

        @pl.when(k == n)
        def _(ref=ref):
            ref[0] = folded


def attend_call(meta, base, qa, qb, rows, held=()):
    count, half, cols = qa.shape
    hw = cols // 3
    heads = hw // HD
    keys = 2 * half
    block = (1, rows // 2, 2 * hw)
    return run(
        functools.partial(attend_kernel, base),
        (count, half // rows),
        meta,
        [
            (qa, (1, half, cols), lambda b, k, m: (b, 0, 0)),
            (qb, (1, half, cols), lambda b, k, m: (b, 0, 0)),
        ],
        [((count,) + block[1:], BF16, block, lambda b, k, m: (b, 0, 0)) for _ in range(2)]
        + [
            (
                (count, heads, keys, keys),
                BF16,
                (1, heads, rows, keys),
                lambda b, k, m: (b, 0, base + k, 0),
            ),
            ((count, keys, 128), F32, (1, rows, 128), lambda b, k, m: (b, base + k, 0)),
        ],
        cost=(
            2 * count * heads * keys * keys * HD * 4,
            count * heads * keys * keys,
            count * heads * keys * keys // 2,
        ),
        name="attend",
        held=[(x, 2 + n) for n, x in enumerate(held)],
    )


def back_kernel(meta, qa, qb, weights, recips, o0, o1, o2, o3, g0, g1, g2, g3, out, dk, dv, og, go):
    j = pl.program_id(1)
    rows = o0.shape[1] * 2
    hw = o0.shape[2] // 2
    heads = hw // HD
    half = qa.shape[1]
    place = lax.rem(j, 2) * rows
    scale = HD**-0.5
    for k, (o, g) in enumerate(((o0, g0), (o1, g1), (o2, g2), (o3, g3))):

        @pl.when(j == k)
        def _(o=o, g=g):
            grad = g[...].astype(F32)
            go[...] = unfold(grad)
            og[...] = unfold(grad * o[0].astype(F32))

    @pl.when(j == 0)
    def _():
        dk[...] = jnp.zeros_like(dk)
        dv[...] = jnp.zeros_like(dv)

    mine = jnp.where(j < 2, qa[0, pl.ds(place, rows), :hw], qb[0, pl.ds(place, rows), :hw])
    grads = []
    for h in range(heads):
        cols = slice(h * HD, (h + 1) * HD)
        grads.append((go[:, cols] * recips[0, :, h : h + 1]).astype(BF16))
    turned, turned_q = flip(jnp.concatenate(grads, axis=1)), flip(mine)
    query_grads = []
    for h in range(heads):
        cols = slice(h * HD, (h + 1) * HD)
        centre = jnp.sum(og[:, cols], axis=1, keepdims=True) * recips[0, :, h : h + 1]
        dq = jnp.zeros((rows, HD), F32)
        for side, ref in enumerate((qa, qb)):
            k = ref[0, :, hw + h * HD : hw + (h + 1) * HD]
            v = ref[0, :, 2 * hw + h * HD : 2 * hw + (h + 1) * HD]
            span = slice(side * half, (side + 1) * half)
            e = weights[0, h, :, span]
            ds = (e.astype(F32) * (dot_bt(grads[h], v) - centre)).astype(BF16)
            dq = dq + dot(ds, k)
            dk[h, :, span] += dot(turned_q[cols], ds)
            dv[h, :, span] += dot(turned[cols], e)
        query_grads.append((dq * scale).astype(BF16))
    out[0, pl.ds(pl.multiple_of(j * rows, rows), rows), :hw] = jnp.concatenate(query_grads, axis=1)

    @pl.when(j == pl.num_programs(1) - 1)
    def _():
        out[0, :, hw : 2 * hw] = unflip([dk[h] for h in range(heads)]).astype(BF16)
        out[0, :, 2 * hw :] = unflip([dv[h] for h in range(heads)]).astype(BF16)


def back_call(meta, base, some, qa, qb, weights, recips, olds, grads, held=()):
    count, half, cols = qa.shape
    hw = cols // 3
    heads = hw // HD
    keys = 2 * half
    rows = olds[0].shape[1] * 2
    block = (1,) + olds[0].shape[1:]
    piece = lambda b, j, m: (base + b, 0, 0)
    ins = [
        (qa, (1, half, cols), piece),
        (qb, (1, half, cols), piece),
        (weights, (1, heads, rows, keys), lambda b, j, m: (base + b, 0, j, 0)),
        (recips, (1, rows, 128), lambda b, j, m: (base + b, j, 0)),
    ]
    ins += [(x, block, piece) for x in olds]
    for k, x in enumerate(grads):
        first = base + (x.shape[0] - ROWS - count * block[1]) // block[1]
        ins.append((x, block[1:], lambda b, j, m, first=first: (first + b, 0)))
    return run(
        back_kernel,
        (some, keys // rows),
        meta,
        ins,
        [((count, keys, cols), BF16, (1, keys, cols), piece)],
        scratch=[
            pltpu.VMEM((heads, HD, keys), F32),
            pltpu.VMEM((heads, HD, keys), F32),
            pltpu.VMEM((rows, hw), F32),
            pltpu.VMEM((rows, hw), F32),
        ],
        cost=(8 * some * heads * keys * keys * HD * 4, 2 * some * heads * keys * keys, 0),
        name="attend_back",
        held=[(x, 0) for x in held],
    )[0]


def mix_kernel(meta, m0, m1, m2, m3, tokens, w_own, w_other, out_bias, mods, residual, mlp_in, w):
    b = pl.program_id(0)
    s, c, prefix = meta[0], meta[1], meta[4 + b]
    rows, width = tokens.shape[1:]
    hw = m0.shape[2] // 2

    @pl.when(b == 0)
    def _():
        for j in range(4):
            there = pl.ds(pl.multiple_of((s ^ j) * hw, hw), hw)
            own, other = w_own[there], w_other[there]
            even = c == 0
            w[j * hw : (j + 1) * hw, : width // 2] = jnp.where(even, own, other)
            w[j * hw : (j + 1) * hw, width // 2 :] = jnp.where(even, other, own)

    total = tokens[0].astype(F32) + out_bias[...]
    for j, ref in enumerate((m0, m1, m2, m3)):
        total = total + dot(unfold(ref[0]), w[j * hw : (j + 1) * hw])
    residual[0] = total
    normed, _ = standardize(total)
    at = s * rows + lax.broadcasted_iota(jnp.int32, (rows, 1), 0)
    clean = at < prefix
    count = pl.num_programs(0)
    noisy_row, clean_row = mods[pl.ds(b, 1)], mods[pl.ds(count, 1)]
    shift, scale = (
        jnp.where(
            clean,
            clean_row[:, part * width : (part + 1) * width],
            noisy_row[:, part * width : (part + 1) * width],
        )
        for part in range(2)
    )
    mlp_in[0] = (normed * (1.0 + scale) + shift).astype(BF16)


def mix_call(meta, parts, tokens, w_own, w_other, out_bias, mods):
    count, rows, width = tokens.shape
    seq = lambda b, m: (b, 0, 0)
    block = (1, rows, width)
    return run(
        mix_kernel,
        (count,),
        meta,
        [(p, (1,) + p.shape[1:], seq) for p in parts]
        + [(tokens, block, seq), whole(w_own), whole(w_other), whole(out_bias), whole(mods)],
        [
            (tokens.shape, F32, block, seq),
            (tokens.shape, BF16, block, seq),
            out_whole((width, width), BF16),
        ],
        cost=(2 * count * rows * width * width, 12 * count * rows * width, 0),
        name="mix",
    )


def mlp_kernel(ranks, meta, x0, x1, og0, og1, up_bias, mods, *refs):
    pieces, refs = refs[:ranks], refs[ranks:]
    own_branch, own_input, other, up_here, up_away, down_here, down_away, *refs = refs
    up_bias_grad, up_acc, down_acc, up, down = refs
    p, b = pl.program_id(0), pl.program_id(1)
    count = pl.num_programs(1)
    s, i, prefix = meta[0], meta[3], meta[4 + b]
    @pl.when(jnp.logical_and(p == 0, b == 0))
    def _():
        place_ff(meta, pieces, up, down)

    rows, width = x0.shape[1:]
    first = p == 0
    x = jnp.where(first, x0[0], x1[0])
    incoming = jnp.where(first, og0[0], og1[0]).astype(F32)
    at = (s ^ p) * rows + lax.broadcasted_iota(jnp.int32, (rows, 1), 0)
    gate = jnp.where(
        at < prefix, mods[pl.ds(count, 1), 2 * width :], mods[pl.ds(b, 1), 2 * width :]
    )
    grad = (incoming * gate).astype(BF16)
    hidden, slope = gelu_both(dot(x, up[...]) + up_bias[...])
    hidden = hidden.astype(BF16)
    branch = dot(hidden, down[...])
    pre = (dot_bt(grad, down[...]) * slope)
    pre_low = pre.astype(BF16)
    back = dot_bt(pre_low, up[...])
    sums = jnp.sum(pre_low.astype(F32), axis=0, keepdims=True)

    @pl.when(first)
    def _():
        own_branch[0] = branch
        own_input[0] = back

    @pl.when(p == 1)
    def _():
        other[0, 0] = branch.astype(BF16)
        other[1, 0] = back.astype(BF16)

    start = jnp.logical_and(first, b == 0)

    @pl.when(start)
    def _():
        up_acc[...] = dot_at(x, pre_low)
        down_acc[...] = dot_at(hidden, grad)
        up_bias_grad[...] = sums

    @pl.when(jnp.logical_not(start))
    def _():
        up_acc[...] += dot_at(x, pre_low)
        down_acc[...] += dot_at(hidden, grad)
        up_bias_grad[...] += sums

    @pl.when(jnp.logical_and(p == 1, b == count - 1))
    def _():
        outer, deep = up_here.shape[0], up_here.shape[1]

        def blocks(o, _):
            for parity in range(2):
                d = 2 * o + parity
                upper = up_acc[pl.ds(pl.multiple_of(d * deep, deep), deep)].astype(BF16)
                base = d * (2 * deep)
                lower = jnp.concatenate(
                    [
                        down_acc[pl.ds(pl.multiple_of(base + n * deep, deep), deep)]
                        for n in range(2)
                    ],
                    axis=1,
                ).astype(BF16)

                @pl.when(i == parity)
                def _(upper=upper, lower=lower):
                    up_here[pl.ds(o, 1)] = upper[None]
                    down_here[pl.ds(o, 1)] = lower[None]

                @pl.when(i != parity)
                def _(upper=upper, lower=lower):
                    up_away[pl.ds(o, 1)] = upper[None]
                    down_away[pl.ds(o, 1)] = lower[None]

            return 0

        lax.fori_loop(0, outer, blocks, 0)


def mlp_call(meta, x0, x1, og0, og1, pieces, up_bias, mods):
    count, rows, width = x0.shape
    hidden, ranks = up_bias.shape[1], len(pieces)
    last = count - 1
    block = (1, rows, width)
    first = lambda p, b, m: (jnp.where(p == 0, b, last), 0, 0)
    second = lambda p, b, m: (jnp.where(p == 0, 0, b), 0, 0)
    shared = (ranks // 2, width // ranks, hidden)
    return run(
        functools.partial(mlp_kernel, ranks),
        (2, count),
        meta,
        [
            (x0, block, first),
            (x1, block, second),
            (og0, block, first),
            (og1, block, second),
            whole(up_bias),
            whole(mods),
            *(whole(x) for x in pieces),
        ],
        [
            (x0.shape, F32, block, first),
            (x0.shape, F32, block, first),
            (
                (2,) + x0.shape,
                BF16,
                (2,) + block,
                lambda p, b, m: (0, jnp.where(p == 0, 0, b), 0, 0),
            ),
            out_whole(shared, BF16),
            out_whole(shared, BF16),
            out_whole(shared, BF16),
            out_whole(shared, BF16),
            out_whole((1, hidden), F32),
        ],
        scratch=[
            pltpu.VMEM((width, hidden), F32),
            pltpu.VMEM((hidden, width), F32),
            pltpu.VMEM((width, hidden), BF16),
            pltpu.VMEM((hidden, width), BF16),
        ],
        cost=(24 * count * rows * width * hidden, 20 * count * rows * width, 0),
        name="mlp",
    )


def turn_kernel(
    meta,
    residual,
    out_grad,
    own_branch,
    own_input,
    got,
    down_bias,
    mods,
    m0,
    m1,
    m2,
    m3,
    w,
    block_out,
    resid_grad,
    g0,
    g1,
    g2,
    g3,
    biases,
    out_here,
    sums,
    acc,
):
    b = pl.program_id(0)
    count = pl.num_programs(0)
    s, c, prefix = meta[0], meta[1], meta[4 + b]
    rows, width = residual.shape[1:]
    hw = m0.shape[2] // 2
    resid = residual[0]
    incoming = out_grad[0].astype(F32)
    at = s * rows + lax.broadcasted_iota(jnp.int32, (rows, 1), 0)
    clean = at < prefix
    noisy_row, clean_row = mods[pl.ds(b, 1)], mods[pl.ds(count, 1)]
    scale, gate = (
        jnp.where(
            clean,
            clean_row[:, part * width : (part + 1) * width],
            noisy_row[:, part * width : (part + 1) * width],
        )
        for part in (1, 2)
    )
    branch = own_branch[0] + got[0, 0].astype(F32) + down_bias[...]
    input_two = own_input[0] + got[1, 0].astype(F32)
    block_out[0] = (resid + gate * branch).astype(BF16)
    normed, inverse = standardize(resid)
    grads = incoming + norm_back(input_two * (1.0 + scale), normed, inverse)
    resid_grad[0] = grads
    low = grads.astype(BF16)
    keep = jnp.where(clean, 1.0, 0.0)
    kept = []
    for part, value in enumerate((input_two, input_two * normed, incoming * branch)):
        value = value.astype(BF16).astype(F32)
        cols = slice(part * width, (part + 1) * width)
        everything = jnp.sum(value, axis=0, keepdims=True)
        old = jnp.sum(value * keep, axis=0, keepdims=True)
        kept.append((everything - old, old))
    branch_low = (incoming * gate).astype(BF16).astype(F32)
    down_sum = jnp.sum(branch_low, axis=0, keepdims=True)
    out_sum = jnp.sum(low.astype(F32), axis=0, keepdims=True)

    @pl.when(b == 0)
    def _():
        acc[...] = jnp.zeros_like(acc)
        biases[...] = jnp.zeros_like(biases)
        sums[...] = jnp.zeros_like(sums)

    for part, (noisy, old) in enumerate(kept):
        cols = slice(part * width, (part + 1) * width)
        sums[pl.ds(b, 1), cols] = noisy
        sums[pl.ds(count, 1), cols] += old
    biases[0:1] += down_sum
    biases[1:2] += out_sum
    for j, (m, g) in enumerate(((m0, g0), (m1, g1), (m2, g2), (m3, g3))):
        at = (width if j == 1 else 0) + b * (rows // 2)
        at = pl.ds(pl.multiple_of(at, rows // 2), rows // 2)
        g[at] = fold(dot_bt(low, w[j * hw : (j + 1) * hw])).astype(BF16)
        acc[j * hw : (j + 1) * hw] += dot_at(unfold(m[0]), low)

    @pl.when(b == count - 1)
    def _():
        for j in range(4):
            here = pl.ds(pl.multiple_of((s ^ j) * hw, hw), hw)
            block = acc[j * hw : (j + 1) * hw].astype(BF16)
            left, right = block[:, : width // 2], block[:, width // 2 :]
            even = c == 0
            out_here[here] = jnp.where(even, left, right)
            g1[here] = jnp.where(even, right, left)
        cols = g0.shape[1]
        kinds = ROWS * cols // (2 * 3 * width)
        value = sums[:kinds]
        high = value.astype(BF16)
        low_part = (value - high.astype(F32)).astype(BF16)
        lines = [
            x[k : k + 1, n * cols : (n + 1) * cols]
            for x in (high, low_part)
            for k in range(kinds)
            for n in range(3 * width // cols)
        ]
        lines = jnp.concatenate(lines, axis=0)
        for g in (g0, g1, g2, g3):
            g[g.shape[0] - ROWS :] = lines


def turn_call(meta, residual, out_grad, own_branch, own_input, got, down_bias, mods, parts, w):
    count, rows, width = residual.shape
    seq = lambda b, m: (b, 0, 0)
    block = (1, rows, width)
    return run(
        turn_kernel,
        (count,),
        meta,
        [
            (residual, block, seq),
            (out_grad, block, seq),
            (own_branch, block, seq),
            (own_input, block, seq),
            (got, (2,) + block, lambda b, m: (0, b, 0, 0)),
            whole(down_bias),
            whole(mods),
        ]
        + [(p, (1,) + p.shape[1:], seq) for p in parts]
        + [whole(w)],
        [
            (residual.shape, BF16, block, seq),
            (residual.shape, F32, block, seq),
        ]
        + [
            out_whole((extra + p.shape[0] * p.shape[1] + ROWS, p.shape[2]), BF16)
            for p, extra in zip(parts, (0, width, 0, 0))
        ]
        + [out_whole((8, width), F32), out_whole((width, width // 2), BF16)],
        scratch=[pltpu.VMEM((8, 3 * width), F32), pltpu.VMEM((width, width), F32)],
        cost=(4 * count * rows * width * width, 24 * count * rows * width, 0),
        name="turn",
    )


def rows_kernel(meta, g0, g1, g2, g3, out):
    def value(g):
        high = g[: g.shape[0] // 2].astype(F32)
        return high + g[g.shape[0] // 2 :].astype(F32)

    both = (value(g0) + value(g1)) + (value(g2) + value(g3))
    each = out.shape[1] // g0.shape[1]
    for k in range(out.shape[0]):
        out[k : k + 1] = jnp.concatenate(
            [both[k * each + n : k * each + n + 1] for n in range(each)], axis=1
        )


def proj_grad_kernel(meta, x0, x1, x2, x3, raw, w, gain, bias, up_bias, biases, cosine, sine, out, even, odd, acc, in_bias):
    b, k = pl.program_id(0), pl.program_id(1)
    hw = w.shape[1] // 3

    @pl.when(jnp.logical_and(b == 0, k == 0))
    def _():
        acc[...] = jnp.zeros_like(acc)
        in_bias[...] = jnp.zeros_like(in_bias)

    x = jnp.where(k < 2, jnp.where(k == 0, x0[0], x1[0]), jnp.where(k == 2, x2[0], x3[0]))
    normed, _ = standardize(x.astype(F32))
    cos, sin = cosine[...], sine[...]
    tiles = []
    for t in range(2 * hw // 128):
        tile = raw[0, :, t * 128 : (t + 1) * 128].astype(F32)
        tiles.append((tile * cos - partner_lanes(tile) * sin).astype(BF16))
    tiles.append(raw[0, :, 2 * hw :])
    grads = jnp.concatenate(tiles, axis=1)
    out[0] = grads
    acc[...] += dot_at(normed.astype(BF16), grads)
    in_bias[...] += jnp.sum(grads.astype(F32), axis=0, keepdims=True)

    @pl.when(jnp.logical_and(b == pl.num_programs(0) - 1, k == 3))
    def _():
        ranks = 2 * even.shape[0]
        deep, cols = acc.shape[0] // ranks, acc.shape[1]
        wide = w[...].astype(F32)
        lane = lax.broadcasted_iota(jnp.int32, (acc.shape[0], 128), 1)
        sums = jnp.where(
            lane == 0,
            jnp.sum(acc[...] * wide, axis=1, keepdims=True),
            jnp.sum(wide * in_bias[...], axis=1, keepdims=True),
        )
        sums = jnp.transpose(sums)
        flat = jnp.concatenate(
            [in_bias[...], up_bias[...], sums[0:1], sums[1:2], biases[1:2], biases[0:1]], axis=1
        )
        count = flat.shape[1] // cols
        extra = jnp.concatenate(
            [flat[:, r * cols : (r + 1) * cols] for r in range(count)]
            + [jnp.zeros((EXTRA - count, cols), F32)],
            axis=0,
        ).astype(BF16)
        gains, biases_in = (
            jnp.transpose(jnp.broadcast_to(x[...], (128, x.shape[1])))[:, :1] for x in (gain, bias)
        )
        acc[...] = acc[...] * gains + biases_in * in_bias[...]
        d = meta[2]
        for m in range(ranks):
            at = pl.ds(pl.multiple_of((d ^ m) * deep, deep), deep)
            ref = odd if m % 2 else even
            ref[m // 2, :deep] = acc[at].astype(BF16)
            ref[m // 2, deep:] = extra


def proj_grad_call(meta, xs, raw, w, gain, bias, up_bias, biases, cosine, sine, ranks):
    count, rows, width = xs[0].shape
    cols = w.shape[1]
    seq = lambda b, k, m: (b, 0, 0)
    part = lambda b, k, m: (b, k, 0)
    keys = raw.shape[1]
    shared = (ranks // 2, width // ranks + EXTRA, cols)
    return run(
        proj_grad_kernel,
        (count, keys // rows),
        meta,
        [(x, (1, rows, width), seq) for x in xs]
        + [(raw, (1, rows, cols), part)]
        + [whole(x) for x in (w, gain, bias, up_bias, biases)]
        + [(t, (rows, 128), lambda b, k, m: (k, 0)) for t in (cosine, sine)],
        [
            (raw.shape, BF16, (1, rows, cols), part),
            out_whole(shared, BF16),
            out_whole(shared, BF16),
        ],
        scratch=[pltpu.VMEM((width, cols), F32), pltpu.VMEM((1, cols), F32)],
        cost=(2 * count * keys * width * cols, 6 * count * keys * width, 0),
        name="proj_grad",
    )


def token_grad_kernel(meta, g1, g3, w, sent):
    sent[0, 0] = dot_bt(g1[0], w[...]).astype(BF16)
    sent[1, 0] = dot_bt(g3[0], w[...]).astype(BF16)


def token_grad_call(meta, grads, w, shape):
    count, rows, width = shape
    cols = w.shape[1]
    return run(
        token_grad_kernel,
        (count,),
        meta,
        [
            (grads, (1, rows, cols), lambda b, m: (b, 1, 0)),
            (grads, (1, rows, cols), lambda b, m: (b, 3, 0)),
            whole(w),
        ],
        [((2,) + shape, BF16, (2, 1, rows, width), lambda b, m: (0, b, 0, 0))],
        name="token_grad",
    )[0]


def across_kernel(meta, g2, w, got, across):
    across[0] = (dot_bt(g2[0], w[...]) + got[0, 0].astype(F32)).astype(BF16)


def across_call(meta, grads, w, got):
    _, count, rows, width = got.shape
    cols = w.shape[1]
    return run(
        across_kernel,
        (count,),
        meta,
        [
            (grads, (1, rows, cols), lambda b, m: (b, 2, 0)),
            whole(w),
            (got, (1, 1, rows, width), lambda b, m: (1, b, 0, 0)),
        ],
        [((count, rows, width), BF16, (1, rows, width), lambda b, m: (b, 0, 0))],
        name="across",
    )[0]


def last_kernel(meta, tokens, resid_grad, g0, w, got, across, gain, out):
    normed, inverse = standardize(tokens[0].astype(F32))
    grad = dot_bt(g0[0], w[...]) + got[0, 0].astype(F32) + across[0].astype(F32)
    out[0] = resid_grad[0] + norm_back(grad * gain[...], normed, inverse)


def last_call(meta, tokens, resid_grad, grads, w, got, across, gain):
    count, rows, width = tokens.shape
    cols = w.shape[1]
    seq = lambda b, m: (b, 0, 0)
    block = (1, rows, width)
    return run(
        last_kernel,
        (count,),
        meta,
        [
            (tokens, block, seq),
            (resid_grad, block, seq),
            (grads, (1, rows, cols), seq),
            whole(w),
            (got, (1,) + block, lambda b, m: (0, b, 0, 0)),
            (across, block, seq),
            whole(gain),
        ],
        [(tokens.shape, F32, block, seq)],
        cost=(2 * count * rows * width * cols, 20 * count * rows * width, 0),
        name="last",
    )[0]


def pack_in_kernel(meta, proj_in, *refs):
    *vectors, out = refs
    s = meta[0]
    deep, width = proj_in.shape[0], proj_in.shape[1] // 3
    cols = out.shape[1]
    hw = cols // 3
    for k in range(width // hw):

        @pl.when(s == k)
        def _(k=k):
            for t in range(3):
                start = t * width + k * hw
                out[:deep, t * hw : (t + 1) * hw] = proj_in[:, start : start + hw]

    out[deep:] = jnp.zeros((out.shape[0] - deep, cols), BF16)
    steps = vectors.pop()[...][None]
    vectors = [v[...].astype(F32)[None] for v in vectors]
    vectors += [(steps >> 5).astype(F32), (steps & 31).astype(F32)]
    vec = jnp.concatenate(vectors, axis=1)
    size = vec.shape[1]
    for r in range(pl.cdiv(size, cols)):
        width_r = min(cols, size - r * cols)
        out[deep + r : deep + r + 1, :width_r] = vec[:, r * cols : r * cols + width_r].astype(BF16)


def place_in_kernel(sizes, meta, *refs):
    outer = len(refs) - 13
    pieces, odd, rows, refs = refs[:outer], refs[outer], refs[outer + 1], refs[outer + 2 :]
    w, gain, bias, in_b, out_bias, ada_bias, up_b, down_bias, chosen, wanted, table = refs
    ranks = 2 * outer
    s, c, d = meta[0], meta[1], meta[2]
    deep, cols = w.shape[0] // ranks, w.shape[1]
    hw = cols // 3
    for m in range(ranks):
        piece = odd.at[m // 2] if m % 2 else pieces[m // 2]
        owner = d ^ m
        w[pl.ds(pl.multiple_of(owner * deep, deep), deep)] = piece[:deep]
        table[pl.ds(owner, 1)] = piece[deep:].astype(F32)[None]
    used = -(-sum(sizes) // cols)
    flat = [
        jnp.concatenate([table[k, r : r + 1] for r in range(used)], axis=1) for k in range(ranks)
    ]
    full, start = [], 0
    for size in sizes:
        full.append([f[:, start : start + size] for f in flat])
        start += size
    steps = [high * 32.0 + low for high, low in zip(full[7], full[8])]
    full = [jnp.concatenate(x, axis=1) for x in full]
    gain[...], bias[...], out_bias[...], ada_bias[...], down_bias[...] = (
        full[0],
        full[1],
        full[3],
        full[4],
        full[6],
    )
    width = w.shape[0]
    half = sizes[5] // 2
    for k in range(width // hw):

        @pl.when(s == k)
        def _(k=k):
            in_b[...] = jnp.concatenate(
                [full[2][:, t * width + k * hw : t * width + (k + 1) * hw] for t in range(3)], axis=1
            )

    for k in range(2):

        @pl.when(c == k)
        def _(k=k):
            up_b[...] = jnp.concatenate(
                [full[5][:, (2 * n + k) * half : (2 * n + k + 1) * half] for n in range(ranks)],
                axis=1,
            )

    want = jnp.concatenate([x for step in steps for x in (step, jnp.zeros((1, 1), F32))], axis=1)
    wanted[...] = want
    at = d * rows.shape[0] + lax.broadcasted_iota(jnp.int32, (rows.shape[0], 1), 0)
    picked = dot_at((at.astype(F32) == want).astype(BF16), rows[...]).astype(BF16)
    part = rows.shape[1] // ranks
    for k in range(ranks):
        chosen[k] = picked[:, k * part : (k + 1) * part]


def pack_rest_kernel(meta, up, down, proj_out, out):
    c = meta[1]
    deep = up.shape[0]
    width = down.shape[1]
    half = down.shape[0] // 2
    ff = up.shape[1] // 2
    for k in range(2):

        @pl.when(c == k)
        def _(k=k):
            for d in range(ff // half):
                out[:, d * half : (d + 1) * half] = up[:, (2 * d + k) * half : (2 * d + k + 1) * half]
            out[:, ff : ff + width] = down[k * half : k * half + deep]
            out[:, ff + width : ff + 2 * width] = down[k * half + deep : (k + 1) * half]
            out[:, ff + 2 * width :] = proj_out[:, k * width // 2 : (k + 1) * width // 2]


def place_out_kernel(meta, *refs):
    *pieces, out = refs
    d = meta[2]
    deep = out.shape[0] // len(pieces)
    for m, piece in enumerate(pieces):
        out[pl.ds(pl.multiple_of((d ^ m) * deep, deep), deep)] = piece[...]


def place_ff(meta, pieces, up, down):
    d = meta[2]
    deep = up.shape[0] // len(pieces)
    ff, width = up.shape[1], down.shape[1]
    for m, piece in enumerate(pieces):
        owner = d ^ m
        up[pl.ds(pl.multiple_of(owner * deep, deep), deep)] = piece[:, :ff]
        for n in range(2):
            base = pl.multiple_of(owner * (2 * deep) + n * deep, deep)
            down[pl.ds(base, deep)] = piece[:, ff + n * width : ff + (n + 1) * width]


def half_kernel(meta, here, came, *outs):
    o = meta[2] // 2
    for m, out in enumerate(outs):
        at = pl.ds(o ^ m, 1)
        out[...] = (here[at].astype(F32) + came[at].astype(F32))[0].astype(BF16)


def join_kernel(meta, down_here, down_away, out_here, out_came, here, away):
    i = meta[3]
    outer, deep, wide = down_here.shape
    here[:, :, :wide] = down_here[...]
    away[:, :, :wide] = down_away[...]
    for k in range(2 * outer):
        rows = slice(k * deep, (k + 1) * deep)
        value = (out_here[rows].astype(F32) + out_came[rows].astype(F32)).astype(BF16)

        @pl.when(i == k % 2)
        def _(k=k, value=value):
            here[k // 2, :, wide:] = value

        @pl.when(i != k % 2)
        def _(k=k, value=value):
            away[k // 2, :, wide:] = value


def pair_kernel(meta, even, came, *outs):
    for m, out in enumerate(outs):
        out[...] = (even[m].astype(F32) + came[m].astype(F32)).astype(out.dtype)


def pair_call(meta, even, odd):
    outer = even.shape[0]
    pieces = run(
        pair_kernel,
        (1,),
        meta,
        [whole(even), whole(dp_swap(odd, 1))],
        [out_whole(even.shape[1:], even.dtype) for _ in range(outer)],
        name="pair",
    )
    return pieces[0], [pieces[0]] + [dp_swap(p, 2 * m) for m, p in enumerate(pieces) if m]


def total(refs):
    result = 0.0
    for ref in refs:
        for k in range(ref.shape[0] if len(ref.shape) == 3 else 1):
            result = result + (ref[k] if len(ref.shape) == 3 else ref[...]).astype(F32)
    return result


def gather_kernel(counts, meta, *refs):
    *refs, out = refs
    start, place = 0, 0
    for n in counts:
        value = total(refs[start : start + n])
        out[:, place : place + value.shape[1]] = value.astype(BF16)
        start, place = start + n, place + value.shape[1]


def gather_call(meta, groups):
    refs = [x for g in groups for x in g]
    shape = (groups[0][0].shape[-2], sum(g[0].shape[-1] for g in groups))
    return run(
        functools.partial(gather_kernel, tuple(len(g) for g in groups)),
        (1,),
        meta,
        [whole(x) for x in refs],
        [out_whole(shape, BF16)],
        name="gather",
    )[0]


def close_rest_kernel(meta, own, across, pair, up, down, out):
    c = meta[1]
    deep = own.shape[0]
    width = out.shape[1]
    half = down.shape[0] // 2
    ff = up.shape[1] // 2
    mine = own[...].astype(F32) + across[...].astype(F32)
    other = pair[0].astype(F32) + pair[1].astype(F32)
    for k in range(2):
        value = jnp.where(c == k, mine, other)
        for d in range(ff // half):
            up[:, (2 * d + k) * half : (2 * d + k + 1) * half] = value[:, d * half : (d + 1) * half]
        down[k * half : k * half + deep] = value[:, ff : ff + width]
        down[k * half + deep : (k + 1) * half] = value[:, ff + width : ff + 2 * width]
        out[:, k * width // 2 : (k + 1) * width // 2] = value[:, ff + 2 * width :]


def close_in_kernel(ranks, meta, own, across, beside, beyond, w, gain, bias, in_bias, out_bias, up_bias, down_bias, held):
    s, d = meta[0], meta[2]
    deep, width = w.shape[0], w.shape[1] // 3
    cols = own.shape[1]
    hw = cols // 3
    held[pl.ds(s, 1)] = own[...].astype(F32)[None]
    held[pl.ds(s ^ 2, 1)] = across[...].astype(F32)[None]
    held[pl.ds(s ^ 1, 1)] = beside[...].astype(F32)[None]
    held[pl.ds(s ^ 3, 1)] = beyond[...].astype(F32)[None]
    for k in range(4):
        for t in range(3):
            w[:, t * width + k * hw : t * width + (k + 1) * hw] = held[k, :deep, t * hw : (t + 1) * hw]
    rows = [
        jnp.concatenate([held[k, deep + r : deep + r + 1] for r in range(EXTRA)], axis=1)
        for k in range(4)
    ]
    biases = jnp.concatenate(
        [rows[k][:, t * hw : (t + 1) * hw] for t in range(3) for k in range(4)], axis=1
    )
    ff = 2 * width
    ups = [rows[0][:, cols : cols + ff] + rows[2][:, cols : cols + ff]]
    ups.append(rows[1][:, cols : cols + ff] + rows[3][:, cols : cols + ff])
    rest = rows[0] + rows[1] + rows[2] + rows[3]
    rest = rest[:, cols + ff :]
    part, third, half = width // ranks, 3 * width // ranks, ff // ranks
    for k in range(ranks):

        @pl.when(d == k)
        def _(k=k):
            for n, out in enumerate((gain, bias, out_bias, down_bias)):
                out[...] = rest[0, n * width + k * part : n * width + (k + 1) * part]
            in_bias[...] = biases[0, k * third : (k + 1) * third]
            up_bias[...] = jnp.concatenate([u[:, k * half : (k + 1) * half] for u in ups], axis=1)[0]


def shards(
    tokens,
    prefix_len,
    timestep,
    norm_gain,
    norm_bias,
    proj_in,
    proj_in_bias,
    proj_out,
    proj_out_bias,
    time_table,
    ada_weight,
    ada_bias,
    mlp_up,
    mlp_up_bias,
    mlp_down,
    mlp_down_bias,
    out_grad,
):
    count, local_len, width = tokens.shape
    members = lax.axis_size("seq")
    ranks = lax.axis_size("dp")
    s = lax.axis_index("seq")
    d = lax.axis_index("dp")
    hw = H // members * HD
    deep = proj_in.shape[0]
    half_ff = mlp_down.shape[0] // 2
    ff = ranks * half_ff
    half_out = width // 2
    meta = jnp.concatenate([jnp.stack([s, s % 2, d, d % 2]).astype(jnp.int32), prefix_len])

    tok_x = seq_swap(tokens, 2)

    half_width = HD // 2
    frequency = np.exp(np.arange(half_width) * (-math.log(10000.0) / half_width))
    angles = np.arange(local_len)[:, None] * frequency[None, :]
    cos_in, sin_in = (jnp.asarray(f(angles), F32)[None] for f in (np.cos, np.sin))
    starts = (jnp.stack([s ^ j for j in range(members)]) * local_len).astype(F32)
    starts = starts[:, None] * jnp.asarray(frequency, F32)[None, :]
    cos_at, sin_at = jnp.cos(starts)[:, None], jnp.sin(starts)[:, None]
    cosine = (cos_at * cos_in - sin_at * sin_in).reshape(-1, half_width)
    sine = (sin_at * cos_in + cos_at * sin_in).reshape(-1, half_width)
    cosine = jnp.concatenate([cosine] * 4, axis=1)
    sine = jnp.concatenate([-sine, sine] * 2, axis=1)

    vectors = [
        norm_gain,
        norm_bias,
        proj_in_bias,
        proj_out_bias,
        ada_bias,
        mlp_up_bias,
        mlp_down_bias,
        timestep,
    ]
    sizes = tuple(v.shape[0] for v in (*vectors, timestep))
    pack_in = run(
        pack_in_kernel,
        (1,),
        meta,
        [whole(proj_in), *(whole(v) for v in vectors)],
        [out_whole((deep + EXTRA, 3 * hw), BF16)],
        name="pack_in",
    )[0]
    in_even = [pack_in] + [dp_swap(pack_in, m) for m in range(2, ranks, 2)]
    pack_rest = run(
        pack_rest_kernel,
        (1,),
        meta,
        [whole(after(mlp_up, pack_in)), whole(mlp_down), whole(proj_out)],
        [out_whole((deep, ff + 2 * width + half_out), BF16)],
        name="pack_rest",
    )[0]
    in_even = after(in_even, pack_rest, cosine, sine)
    in_stack = jnp.stack(in_even)
    in_odd = dp_swap(in_stack, 1)
    tok_c = seq_swap(after(tokens, in_stack), 1)
    kinds = count + 1
    in_w, gain, bias, in_b, out_bias, ada_bias_full, up_b, down_bias, chosen, wanted = run(
        functools.partial(place_in_kernel, sizes),
        (1,),
        meta,
        [whole(x) for x in (*in_even, in_odd, time_table)],
        [
            out_whole((width, 3 * hw), BF16),
            out_whole((1, width), F32),
            out_whole((1, width), F32),
            out_whole((1, 3 * hw), F32),
            out_whole((1, width), F32),
            out_whole((1, 3 * width), F32),
            out_whole((1, ff), F32),
            out_whole((1, width), F32),
            out_whole((ranks, ranks * kinds, width // ranks), BF16),
            out_whole((1, ranks * kinds), F32),
        ],
        scratch=[pltpu.VMEM((ranks, EXTRA, 3 * hw), F32)],
        name="place_in",
    )
    chosen_got = dp_turn(chosen)

    outer = ranks // 2
    early = max(1, outer // 4)
    one, two = slice(1, 1 + early), slice(1 + early, 1 + 2 * early)
    three = slice(1 + 2 * early, outer)
    rest_even = [pack_rest] + [
        dp_swap(after(pack_rest, in_even) if m > early else pack_rest, 2 * m)
        for m in range(1, 1 + 2 * early)
    ]
    rest_odd = [dp_swap(after(pack_rest, in_w), 1)]

    cosine_near = cosine
    qkv_near = qkv_call(meta, 0, tokens, tok_c, gain, bias, in_w, in_b, cosine_near, sine)
    rest_even += [
        dp_swap(after(pack_rest, qkv_near), 2 * m) for m in range(1 + 2 * early, outer)
    ]
    rest_even[one] = after(rest_even[one], qkv_near)
    rest_odd += [dp_swap(piece, 1) for piece in rest_even[one]]
    tok_x = after(tok_x, in_stack)
    tok_d = seq_swap(tok_x, 1)
    qkv_far = qkv_call(meta, 2, tok_x, tok_d, gain, bias, in_w, in_b, after(cosine, qkv_near, rest_odd[0]), sine)
    near_again = after(qkv_near, rest_even[two])
    rest_even[two] = after(rest_even[two], qkv_far)
    rest_odd += [dp_swap(piece, 1) for piece in rest_even[two]]
    mixed_2, mixed_3, weights, recips = attend_call(meta, 2, near_again, qkv_far, local_len)
    across_2, across_3 = seq_swap(mixed_2, 2), seq_swap(mixed_3, 3)
    embedded = jnp.sum(after(chosen_got, mixed_2).astype(F32), axis=0)
    activated = jax.nn.silu(embedded).astype(BF16)
    mod_parts = dot(activated, ada_weight).reshape(ranks, kinds, 3 * width)
    mod_got = dp_turn(mod_parts)
    near_again = after(
        qkv_near, mixed_2, mod_parts, rest_odd[one], rest_odd[two], rest_even[three]
    )
    rest_even[three] = after(rest_even[three], mixed_2)
    rest_odd += [dp_swap(piece, 1) for piece in rest_even[three]]
    mixed_0, mixed_1, weights, recips = attend_call(
        meta, 0, near_again, qkv_far, local_len, (weights, recips)
    )
    mixed = [mixed_0, mixed_1, mixed_2, mixed_3]
    mixed_own = [mixed_0, seq_swap(mixed_1, 1), across_2, across_3]
    mods = jnp.sum(after(mod_got, mixed_0), axis=0) + ada_bias_full
    pieces = [
        x for pair in zip([after(pack_rest, mixed_0), *rest_even[1:]], rest_odd) for x in pair
    ]
    last_cols = (ff + 2 * width) // half_out
    out_own = run(
        place_out_kernel,
        (1,),
        meta,
        [(x, (deep, half_out), lambda i, m: (0, last_cols)) for x in pieces],
        [out_whole((width, half_out), BF16)],
        name="place_out",
    )[0]
    out_other = seq_swap(out_own, 1)
    og_other = seq_swap(after(out_grad, out_own), 1)

    residual, mlp_own, out_rel = mix_call(
        meta, mixed_own, tokens, out_own, out_other, out_bias, mods
    )
    mlp_other = seq_swap(mlp_own, 1)
    own_branch, own_input, other, up_here, up_away, down_here, down_away, up_bias_part = mlp_call(
        meta, mlp_own, mlp_other, out_grad, og_other, pieces, up_b, mods
    )
    got = seq_swap(other, 1)
    up_came = dp_swap(up_away, 1)
    block_out, resid_grad, *others = turn_call(
        meta, residual, out_grad, own_branch, own_input, got, down_bias, mods, mixed_own, out_rel
    )
    grads_sent, (biases, out_here) = others[:4], others[4:]
    head_grads = [grads_sent[0]] + [seq_swap(grads_sent[j], j) for j in (1, 2, 3)]

    def halves(here, came):
        return run(
            half_kernel,
            (1,),
            meta,
            [whole(here), whole(came)],
            [out_whole(here.shape[1:], BF16) for _ in range(outer)],
            name="half",
        )

    def spread(pieces):
        return [pieces[0]] + [dp_swap(p, 2 * m) for m, p in enumerate(pieces) if m]

    joined = (outer, deep, ff + half_out)
    down_here, down_away = run(
        join_kernel,
        (1,),
        meta,
        [
            whole(down_here),
            whole(down_away),
            whole(out_here),
            (head_grads[1], (width, half_out), lambda i, m: (0, 0)),
        ],
        [out_whole(joined, BF16), out_whole(joined, BF16)],
        name="join",
    )
    down_came = dp_swap(down_away, 1)
    up_half = halves(after(up_here, down_away), up_came)
    up_got = spread(after(up_half, head_grads))

    raw = back_call(
        meta, 0, count, after(qkv_near, up_half), qkv_far, weights, recips, mixed, head_grads
    )
    down_half = halves(after(down_here, raw), down_came)
    down_got = spread(down_half)
    row_grad = run(
        rows_kernel,
        (1,),
        meta,
        [
            (g, (ROWS, g.shape[1]), lambda i, m, n=g.shape[0] // ROWS - 1: (n, 0))
            for g in after(head_grads, down_half)
        ],
        [out_whole((kinds, 3 * width), F32)],
        name="rows",
    )[0]
    rows_got = dp_all(row_grad)
    grads, in_even, in_odd = proj_grad_call(
        meta,
        (tokens, tok_c, tok_x, tok_d),
        after(raw, down_half, up_got, row_grad),
        in_w,
        gain,
        bias,
        up_bias_part,
        biases,
        cosine,
        sine,
        ranks,
    )
    in_came = dp_swap(in_odd, 1)
    sent = token_grad_call(meta, grads, in_w, tokens.shape)
    rest_sum = gather_call(meta, [up_got, after(down_got, sent, rows_got)])
    came = seq_swap(after(sent, rest_sum), 1)
    rest_x = seq_swap(rest_sum, 2)
    across = across_call(meta, after(grads, rest_sum), in_w, came)
    across_got = seq_swap(across, 2)

    in_pieces = run(
        pair_kernel,
        (1,),
        meta,
        [whole(after(in_even, across)), whole(in_came)],
        [out_whole(in_even.shape[1:], BF16) for _ in range(outer)],
        name="pair",
    )
    in_got = spread(in_pieces)
    exact = functools.partial(lax.dot_general, precision=HIGHEST, preferred_element_type=F32)
    all_rows = after(rows_got, in_pieces[0]).reshape(ranks * kinds, 3 * width)
    act_rows_grad = exact(all_rows, ada_weight.astype(F32), (((1,), (1,)), ((), ())))
    embed_grad = jax.vjp(jax.nn.silu, embedded)[1](act_rows_grad)[0]
    ada_bias_grad = lax.dynamic_slice_in_dim(
        jnp.sum(after(all_rows, in_pieces[0]), axis=0), d * ada_bias.shape[0], ada_bias.shape[0], 0
    )
    ada_grad = exact(activated.astype(F32), after(all_rows, in_pieces[0]), (((0,), (0,)), ((), ())))
    rest_x = after(rest_x, in_pieces[0])
    rest_pair = seq_swap(jnp.stack([rest_sum, rest_x]), 1)
    up_final, down_final, out_final = run(
        close_rest_kernel,
        (1,),
        meta,
        [whole(x) for x in (after(rest_sum, in_pieces[0]), rest_x, rest_pair)],
        [
            out_whole(mlp_up.shape, F32),
            out_whole(mlp_down.shape, F32),
            out_whole(proj_out.shape, F32),
        ],
        name="close_rest",
    )

    in_sum = gather_call(meta, [after(in_got, ada_bias_grad, ada_grad, up_final)])
    in_parts = [in_sum] + [seq_swap(in_sum, j) for j in (2, 1, 3)]
    embed_got = dp_all(after(embed_grad, in_sum))
    tokens_grad = last_call(
        meta, tokens, after(resid_grad, in_sum), grads, in_w, came, across_got, gain
    )
    embed_all = after(embed_got, tokens_grad).transpose(1, 0, 2).reshape(ranks * kinds, width)
    table_at = d * time_table.shape[0] + jnp.arange(time_table.shape[0], dtype=jnp.int32)
    selector = (table_at.astype(F32)[:, None] == wanted).astype(F32)
    table_grad = exact(selector, embed_all, (((1,), (0,)), ((), ())))
    part, third, ff_part = width // ranks, 3 * width // ranks, 4 * width // ranks
    in_final, gain_f, bias_f, in_bias_f, out_bias_f, up_bias_f, down_bias_f = run(
        functools.partial(close_in_kernel, ranks),
        (1,),
        meta,
        [whole(x) for x in in_parts],
        [
            out_whole(proj_in.shape, F32),
            out_whole((part,), F32),
            out_whole((part,), F32),
            out_whole((third,), F32),
            out_whole((part,), F32),
            out_whole((ff_part,), F32),
            out_whole((part,), F32),
        ],
        scratch=[pltpu.VMEM((members, deep + EXTRA, 3 * hw), F32)],
        name="close_in",
    )
    return (
        block_out,
        tokens_grad,
        gain_f.reshape(-1),
        bias_f.reshape(-1),
        in_final,
        in_bias_f.reshape(-1),
        out_final,
        out_bias_f.reshape(-1),
        table_grad,
        ada_grad,
        ada_bias_grad,
        up_final,
        up_bias_f.reshape(-1),
        down_final,
        down_bias_f.reshape(-1),
    )


def solution(mesh):
    rows = P("dp", None)
    vector = P("dp")
    stream = P("dp", "seq", None)
    in_specs = (
        stream,
        vector,
        vector,
        vector,
        vector,
        rows,
        vector,
        rows,
        vector,
        rows,
        rows,
        vector,
        rows,
        vector,
        rows,
        vector,
        stream,
    )
    out_specs = (
        stream,
        stream,
        vector,
        vector,
        rows,
        vector,
        rows,
        vector,
        rows,
        rows,
        vector,
        rows,
        vector,
        rows,
        vector,
    )
    return jax.shard_map(shards, mesh=mesh, in_specs=in_specs, out_specs=out_specs, check_vma=False)
```

```python
import functools
import math

import jax
import jax.numpy as jnp
import numpy as np
from jax import lax
from jax.experimental import pallas as pl
from jax.experimental.pallas import tpu as pltpu
from jax.sharding import PartitionSpec as P

H = 12
HD = 64
EPS = 1e-05
NEG = -1e30
COST = 30
F32 = jnp.float32
BF16 = jnp.bfloat16
HIGHEST = lax.Precision.HIGHEST
VMEM_LIMIT = 62 * 1024 * 1024
ROWS = 48
EXTRA = 16


def standardize(values):
    centred = values - jnp.mean(values, axis=-1, keepdims=True)
    inverse = lax.rsqrt(jnp.mean(centred * centred, axis=-1, keepdims=True) + EPS)
    return centred * inverse, inverse


def norm_back(gradient, normed, inverse):
    return inverse * (
        gradient
        - jnp.mean(gradient, axis=-1, keepdims=True)
        - normed * jnp.mean(gradient * normed, axis=-1, keepdims=True)
    )


def dot(left, right):
    return jnp.dot(left, right, preferred_element_type=F32)


def dot_bt(left, right):
    return lax.dot_general(left, right, (((1,), (1,)), ((), ())), preferred_element_type=F32)


def dot_at(left, right):
    return lax.dot_general(left, right, (((0,), (0,)), ((), ())), preferred_element_type=F32)


TAIL_P = 0.55
TAIL = (
    0.001045374169866761,
    0.2933056852691112,
    0.41788788917041303,
    -0.08811700935317877,
    0.8046529189842585,
    -0.5409110079247637,
    0.11213617568673577,
)


def gelu_both(values):
    bell = jnp.exp(values * values * -0.5)
    inner = 1.0 / (1.0 + (TAIL_P / math.sqrt(2.0)) * jnp.abs(values))
    tail = TAIL[6]
    for coefficient in TAIL[5::-1]:
        tail = tail * inner + coefficient
    tail = tail * bell * 0.5
    cumulative = jnp.where(values >= 0.0, 1.0 - tail, tail)
    return values * cumulative, cumulative + values * bell * (1.0 / math.sqrt(2.0 * math.pi))


def after(value, *others):
    return lax.optimization_barrier((value, others))[0]


def seq_swap(value, mask):
    return lax.ppermute(value, "seq", [(s, s ^ mask) for s in range(lax.axis_size("seq"))])


def dp_swap(value, mask):
    return lax.ppermute(value, "dp", [(d, d ^ mask) for d in range(lax.axis_size("dp"))])


def dp_collect(value):
    mine = [value] + [dp_swap(value, m) for m in range(2, lax.axis_size("dp"), 2)]
    return mine, dp_swap(jnp.stack(mine), 1)


def quad(value):
    across = seq_swap(value, 2)
    return value, across, seq_swap(jnp.stack([value, across]), 1)


def dp_turn(value, outer_only=False):
    groups = None
    if outer_only:
        outer = lax.axis_size("dp") // 2
        groups = [[o * 2 + i for o in range(outer)] for i in range(2)]
    return lax.all_to_all(
        value, "dp", split_axis=0, concat_axis=0, tiled=True, axis_index_groups=groups
    )


def dp_all(value):
    return dp_turn(jnp.broadcast_to(value[None], (lax.axis_size("dp"),) + value.shape))


def run(body, grid, meta, ins, outs, scratch=(), cost=(0, 0, 0), name=None, held=()):
    specs = [pl.BlockSpec(block, index) for _, block, index in ins]
    specs += [pl.BlockSpec(memory_space=pl.ANY) for _ in held]
    first = 1 + len(ins)
    kernel = body
    if held:

        def kernel(meta, *refs):
            return body(meta, *refs[: len(ins)], *refs[len(ins) + len(held) :])

    return pl.pallas_call(
        kernel,
        grid_spec=pltpu.PrefetchScalarGridSpec(
            num_scalar_prefetch=1,
            grid=grid,
            in_specs=specs,
            out_specs=[pl.BlockSpec(block, index) for _, _, block, index in outs],
            scratch_shapes=list(scratch),
        ),
        out_shape=[jax.ShapeDtypeStruct(shape, dtype) for shape, dtype, _, _ in outs],
        input_output_aliases={first + n: k for n, (_, k) in enumerate(held)},
        compiler_params=pltpu.CompilerParams(
            dimension_semantics=("arbitrary",) * len(grid), vmem_limit_bytes=VMEM_LIMIT
        ),
        cost_estimate=pl.CostEstimate(
            flops=int(cost[0] * COST), bytes_accessed=int(cost[1] * COST), transcendentals=0
        ),
        name=name,
    )(meta, *[array for array, _, _ in ins], *[array for array, _ in held])


def whole(array):
    zeros = (0,) * array.ndim
    return (array, array.shape, lambda *_: zeros)


def out_whole(shape, dtype):
    zeros = (0,) * len(shape)
    return (shape, dtype, shape, lambda *_: zeros)


def partner_lanes(tile):
    lane = lax.broadcasted_iota(jnp.int32, tile.shape, 1)
    ahead = pltpu.roll(tile, 96, 1)
    behind = pltpu.roll(tile, 32, 1)
    return jnp.where((lane & (HD // 2)) == 0, ahead, behind)


def qkv_kernel(meta, x0, x1, gain, bias, w, b, cosine, sine, out):
    half = w.shape[1] // 3
    tokens = jnp.where(pl.program_id(0) == 0, x0[0], x1[0]).astype(F32)
    normed, _ = standardize(tokens)
    attn_input = (normed * gain[...] + bias[...]).astype(BF16)
    projected = dot(attn_input, w[...]) + b[...]
    cos, sin = cosine[...], sine[...]
    scale = HD**-0.5
    lane = lax.broadcasted_iota(jnp.int32, cos.shape, 1)
    for t in range(2 * half // 128):
        tile = projected[:, t * 128 : (t + 1) * 128]
        turned = tile * cos + partner_lanes(tile) * sin
        if (t + 1) * 128 <= half:
            turned = turned * scale
        elif t * 128 < half:
            turned = turned * jnp.where(lane < half - t * 128, scale, 1.0)
        out[0, :, t * 128 : (t + 1) * 128] = turned.astype(BF16)
    out[0, :, 2 * half :] = projected[:, 2 * half :].astype(BF16)


def qkv_call(meta, base, x0, x1, gain, bias, w, b, cosine, sine):
    count, rows, width = x0.shape
    last = count - 1
    return run(
        qkv_kernel,
        (2, count),
        meta,
        [
            (x0, (1, rows, width), lambda p, q, m: (jnp.where(p == 0, q, last), 0, 0)),
            (x1, (1, rows, width), lambda p, q, m: (jnp.where(p == 0, 0, q), 0, 0)),
            whole(gain),
            whole(bias),
            whole(w),
            whole(b),
            (cosine, (rows, 128), lambda p, q, m: (base + p, 0)),
            (sine, (rows, 128), lambda p, q, m: (base + p, 0)),
        ],
        [
            (
                (count, 2 * rows, w.shape[1]),
                BF16,
                (1, rows, w.shape[1]),
                lambda p, q, m: (q, p, 0),
            )
        ],
        cost=(4 * count * rows * width * w.shape[1], 10 * count * rows * width, 0),
        name="qkv",
    )[0]


def fold(rows):
    half = rows.shape[0] // 2
    return jnp.concatenate([rows[:half], rows[half:]], axis=1)


def unfold(pair):
    width = pair.shape[1] // 2
    return jnp.concatenate([pair[:, :width], pair[:, width:]], axis=0)


def flip(value):
    rows, width = value.shape
    spare = -width % 128
    if spare:
        value = jnp.concatenate([value, jnp.zeros((rows, spare), value.dtype)], axis=1)
    return jnp.transpose(value)[:width]


def unflip(parts):
    width = sum(p.shape[0] for p in parts)
    spare = -width % 128
    if spare:
        parts = [*parts, jnp.zeros((spare, parts[0].shape[1]), parts[0].dtype)]
    return jnp.transpose(jnp.concatenate(parts, axis=0))[:, :width]


def attend_kernel(base, meta, qa, qb, o0, o1, weights, recips):
    b, k = pl.program_id(0), pl.program_id(1)
    j = base + k
    s, prefix = meta[0], meta[4 + b]
    rows = o0.shape[1] * 2
    hw = o0.shape[2] // 2
    heads = hw // HD
    half = qa.shape[1]
    source = qb if base else qa
    mine = source[0, pl.ds(pl.multiple_of(k * rows, rows), rows), :hw]
    at = (s ^ j) * rows + lax.broadcasted_iota(jnp.int32, (rows, 1), 0)
    hidden_from = jnp.where(at < prefix, 1.0, 0.0)
    lane = lax.broadcasted_iota(jnp.int32, (1, rows), 1)
    fills = []
    for side in range(2):
        places = [(s ^ (2 * side + piece)) * rows + lane for piece in range(half // rows)]
        where = jnp.concatenate(places, axis=1)
        fills.append(jnp.where(where < prefix, 0.0, NEG))
    lane128 = lax.broadcasted_iota(jnp.int32, (rows, 128), 1)
    kept = jnp.zeros((rows, 128), F32)
    outs = []
    for h in range(heads):
        q = mine[:, h * HD : (h + 1) * HD]
        scores = []
        for side, ref in enumerate((qa, qb)):
            keys = ref[0, :, hw + h * HD : hw + (h + 1) * HD]
            scores.append(dot_bt(q, keys) + hidden_from * fills[side])
        top = jnp.maximum(
            jnp.max(scores[0], axis=1, keepdims=True), jnp.max(scores[1], axis=1, keepdims=True)
        )
        sums = jnp.zeros((rows, 1), F32)
        mixed = jnp.zeros((rows, HD), F32)
        for side, ref in enumerate((qa, qb)):
            v = ref[0, :, 2 * hw + h * HD : 2 * hw + (h + 1) * HD]
            e = jnp.exp(scores[side] - top)
            sums = sums + jnp.sum(e, axis=1, keepdims=True)
            e = e.astype(BF16)
            weights[0, h, :, side * half : (side + 1) * half] = e
            mixed = mixed + dot(e, v)
        recip = 1.0 / sums
        kept = jnp.where(lane128 == h, recip, kept)
        outs.append((mixed * recip).astype(BF16))
    recips[0] = kept
    folded = fold(jnp.concatenate(outs, axis=1))
    for n, ref in enumerate((o0, o1)):

        @pl.when(k == n)
        def _(ref=ref):
            ref[0] = folded


def attend_call(meta, base, qa, qb, rows, held=()):
    count, half, cols = qa.shape
    hw = cols // 3
    heads = hw // HD
    keys = 2 * half
    block = (1, rows // 2, 2 * hw)
    return run(
        functools.partial(attend_kernel, base),
        (count, half // rows),
        meta,
        [
            (qa, (1, half, cols), lambda b, k, m: (b, 0, 0)),
            (qb, (1, half, cols), lambda b, k, m: (b, 0, 0)),
        ],
        [((count,) + block[1:], BF16, block, lambda b, k, m: (b, 0, 0)) for _ in range(2)]
        + [
            (
                (count, heads, keys, keys),
                BF16,
                (1, heads, rows, keys),
                lambda b, k, m: (b, 0, base + k, 0),
            ),
            ((count, keys, 128), F32, (1, rows, 128), lambda b, k, m: (b, base + k, 0)),
        ],
        cost=(
            2 * count * heads * keys * keys * HD * 4,
            count * heads * keys * keys,
            count * heads * keys * keys // 2,
        ),
        name="attend",
        held=[(x, 2 + n) for n, x in enumerate(held)],
    )


def back_kernel(meta, qa, qb, weights, recips, o0, o1, o2, o3, g0, g1, g2, g3, out, dk, dv, og, go):
    j = pl.program_id(1)
    rows = o0.shape[1] * 2
    hw = o0.shape[2] // 2
    heads = hw // HD
    half = qa.shape[1]
    place = lax.rem(j, 2) * rows
    scale = HD**-0.5
    for k, (o, g) in enumerate(((o0, g0), (o1, g1), (o2, g2), (o3, g3))):

        @pl.when(j == k)
        def _(o=o, g=g):
            grad = g[...].astype(F32)
            go[...] = unfold(grad)
            og[...] = unfold(grad * o[0].astype(F32))

    @pl.when(j == 0)
    def _():
        dk[...] = jnp.zeros_like(dk)
        dv[...] = jnp.zeros_like(dv)

    mine = jnp.where(j < 2, qa[0, pl.ds(place, rows), :hw], qb[0, pl.ds(place, rows), :hw])
    grads = []
    for h in range(heads):
        cols = slice(h * HD, (h + 1) * HD)
        grads.append((go[:, cols] * recips[0, :, h : h + 1]).astype(BF16))
    turned, turned_q = flip(jnp.concatenate(grads, axis=1)), flip(mine)
    query_grads = []
    for h in range(heads):
        cols = slice(h * HD, (h + 1) * HD)
        centre = jnp.sum(og[:, cols], axis=1, keepdims=True) * recips[0, :, h : h + 1]
        dq = jnp.zeros((rows, HD), F32)
        for side, ref in enumerate((qa, qb)):
            k = ref[0, :, hw + h * HD : hw + (h + 1) * HD]
            v = ref[0, :, 2 * hw + h * HD : 2 * hw + (h + 1) * HD]
            span = slice(side * half, (side + 1) * half)
            e = weights[0, h, :, span]
            ds = (e.astype(F32) * (dot_bt(grads[h], v) - centre)).astype(BF16)
            dq = dq + dot(ds, k)
            dk[h, :, span] += dot(turned_q[cols], ds)
            dv[h, :, span] += dot(turned[cols], e)
        query_grads.append((dq * scale).astype(BF16))
    out[0, pl.ds(pl.multiple_of(j * rows, rows), rows), :hw] = jnp.concatenate(query_grads, axis=1)

    @pl.when(j == pl.num_programs(1) - 1)
    def _():
        out[0, :, hw : 2 * hw] = unflip([dk[h] for h in range(heads)]).astype(BF16)
        out[0, :, 2 * hw :] = unflip([dv[h] for h in range(heads)]).astype(BF16)


def back_call(meta, base, some, qa, qb, weights, recips, olds, grads, held=()):
    count, half, cols = qa.shape
    hw = cols // 3
    heads = hw // HD
    keys = 2 * half
    rows = olds[0].shape[1] * 2
    block = (1,) + olds[0].shape[1:]
    piece = lambda b, j, m: (base + b, 0, 0)
    ins = [
        (qa, (1, half, cols), piece),
        (qb, (1, half, cols), piece),
        (weights, (1, heads, rows, keys), lambda b, j, m: (base + b, 0, j, 0)),
        (recips, (1, rows, 128), lambda b, j, m: (base + b, j, 0)),
    ]
    ins += [(x, block, piece) for x in olds]
    for k, x in enumerate(grads):
        first = base + (x.shape[0] - ROWS - count * block[1]) // block[1]
        ins.append((x, block[1:], lambda b, j, m, first=first: (first + b, 0)))
    return run(
        back_kernel,
        (some, keys // rows),
        meta,
        ins,
        [((count, keys, cols), BF16, (1, keys, cols), piece)],
        scratch=[
            pltpu.VMEM((heads, HD, keys), F32),
            pltpu.VMEM((heads, HD, keys), F32),
            pltpu.VMEM((rows, hw), F32),
            pltpu.VMEM((rows, hw), F32),
        ],
        cost=(8 * some * heads * keys * keys * HD * 4, 2 * some * heads * keys * keys, 0),
        name="attend_back",
        held=[(x, 0) for x in held],
    )[0]


def mix_kernel(meta, m0, m1, m2, m3, tokens, w_own, w_other, out_bias, mods, residual, mlp_in, w):
    b = pl.program_id(0)
    s, c, prefix = meta[0], meta[1], meta[4 + b]
    rows, width = tokens.shape[1:]
    hw = m0.shape[2] // 2

    @pl.when(b == 0)
    def _():
        for j in range(4):
            there = pl.ds(pl.multiple_of((s ^ j) * hw, hw), hw)
            own, other = w_own[there], w_other[there]
            even = c == 0
            w[j * hw : (j + 1) * hw, : width // 2] = jnp.where(even, own, other)
            w[j * hw : (j + 1) * hw, width // 2 :] = jnp.where(even, other, own)

    total = tokens[0].astype(F32) + out_bias[...]
    for j, ref in enumerate((m0, m1, m2, m3)):
        total = total + dot(unfold(ref[0]), w[j * hw : (j + 1) * hw])
    residual[0] = total
    normed, _ = standardize(total)
    at = s * rows + lax.broadcasted_iota(jnp.int32, (rows, 1), 0)
    clean = at < prefix
    count = pl.num_programs(0)
    noisy_row, clean_row = mods[pl.ds(b, 1)], mods[pl.ds(count, 1)]
    shift, scale = (
        jnp.where(
            clean,
            clean_row[:, part * width : (part + 1) * width],
            noisy_row[:, part * width : (part + 1) * width],
        )
        for part in range(2)
    )
    mlp_in[0] = (normed * (1.0 + scale) + shift).astype(BF16)


def mix_call(meta, parts, tokens, w_own, w_other, out_bias, mods):
    count, rows, width = tokens.shape
    seq = lambda b, m: (b, 0, 0)
    block = (1, rows, width)
    return run(
        mix_kernel,
        (count,),
        meta,
        [(p, (1,) + p.shape[1:], seq) for p in parts]
        + [(tokens, block, seq), whole(w_own), whole(w_other), whole(out_bias), whole(mods)],
        [
            (tokens.shape, F32, block, seq),
            (tokens.shape, BF16, block, seq),
            out_whole((width, width), BF16),
        ],
        cost=(2 * count * rows * width * width, 12 * count * rows * width, 0),
        name="mix",
    )


def mlp_kernel(ranks, meta, x0, x1, og0, og1, up_bias, mods, *refs):
    pieces, refs = refs[:ranks], refs[ranks:]
    own_branch, own_input, other, up_here, up_away, down_here, down_away, *refs = refs
    up_bias_grad, up_acc, down_acc, up, down = refs
    p, b = pl.program_id(0), pl.program_id(1)
    count = pl.num_programs(1)
    s, i, prefix = meta[0], meta[3], meta[4 + b]
    @pl.when(jnp.logical_and(p == 0, b == 0))
    def _():
        place_ff(meta, pieces, up, down)

    rows, width = x0.shape[1:]
    first = p == 0
    x = jnp.where(first, x0[0], x1[0])
    incoming = jnp.where(first, og0[0], og1[0]).astype(F32)
    at = (s ^ p) * rows + lax.broadcasted_iota(jnp.int32, (rows, 1), 0)
    gate = jnp.where(
        at < prefix, mods[pl.ds(count, 1), 2 * width :], mods[pl.ds(b, 1), 2 * width :]
    )
    grad = (incoming * gate).astype(BF16)
    hidden, slope = gelu_both(dot(x, up[...]) + up_bias[...])
    hidden = hidden.astype(BF16)
    branch = dot(hidden, down[...])
    pre = (dot_bt(grad, down[...]) * slope)
    pre_low = pre.astype(BF16)
    back = dot_bt(pre_low, up[...])
    sums = jnp.sum(pre_low.astype(F32), axis=0, keepdims=True)

    @pl.when(first)
    def _():
        own_branch[0] = branch
        own_input[0] = back

    @pl.when(p == 1)
    def _():
        other[0, 0] = branch.astype(BF16)
        other[1, 0] = back.astype(BF16)

    start = jnp.logical_and(first, b == 0)

    @pl.when(start)
    def _():
        up_acc[...] = dot_at(x, pre_low)
        down_acc[...] = dot_at(hidden, grad)
        up_bias_grad[...] = sums

    @pl.when(jnp.logical_not(start))
    def _():
        up_acc[...] += dot_at(x, pre_low)
        down_acc[...] += dot_at(hidden, grad)
        up_bias_grad[...] += sums

    @pl.when(jnp.logical_and(p == 1, b == count - 1))
    def _():
        outer, deep = up_here.shape[0], up_here.shape[1]

        def blocks(o, _):
            for parity in range(2):
                d = 2 * o + parity
                upper = up_acc[pl.ds(pl.multiple_of(d * deep, deep), deep)].astype(BF16)
                base = d * (2 * deep)
                lower = jnp.concatenate(
                    [
                        down_acc[pl.ds(pl.multiple_of(base + n * deep, deep), deep)]
                        for n in range(2)
                    ],
                    axis=1,
                ).astype(BF16)

                @pl.when(i == parity)
                def _(upper=upper, lower=lower):
                    up_here[pl.ds(o, 1)] = upper[None]
                    down_here[pl.ds(o, 1)] = lower[None]

                @pl.when(i != parity)
                def _(upper=upper, lower=lower):
                    up_away[pl.ds(o, 1)] = upper[None]
                    down_away[pl.ds(o, 1)] = lower[None]

            return 0

        lax.fori_loop(0, outer, blocks, 0)


def mlp_call(meta, x0, x1, og0, og1, pieces, up_bias, mods):
    count, rows, width = x0.shape
    hidden, ranks = up_bias.shape[1], len(pieces)
    last = count - 1
    block = (1, rows, width)
    first = lambda p, b, m: (jnp.where(p == 0, b, last), 0, 0)
    second = lambda p, b, m: (jnp.where(p == 0, 0, b), 0, 0)
    shared = (ranks // 2, width // ranks, hidden)
    return run(
        functools.partial(mlp_kernel, ranks),
        (2, count),
        meta,
        [
            (x0, block, first),
            (x1, block, second),
            (og0, block, first),
            (og1, block, second),
            whole(up_bias),
            whole(mods),
            *(whole(x) for x in pieces),
        ],
        [
            (x0.shape, F32, block, first),
            (x0.shape, F32, block, first),
            (
                (2,) + x0.shape,
                BF16,
                (2,) + block,
                lambda p, b, m: (0, jnp.where(p == 0, 0, b), 0, 0),
            ),
            out_whole(shared, BF16),
            out_whole(shared, BF16),
            out_whole(shared, BF16),
            out_whole(shared, BF16),
            out_whole((1, hidden), F32),
        ],
        scratch=[
            pltpu.VMEM((width, hidden), F32),
            pltpu.VMEM((hidden, width), F32),
            pltpu.VMEM((width, hidden), BF16),
            pltpu.VMEM((hidden, width), BF16),
        ],
        cost=(24 * count * rows * width * hidden, 20 * count * rows * width, 0),
        name="mlp",
    )


def turn_kernel(
    meta,
    residual,
    out_grad,
    own_branch,
    own_input,
    got,
    down_bias,
    mods,
    m0,
    m1,
    m2,
    m3,
    w,
    block_out,
    resid_grad,
    g0,
    g1,
    g2,
    g3,
    biases,
    out_here,
    sums,
    acc,
):
    b = pl.program_id(0)
    count = pl.num_programs(0)
    s, c, prefix = meta[0], meta[1], meta[4 + b]
    rows, width = residual.shape[1:]
    hw = m0.shape[2] // 2
    resid = residual[0]
    incoming = out_grad[0].astype(F32)
    at = s * rows + lax.broadcasted_iota(jnp.int32, (rows, 1), 0)
    clean = at < prefix
    noisy_row, clean_row = mods[pl.ds(b, 1)], mods[pl.ds(count, 1)]
    scale, gate = (
        jnp.where(
            clean,
            clean_row[:, part * width : (part + 1) * width],
            noisy_row[:, part * width : (part + 1) * width],
        )
        for part in (1, 2)
    )
    branch = own_branch[0] + got[0, 0].astype(F32) + down_bias[...]
    input_two = own_input[0] + got[1, 0].astype(F32)
    block_out[0] = (resid + gate * branch).astype(BF16)
    normed, inverse = standardize(resid)
    grads = incoming + norm_back(input_two * (1.0 + scale), normed, inverse)
    resid_grad[0] = grads
    low = grads.astype(BF16)
    keep = jnp.where(clean, 1.0, 0.0)
    kept = []
    for part, value in enumerate((input_two, input_two * normed, incoming * branch)):
        value = value.astype(BF16).astype(F32)
        cols = slice(part * width, (part + 1) * width)
        everything = jnp.sum(value, axis=0, keepdims=True)
        old = jnp.sum(value * keep, axis=0, keepdims=True)
        kept.append((everything - old, old))
    branch_low = (incoming * gate).astype(BF16).astype(F32)
    down_sum = jnp.sum(branch_low, axis=0, keepdims=True)
    out_sum = jnp.sum(low.astype(F32), axis=0, keepdims=True)

    @pl.when(b == 0)
    def _():
        acc[...] = jnp.zeros_like(acc)
        biases[...] = jnp.zeros_like(biases)
        sums[...] = jnp.zeros_like(sums)

    for part, (noisy, old) in enumerate(kept):
        cols = slice(part * width, (part + 1) * width)
        sums[pl.ds(b, 1), cols] = noisy
        sums[pl.ds(count, 1), cols] += old
    biases[0:1] += down_sum
    biases[1:2] += out_sum
    for j, (m, g) in enumerate(((m0, g0), (m1, g1), (m2, g2), (m3, g3))):
        at = (width if j == 1 else 0) + b * (rows // 2)
        at = pl.ds(pl.multiple_of(at, rows // 2), rows // 2)
        g[at] = fold(dot_bt(low, w[j * hw : (j + 1) * hw])).astype(BF16)
        acc[j * hw : (j + 1) * hw] += dot_at(unfold(m[0]), low)

    @pl.when(b == count - 1)
    def _():
        for j in range(4):
            here = pl.ds(pl.multiple_of((s ^ j) * hw, hw), hw)
            block = acc[j * hw : (j + 1) * hw].astype(BF16)
            left, right = block[:, : width // 2], block[:, width // 2 :]
            even = c == 0
            out_here[here] = jnp.where(even, left, right)
            g1[here] = jnp.where(even, right, left)
        cols = g0.shape[1]
        kinds = ROWS * cols // (2 * 3 * width)
        value = sums[:kinds]
        high = value.astype(BF16)
        low_part = (value - high.astype(F32)).astype(BF16)
        lines = [
            x[k : k + 1, n * cols : (n + 1) * cols]
            for x in (high, low_part)
            for k in range(kinds)
            for n in range(3 * width // cols)
        ]
        lines = jnp.concatenate(lines, axis=0)
        for g in (g0, g1, g2, g3):
            g[g.shape[0] - ROWS :] = lines


def turn_call(meta, residual, out_grad, own_branch, own_input, got, down_bias, mods, parts, w):
    count, rows, width = residual.shape
    seq = lambda b, m: (b, 0, 0)
    block = (1, rows, width)
    return run(
        turn_kernel,
        (count,),
        meta,
        [
            (residual, block, seq),
            (out_grad, block, seq),
            (own_branch, block, seq),
            (own_input, block, seq),
            (got, (2,) + block, lambda b, m: (0, b, 0, 0)),
            whole(down_bias),
            whole(mods),
        ]
        + [(p, (1,) + p.shape[1:], seq) for p in parts]
        + [whole(w)],
        [
            (residual.shape, BF16, block, seq),
            (residual.shape, F32, block, seq),
        ]
        + [
            out_whole((extra + p.shape[0] * p.shape[1] + ROWS, p.shape[2]), BF16)
            for p, extra in zip(parts, (0, width, 0, 0))
        ]
        + [out_whole((8, width), F32), out_whole((width, width // 2), BF16)],
        scratch=[pltpu.VMEM((8, 3 * width), F32), pltpu.VMEM((width, width), F32)],
        cost=(4 * count * rows * width * width, 24 * count * rows * width, 0),
        name="turn",
    )


def rows_kernel(meta, g0, g1, g2, g3, out):
    def value(g):
        high = g[: g.shape[0] // 2].astype(F32)
        return high + g[g.shape[0] // 2 :].astype(F32)

    both = (value(g0) + value(g1)) + (value(g2) + value(g3))
    each = out.shape[1] // g0.shape[1]
    for k in range(out.shape[0]):
        out[k : k + 1] = jnp.concatenate(
            [both[k * each + n : k * each + n + 1] for n in range(each)], axis=1
        )


def proj_grad_kernel(meta, x0, x1, x2, x3, raw, w, gain, bias, up_bias, biases, cosine, sine, out, even, odd, acc, in_bias):
    b, k = pl.program_id(0), pl.program_id(1)
    hw = w.shape[1] // 3

    @pl.when(jnp.logical_and(b == 0, k == 0))
    def _():
        acc[...] = jnp.zeros_like(acc)
        in_bias[...] = jnp.zeros_like(in_bias)

    x = jnp.where(k < 2, jnp.where(k == 0, x0[0], x1[0]), jnp.where(k == 2, x2[0], x3[0]))
    normed, _ = standardize(x.astype(F32))
    cos, sin = cosine[...], sine[...]
    tiles = []
    for t in range(2 * hw // 128):
        tile = raw[0, :, t * 128 : (t + 1) * 128].astype(F32)
        tiles.append((tile * cos - partner_lanes(tile) * sin).astype(BF16))
    tiles.append(raw[0, :, 2 * hw :])
    grads = jnp.concatenate(tiles, axis=1)
    out[0] = grads
    acc[...] += dot_at(normed.astype(BF16), grads)
    in_bias[...] += jnp.sum(grads.astype(F32), axis=0, keepdims=True)

    @pl.when(jnp.logical_and(b == pl.num_programs(0) - 1, k == 3))
    def _():
        ranks = 2 * even.shape[0]
        deep, cols = acc.shape[0] // ranks, acc.shape[1]
        wide = w[...].astype(F32)
        lane = lax.broadcasted_iota(jnp.int32, (acc.shape[0], 128), 1)
        sums = jnp.where(
            lane == 0,
            jnp.sum(acc[...] * wide, axis=1, keepdims=True),
            jnp.sum(wide * in_bias[...], axis=1, keepdims=True),
        )
        sums = jnp.transpose(sums)
        flat = jnp.concatenate(
            [in_bias[...], up_bias[...], sums[0:1], sums[1:2], biases[1:2], biases[0:1]], axis=1
        )
        count = flat.shape[1] // cols
        extra = jnp.concatenate(
            [flat[:, r * cols : (r + 1) * cols] for r in range(count)]
            + [jnp.zeros((EXTRA - count, cols), F32)],
            axis=0,
        ).astype(BF16)
        gains, biases_in = (
            jnp.transpose(jnp.broadcast_to(x[...], (128, x.shape[1])))[:, :1] for x in (gain, bias)
        )
        acc[...] = acc[...] * gains + biases_in * in_bias[...]
        d = meta[2]
        for m in range(ranks):
            at = pl.ds(pl.multiple_of((d ^ m) * deep, deep), deep)
            ref = odd if m % 2 else even
            ref[m // 2, :deep] = acc[at].astype(BF16)
            ref[m // 2, deep:] = extra


def proj_grad_call(meta, xs, raw, w, gain, bias, up_bias, biases, cosine, sine, ranks):
    count, rows, width = xs[0].shape
    cols = w.shape[1]
    seq = lambda b, k, m: (b, 0, 0)
    part = lambda b, k, m: (b, k, 0)
    keys = raw.shape[1]
    shared = (ranks // 2, width // ranks + EXTRA, cols)
    return run(
        proj_grad_kernel,
        (count, keys // rows),
        meta,
        [(x, (1, rows, width), seq) for x in xs]
        + [(raw, (1, rows, cols), part)]
        + [whole(x) for x in (w, gain, bias, up_bias, biases)]
        + [(t, (rows, 128), lambda b, k, m: (k, 0)) for t in (cosine, sine)],
        [
            (raw.shape, BF16, (1, rows, cols), part),
            out_whole(shared, BF16),
            out_whole(shared, BF16),
        ],
        scratch=[pltpu.VMEM((width, cols), F32), pltpu.VMEM((1, cols), F32)],
        cost=(2 * count * keys * width * cols, 6 * count * keys * width, 0),
        name="proj_grad",
    )


def token_grad_kernel(meta, g1, g3, w, sent):
    sent[0, 0] = dot_bt(g1[0], w[...]).astype(BF16)
    sent[1, 0] = dot_bt(g3[0], w[...]).astype(BF16)


def token_grad_call(meta, grads, w, shape):
    count, rows, width = shape
    cols = w.shape[1]
    return run(
        token_grad_kernel,
        (count,),
        meta,
        [
            (grads, (1, rows, cols), lambda b, m: (b, 1, 0)),
            (grads, (1, rows, cols), lambda b, m: (b, 3, 0)),
            whole(w),
        ],
        [((2,) + shape, BF16, (2, 1, rows, width), lambda b, m: (0, b, 0, 0))],
        name="token_grad",
    )[0]


def across_kernel(meta, g2, w, got, across):
    across[0] = (dot_bt(g2[0], w[...]) + got[0, 0].astype(F32)).astype(BF16)


def across_call(meta, grads, w, got):
    _, count, rows, width = got.shape
    cols = w.shape[1]
    return run(
        across_kernel,
        (count,),
        meta,
        [
            (grads, (1, rows, cols), lambda b, m: (b, 2, 0)),
            whole(w),
            (got, (1, 1, rows, width), lambda b, m: (1, b, 0, 0)),
        ],
        [((count, rows, width), BF16, (1, rows, width), lambda b, m: (b, 0, 0))],
        name="across",
    )[0]


def last_kernel(meta, tokens, resid_grad, g0, w, got, across, gain, out):
    normed, inverse = standardize(tokens[0].astype(F32))
    grad = dot_bt(g0[0], w[...]) + got[0, 0].astype(F32) + across[0].astype(F32)
    out[0] = resid_grad[0] + norm_back(grad * gain[...], normed, inverse)


def last_call(meta, tokens, resid_grad, grads, w, got, across, gain):
    count, rows, width = tokens.shape
    cols = w.shape[1]
    seq = lambda b, m: (b, 0, 0)
    block = (1, rows, width)
    return run(
        last_kernel,
        (count,),
        meta,
        [
            (tokens, block, seq),
            (resid_grad, block, seq),
            (grads, (1, rows, cols), seq),
            whole(w),
            (got, (1,) + block, lambda b, m: (0, b, 0, 0)),
            (across, block, seq),
            whole(gain),
        ],
        [(tokens.shape, F32, block, seq)],
        cost=(2 * count * rows * width * cols, 20 * count * rows * width, 0),
        name="last",
    )[0]


def pack_in_kernel(meta, proj_in, *refs):
    *vectors, out = refs
    s = meta[0]
    deep, width = proj_in.shape[0], proj_in.shape[1] // 3
    cols = out.shape[1]
    hw = cols // 3
    for k in range(width // hw):

        @pl.when(s == k)
        def _(k=k):
            for t in range(3):
                start = t * width + k * hw
                out[:deep, t * hw : (t + 1) * hw] = proj_in[:, start : start + hw]

    out[deep:] = jnp.zeros((out.shape[0] - deep, cols), BF16)
    steps = vectors.pop()[...][None]
    vectors = [v[...].astype(F32)[None] for v in vectors]
    vectors += [(steps >> 5).astype(F32), (steps & 31).astype(F32)]
    vec = jnp.concatenate(vectors, axis=1)
    size = vec.shape[1]
    for r in range(pl.cdiv(size, cols)):
        width_r = min(cols, size - r * cols)
        out[deep + r : deep + r + 1, :width_r] = vec[:, r * cols : r * cols + width_r].astype(BF16)


def place_in_kernel(sizes, meta, *refs):
    outer = len(refs) - 13
    pieces, odd, rows, refs = refs[:outer], refs[outer], refs[outer + 1], refs[outer + 2 :]
    w, gain, bias, in_b, out_bias, ada_bias, up_b, down_bias, chosen, wanted, table = refs
    ranks = 2 * outer
    s, c, d = meta[0], meta[1], meta[2]
    deep, cols = w.shape[0] // ranks, w.shape[1]
    hw = cols // 3
    for m in range(ranks):
        piece = odd.at[m // 2] if m % 2 else pieces[m // 2]
        owner = d ^ m
        w[pl.ds(pl.multiple_of(owner * deep, deep), deep)] = piece[:deep]
        table[pl.ds(owner, 1)] = piece[deep:].astype(F32)[None]
    used = -(-sum(sizes) // cols)
    flat = [
        jnp.concatenate([table[k, r : r + 1] for r in range(used)], axis=1) for k in range(ranks)
    ]
    full, start = [], 0
    for size in sizes:
        full.append([f[:, start : start + size] for f in flat])
        start += size
    steps = [high * 32.0 + low for high, low in zip(full[7], full[8])]
    full = [jnp.concatenate(x, axis=1) for x in full]
    gain[...], bias[...], out_bias[...], ada_bias[...], down_bias[...] = (
        full[0],
        full[1],
        full[3],
        full[4],
        full[6],
    )
    width = w.shape[0]
    half = sizes[5] // 2
    for k in range(width // hw):

        @pl.when(s == k)
        def _(k=k):
            in_b[...] = jnp.concatenate(
                [full[2][:, t * width + k * hw : t * width + (k + 1) * hw] for t in range(3)], axis=1
            )

    for k in range(2):

        @pl.when(c == k)
        def _(k=k):
            up_b[...] = jnp.concatenate(
                [full[5][:, (2 * n + k) * half : (2 * n + k + 1) * half] for n in range(ranks)],
                axis=1,
            )

    want = jnp.concatenate([x for step in steps for x in (step, jnp.zeros((1, 1), F32))], axis=1)
    wanted[...] = want
    at = d * rows.shape[0] + lax.broadcasted_iota(jnp.int32, (rows.shape[0], 1), 0)
    picked = dot_at((at.astype(F32) == want).astype(BF16), rows[...]).astype(BF16)
    part = rows.shape[1] // ranks
    for k in range(ranks):
        chosen[k] = picked[:, k * part : (k + 1) * part]


def pack_rest_kernel(meta, up, down, proj_out, out):
    c = meta[1]
    deep = up.shape[0]
    width = down.shape[1]
    half = down.shape[0] // 2
    ff = up.shape[1] // 2
    for k in range(2):

        @pl.when(c == k)
        def _(k=k):
            for d in range(ff // half):
                out[:, d * half : (d + 1) * half] = up[:, (2 * d + k) * half : (2 * d + k + 1) * half]
            out[:, ff : ff + width] = down[k * half : k * half + deep]
            out[:, ff + width : ff + 2 * width] = down[k * half + deep : (k + 1) * half]
            out[:, ff + 2 * width :] = proj_out[:, k * width // 2 : (k + 1) * width // 2]


def place_out_kernel(meta, *refs):
    *pieces, out = refs
    d = meta[2]
    deep = out.shape[0] // len(pieces)
    for m, piece in enumerate(pieces):
        out[pl.ds(pl.multiple_of((d ^ m) * deep, deep), deep)] = piece[...]


def place_ff(meta, pieces, up, down):
    d = meta[2]
    deep = up.shape[0] // len(pieces)
    ff, width = up.shape[1], down.shape[1]
    for m, piece in enumerate(pieces):
        owner = d ^ m
        up[pl.ds(pl.multiple_of(owner * deep, deep), deep)] = piece[:, :ff]
        for n in range(2):
            base = pl.multiple_of(owner * (2 * deep) + n * deep, deep)
            down[pl.ds(base, deep)] = piece[:, ff + n * width : ff + (n + 1) * width]


def half_kernel(meta, here, came, *outs):
    o = meta[2] // 2
    for m, out in enumerate(outs):
        at = pl.ds(o ^ m, 1)
        out[...] = (here[at].astype(F32) + came[at].astype(F32))[0].astype(BF16)


def join_kernel(meta, down_here, down_away, out_here, out_came, here, away):
    i = meta[3]
    outer, deep, wide = down_here.shape
    here[:, :, :wide] = down_here[...]
    away[:, :, :wide] = down_away[...]
    for k in range(2 * outer):
        rows = slice(k * deep, (k + 1) * deep)
        value = (out_here[rows].astype(F32) + out_came[rows].astype(F32)).astype(BF16)

        @pl.when(i == k % 2)
        def _(k=k, value=value):
            here[k // 2, :, wide:] = value

        @pl.when(i != k % 2)
        def _(k=k, value=value):
            away[k // 2, :, wide:] = value


def pair_kernel(meta, even, came, *outs):
    for m, out in enumerate(outs):
        out[...] = (even[m].astype(F32) + came[m].astype(F32)).astype(out.dtype)


def pair_call(meta, even, odd):
    outer = even.shape[0]
    pieces = run(
        pair_kernel,
        (1,),
        meta,
        [whole(even), whole(dp_swap(odd, 1))],
        [out_whole(even.shape[1:], even.dtype) for _ in range(outer)],
        name="pair",
    )
    return pieces[0], [pieces[0]] + [dp_swap(p, 2 * m) for m, p in enumerate(pieces) if m]


def total(refs):
    result = 0.0
    for ref in refs:
        for k in range(ref.shape[0] if len(ref.shape) == 3 else 1):
            result = result + (ref[k] if len(ref.shape) == 3 else ref[...]).astype(F32)
    return result


def gather_kernel(counts, meta, *refs):
    *refs, out = refs
    start, place = 0, 0
    for n in counts:
        value = total(refs[start : start + n])
        out[:, place : place + value.shape[1]] = value.astype(BF16)
        start, place = start + n, place + value.shape[1]


def gather_call(meta, groups):
    refs = [x for g in groups for x in g]
    shape = (groups[0][0].shape[-2], sum(g[0].shape[-1] for g in groups))
    return run(
        functools.partial(gather_kernel, tuple(len(g) for g in groups)),
        (1,),
        meta,
        [whole(x) for x in refs],
        [out_whole(shape, BF16)],
        name="gather",
    )[0]


def close_rest_kernel(meta, own, across, pair, up, down, out):
    c = meta[1]
    deep = own.shape[0]
    width = out.shape[1]
    half = down.shape[0] // 2
    ff = up.shape[1] // 2
    mine = own[...].astype(F32) + across[...].astype(F32)
    other = pair[0].astype(F32) + pair[1].astype(F32)
    for k in range(2):
        value = jnp.where(c == k, mine, other)
        for d in range(ff // half):
            up[:, (2 * d + k) * half : (2 * d + k + 1) * half] = value[:, d * half : (d + 1) * half]
        down[k * half : k * half + deep] = value[:, ff : ff + width]
        down[k * half + deep : (k + 1) * half] = value[:, ff + width : ff + 2 * width]
        out[:, k * width // 2 : (k + 1) * width // 2] = value[:, ff + 2 * width :]


def close_in_kernel(ranks, meta, own, across, beside, beyond, w, gain, bias, in_bias, out_bias, up_bias, down_bias, held):
    s, d = meta[0], meta[2]
    deep, width = w.shape[0], w.shape[1] // 3
    cols = own.shape[1]
    hw = cols // 3
    held[pl.ds(s, 1)] = own[...].astype(F32)[None]
    held[pl.ds(s ^ 2, 1)] = across[...].astype(F32)[None]
    held[pl.ds(s ^ 1, 1)] = beside[...].astype(F32)[None]
    held[pl.ds(s ^ 3, 1)] = beyond[...].astype(F32)[None]
    for k in range(4):
        for t in range(3):
            w[:, t * width + k * hw : t * width + (k + 1) * hw] = held[k, :deep, t * hw : (t + 1) * hw]
    rows = [
        jnp.concatenate([held[k, deep + r : deep + r + 1] for r in range(EXTRA)], axis=1)
        for k in range(4)
    ]
    biases = jnp.concatenate(
        [rows[k][:, t * hw : (t + 1) * hw] for t in range(3) for k in range(4)], axis=1
    )
    ff = 2 * width
    ups = [rows[0][:, cols : cols + ff] + rows[2][:, cols : cols + ff]]
    ups.append(rows[1][:, cols : cols + ff] + rows[3][:, cols : cols + ff])
    rest = rows[0] + rows[1] + rows[2] + rows[3]
    rest = rest[:, cols + ff :]
    part, third, half = width // ranks, 3 * width // ranks, ff // ranks
    for k in range(ranks):

        @pl.when(d == k)
        def _(k=k):
            for n, out in enumerate((gain, bias, out_bias, down_bias)):
                out[...] = rest[0, n * width + k * part : n * width + (k + 1) * part]
            in_bias[...] = biases[0, k * third : (k + 1) * third]
            up_bias[...] = jnp.concatenate([u[:, k * half : (k + 1) * half] for u in ups], axis=1)[0]


def shards(
    tokens,
    prefix_len,
    timestep,
    norm_gain,
    norm_bias,
    proj_in,
    proj_in_bias,
    proj_out,
    proj_out_bias,
    time_table,
    ada_weight,
    ada_bias,
    mlp_up,
    mlp_up_bias,
    mlp_down,
    mlp_down_bias,
    out_grad,
):
    count, local_len, width = tokens.shape
    members = lax.axis_size("seq")
    ranks = lax.axis_size("dp")
    s = lax.axis_index("seq")
    d = lax.axis_index("dp")
    hw = H // members * HD
    deep = proj_in.shape[0]
    half_ff = mlp_down.shape[0] // 2
    ff = ranks * half_ff
    half_out = width // 2
    meta = jnp.concatenate([jnp.stack([s, s % 2, d, d % 2]).astype(jnp.int32), prefix_len])

    tok_x = seq_swap(tokens, 2)

    half_width = HD // 2
    frequency = np.exp(np.arange(half_width) * (-math.log(10000.0) / half_width))
    angles = np.arange(local_len)[:, None] * frequency[None, :]
    cos_in, sin_in = (jnp.asarray(f(angles), F32)[None] for f in (np.cos, np.sin))
    starts = (jnp.stack([s ^ j for j in range(members)]) * local_len).astype(F32)
    starts = starts[:, None] * jnp.asarray(frequency, F32)[None, :]
    cos_at, sin_at = jnp.cos(starts)[:, None], jnp.sin(starts)[:, None]
    cosine = (cos_at * cos_in - sin_at * sin_in).reshape(-1, half_width)
    sine = (sin_at * cos_in + cos_at * sin_in).reshape(-1, half_width)
    cosine = jnp.concatenate([cosine] * 4, axis=1)
    sine = jnp.concatenate([-sine, sine] * 2, axis=1)

    vectors = [
        norm_gain,
        norm_bias,
        proj_in_bias,
        proj_out_bias,
        ada_bias,
        mlp_up_bias,
        mlp_down_bias,
        timestep,
    ]
    sizes = tuple(v.shape[0] for v in (*vectors, timestep))
    pack_in = run(
        pack_in_kernel,
        (1,),
        s.astype(jnp.int32)[None],
        [whole(proj_in), *(whole(v) for v in vectors)],
        [out_whole((deep + EXTRA, 3 * hw), BF16)],
        name="pack_in",
    )[0]
    in_even = [pack_in] + [dp_swap(pack_in, m) for m in range(2, ranks, 2)]
    pack_rest = run(
        pack_rest_kernel,
        (1,),
        meta,
        [whole(after(mlp_up, pack_in)), whole(mlp_down), whole(proj_out)],
        [out_whole((deep, ff + 2 * width + half_out), BF16)],
        name="pack_rest",
    )[0]
    in_even = after(in_even, pack_rest, cosine, sine)
    in_stack = jnp.stack(in_even)
    in_odd = dp_swap(in_stack, 1)
    tok_c = seq_swap(after(tokens, in_stack), 1)
    kinds = count + 1
    in_w, gain, bias, in_b, out_bias, ada_bias_full, up_b, down_bias, chosen, wanted = run(
        functools.partial(place_in_kernel, sizes),
        (1,),
        meta,
        [whole(x) for x in (*in_even, in_odd, time_table)],
        [
            out_whole((width, 3 * hw), BF16),
            out_whole((1, width), F32),
            out_whole((1, width), F32),
            out_whole((1, 3 * hw), F32),
            out_whole((1, width), F32),
            out_whole((1, 3 * width), F32),
            out_whole((1, ff), F32),
            out_whole((1, width), F32),
            out_whole((ranks, ranks * kinds, width // ranks), BF16),
            out_whole((1, ranks * kinds), F32),
        ],
        scratch=[pltpu.VMEM((ranks, EXTRA, 3 * hw), F32)],
        name="place_in",
    )
    chosen_got = dp_turn(chosen)

    outer = ranks // 2
    early = max(1, outer // 4)
    one, two = slice(1, 1 + early), slice(1 + early, 1 + 2 * early)
    three = slice(1 + 2 * early, outer)
    rest_even = [pack_rest] + [
        dp_swap(after(pack_rest, in_even) if m > early else pack_rest, 2 * m)
        for m in range(1, 1 + 2 * early)
    ]
    rest_odd = [dp_swap(after(pack_rest, in_w), 1)]

    cosine_near = cosine
    qkv_near = qkv_call(meta, 0, tokens, tok_c, gain, bias, in_w, in_b, cosine_near, sine)
    rest_even += [
        dp_swap(after(pack_rest, qkv_near), 2 * m) for m in range(1 + 2 * early, outer)
    ]
    rest_even[one] = after(rest_even[one], qkv_near)
    rest_odd += [dp_swap(piece, 1) for piece in rest_even[one]]
    tok_x = after(tok_x, in_stack)
    tok_d = seq_swap(tok_x, 1)
    qkv_far = qkv_call(meta, 2, tok_x, tok_d, gain, bias, in_w, in_b, after(cosine, qkv_near, rest_odd[0]), sine)
    near_again = after(qkv_near, rest_even[two])
    rest_even[two] = after(rest_even[two], qkv_far)
    rest_odd += [dp_swap(piece, 1) for piece in rest_even[two]]
    mixed_2, mixed_3, weights, recips = attend_call(meta, 2, near_again, qkv_far, local_len)
    across_2, across_3 = seq_swap(mixed_2, 2), seq_swap(mixed_3, 3)
    embedded = jnp.sum(after(chosen_got, mixed_2).astype(F32), axis=0)
    activated = jax.nn.silu(embedded).astype(BF16)
    mod_parts = dot(activated, ada_weight).reshape(ranks, kinds, 3 * width)
    mod_got = dp_turn(mod_parts)
    near_again = after(
        qkv_near, mixed_2, mod_parts, rest_odd[one], rest_odd[two], rest_even[three]
    )
    rest_even[three] = after(rest_even[three], mixed_2)
    rest_odd += [dp_swap(piece, 1) for piece in rest_even[three]]
    mixed_0, mixed_1, weights, recips = attend_call(
        meta, 0, near_again, qkv_far, local_len, (weights, recips)
    )
    mixed = [mixed_0, mixed_1, mixed_2, mixed_3]
    mixed_own = [mixed_0, seq_swap(mixed_1, 1), across_2, across_3]
    mods = jnp.sum(after(mod_got, mixed_0), axis=0) + ada_bias_full
    pieces = [
        x for pair in zip([after(pack_rest, mixed_0), *rest_even[1:]], rest_odd) for x in pair
    ]
    last_cols = (ff + 2 * width) // half_out
    out_own = run(
        place_out_kernel,
        (1,),
        meta,
        [(x, (deep, half_out), lambda i, m: (0, last_cols)) for x in pieces],
        [out_whole((width, half_out), BF16)],
        name="place_out",
    )[0]
    out_other = seq_swap(out_own, 1)
    og_other = seq_swap(after(out_grad, out_own), 1)

    residual, mlp_own, out_rel = mix_call(
        meta, mixed_own, tokens, out_own, out_other, out_bias, mods
    )
    mlp_other = seq_swap(mlp_own, 1)
    own_branch, own_input, other, up_here, up_away, down_here, down_away, up_bias_part = mlp_call(
        meta, mlp_own, mlp_other, out_grad, og_other, pieces, up_b, mods
    )
    got = seq_swap(other, 1)
    up_came = dp_swap(up_away, 1)
    block_out, resid_grad, *others = turn_call(
        meta, residual, out_grad, own_branch, own_input, got, down_bias, mods, mixed_own, out_rel
    )
    grads_sent, (biases, out_here) = others[:4], others[4:]
    head_grads = [grads_sent[0]] + [seq_swap(grads_sent[j], j) for j in (1, 2, 3)]

    def halves(here, came):
        return run(
            half_kernel,
            (1,),
            meta,
            [whole(here), whole(came)],
            [out_whole(here.shape[1:], BF16) for _ in range(outer)],
            name="half",
        )

    def spread(pieces):
        return [pieces[0]] + [dp_swap(p, 2 * m) for m, p in enumerate(pieces) if m]

    joined = (outer, deep, ff + half_out)
    down_here, down_away = run(
        join_kernel,
        (1,),
        meta,
        [
            whole(down_here),
            whole(down_away),
            whole(out_here),
            (head_grads[1], (width, half_out), lambda i, m: (0, 0)),
        ],
        [out_whole(joined, BF16), out_whole(joined, BF16)],
        name="join",
    )
    down_came = dp_swap(down_away, 1)
    up_half = halves(after(up_here, down_away), up_came)
    up_got = spread(after(up_half, head_grads))

    raw = back_call(
        meta, 0, count, after(qkv_near, up_half), qkv_far, weights, recips, mixed, head_grads
    )
    down_half = halves(after(down_here, raw), down_came)
    down_got = spread(down_half)
    row_grad = run(
        rows_kernel,
        (1,),
        meta,
        [
            (g, (ROWS, g.shape[1]), lambda i, m, n=g.shape[0] // ROWS - 1: (n, 0))
            for g in after(head_grads, down_half)
        ],
        [out_whole((kinds, 3 * width), F32)],
        name="rows",
    )[0]
    rows_got = dp_all(row_grad)
    grads, in_even, in_odd = proj_grad_call(
        meta,
        (tokens, tok_c, tok_x, tok_d),
        after(raw, down_half, up_got, row_grad),
        in_w,
        gain,
        bias,
        up_bias_part,
        biases,
        cosine,
        sine,
        ranks,
    )
    in_came = dp_swap(in_odd, 1)
    sent = token_grad_call(meta, grads, in_w, tokens.shape)
    rest_sum = gather_call(meta, [up_got, after(down_got, sent, rows_got)])
    came = seq_swap(after(sent, rest_sum), 1)
    rest_x = seq_swap(rest_sum, 2)
    across = across_call(meta, after(grads, rest_sum), in_w, came)
    across_got = seq_swap(across, 2)

    exact = functools.partial(lax.dot_general, precision=HIGHEST, preferred_element_type=F32)
    all_rows = after(rows_got, across).reshape(ranks * kinds, 3 * width)
    act_rows_grad = exact(all_rows, ada_weight.astype(F32), (((1,), (1,)), ((), ())))
    embed_grad = jax.vjp(jax.nn.silu, embedded)[1](act_rows_grad)[0]
    ada_bias_grad = lax.dynamic_slice_in_dim(
        jnp.sum(all_rows, axis=0), d * ada_bias.shape[0], ada_bias.shape[0], 0
    )
    ada_grad = exact(activated.astype(F32), all_rows, (((0,), (0,)), ((), ())))
    in_pieces = run(
        pair_kernel,
        (1,),
        meta,
        [whole(after(in_even, across, embed_grad, ada_grad, ada_bias_grad)), whole(in_came)],
        [out_whole(in_even.shape[1:], BF16) for _ in range(outer)],
        name="pair",
    )
    in_got = spread(in_pieces)
    rest_x = after(rest_x, in_pieces[0])
    rest_pair = seq_swap(jnp.stack([rest_sum, rest_x]), 1)
    up_final, down_final, out_final = run(
        close_rest_kernel,
        (1,),
        meta,
        [whole(x) for x in (after(rest_sum, in_pieces[0]), rest_x, rest_pair)],
        [
            out_whole(mlp_up.shape, F32),
            out_whole(mlp_down.shape, F32),
            out_whole(proj_out.shape, F32),
        ],
        name="close_rest",
    )

    in_sum = gather_call(meta, [after(in_got, ada_bias_grad, ada_grad, up_final)])
    in_parts = [in_sum] + [seq_swap(in_sum, j) for j in (2, 1, 3)]
    embed_got = dp_all(after(embed_grad, up_final))
    tokens_grad = last_call(
        meta, tokens, after(resid_grad, in_sum), grads, in_w, came, across_got, gain
    )
    embed_all = after(embed_got, tokens_grad).transpose(1, 0, 2).reshape(ranks * kinds, width)
    table_at = d * time_table.shape[0] + jnp.arange(time_table.shape[0], dtype=jnp.int32)
    selector = (table_at.astype(F32)[:, None] == wanted).astype(F32)
    table_grad = exact(selector, embed_all, (((1,), (0,)), ((), ())))
    part, third, ff_part = width // ranks, 3 * width // ranks, 4 * width // ranks
    in_final, gain_f, bias_f, in_bias_f, out_bias_f, up_bias_f, down_bias_f = run(
        functools.partial(close_in_kernel, ranks),
        (1,),
        meta,
        [whole(x) for x in in_parts],
        [
            out_whole(proj_in.shape, F32),
            out_whole((part,), F32),
            out_whole((part,), F32),
            out_whole((third,), F32),
            out_whole((part,), F32),
            out_whole((ff_part,), F32),
            out_whole((part,), F32),
        ],
        scratch=[pltpu.VMEM((members, deep + EXTRA, 3 * hw), F32)],
        name="close_in",
    )
    return (
        block_out,
        tokens_grad,
        gain_f.reshape(-1),
        bias_f.reshape(-1),
        in_final,
        in_bias_f.reshape(-1),
        out_final,
        out_bias_f.reshape(-1),
        table_grad,
        ada_grad,
        ada_bias_grad,
        up_final,
        up_bias_f.reshape(-1),
        down_final,
        down_bias_f.reshape(-1),
    )


def solution(mesh):
    rows = P("dp", None)
    vector = P("dp")
    stream = P("dp", "seq", None)
    in_specs = (
        stream,
        vector,
        vector,
        vector,
        vector,
        rows,
        vector,
        rows,
        vector,
        rows,
        rows,
        vector,
        rows,
        vector,
        rows,
        vector,
        stream,
    )
    out_specs = (
        stream,
        stream,
        vector,
        vector,
        rows,
        vector,
        rows,
        vector,
        rows,
        rows,
        vector,
        rows,
        vector,
        rows,
        vector,
    )
    return jax.shard_map(shards, mesh=mesh, in_specs=in_specs, out_specs=out_specs, check_vma=False)
```
